32 devices in a mesh: dev: 32 (over z, y, x, core).
Axes of the slice: x: 2, y: 2, z: 4, core: 2. Of those that a mesh axis runs over, the one named last changes fastest.
Arguments:
- inputs: bfloat16 [65536, 227], P('dev'), may hold values from -6 to 6
- targets: float32 [65536, 227], P('dev'), may hold values from -6 to 6
- geometry: bfloat16 [8192, 4], P('dev'), may hold values from -6 to 6
- land_sea: int32 [65536], P('dev'), may hold values 0 or 1
- level_mask: int32 [65536, 227], P('dev'), may hold values from 0 to 1
- edge_owners: int32 [8192, 2], P('dev'), may hold values from 0 to 31, all different within a row; in each aligned block of 256 rows (0 to 255, 256 to 511, ...) at most 20 rows name the same one
- edge_local: int32 [8192, 2], P('dev'), may hold values from 0 to 2047
- step_count: int32 [1], replicated, may hold values from 1 to 20
- master: float32 [6545408], P('dev'), as said below
- first_moment: float32 [6545408], P('dev'), as said below
- second_moment: float32 [6545408], P('dev'), as said below
- ema: float32 [6545408], P('dev'), as said below
Outputs:
- new_master: float32 [6545408], P('dev')
- new_first: float32 [6545408], P('dev')
- new_second: float32 [6545408], P('dev')
- new_ema: float32 [6545408], P('dev')
- loss: float32 [], replicated
- grad_norm: float32 [], replicated
The draws below stay inside these ranges and needn't reach their ends.
Inputs may be any that keep to these rules, and one draw needn't show every extreme that they name: `edge_owners`: the two columns of a row differ; within the rows of one device no device is named more than 20 times, and some device is named exactly 20 times. `master`: Finite, of the size of fan-in scaled weights, gains near 1. `first_moment`: Finite, both signs. `second_moment`: Positive. `ema`: Finite, of the size of fan-in scaled weights, gains near 1.
All inputs are finite; a program needn't handle non-finite values. No bound on the sum of `land_sea` on one device may be relied on, other than what follows from the above.
Results may differ from the reference program's by a relative error of at most 0.00045.
The reference program's roundings to bfloat16 on the way count: a program that leaves them out, or rounds other values in their place, can miss the bound.
Values may be sent and summed in bfloat16 or wider, within the bound.
A program may use at most 192 MiB of HBM per device.

```python
import math
import jax
import jax.numpy as jnp
import numpy as np
from jax import lax

LATENT = 512
VARS = 227
GEO = 4
SEA_VARS = 4
LAYERS = 3
NODES_DEV = 2048
EDGES_DEV = 256
NODES = 65536
EDGES = 8192
CAP = 20
PARAMS = 6545408
N_DEV = 32


def layout_drawn(width, variables, geometry, layers):
    shapes = [(variables, width, True), (geometry, width, True)]
    for k in range(layers):
        shapes.append((3 * width, width, True))
        shapes.append((2 * width, width, True))
    shapes.append((width, variables, False))
    segments = []
    offset = 0
    for block_id, (fan_in, fan_out, normed) in enumerate(shapes):
        members = [('w_in', (fan_in, width)), ('b_in', (width,)), ('w_out', (width, fan_out)), ('b_out', (fan_out,))]
        if normed:
            members = members + [('gain', (fan_out,)), ('shift', (fan_out,))]
        for part_name, part_shape in members:
            entries = int(np.prod(part_shape))
            segments.append((block_id, part_name, part_shape, offset, entries))
            offset += entries
    return (segments, offset)


def weights_draw(key):
    segments, total = layout_drawn(LATENT, VARS, GEO, LAYERS)
    pieces = []
    for number, (block_id, part_name, part_shape, offset, entries) in enumerate(segments):
        sub_key = jax.random.fold_in(key, number)
        if part_name == 'w_in' or part_name == 'w_out':
            values = jax.random.truncated_normal(sub_key, -4.0, 4.0, (entries,), jnp.float32) / math.sqrt(part_shape[0])
        elif part_name == 'gain':
            values = 1.0 + 0.3 * jax.random.uniform(sub_key, (entries,), jnp.float32, -1.0, 1.0)
        else:
            values = 0.3 * jax.random.truncated_normal(sub_key, -4.0, 4.0, (entries,), jnp.float32)
        pieces.append(values)
    pieces.append(jnp.zeros((PARAMS - total,), jnp.float32))
    return jnp.concatenate(pieces)


def grad_scale():
    return 0.01 / math.sqrt(PARAMS)


def draw_master(key, part):
    return weights_draw(jax.random.fold_in(key, 101))


def draw_ema(key, part):
    return weights_draw(jax.random.fold_in(key, 202))


def draw_first_moment(key, part):
    values = jax.random.truncated_normal(jax.random.fold_in(key, 303), -4.0, 4.0, (PARAMS,), jnp.float32)
    return values * (0.111 * grad_scale())


def draw_second_moment(key, part):
    spread = jax.random.uniform(jax.random.fold_in(key, 404), (PARAMS,), jnp.float32, 0.0, math.log(4.0))
    return jnp.exp(spread) * (0.001001 * grad_scale() * grad_scale())


def draw_level_mask(key, part):
    node_ids = jnp.arange(NODES, dtype=jnp.int32)[:, None]
    threshold = 300 + 600 * node_ids // NODES
    rolls = jax.random.randint(jax.random.fold_in(key, 505), (NODES, VARS), 0, 1000, dtype=jnp.int32)
    return (rolls < threshold).astype(jnp.int32)


def set_ends(values, own_key, low, largest):
    longest = values.shape.index(max(values.shape))
    spots = []
    for shift in (0, 1):
        where = [jax.random.randint(jax.random.fold_in(own_key, axis), (), 0, length) for axis, length in enumerate(values.shape)]
        where[longest] = (where[longest] + shift) % values.shape[longest]
        spots.append(tuple(where))
    return values.at[spots[0]].set(low).at[spots[1]].set(largest)


def level_of(key, dims, split, low, high):
    loudness, own = 1.0, jax.random.fold_in(key, 6)
    for axis_at, parts in split:
        draws = jnp.exp(jax.random.uniform(jax.random.fold_in(own, axis_at), (parts,), jnp.float32, low / len(split), high / len(split)))
        loudness = loudness * jnp.repeat(draws, dims[axis_at] // parts).reshape([-1 if axis == axis_at else 1 for axis in range(len(dims))])
    return loudness


def routed_block(rng, own, number, rows, amount, top, bound, slope):
    sequence = jax.random.permutation(rng, amount)
    heavy_load, ordinary = shares(amount, rows * top, bound, slope, True), shares(amount, rows * top, bound, slope, False)
    places = jnp.arange(amount)

    def named(lengths, rotation):
        used = int((lengths > 0).sum())
        fixed = max(1, used // 4)
        shifted = fixed + (places - fixed + rotation * (used - fixed)) % max(1, amount - fixed)
        return jnp.zeros((amount,), jnp.int32).at[sequence[jnp.where(places < fixed, places, shifted)]].set(jnp.asarray(lengths, jnp.int32))

    lengths = jnp.where(number % 4 == 0, named(heavy_load, number // 4), named(ordinary, number - number // 4 - 1))
    mixed = jax.random.permutation(jax.random.fold_in(own, 3), amount)
    source_of, sink = mixed[0:amount // 2 * 2:2], mixed[1:amount // 2 * 2:2]
    margin = jnp.minimum(lengths[source_of] - 1, bound - lengths[sink]) // 2
    margin = jnp.where((source_of == sequence[0]) | (sink == sequence[0]) | (lengths[sink] == 0), 0, jnp.maximum(margin, 0))
    shifted = jax.random.randint(jax.random.fold_in(own, 4), (amount // 2,), 0, 1 << 20) % (margin + 1)
    lengths = lengths.at[source_of].add(-shifted).at[sink].add(shifted)
    items = jnp.searchsorted(jnp.cumsum(lengths), jnp.arange(rows * top), side="right").astype(jnp.int32)
    table = items.reshape(top, rows).T
    table = table[jax.random.permutation(jax.random.fold_in(own, 1), rows)]
    rotation = jax.random.randint(jax.random.fold_in(own, 2), (rows, 1), 0, top)
    return jnp.take_along_axis(table, (jnp.arange(top)[None, :] + rotation) % top, axis=1)


def shares(count, total, bound, skew, full):
    weights = [(1 << 20) // math.isqrt(standing ** skew) + 1 for standing in range(1, count + 1)]
    largest = bound if full else min(bound, max(-(-total // count), total * weights[0] // sum(weights)))
    least = 1 if total - largest >= count - 1 else 0
    counts, surplus = [largest] + [least] * (count - 1), total - largest - least * (count - 1)
    while surplus > 0:
        free = [i for i in range(1, count) if counts[i] < largest] or [i for i in range(1, count) if counts[i] < bound]
        pool, left = sum([weights[i] for i in free]), surplus
        for i in free:
            more = min(bound - counts[i], max(1, left * weights[i] // pool), surplus)
            counts[i] = counts[i] + more
            surplus = surplus - more
    return np.array(counts)


def noise(own_key, extent, scale, bound, cuts=(), held_as=jnp.bfloat16):
    array = scale * jax.random.normal(own_key, extent, jnp.float32)
    if cuts:
        array = array * level_of(own_key, extent, cuts, -0.22, 0.18)
    return jnp.clip(array, -bound, bound).astype(held_as)


def setup_inputs(seed: int = 0) -> dict:
    streams_of = jax.random.split(jax.random.key(seed), 13)
    inputs = noise(streams_of[0], (NODES, VARS), 1.0, 6.0, ((0, 32),))
    targets = noise(streams_of[1], (NODES, VARS), 1.0, 6.0, ((0, 32),), jnp.float32)
    geometry = noise(streams_of[2], (EDGES, GEO), 1.0, 6.0, ((0, 32),))
    land_sea = set_ends((jax.random.randint(streams_of[3], (NODES,), 0, 10) < 3).astype(jnp.int32), jax.random.fold_in(streams_of[3], 1), 0, 1)
    level_mask = draw_level_mask(jax.random.fold_in(streams_of[12], 71), 0)
    edge_owners_keys = jax.random.split(jax.random.fold_in(streams_of[5], 1), EDGES // EDGES_DEV)
    edge_owners_turns = jax.random.permutation(jax.random.fold_in(streams_of[5], 3), EDGES // EDGES_DEV)
    edge_owners = jax.vmap(lambda own, number: routed_block(jax.random.fold_in(streams_of[5], 2), own, number, EDGES_DEV, N_DEV, 2, CAP, 2))(edge_owners_keys, edge_owners_turns).reshape((EDGES, 2))
    edge_local = set_ends(jax.random.randint(streams_of[6], (EDGES, 2), 0, NODES_DEV), jax.random.fold_in(streams_of[6], 1), 0, NODES_DEV - 1).astype(jnp.int32)
    step_count = jax.random.randint(streams_of[7], (1,), 1, 21).astype(jnp.int32)
    master = draw_master(jax.random.fold_in(streams_of[12], 71), 0)
    first_moment = draw_first_moment(jax.random.fold_in(streams_of[12], 71), 0)
    second_moment = draw_second_moment(jax.random.fold_in(streams_of[12], 71), 0)
    ema = draw_ema(jax.random.fold_in(streams_of[12], 71), 0)
    return {"inputs": inputs, "targets": targets, "geometry": geometry, "land_sea": land_sea, "level_mask": level_mask, "edge_owners": edge_owners, "edge_local": edge_local, "step_count": step_count, "master": master, "first_moment": first_moment, "second_moment": second_moment, "ema": ema}


norm_eps = 1e-05
clip_limit = 0.01
beta_one = 0.9
beta_two = 0.999
adam_eps = 1e-08
learn_rate = 0.03
decay_rate = 0.1
ema_keep = 0.9

@jax.custom_vjp
def low(v):
    return lax.optimization_barrier(v.astype(jnp.bfloat16)).astype(jnp.float32)

@jax.custom_vjp
def low_back(v):
    return v

def low_keep(v):
    return (low(v), None)

def low_pass(kept, grad):
    return (grad,)

def back_keep(v):
    return (v, None)

def back_low(kept, grad):
    return (low(grad),)
low.defvjp(low_keep, low_pass)
low_back.defvjp(back_keep, back_low)

def layout(width, variables, geometry, layers):
    shapes = [(variables, width, True), (geometry, width, True)]
    for k in range(layers):
        shapes.append((3 * width, width, True))
        shapes.append((2 * width, width, True))
    shapes.append((width, variables, False))
    segments = []
    offset = 0
    for block_id, (fan_in, fan_out, normed) in enumerate(shapes):
        members = [('w_in', (fan_in, width)), ('b_in', (width,)), ('w_out', (width, fan_out)), ('b_out', (fan_out,))]
        if normed:
            members = members + [('gain', (fan_out,)), ('shift', (fan_out,))]
        for part_name, part_shape in members:
            entries = int(np.prod(part_shape))
            segments.append((block_id, part_name, part_shape, offset, entries))
            offset += entries
    return (segments, offset)

def unpack(flat, segments):
    blocks = [dict() for k in range(segments[-1][0] + 1)]
    for block_id, part_name, part_shape, offset, entries in segments:
        blocks[block_id][part_name] = flat[offset:offset + entries].reshape(part_shape)
    return blocks

def apply_mlp(params, source):
    pre = low_back(jnp.dot(source, params['w_in'], precision=lax.Precision.HIGHEST) + params['b_in'])
    act = low(jax.nn.silu(pre))
    post = low_back(jnp.dot(act, params['w_out'], precision=lax.Precision.HIGHEST) + params['b_out'])
    if 'gain' in params:
        centred = post - lax.optimization_barrier(jnp.mean(post, axis=-1, keepdims=True))
        inv_std = lax.rsqrt(lax.optimization_barrier(jnp.mean(centred * centred, axis=-1, keepdims=True)) + norm_eps)
        return centred * inv_std * params['gain'] + params['shift']
    return post

def reference(inputs, targets, geometry, land_sea, level_mask, edge_owners, edge_local, step_count, master, first_moment, second_moment, ema):
    segments, total = layout(LATENT, VARS, GEO, LAYERS)
    senders = (edge_owners[:, 0] * NODES_DEV + edge_local[:, 0]).astype(jnp.int32)
    receivers = (edge_owners[:, 1] * NODES_DEV + edge_local[:, 1]).astype(jnp.int32)
    ocean = (jnp.arange(VARS) < SEA_VARS).astype(jnp.float32)
    mask = level_mask.astype(jnp.float32) * (1.0 - land_sea.astype(jnp.float32)[:, None] * ocean[None, :])
    state = inputs.astype(jnp.float32)
    geo_rows = geometry.astype(jnp.float32)

    def loss_of(flat):
        blocks = unpack(low(flat), segments)
        node = apply_mlp(blocks[0], state)
        edge = apply_mlp(blocks[1], geo_rows)
        for k in range(LAYERS):
            node_low = low(node)
            from_send = low_back(node_low[senders])
            from_recv = low_back(node_low[receivers])
            edge_in = jnp.concatenate([low(edge), from_send, from_recv], axis=1)
            edge = edge + apply_mlp(blocks[2 + 2 * k], edge_in)
            summed = jax.ops.segment_sum(low(edge), receivers, num_segments=NODES)
            node_in = jnp.concatenate([node_low, low(low_back(summed))], axis=1)
            node = node + apply_mlp(blocks[3 + 2 * k], node_in)
        pred = state + apply_mlp(blocks[2 + 2 * LAYERS], low(node))
        count = jnp.sum(mask)
        return jnp.sum(mask * (pred - targets) ** 2) / jnp.maximum(count, 1.0)
    loss, pull = jax.vjp(loss_of, master)
    gradient, = pull(jnp.ones_like(loss))
    grad_norm = jnp.sqrt(jnp.sum(gradient * gradient))
    clipped = gradient * jnp.minimum(1.0, clip_limit / grad_norm)
    step = step_count[0].astype(jnp.float32)
    new_first = beta_one * first_moment + (1.0 - beta_one) * clipped
    new_second = beta_two * second_moment + (1.0 - beta_two) * clipped * clipped
    first_hat = new_first / (1.0 - beta_one ** step)
    second_hat = new_second / (1.0 - beta_two ** step)
    new_master = master - learn_rate * (first_hat / (jnp.sqrt(second_hat) + adam_eps) + decay_rate * master)
    new_ema = ema_keep * ema + (1.0 - ema_keep) * new_master
    return (new_master, new_first, new_second, new_ema, loss, grad_norm)
```

```python
import functools

import jax
import jax.numpy as jnp
import numpy as np
from jax import lax
from jax.experimental import pallas as pl
from jax.experimental.pallas import tpu as pltpu
from jax.sharding import PartitionSpec as P

LATENT = 512
VARS = 227
GEO = 4
SEA_VARS = 4
LAYERS = 3
PARAMS = 6545408


norm_eps = 1e-05
clip_limit = 0.01
beta_one = 0.9
beta_two = 0.999
adam_eps = 1e-08
learn_rate = 0.03
decay_rate = 0.1
ema_keep = 0.9


def layout(width, variables, geometry, layers):
    shapes = [(variables, width, True), (geometry, width, True)]
    for k in range(layers):
        shapes.append((3 * width, width, True))
        shapes.append((2 * width, width, True))
    shapes.append((width, variables, False))
    segments = []
    offset = 0
    for block_id, (fan_in, fan_out, normed) in enumerate(shapes):
        members = [
            ("w_in", (fan_in, width)),
            ("b_in", (width,)),
            ("w_out", (width, fan_out)),
            ("b_out", (fan_out,)),
        ]
        if normed:
            members = members + [("gain", (fan_out,)), ("shift", (fan_out,))]
        for part_name, part_shape in members:
            entries = int(np.prod(part_shape))
            segments.append((block_id, part_name, part_shape, offset, entries))
            offset += entries
    return (segments, offset)


def unpack(flat, segments):
    blocks = [dict() for k in range(segments[-1][0] + 1)]
    for block_id, part_name, part_shape, offset, entries in segments:
        blocks[block_id][part_name] = flat[offset : offset + entries].reshape(part_shape)
    return blocks


MESH = pl.DeviceIdType.MESH

def remote(src, dst, send, recv, target):
    return pltpu.make_async_remote_copy(src, dst, send, recv, device_id=(target,), device_id_type=MESH)

def greet(n, me):
    barrier = pltpu.get_barrier_semaphore()
    def hello(j, c):
        pl.semaphore_signal(barrier, inc=1, device_id=(lax.rem(me + j, n),), device_id_type=MESH)
        return c
    lax.fori_loop(1, n, hello, 0)
    pl.semaphore_wait(barrier, n - 1)

def a2a_kernel(n, a_ref, o_ref, own, ssem, rsem):
    me = lax.axis_index('dev')
    greet(n, me)
    here = pltpu.make_async_copy(a_ref.at[me], o_ref.at[me], own)
    here.start()
    def go(j, c):
        t = lax.rem(me + j, n)
        remote(a_ref.at[t], o_ref.at[me], ssem.at[j], rsem.at[j], t).start()
        return c
    lax.fori_loop(1, n, go, 0)
    def end(j, c):
        t = lax.rem(me + j, n)
        remote(a_ref.at[t], o_ref.at[me], ssem.at[j], rsem.at[j], t).wait()
        return c
    lax.fori_loop(1, n, end, 0)
    here.wait()

def a2a(x, cid, space=pl.ANY):
    n = x.shape[0]
    return pl.pallas_call(
        functools.partial(a2a_kernel, n),
        out_shape=jax.ShapeDtypeStruct(x.shape, x.dtype),
        in_specs=[pl.BlockSpec(memory_space=space)],
        out_specs=pl.BlockSpec(memory_space=space),
        scratch_shapes=[pltpu.SemaphoreType.DMA, pltpu.SemaphoreType.DMA((n,)), pltpu.SemaphoreType.DMA((n,))],
        compiler_params=pltpu.CompilerParams(collective_id=cid, has_side_effects=True),
    )(x)

def gather_kernel(w_ref, ask_ref, num_ref, o_ref, served_ref, nums_ref, own, small_s, small_r, zs, zr, hs, hr, cs, cr, ds, dr, bs, br):
    n = 32
    me = lax.axis_index('dev')
    c, x, y, z = lax.rem(me, 2), lax.rem(me // 2, 2), lax.rem(me // 4, 2), me // 8
    rows = w_ref.shape[0]
    half = rows // 2
    A, B = pl.ds(0, half), pl.ds(half, half)
    def dev(z, y, x, c):
        return ((z * 2 + y) * 2 + x) * 2 + c
    greet(n, me)
    tx, ty, tc = dev(z, y, 1 - x, c), dev(z, 1 - y, x, c), dev(z, y, x, 1 - c)
    pend = []
    def start(cp):
        cp.start(); pend.append(cp)
    mine = pltpu.make_async_copy(w_ref, o_ref.at[me], own.at[0])
    mine.start()
    start(remote(w_ref.at[A], o_ref.at[me, A], hs.at[0, 0], hr.at[0, 0], tx))
    start(remote(w_ref.at[B], o_ref.at[me, B], hs.at[0, 1], hr.at[0, 1], ty))
    for j in (1, 3, 2):
        start(remote(w_ref, o_ref.at[me], zs.at[j], zr.at[4 - j], dev(lax.rem(z + j, 4), y, x, c)))
    start(remote(w_ref, o_ref.at[me], bs.at[0], br.at[0], tc))
    mine2 = pltpu.make_async_copy(ask_ref.at[me], served_ref.at[me], own.at[1])
    mine2.start()
    mine3 = pltpu.make_async_copy(num_ref, nums_ref.at[me], own.at[2])
    mine3.start()
    def go(j, carry):
        t = lax.rem(me + j, n)
        remote(ask_ref.at[t], served_ref.at[me], small_s.at[0, j], small_r.at[0, j], t).start()
        remote(num_ref, nums_ref.at[me], small_s.at[1, j], small_r.at[1, j], t).start()
        return carry
    lax.fori_loop(1, n, go, 0)
    nb = [1]
    def sib(slot, part):
        i = nb[0]; nb[0] += 1
        ref = o_ref.at[slot] if part is None else o_ref.at[slot, part]
        start(remote(ref, ref, bs.at[i], br.at[i], tc))
    def second(k, zz):
        s = dev(zz, y, x, c)
        sx, sy = dev(zz, y, 1 - x, c), dev(zz, 1 - y, x, c)
        own_a = w_ref.at[A] if k == 0 else o_ref.at[s, A]
        own_b = w_ref.at[B] if k == 0 else o_ref.at[s, B]
        remote(own_a, o_ref.at[sx, A], hs.at[k, 0], hr.at[k, 0], tx).wait_recv()
        start(remote(own_a, o_ref.at[s, A], cs.at[k, 0], cr.at[k, 0], ty))
        start(remote(o_ref.at[sx, A], o_ref.at[sx, A], cs.at[k, 1], cr.at[k, 1], ty))
        remote(own_b, o_ref.at[sy, B], hs.at[k, 1], hr.at[k, 1], ty).wait_recv()
        start(remote(own_b, o_ref.at[s, B], ds.at[k, 0], dr.at[k, 0], tx))
        start(remote(o_ref.at[sy, B], o_ref.at[sy, B], ds.at[k, 1], dr.at[k, 1], tx))
        sib(sx, A)
        sib(sy, B)
    def third(k, zz):
        sx, sy, sd = dev(zz, y, 1 - x, c), dev(zz, 1 - y, x, c), dev(zz, 1 - y, 1 - x, c)
        w = w_ref.at[A]
        remote(w, o_ref.at[sy, A], cs.at[k, 0], cr.at[k, 0], ty).wait_recv()
        sib(sy, A)
        remote(w, o_ref.at[sx, B], ds.at[k, 0], dr.at[k, 0], tx).wait_recv()
        sib(sx, B)
        remote(w, o_ref.at[sd, A], cs.at[k, 1], cr.at[k, 1], ty).wait_recv()
        sib(sd, A)
        remote(w, o_ref.at[sd, B], ds.at[k, 1], dr.at[k, 1], tx).wait_recv()
        sib(sd, B)
    def first(k, zz):
        s = dev(zz, y, x, c)
        remote(w_ref, o_ref.at[s], zs.at[k], zr.at[k], tc).wait_recv()
        start(remote(o_ref.at[s, A], o_ref.at[s, A], hs.at[k, 0], hr.at[k, 0], tx))
        start(remote(o_ref.at[s, B], o_ref.at[s, B], hs.at[k, 1], hr.at[k, 1], ty))
        sib(s, None)
    order = [0, 1, 3, 2]
    zz = [lax.rem(z + k, 4) for k in range(4)]
    second(0, zz[0])
    first(1, zz[1])
    second(1, zz[1])
    first(3, zz[3])
    third(0, zz[0])
    second(3, zz[3])
    first(2, zz[2])
    third(1, zz[1])
    second(2, zz[2])
    third(3, zz[3])
    third(2, zz[2])
    nb2 = [0]
    def got(part):
        i = nb2[0]; nb2[0] += 1
        ref = w_ref if part is None else w_ref.at[part]
        o = o_ref.at[me] if part is None else o_ref.at[me, part]
        remote(ref, o, bs.at[i], br.at[i], tc).wait_recv()
    got(None)
    def g2(): got(A); got(B)
    def g3(): got(A); got(B); got(A); got(B)
    def g1(): got(None)
    g2(); g1(); g2(); g1(); g3(); g2(); g1(); g3(); g2(); g3(); g3()
    def end(j, carry):
        t = lax.rem(me + j, n)
        remote(ask_ref.at[t], served_ref.at[me], small_s.at[0, j], small_r.at[0, j], t).wait()
        remote(num_ref, nums_ref.at[me], small_s.at[1, j], small_r.at[1, j], t).wait()
        return carry
    lax.fori_loop(1, n, end, 0)
    for cp in pend:
        cp.wait_send()
    mine.wait(); mine2.wait(); mine3.wait()

def gather_weights(w, ask, num, cid):
    n = 32
    rows = w.shape[0]
    D = pltpu.SemaphoreType.DMA
    sib = 1 + 4 * 2 + 3 + 4 * 4
    anyspec = pl.BlockSpec(memory_space=pl.ANY)
    return pl.pallas_call(
        gather_kernel,
        out_shape=(jax.ShapeDtypeStruct((n, rows, 128), w.dtype), jax.ShapeDtypeStruct(ask.shape, ask.dtype), jax.ShapeDtypeStruct((n,) + num.shape, num.dtype)),
        in_specs=[anyspec] * 3, out_specs=(anyspec,) * 3,
        scratch_shapes=[D((3,)), D((2, n)), D((2, n)), D((4,)), D((4,)), D((4, 2)), D((4, 2)), D((4, 2)), D((4, 2)), D((4, 2)), D((4, 2)), D((sib,)), D((sib,))],
        compiler_params=pltpu.CompilerParams(collective_id=cid, has_side_effects=True),
    )(w, ask, num)


def accumulate(dst, src, rows):
    step = 80
    whole = rows // step
    def body(i, carry):
        at = pl.ds(pl.multiple_of(i * step, 8), step)
        dst[at] = dst[at] + src[at]
        return carry
    lax.fori_loop(0, whole, body, 0)
    if rows % step:
        at = pl.ds(whole * step, rows % step)
        dst[at] = dst[at] + src[at]

def reduce_kernel(share_rows, lead, g_ref, err_ref, o_ref, sq_ref, errs_ref, L, R, YA, XA, XB, YB, Z, sq, own, ls, rs0_s, rs0_r, as1, ar1, as2, ar2, bs1, br1, bs2, br2, zs, zr, es, er, qs, qr):
    n = 32
    me = lax.axis_index('dev')
    c, x, y, z = lax.rem(me, 2), lax.rem(me // 2, 2), lax.rem(me // 4, 2), me // 8
    rows = L.shape[2]
    half = rows // 2
    A, B = pl.ds(0, half), pl.ds(half, half)
    def dev(z, y, x, c):
        return ((z * 2 + y) * 2 + x) * 2 + c
    def begin(d):
        return pl.multiple_of((lead + share_rows * d) // 8 * 8, 8)
    greet(n, me)
    tx, ty, tc = dev(z, y, 1 - x, c), dev(z, 1 - y, x, c), dev(z, y, x, 1 - c)
    pend = []
    def start(cp):
        cp.start(); pend.append(cp)
    order = [1, 2, 3, 0]
    zz = [lax.rem(z + k, 4) for k in range(4)]
    for k in order:
        for i in range(4):
            ys, xs = i // 2, i % 2
            start(remote(g_ref.at[pl.ds(begin(dev(zz[k], ys, xs, 1 - c)), rows)], R.at[k, i], rs0_s.at[k, i], rs0_r.at[k, i], tc))
            pltpu.make_async_copy(g_ref.at[pl.ds(begin(dev(zz[k], ys, xs, c)), rows)], L.at[k, i], ls.at[k, i]).start()
    e_own = pltpu.make_async_copy(err_ref, errs_ref.at[me], own.at[0])
    e_own.start()
    def go(j, carry):
        t = lax.rem(me + j, n)
        remote(err_ref, errs_ref.at[me], es.at[j], er.at[j], t).start()
        return carry
    lax.fori_loop(1, n, go, 0)
    i_own, i_x, i_y = y * 2 + x, y * 2 + 1 - x, (1 - y) * 2 + x
    def s0(k):
        for i in range(4):
            pltpu.make_async_copy(g_ref.at[pl.ds(0, rows)], L.at[k, i], ls.at[k, i]).wait()
            remote(L.at[k, i], R.at[k, i], rs0_s.at[k, i], rs0_r.at[k, i], tc).wait_recv()
            accumulate(L.at[k, i], R.at[k, i], rows)
        for j in range(2):
            start(remote(L.at[k, (1 - y) * 2 + j, A], YA.at[k, j], as1.at[k, j], ar1.at[k, j], ty))
            start(remote(L.at[k, j * 2 + 1 - x, B], XB.at[k, j], bs1.at[k, j], br1.at[k, j], tx))
    def mid(k):
        for j in range(2):
            remote(L.at[k, 0, A], YA.at[k, j], as1.at[k, j], ar1.at[k, j], ty).wait_recv()
            accumulate(L.at[k, y * 2 + j, A], YA.at[k, j], half)
        start(remote(L.at[k, i_x, A], XA.at[k], as2.at[k], ar2.at[k], tx))
        for j in range(2):
            remote(L.at[k, 0, B], XB.at[k, j], bs1.at[k, j], br1.at[k, j], tx).wait_recv()
            accumulate(L.at[k, j * 2 + x, B], XB.at[k, j], half)
        start(remote(L.at[k, i_y, B], YB.at[k], bs2.at[k], br2.at[k], ty))
    def fin(k):
        remote(L.at[k, 0, A], XA.at[k], as2.at[k], ar2.at[k], tx).wait_recv()
        accumulate(L.at[k, i_own, A], XA.at[k], half)
        remote(L.at[k, 0, B], YB.at[k], bs2.at[k], br2.at[k], ty).wait_recv()
        accumulate(L.at[k, i_own, B], YB.at[k], half)
        if k:
            start(remote(L.at[k, i_own], Z.at[k - 1], zs.at[k - 1], zr.at[k - 1], dev(zz[k], y, x, c)))
    s0(1)
    s0(2)
    mid(1)
    s0(3)
    mid(2)
    fin(1)
    s0(0)
    mid(3)
    fin(2)
    mid(0)
    fin(3)
    fin(0)
    for k in range(3):
        remote(L.at[0, 0], Z.at[k], zs.at[k], zr.at[k], tc).wait_recv()
    first = lax.rem(lead + share_rows * me, 8)
    sq[...] = jnp.zeros_like(sq)
    mine = L.at[0, i_own]
    def total(i, carry):
        r = pl.multiple_of(i * 8, 8)
        at = pl.ds(r, 8)
        v = mine[at] + Z[0, at] + (Z[1, at] + Z[2, at])
        o_ref[at] = v
        row = r + lax.broadcasted_iota(jnp.int32, (8, 128), 0)
        inside = (row >= first) & (row < first + share_rows)
        v = jnp.where(inside, v, 0.0)
        sq[...] += v * v
        return carry
    lax.fori_loop(0, rows // 8, total, 0)
    q_own = pltpu.make_async_copy(sq, sq_ref.at[me], own.at[1])
    q_own.start()
    def go2(j, carry):
        t = lax.rem(me + j, n)
        remote(sq, sq_ref.at[me], qs.at[j], qr.at[j], t).start()
        return carry
    lax.fori_loop(1, n, go2, 0)
    for cp in pend:
        cp.wait_send()
    def end(j, carry):
        t = lax.rem(me + j, n)
        remote(err_ref, errs_ref.at[me], es.at[j], er.at[j], t).wait()
        remote(sq, sq_ref.at[me], qs.at[j], qr.at[j], t).wait()
        return carry
    lax.fori_loop(1, n, end, 0)
    e_own.wait()
    q_own.wait()

def reduce_gradient(g, err, share_rows, lead, rows, cid):
    n = 32
    D = pltpu.SemaphoreType.DMA
    anyspec = pl.BlockSpec(memory_space=pl.ANY)
    vm = pl.BlockSpec(memory_space=pltpu.VMEM)
    half = rows // 2
    F = lambda *s: pltpu.VMEM(s + (128,), jnp.float32)
    return pl.pallas_call(
        functools.partial(reduce_kernel, share_rows, lead),
        out_shape=(jax.ShapeDtypeStruct((rows, 128), jnp.float32), jax.ShapeDtypeStruct((n, 8, 128), jnp.float32), jax.ShapeDtypeStruct((n, 8, 128), jnp.float32)),
        in_specs=[anyspec, vm], out_specs=(vm, vm, vm),
        scratch_shapes=[F(4, 4, rows), F(4, 4, rows), F(4, 2, half), F(4, half), F(4, 2, half), F(4, half), F(3, rows), F(8),
            D((2,)), D((4, 4)), D((4, 4)), D((4, 4)), D((4, 2)), D((4, 2)), D((4,)), D((4,)), D((4, 2)), D((4, 2)), D((4,)), D((4,)), D((3,)), D((3,)), D((n,)), D((n,)), D((n,)), D((n,))],
        compiler_params=pltpu.CompilerParams(collective_id=cid, has_side_effects=True, vmem_limit_bytes=48 << 20),
    )(g, err)


F32, BF16 = jnp.float32, jnp.bfloat16
VMEM_LIMIT = 56 << 20


def mm(a, b):
    return jnp.dot(a, b, preferred_element_type=F32)


def mm_nt(a, b):
    return lax.dot_general(a, b, (((1,), (1,)), ((), ())), preferred_element_type=F32)


def mm_tn(a, b):
    return lax.dot_general(a, b, (((0,), (0,)), ((), ())), preferred_element_type=F32)


def col(v):
    return jnp.sum(v, axis=0, keepdims=True)


def pick(slots, first, rows):
    r = first + lax.broadcasted_iota(jnp.int32, (slots.shape[0], rows), 1)
    return jnp.where(slots == r, 1.0, 0.0).astype(BF16)


def place(slots, first, rows):
    r = first + lax.broadcasted_iota(jnp.int32, (rows, slots.shape[1]), 0)
    return jnp.where(slots == r, 1.0, 0.0).astype(BF16)


def activate(pre):
    sigma = jax.nn.sigmoid(pre)
    return sigma, (pre * sigma).astype(BF16)


def normalize(post):
    centred = post - jnp.mean(post, axis=-1, keepdims=True)
    inv = lax.rsqrt(jnp.mean(centred * centred, axis=-1, keepdims=True) + norm_eps)
    return centred * inv, inv


def forward(us, w_in, w_out, vec):
    pre = vec[0:1, :]
    at = 0
    for u in us:
        pre = pre + mm(u, w_in[at : at + u.shape[1], :])
        at += u.shape[1]
    _, act = activate(pre)
    post = mm(act, w_out[...]) + vec[1:2, :]
    hat, inv = normalize(post)
    return hat * vec[2:3, :] + vec[3:4, :], pre, hat, inv


def norm_back(g, hat, inv, gain):
    s = g * gain
    return inv * (
        s - jnp.mean(s, axis=-1, keepdims=True) - hat * jnp.mean(s * hat, axis=-1, keepdims=True)
    )


def back(us, g_post, pre, w_out, d_in, d_out, d_vec):
    low = g_post.astype(BF16)
    sigma, act = activate(pre)
    d_out[...] += mm_tn(act, low)
    d_vec[1:2, : low.shape[1]] += col(low.astype(F32))
    g_act = mm_nt(low, w_out[...])
    g_pre = (g_act * sigma * (1.0 + pre * (1.0 - sigma))).astype(BF16)
    d_vec[0:1, :] += col(g_pre.astype(F32))
    at = 0
    for u in us:
        d_in[at : at + u.shape[1], :] += mm_tn(u, g_pre)
        at += u.shape[1]
    return g_pre


def pack(packed, lead, rows_in, d_in, d_out, d_vec):
    at = lead
    def matrix(ref, rows, at):
        for j in range(4):
            packed[pl.ds(at + j, rows, stride=4), :] = ref[:rows, 128 * j : 128 * (j + 1)]
        return at + 4 * rows
    def vector(i, at):
        for j in range(4):
            packed[at + j : at + j + 1, :] = d_vec[i : i + 1, 128 * j : 128 * (j + 1)]
        return at + 4
    at = matrix(d_in, rows_in, at)
    at = vector(0, at)
    if d_out is not None:
        at = matrix(d_out, d_out.shape[0], at)
        for i in (1, 2, 3):
            at = vector(i, at)
    return at


def clear(*refs):
    for ref in refs:
        ref[...] = jnp.zeros_like(ref)


def spec(shape, fixed=True):
    if fixed:
        return pl.BlockSpec(shape, lambda i: (0,) * len(shape))
    return pl.BlockSpec(shape, lambda i: (i,) + (0,) * (len(shape) - 1))


def params(**more):
    return pltpu.CompilerParams(vmem_limit_bytes=VMEM_LIMIT, **more)


def shaped(*shape, dtype=F32):
    return jax.ShapeDtypeStruct(shape, dtype)


ANY = pl.BlockSpec(memory_space=pl.ANY)


def encode_kernel(bm, x, w_in, w_out, vec, want, node, low, pre, hat, inv, out, acc):
    i = pl.program_id(0)
    r, p, h, v = forward([x[...]], w_in, w_out, vec)
    node[...] = r
    low[...] = r.astype(BF16)
    pre[...], hat[...], inv[...] = p, h, v
    send_rows(i, bm, low[...], want, out, acc)


def send_rows(i, bm, low, want, out, acc):
    @pl.when(i == 0)
    def _():
        clear(acc)
    acc[...] += mm(pick(want[...], i * bm, bm), low)
    @pl.when(i == pl.num_programs(0) - 1)
    def _():
        out[...] = acc[...].astype(BF16)


def kept_shapes(rows):
    return (shaped(rows, LATENT), shaped(rows, LATENT), shaped(rows, 1))


def kept_specs(bm):
    return (spec((bm, LATENT), False), spec((bm, LATENT), False), spec((bm, 1), False))


def encode(x, block, want, bm=256):
    rows, k = x.shape
    slots = want.shape[0]
    w_in, w_out, vec = block
    return pl.pallas_call(
        functools.partial(encode_kernel, bm),
        grid=(rows // bm,),
        out_shape=(shaped(rows, LATENT), shaped(rows, LATENT, dtype=BF16)) + kept_shapes(rows) + (shaped(slots, LATENT, dtype=BF16),),
        in_specs=[spec((bm, k), False), spec(w_in.shape), spec(w_out.shape), spec(vec.shape), spec((slots, 1))],
        out_specs=(spec((bm, LATENT), False), spec((bm, LATENT), False)) + kept_specs(bm) + (spec((slots, LATENT)),),
        scratch_shapes=[pltpu.VMEM((slots, LATENT), F32)],
        compiler_params=params(),
        name="encode",
    )(x, w_in, w_out, vec, want)


def node_kernel(bm, served, want, landed, node, low, w_in, w_out, vec, node_new, low_new, sums, pre, hat, inv, out, acc):
    i = pl.program_id(0)
    got = mm(place(served[...], i * bm, bm), landed[...]).astype(BF16)
    sums[...] = got
    r, p, h, v = forward([low[...], got], w_in, w_out, vec)
    r = node[...] + r
    node_new[...] = r
    low_new[...] = r.astype(BF16)
    pre[...], hat[...], inv[...] = p, h, v
    send_rows(i, bm, low_new[...], want, out, acc)


def node_forward(served, want, landed, node, low, block, bm=256):
    rows = node.shape[0]
    slots = want.shape[0]
    w_in, w_out, vec = block
    b = lambda: spec((bm, LATENT), False)
    return pl.pallas_call(
        functools.partial(node_kernel, bm),
        grid=(rows // bm,),
        out_shape=(shaped(rows, LATENT), shaped(rows, LATENT, dtype=BF16), shaped(rows, LATENT, dtype=BF16)) + kept_shapes(rows) + (shaped(slots, LATENT, dtype=BF16),),
        in_specs=[spec((1, slots)), spec((slots, 1)), spec((slots, LATENT)), b(), b(), spec(w_in.shape), spec(w_out.shape), spec(vec.shape)],
        out_specs=(b(), b(), b()) + kept_specs(bm) + (spec((slots, LATENT)),),
        scratch_shapes=[pltpu.VMEM((slots, LATENT), F32)],
        compiler_params=params(),
        name="node_forward",
    )(served, want, landed, node, low, w_in, w_out, vec)


def edge_kernel(first, pos, pos_r, arrived, source, w_in, w_out, vec, *rest):
    if first:
        g_in, g_out, g_vec, edge_new, buffer, edge_low, sent, recv, pre, hat, inv, g_pre, g_hat, g_inv = rest
        edge, p, h, v = forward([source[...]], g_in, g_out, g_vec)
        g_pre[...], g_hat[...], g_inv[...] = p, h, v
    else:
        edge_new, buffer, edge_low, sent, recv, pre, hat, inv = rest
        edge = source[...]
    slots = arrived.shape[0]
    e = edge.astype(BF16)
    s = mm(pick(pos[:, 0:1], 0, slots), arrived[...]).astype(BF16)
    r = mm(pick(pos[:, 1:2], 0, slots), arrived[...]).astype(BF16)
    edge_low[...], sent[...], recv[...] = e, s, r
    out, p, h, v = forward([e, s, r], w_in, w_out, vec)
    new = edge + out
    edge_new[...] = new
    pre[...], hat[...], inv[...] = p, h, v
    buffer[...] = mm(place(pos_r[...], 0, slots), new.astype(BF16)).astype(BF16)


def edge_forward(pos, pos_r, arrived, source, block, geo=None):
    rows = source.shape[0]
    slots = arrived.shape[0]
    kept = kept_shapes(rows)
    return pl.pallas_call(
        functools.partial(edge_kernel, geo is not None),
        out_shape=(shaped(rows, LATENT), shaped(slots, LATENT, dtype=BF16)) + (shaped(rows, LATENT, dtype=BF16),) * 3 + kept + (kept if geo is not None else ()),
        compiler_params=params(),
        name="edge_forward",
    )(pos, pos_r, arrived, source, *block, *(geo or ()))


def decode_kernel(bm, at, x, target, level, land, count, low, w_in, w_out, vec, flat, g_node, d_out_o, d_vec_o, err_o, packed, d_in, d_out, d_vec, err, sem):
    i = pl.program_id(0)
    @pl.when(i == 0)
    def _():
        clear(d_in, d_out, d_vec, err)
    u = low[...]
    pre = vec[0:1, :] + mm(u, w_in[...])
    _, act = activate(pre)
    wide = w_out.shape[1]
    post = mm(act, w_out[...]) + vec[1:2, :wide]
    sea = (lax.broadcasted_iota(jnp.int32, (1, VARS), 1) < SEA_VARS).astype(F32)
    mask = level[...].astype(F32) * (1.0 - land[...].astype(F32) * sea)
    residual = x[...].astype(F32) + post[:, :VARS] - target[...]
    divisor = jnp.maximum(count[...], 1.0)
    err[:, :VARS] += col(mask * residual * residual)
    g = 2.0 * mask * residual / divisor
    g_low = jnp.concatenate([g, jnp.zeros((bm, wide - VARS), F32)], axis=1)
    g_pre = back([u], g_low, pre, w_out, d_in, d_out, d_vec)
    g_node[...] = mm_nt(g_pre, w_in[...])
    @pl.when(i == pl.num_programs(0) - 1)
    def _():
        d_out_o[...] = d_out[...]
        d_vec_o[...] = d_vec[...]
        err_o[...] = err[...]
        for j in range(4):
            packed[pl.ds(j, LATENT, stride=4), :] = d_in[:, 128 * j : 128 * (j + 1)]
        cp = pltpu.make_async_copy(packed, flat.at[pl.ds(at, 4 * LATENT)], sem)
        cp.start()
        cp.wait()


def decode(x, target, level, land, count, low, block, flat_rows, at, bm=256):
    rows = low.shape[0]
    w_in, w_out, vec = block
    wide = w_out.shape[1]
    v = lambda: spec((bm, VARS), False)
    return pl.pallas_call(
        functools.partial(decode_kernel, bm, at),
        grid=(rows // bm,),
        out_shape=(shaped(flat_rows, 128), shaped(rows, LATENT), shaped(LATENT, wide), shaped(8, LATENT), shaped(1, wide)),
        in_specs=[v(), v(), v(), spec((bm, 1), False), spec((1, 1)), spec((bm, LATENT), False), spec(w_in.shape), spec(w_out.shape), spec(vec.shape)],
        out_specs=(ANY, spec((bm, LATENT), False), spec((LATENT, wide)), spec((8, LATENT)), spec((1, wide))),
        scratch_shapes=[pltpu.VMEM((4 * LATENT, 128), F32), pltpu.VMEM((LATENT, LATENT), F32), pltpu.VMEM((LATENT, wide), F32), pltpu.VMEM((8, LATENT), F32), pltpu.VMEM((1, wide), F32), pltpu.SemaphoreType.DMA],
        compiler_params=params(),
        name="decode",
    )(x, target, level, land, count, low, w_in, w_out, vec)


def layer_norm_back(g, hat, inv, vec, d_vec):
    d_vec[2:3, :] += col(g * hat)
    d_vec[3:4, :] += col(g)
    return norm_back(g, hat, inv, vec[2:3, :])


def node_back_kernel(bm, at, landed_given, tail_at, served, want, g_node, low, sums, pre, hat, inv, w_in, w_out, vec, flat_in, extra, flat, g_prev, out, packed, d_in, d_out, d_vec, acc, sem):
    i = pl.program_id(0)
    @pl.when(i == 0)
    def _():
        clear(d_in, d_out, d_vec, acc)
        if tail_at is not None:
            pltpu.make_async_copy(extra, flat.at[pl.ds(tail_at, extra.shape[0])], sem.at[0]).start()
    g = g_node[...]
    if landed_given:
        g = g + mm(place(served[...], i * bm, bm), extra[...])
    g_post = layer_norm_back(g, hat[...], inv[...], vec, d_vec)
    u, s = low[...], sums[...]
    g_pre = back([u, s], g_post, pre[...], w_out, d_in, d_out, d_vec)
    g_prev[...] = g + mm_nt(g_pre, w_in[:LATENT, :])
    g_sum = mm_nt(g_pre, w_in[LATENT:, :]).astype(BF16)
    send_rows(i, bm, g_sum, want, out, acc)
    @pl.when(i == pl.num_programs(0) - 1)
    def _():
        pack(packed, 0, 2 * LATENT, d_in, d_out, d_vec)
        cp = pltpu.make_async_copy(packed, flat.at[pl.ds(at, packed.shape[0])], sem.at[1])
        cp.start()
        if tail_at is not None:
            pltpu.make_async_copy(extra, flat.at[pl.ds(tail_at, extra.shape[0])], sem.at[0]).wait()
        cp.wait()


def node_backward(served, want, g_node, low, sums, kept, block, flat, at, landed=None, tail=None, tail_at=None, bm=256):
    rows = low.shape[0]
    slots = want.shape[0]
    w_in, w_out, vec = block
    b = lambda: spec((bm, LATENT), False)
    extra = landed if landed is not None else tail
    return pl.pallas_call(
        functools.partial(node_back_kernel, bm, at, landed is not None, tail_at),
        grid=(rows // bm,),
        out_shape=(shaped(*flat.shape), shaped(rows, LATENT), shaped(slots, LATENT, dtype=BF16)),
        in_specs=[spec((1, slots)), spec((slots, 1)), b(), b(), b()] + list(kept_specs(bm)) + [spec(w_in.shape), spec(w_out.shape), spec(vec.shape), ANY, spec(extra.shape)],
        out_specs=(ANY, b(), spec((slots, LATENT))),
        scratch_shapes=[pltpu.VMEM((8 * LATENT + 4 * LATENT + 16, 128), F32), pltpu.VMEM((2 * LATENT, LATENT), F32), pltpu.VMEM((LATENT, LATENT), F32), pltpu.VMEM((8, LATENT), F32), pltpu.VMEM((slots, LATENT), F32), pltpu.SemaphoreType.DMA((2,))],
        input_output_aliases={11: 0},
        compiler_params=params(),
        name="node_backward",
    )(served, want, g_node, low, sums, *kept, w_in, w_out, vec, flat, extra)


def edge_back_kernel(at, has_edge, geo_at, pos, pos_s, pos_r, returned, edge_low, sent, recv, pre, hat, inv, w_in, w_out, vec, flat_in, *rest):
    rest = list(rest)
    g_edge = rest.pop(0) if has_edge else None
    if geo_at is not None:
        geo, g_pre, g_hat, g_inv, g_out, g_vec = rest[:6]
        rest = rest[6:]
    flat, edge_prev, buffer, packed, d_in, d_out, d_vec, sem = rest[:8]
    slots = returned.shape[0]
    clear(d_in, d_out, d_vec)
    g = mm(pick(pos[:, 1:2], 0, slots), returned[...])
    if has_edge:
        g = g_edge[...] + g
    g_post = layer_norm_back(g, hat[...], inv[...], vec, d_vec)
    p = back([edge_low[...], sent[...], recv[...]], g_post, pre[...], w_out, d_in, d_out, d_vec)
    prev = g + mm_nt(p, w_in[:LATENT, :])
    edge_prev[...] = prev
    s = mm_nt(p, w_in[LATENT : 2 * LATENT, :]).astype(BF16)
    r = mm_nt(p, w_in[2 * LATENT :, :]).astype(BF16)
    buffer[...] = (mm(place(pos_s[...], 0, slots), s) + mm(place(pos_r[...], 0, slots), r)).astype(BF16)
    pack(packed, 0, 3 * LATENT, d_in, d_out, d_vec)
    cp = pltpu.make_async_copy(packed, flat.at[pl.ds(at, packed.shape[0])], sem.at[0])
    cp.start()
    if geo_at is not None:
        packed2, c_in, c_out, c_vec = rest[8:]
        clear(c_in, c_out, c_vec)
        g_post = layer_norm_back(prev, g_hat[...], g_inv[...], g_vec, c_vec)
        back([geo[...]], g_post, g_pre[...], g_out, c_in, c_out, c_vec)
        pack(packed2, 0, GEO, c_in, c_out, c_vec)
        cp2 = pltpu.make_async_copy(packed2, flat.at[pl.ds(geo_at, packed2.shape[0])], sem.at[1])
        cp2.start()
        cp2.wait()
    cp.wait()


def edge_backward(pos, pos_s, pos_r, returned, ins, kept, block, flat, at, g_edge=None, geo=None, geo_at=None):
    rows = pos.shape[0]
    slots = returned.shape[0]
    V = pl.BlockSpec(memory_space=pltpu.VMEM)
    args = [pos, pos_s, pos_r, returned, *ins, *kept, *block, flat]
    which = len(args) - 1
    if g_edge is not None:
        args.append(g_edge)
    scratch = [pltpu.VMEM((12 * LATENT + 4 * LATENT + 16, 128), F32), pltpu.VMEM((3 * LATENT, LATENT), F32), pltpu.VMEM((LATENT, LATENT), F32), pltpu.VMEM((8, LATENT), F32), pltpu.SemaphoreType.DMA((2,))]
    if geo is not None:
        args += geo
        wide = geo[0].shape[1]
        scratch += [pltpu.VMEM((4 * GEO + 4 * LATENT + 16, 128), F32), pltpu.VMEM((wide, LATENT), F32), pltpu.VMEM((LATENT, LATENT), F32), pltpu.VMEM((8, LATENT), F32)]
    return pl.pallas_call(
        functools.partial(edge_back_kernel, at, g_edge is not None, geo_at),
        out_shape=(shaped(*flat.shape), shaped(rows, LATENT), shaped(slots, LATENT, dtype=BF16)),
        in_specs=[ANY if i == which else V for i in range(len(args))],
        out_specs=(ANY, V, V),
        scratch_shapes=scratch,
        input_output_aliases={which: 0},
        compiler_params=params(),
        name="edge_backward",
    )(*args)


def encode_back_kernel(bm, served, landed, g_node, x, pre, hat, inv, w_out, vec, flat_in, flat, packed, d_in, d_out, d_vec, sem):
    i = pl.program_id(0)
    @pl.when(i == 0)
    def _():
        clear(d_in, d_out, d_vec)
    g = g_node[...] + mm(place(served[...], i * bm, bm), landed[...])
    g_post = layer_norm_back(g, hat[...], inv[...], vec, d_vec)
    back([x[...]], g_post, pre[...], w_out, d_in, d_out, d_vec)
    @pl.when(i == pl.num_programs(0) - 1)
    def _():
        packed[0:4, :] = jnp.zeros((4, 128), F32)
        pack(packed, 4, VARS, d_in, d_out, d_vec)
        cp = pltpu.make_async_copy(packed, flat.at[pl.ds(0, packed.shape[0])], sem)
        cp.start()
        cp.wait()


def encode_backward(served, landed, g_node, x, kept, block, flat, bm=256):
    rows, k = x.shape
    slots = landed.shape[0]
    w_in, w_out, vec = block
    return pl.pallas_call(
        functools.partial(encode_back_kernel, bm),
        grid=(rows // bm,),
        out_shape=shaped(*flat.shape),
        in_specs=[spec((1, slots)), spec((slots, LATENT)), spec((bm, LATENT), False), spec((bm, k), False)] + list(kept_specs(bm)) + [spec(w_out.shape), spec(vec.shape), ANY],
        out_specs=ANY,
        scratch_shapes=[pltpu.VMEM((4 + 4 * VARS + 4 * LATENT + 16, 128), F32), pltpu.VMEM((k, LATENT), F32), pltpu.VMEM((LATENT, LATENT), F32), pltpu.VMEM((8, LATENT), F32), pltpu.SemaphoreType.DMA],
        input_output_aliases={9: 0},
        compiler_params=params(),
        name="encode_backward",
    )(served, landed, g_node, x, *kept, w_out, vec, flat)


def make_asks(edge_owners, edge_local, devices):
    edges_here = edge_owners.shape[0]
    capacity = (5 * edges_here // (2 * devices) + 7) // 8 * 8
    owner = edge_owners.reshape(-1)
    local = edge_local.reshape(-1)
    wants = owner.shape[0]
    order = jnp.arange(wants, dtype=jnp.int32)
    before = (owner[:, None] == owner[None, :]) & (order[None, :] < order[:, None])
    ranking = jnp.sum(before.astype(jnp.int32), axis=1)
    position = owner * capacity + ranking
    slots = jnp.arange(devices * capacity, dtype=jnp.int32)
    asking = jnp.sum(jnp.where(slots[:, None] == position[None, :], local[None, :] + 1, 0), axis=1) - 1
    return (position, asking, capacity)


def widen(values, width):
    return jnp.pad(values, ((0, 0), (0, width - values.shape[1])))


def make_block(params):
    rows = params["w_in"].shape[0]
    w_in = jnp.pad(params["w_in"], ((0, -rows % 128), (0, 0)))
    w_out = widen(params["w_out"], (params["w_out"].shape[1] + 127) // 128 * 128)
    names = [name for name in ("b_in", "b_out", "gain", "shift") if name in params]
    vectors = [widen(params[name][None], LATENT) for name in names]
    vectors.append(jnp.zeros((8 - len(vectors), LATENT), jnp.bfloat16))
    return (w_in, w_out, jnp.concatenate(vectors).astype(jnp.float32))


def local(
    inputs,
    targets,
    geometry,
    land_sea,
    level_mask,
    edge_owners,
    edge_local,
    step_count,
    master,
    first_moment,
    second_moment,
    ema,
):
    segments, total = layout(LATENT, VARS, GEO, LAYERS)
    devices = lax.axis_size("dev")
    share = master.shape[0]
    mine = devices == 32 and share % 128 == 0
    ocean = (jnp.arange(VARS) < SEA_VARS).astype(jnp.float32)
    position, asking, capacity = make_asks(edge_owners, edge_local, devices)
    slots = devices * capacity
    counted = jnp.sum(level_mask * (1 - land_sea[:, None] * ocean.astype(jnp.int32)[None, :])).astype(jnp.float32)
    if mine:
        share_rows = share // 128
        pad_rows = (share_rows + 31) // 32 * 32
        low = jnp.pad(master.astype(jnp.bfloat16).reshape(share_rows, 128), ((0, pad_rows - share_rows), (0, 0)))
        ask = jnp.pad(asking.reshape(devices, 1, capacity), ((0, 0), (0, 0), (0, 128 - capacity)))
        number = jnp.zeros((8, 128), jnp.float32).at[0, 0].set(counted)
        gathered, served, numbers = gather_weights(low, ask, number, 1)
        full_weights = gathered[:, :share_rows].reshape(-1)
        served = served[:, 0, :capacity].reshape(-1)
        count = jnp.sum(numbers)
    else:
        full_weights = lax.all_gather(master.astype(jnp.bfloat16), "dev", axis=0, tiled=True)
        served = lax.all_to_all(asking.reshape(devices, capacity), "dev", 0, 0, tiled=True).reshape(-1)
        count = lax.psum(counted, "dev")
    blocks = [make_block(b) for b in unpack(full_weights, segments)]
    want = served[:, None]
    served = served[None, :]
    pos = position.reshape(-1, 2)
    pos_s, pos_r = pos[:, 0][None, :], pos[:, 1][None, :]

    def exchange(rows):
        return a2a(rows.reshape(devices, capacity, LATENT), 0).reshape(slots, LATENT)

    x = widen(inputs, 256)
    geo = widen(geometry, 128)
    node, low, *enc_kept, outgoing = encode(x, blocks[0], want)
    node_kept, edge_kept = [], []
    edge = geo
    for k in range(LAYERS):
        arrived = exchange(outgoing)
        edge, buffer, *kept = edge_forward(pos, pos_r, arrived, edge, blocks[2 + 2 * k], blocks[1] if k == 0 else None)
        edge_kept.append((kept[:3], kept[3:6]))
        if k == 0:
            geo_kept = kept[6:]
        landed = exchange(buffer)
        before = low
        node, low, sums, *kept, outgoing = node_forward(served, want, landed, node, low, blocks[3 + 2 * k])
        node_kept.append((before, sums, kept))
    pieces = [4 * s for s in (VARS + LATENT + 4, GEO + LATENT + 4) + (3 * LATENT + LATENT + 4, 2 * LATENT + LATENT + 4) * LAYERS]
    lead = 4
    places = [0] + [lead + sum(pieces[: i + 1]) for i in range(len(pieces))]
    flat_rows = (lead + PARAMS // 128 + 15) // 16 * 16 + 8
    dec_at = places[-1]
    tail_at = dec_at + 4 * LATENT
    flat, g_node, d_out, d_vec, errors = decode(
        inputs, targets, level_mask, land_sea[:, None], count.reshape(1, 1), low, blocks[-1], flat_rows, dec_at
    )
    error_here = jnp.sum(errors)
    tail = jnp.concatenate([d_vec[0], d_out[:, :VARS].reshape(-1), d_vec[1, :VARS]])
    tail_rows = flat_rows - tail_at
    tail = jnp.pad(tail, (0, tail_rows * 128 - tail.shape[0])).reshape(tail_rows, 128)
    landed, g_edge = None, None
    for k in reversed(range(LAYERS)):
        before, sums, kept = node_kept[k]
        more = dict(landed=landed) if landed is not None else dict(tail=tail, tail_at=tail_at)
        flat, g_node, outgoing = node_backward(served, want, g_node, before, sums, kept, blocks[3 + 2 * k], flat, places[3 + 2 * k], **more)
        returned = exchange(outgoing)
        ins, kept = edge_kept[k]
        more = dict(geo=[geo, *geo_kept, blocks[1][1], blocks[1][2]], geo_at=places[1]) if k == 0 else {}
        flat, g_edge, buffer = edge_backward(pos, pos_s, pos_r, returned, ins, kept, blocks[2 + 2 * k], flat, places[2 + 2 * k], g_edge=g_edge, **more)
        landed = exchange(buffer)
    flat = encode_backward(served, landed, g_node, x, enc_kept, blocks[0], flat)
    if mine:
        rows = (share_rows + 6 + 15) // 16 * 16
        error = jnp.zeros((8, 128), jnp.float32).at[0, 0].set(error_here)
        summed, squares, errors = reduce_gradient(flat, error, share_rows, lead, rows, 2)
        skip = lax.rem(lead + share_rows * lax.axis_index("dev"), 8)
        own_grad = lax.dynamic_slice_in_dim(summed, skip, share_rows).reshape(-1)
        grad_norm = jnp.sqrt(jnp.sum(squares))
        error_sum = jnp.sum(errors)
    else:
        own_grad = lax.psum_scatter(flat[lead : lead + PARAMS // 128].reshape(-1), "dev", scatter_dimension=0, tiled=True)
        error_sum, squares = lax.psum((error_here, jnp.sum(own_grad * own_grad)), "dev")
        grad_norm = jnp.sqrt(squares)
    loss = error_sum / jnp.maximum(count, 1.0)
    clipped = own_grad * jnp.minimum(1.0, clip_limit / grad_norm)
    step = step_count[0].astype(jnp.float32)
    new_first = beta_one * first_moment + (1.0 - beta_one) * clipped
    new_second = beta_two * second_moment + (1.0 - beta_two) * clipped * clipped
    first_hat = new_first / (1.0 - beta_one**step)
    second_hat = new_second / (1.0 - beta_two**step)
    new_master = master - learn_rate * (
        first_hat / (jnp.sqrt(second_hat) + adam_eps) + decay_rate * master
    )
    new_ema = ema_keep * ema + (1.0 - ema_keep) * new_master
    return (new_master, new_first, new_second, new_ema, loss, grad_norm)


def solution(mesh):
    in_specs = (
        P("dev", None),
        P("dev", None),
        P("dev", None),
        P("dev"),
        P("dev", None),
        P("dev", None),
        P("dev", None),
        P(),
        P("dev"),
        P("dev"),
        P("dev"),
        P("dev"),
    )
    out_specs = (P("dev"), P("dev"), P("dev"), P("dev"), P(), P())
    return jax.shard_map(local, mesh=mesh, in_specs=in_specs, out_specs=out_specs, check_vma=False)
```

```python
import functools

import jax
import jax.numpy as jnp
import numpy as np
from jax import lax
from jax.experimental import pallas as pl
from jax.experimental.pallas import tpu as pltpu
from jax.sharding import PartitionSpec as P

LATENT = 512
VARS = 227
GEO = 4
SEA_VARS = 4
LAYERS = 3
PARAMS = 6545408


norm_eps = 1e-05
clip_limit = 0.01
beta_one = 0.9
beta_two = 0.999
adam_eps = 1e-08
learn_rate = 0.03
decay_rate = 0.1
ema_keep = 0.9


def layout(width, variables, geometry, layers):
    shapes = [(variables, width, True), (geometry, width, True)]
    for k in range(layers):
        shapes.append((3 * width, width, True))
        shapes.append((2 * width, width, True))
    shapes.append((width, variables, False))
    segments = []
    offset = 0
    for block_id, (fan_in, fan_out, normed) in enumerate(shapes):
        members = [
            ("w_in", (fan_in, width)),
            ("b_in", (width,)),
            ("w_out", (width, fan_out)),
            ("b_out", (fan_out,)),
        ]
        if normed:
            members = members + [("gain", (fan_out,)), ("shift", (fan_out,))]
        for part_name, part_shape in members:
            entries = int(np.prod(part_shape))
            segments.append((block_id, part_name, part_shape, offset, entries))
            offset += entries
    return (segments, offset)


def unpack(flat, segments):
    blocks = [dict() for k in range(segments[-1][0] + 1)]
    for block_id, part_name, part_shape, offset, entries in segments:
        blocks[block_id][part_name] = flat[offset : offset + entries].reshape(part_shape)
    return blocks


MESH = pl.DeviceIdType.MESH

def remote(src, dst, send, recv, target):
    return pltpu.make_async_remote_copy(src, dst, send, recv, device_id=(target,), device_id_type=MESH)

def greet(n, me):
    barrier = pltpu.get_barrier_semaphore()
    def hello(j, c):
        pl.semaphore_signal(barrier, inc=1, device_id=(lax.rem(me + j, n),), device_id_type=MESH)
        return c
    lax.fori_loop(1, n, hello, 0)
    pl.semaphore_wait(barrier, n - 1)

def a2a_kernel(n, a_ref, o_ref, own, ssem, rsem):
    me = lax.axis_index('dev')
    greet(n, me)
    here = pltpu.make_async_copy(a_ref.at[me], o_ref.at[me], own)
    here.start()
    def go(j, c):
        t = lax.rem(me + j, n)
        remote(a_ref.at[t], o_ref.at[me], ssem.at[j], rsem.at[j], t).start()
        return c
    lax.fori_loop(1, n, go, 0)
    def end(j, c):
        t = lax.rem(me + j, n)
        remote(a_ref.at[t], o_ref.at[me], ssem.at[j], rsem.at[j], t).wait()
        return c
    lax.fori_loop(1, n, end, 0)
    here.wait()

def a2a(x, cid, space=pl.ANY):
    n = x.shape[0]
    return pl.pallas_call(
        functools.partial(a2a_kernel, n),
        out_shape=jax.ShapeDtypeStruct(x.shape, x.dtype),
        in_specs=[pl.BlockSpec(memory_space=space)],
        out_specs=pl.BlockSpec(memory_space=space),
        scratch_shapes=[pltpu.SemaphoreType.DMA, pltpu.SemaphoreType.DMA((n,)), pltpu.SemaphoreType.DMA((n,))],
        compiler_params=pltpu.CompilerParams(collective_id=cid, has_side_effects=True),
    )(x)

def gather_kernel(w_ref, ask_ref, num_ref, o_ref, served_ref, nums_ref, own, small_s, small_r, zs, zr, hs, hr, cs, cr, ds, dr, bs, br):
    n = 32
    me = lax.axis_index('dev')
    c, x, y, z = lax.rem(me, 2), lax.rem(me // 2, 2), lax.rem(me // 4, 2), me // 8
    rows = w_ref.shape[0]
    half = rows // 2
    A, B = pl.ds(0, half), pl.ds(half, half)
    def dev(z, y, x, c):
        return ((z * 2 + y) * 2 + x) * 2 + c
    greet(n, me)
    tx, ty, tc = dev(z, y, 1 - x, c), dev(z, 1 - y, x, c), dev(z, y, x, 1 - c)
    pend = []
    def start(cp):
        cp.start(); pend.append(cp)
    mine = pltpu.make_async_copy(w_ref, o_ref.at[me], own.at[0])
    mine.start()
    start(remote(w_ref.at[A], o_ref.at[me, A], hs.at[0, 0], hr.at[0, 0], tx))
    start(remote(w_ref.at[B], o_ref.at[me, B], hs.at[0, 1], hr.at[0, 1], ty))
    for j in (1, 3, 2):
        start(remote(w_ref, o_ref.at[me], zs.at[j], zr.at[4 - j], dev(lax.rem(z + j, 4), y, x, c)))
    start(remote(w_ref, o_ref.at[me], bs.at[0], br.at[0], tc))
    mine2 = pltpu.make_async_copy(ask_ref.at[me], served_ref.at[me], own.at[1])
    mine2.start()
    mine3 = pltpu.make_async_copy(num_ref, nums_ref.at[me], own.at[2])
    mine3.start()
    def go(j, carry):
        t = lax.rem(me + j, n)
        remote(ask_ref.at[t], served_ref.at[me], small_s.at[0, j], small_r.at[0, j], t).start()
        remote(num_ref, nums_ref.at[me], small_s.at[1, j], small_r.at[1, j], t).start()
        return carry
    lax.fori_loop(1, n, go, 0)
    nb = [1]
    def sib(slot, part):
        i = nb[0]; nb[0] += 1
        ref = o_ref.at[slot] if part is None else o_ref.at[slot, part]
        start(remote(ref, ref, bs.at[i], br.at[i], tc))
    def second(k, zz):
        s = dev(zz, y, x, c)
        sx, sy = dev(zz, y, 1 - x, c), dev(zz, 1 - y, x, c)
        own_a = w_ref.at[A] if k == 0 else o_ref.at[s, A]
        own_b = w_ref.at[B] if k == 0 else o_ref.at[s, B]
        remote(own_a, o_ref.at[sx, A], hs.at[k, 0], hr.at[k, 0], tx).wait_recv()
        start(remote(own_a, o_ref.at[s, A], cs.at[k, 0], cr.at[k, 0], ty))
        start(remote(o_ref.at[sx, A], o_ref.at[sx, A], cs.at[k, 1], cr.at[k, 1], ty))
        remote(own_b, o_ref.at[sy, B], hs.at[k, 1], hr.at[k, 1], ty).wait_recv()
        start(remote(own_b, o_ref.at[s, B], ds.at[k, 0], dr.at[k, 0], tx))
        start(remote(o_ref.at[sy, B], o_ref.at[sy, B], ds.at[k, 1], dr.at[k, 1], tx))
        sib(sx, A)
        sib(sy, B)
    def third(k, zz):
        sx, sy, sd = dev(zz, y, 1 - x, c), dev(zz, 1 - y, x, c), dev(zz, 1 - y, 1 - x, c)
        w = w_ref.at[A]
        remote(w, o_ref.at[sy, A], cs.at[k, 0], cr.at[k, 0], ty).wait_recv()
        sib(sy, A)
        remote(w, o_ref.at[sx, B], ds.at[k, 0], dr.at[k, 0], tx).wait_recv()
        sib(sx, B)
        remote(w, o_ref.at[sd, A], cs.at[k, 1], cr.at[k, 1], ty).wait_recv()
        sib(sd, A)
        remote(w, o_ref.at[sd, B], ds.at[k, 1], dr.at[k, 1], tx).wait_recv()
        sib(sd, B)
    def first(k, zz):
        s = dev(zz, y, x, c)
        remote(w_ref, o_ref.at[s], zs.at[k], zr.at[k], tc).wait_recv()
        start(remote(o_ref.at[s, A], o_ref.at[s, A], hs.at[k, 0], hr.at[k, 0], tx))
        start(remote(o_ref.at[s, B], o_ref.at[s, B], hs.at[k, 1], hr.at[k, 1], ty))
        sib(s, None)
    order = [0, 1, 3, 2]
    zz = [lax.rem(z + k, 4) for k in range(4)]
    second(0, zz[0])
    first(1, zz[1])
    second(1, zz[1])
    first(3, zz[3])
    third(0, zz[0])
    second(3, zz[3])
    first(2, zz[2])
    third(1, zz[1])
    second(2, zz[2])
    third(3, zz[3])
    third(2, zz[2])
    nb2 = [0]
    def got(part):
        i = nb2[0]; nb2[0] += 1
        ref = w_ref if part is None else w_ref.at[part]
        o = o_ref.at[me] if part is None else o_ref.at[me, part]
        remote(ref, o, bs.at[i], br.at[i], tc).wait_recv()
    got(None)
    def g2(): got(A); got(B)
    def g3(): got(A); got(B); got(A); got(B)
    def g1(): got(None)
    g2(); g1(); g2(); g1(); g3(); g2(); g1(); g3(); g2(); g3(); g3()
    def end(j, carry):
        t = lax.rem(me + j, n)
        remote(ask_ref.at[t], served_ref.at[me], small_s.at[0, j], small_r.at[0, j], t).wait()
        remote(num_ref, nums_ref.at[me], small_s.at[1, j], small_r.at[1, j], t).wait()
        return carry
    lax.fori_loop(1, n, end, 0)
    for cp in pend:
        cp.wait_send()
    mine.wait(); mine2.wait(); mine3.wait()

def gather_weights(w, ask, num, cid):
    n = 32
    rows = w.shape[0]
    D = pltpu.SemaphoreType.DMA
    sib = 1 + 4 * 2 + 3 + 4 * 4
    anyspec = pl.BlockSpec(memory_space=pl.ANY)
    return pl.pallas_call(
        gather_kernel,
        out_shape=(jax.ShapeDtypeStruct((n, rows, 128), w.dtype), jax.ShapeDtypeStruct(ask.shape, ask.dtype), jax.ShapeDtypeStruct((n,) + num.shape, num.dtype)),
        in_specs=[anyspec] * 3, out_specs=(anyspec,) * 3,
        scratch_shapes=[D((3,)), D((2, n)), D((2, n)), D((4,)), D((4,)), D((4, 2)), D((4, 2)), D((4, 2)), D((4, 2)), D((4, 2)), D((4, 2)), D((sib,)), D((sib,))],
        compiler_params=pltpu.CompilerParams(collective_id=cid, has_side_effects=True),
    )(w, ask, num)


def accumulate(dst, src, rows):
    step = 80
    whole = rows // step
    def body(i, carry):
        at = pl.ds(pl.multiple_of(i * step, 8), step)
        dst[at] = dst[at] + src[at]
        return carry
    lax.fori_loop(0, whole, body, 0)
    if rows % step:
        at = pl.ds(whole * step, rows % step)
        dst[at] = dst[at] + src[at]

def reduce_kernel(share_rows, lead, g_ref, err_ref, o_ref, sq_ref, errs_ref, L, R, YA, XA, XB, YB, Z, sq, own, ls, rs0_s, rs0_r, as1, ar1, as2, ar2, bs1, br1, bs2, br2, zs, zr, es, er, qs, qr):
    n = 32
    me = lax.axis_index('dev')
    c, x, y, z = lax.rem(me, 2), lax.rem(me // 2, 2), lax.rem(me // 4, 2), me // 8
    rows = L.shape[2]
    half = rows // 2
    A, B = pl.ds(0, half), pl.ds(half, half)
    def dev(z, y, x, c):
        return ((z * 2 + y) * 2 + x) * 2 + c
    def begin(d):
        return pl.multiple_of((lead + share_rows * d) // 8 * 8, 8)
    greet(n, me)
    tx, ty, tc = dev(z, y, 1 - x, c), dev(z, 1 - y, x, c), dev(z, y, x, 1 - c)
    pend = []
    def start(cp):
        cp.start(); pend.append(cp)
    order = [1, 2, 3, 0]
    zz = [lax.rem(z + k, 4) for k in range(4)]
    for k in order:
        for i in range(4):
            ys, xs = i // 2, i % 2
            start(remote(g_ref.at[pl.ds(begin(dev(zz[k], ys, xs, 1 - c)), rows)], R.at[k, i], rs0_s.at[k, i], rs0_r.at[k, i], tc))
            pltpu.make_async_copy(g_ref.at[pl.ds(begin(dev(zz[k], ys, xs, c)), rows)], L.at[k, i], ls.at[k, i]).start()
    e_own = pltpu.make_async_copy(err_ref, errs_ref.at[me], own.at[0])
    e_own.start()
    def go(j, carry):
        t = lax.rem(me + j, n)
        remote(err_ref, errs_ref.at[me], es.at[j], er.at[j], t).start()
        return carry
    lax.fori_loop(1, n, go, 0)
    i_own, i_x, i_y = y * 2 + x, y * 2 + 1 - x, (1 - y) * 2 + x
    def s0(k):
        for i in range(4):
            pltpu.make_async_copy(g_ref.at[pl.ds(0, rows)], L.at[k, i], ls.at[k, i]).wait()
            remote(L.at[k, i], R.at[k, i], rs0_s.at[k, i], rs0_r.at[k, i], tc).wait_recv()
            accumulate(L.at[k, i], R.at[k, i], rows)
        for j in range(2):
            start(remote(L.at[k, (1 - y) * 2 + j, A], YA.at[k, j], as1.at[k, j], ar1.at[k, j], ty))
            start(remote(L.at[k, j * 2 + 1 - x, B], XB.at[k, j], bs1.at[k, j], br1.at[k, j], tx))
    def mid(k):
        for j in range(2):
            remote(L.at[k, 0, A], YA.at[k, j], as1.at[k, j], ar1.at[k, j], ty).wait_recv()
            accumulate(L.at[k, y * 2 + j, A], YA.at[k, j], half)
        start(remote(L.at[k, i_x, A], XA.at[k], as2.at[k], ar2.at[k], tx))
        for j in range(2):
            remote(L.at[k, 0, B], XB.at[k, j], bs1.at[k, j], br1.at[k, j], tx).wait_recv()
            accumulate(L.at[k, j * 2 + x, B], XB.at[k, j], half)
        start(remote(L.at[k, i_y, B], YB.at[k], bs2.at[k], br2.at[k], ty))
    def fin(k):
        remote(L.at[k, 0, A], XA.at[k], as2.at[k], ar2.at[k], tx).wait_recv()
        accumulate(L.at[k, i_own, A], XA.at[k], half)
        remote(L.at[k, 0, B], YB.at[k], bs2.at[k], br2.at[k], ty).wait_recv()
        accumulate(L.at[k, i_own, B], YB.at[k], half)
        if k:
            start(remote(L.at[k, i_own], Z.at[k - 1], zs.at[k - 1], zr.at[k - 1], dev(zz[k], y, x, c)))
    s0(1)
    s0(2)
    mid(1)
    s0(3)
    mid(2)
    fin(1)
    s0(0)
    mid(3)
    fin(2)
    mid(0)
    fin(3)
    fin(0)
    for k in range(3):
        remote(L.at[0, 0], Z.at[k], zs.at[k], zr.at[k], tc).wait_recv()
    first = lax.rem(lead + share_rows * me, 8)
    sq[...] = jnp.zeros_like(sq)
    mine = L.at[0, i_own]
    def total(i, carry):
        r = pl.multiple_of(i * 8, 8)
        at = pl.ds(r, 8)
        v = mine[at] + Z[0, at] + (Z[1, at] + Z[2, at])
        o_ref[at] = v
        row = r + lax.broadcasted_iota(jnp.int32, (8, 128), 0)
        inside = (row >= first) & (row < first + share_rows)
        v = jnp.where(inside, v, 0.0)
        sq[...] += v * v
        return carry
    lax.fori_loop(0, rows // 8, total, 0)
    q_own = pltpu.make_async_copy(sq, sq_ref.at[me], own.at[1])
    q_own.start()
    def go2(j, carry):
        t = lax.rem(me + j, n)
        remote(sq, sq_ref.at[me], qs.at[j], qr.at[j], t).start()
        return carry
    lax.fori_loop(1, n, go2, 0)
    for cp in pend:
        cp.wait_send()
    def end(j, carry):
        t = lax.rem(me + j, n)
        remote(err_ref, errs_ref.at[me], es.at[j], er.at[j], t).wait()
        remote(sq, sq_ref.at[me], qs.at[j], qr.at[j], t).wait()
        return carry
    lax.fori_loop(1, n, end, 0)
    e_own.wait()
    q_own.wait()

def reduce_gradient(g, err, share_rows, lead, rows, cid):
    n = 32
    D = pltpu.SemaphoreType.DMA
    anyspec = pl.BlockSpec(memory_space=pl.ANY)
    vm = pl.BlockSpec(memory_space=pltpu.VMEM)
    half = rows // 2
    F = lambda *s: pltpu.VMEM(s + (128,), jnp.float32)
    return pl.pallas_call(
        functools.partial(reduce_kernel, share_rows, lead),
        out_shape=(jax.ShapeDtypeStruct((rows, 128), jnp.float32), jax.ShapeDtypeStruct((n, 8, 128), jnp.float32), jax.ShapeDtypeStruct((n, 8, 128), jnp.float32)),
        in_specs=[anyspec, vm], out_specs=(vm, vm, vm),
        scratch_shapes=[F(4, 4, rows), F(4, 4, rows), F(4, 2, half), F(4, half), F(4, 2, half), F(4, half), F(3, rows), F(8),
            D((2,)), D((4, 4)), D((4, 4)), D((4, 4)), D((4, 2)), D((4, 2)), D((4,)), D((4,)), D((4, 2)), D((4, 2)), D((4,)), D((4,)), D((3,)), D((3,)), D((n,)), D((n,)), D((n,)), D((n,))],
        compiler_params=pltpu.CompilerParams(collective_id=cid, has_side_effects=True, vmem_limit_bytes=48 << 20),
    )(g, err)


F32, BF16 = jnp.float32, jnp.bfloat16
VMEM_LIMIT = 56 << 20
ANY = pl.BlockSpec(memory_space=pl.ANY)
DMA = pltpu.SemaphoreType.DMA


def mm(a, b):
    return jnp.dot(a, b, preferred_element_type=F32)


def mm_nt(a, b):
    return lax.dot_general(a, b, (((1,), (1,)), ((), ())), preferred_element_type=F32)


def mm_tn(a, b):
    return lax.dot_general(a, b, (((0,), (0,)), ((), ())), preferred_element_type=F32)


def col(v):
    return jnp.sum(v, axis=0, keepdims=True)


def pick(slots, first, rows):
    r = first + lax.broadcasted_iota(jnp.int32, (slots.shape[0], rows), 1)
    return jnp.where(slots == r, 1.0, 0.0).astype(BF16)


def place(slots, first, rows):
    r = first + lax.broadcasted_iota(jnp.int32, (rows, slots.shape[1]), 0)
    return jnp.where(slots == r, 1.0, 0.0).astype(BF16)


def first_half(us, w_in, vec):
    pre = vec[0:1, :]
    at = 0
    for u in us:
        pre = pre + mm(u, w_in[at : at + u.shape[1], :])
        at += u.shape[1]
    return pre


def activate(pre):
    sigma = jax.nn.sigmoid(pre)
    return sigma, (pre * sigma).astype(BF16)


def normalize(post):
    centred = post - jnp.mean(post, axis=-1, keepdims=True)
    inv = lax.rsqrt(jnp.mean(centred * centred, axis=-1, keepdims=True) + norm_eps)
    return centred * inv, inv


def second_half(act, w_out, vec):
    return normalize(mm(act, w_out[...]) + vec[1:2, :])


def scale_shift(hat, vec):
    return hat * vec[2:3, :] + vec[3:4, :]


def norm_back(g, hat, inv, vec, d_vec):
    d_vec[2:3, :] += col(g * hat)
    d_vec[3:4, :] += col(g)
    s = g * vec[2:3, :]
    post = inv * (
        s - jnp.mean(s, axis=-1, keepdims=True) - hat * jnp.mean(s * hat, axis=-1, keepdims=True)
    )
    return post.astype(BF16)


def act_back(low, pre, sigma, w_out):
    g_act = mm_nt(low, w_out[...])
    return (g_act * sigma * (1.0 + pre * (1.0 - sigma))).astype(BF16)


def weight_sums(us, act, low, g_pre, d_in, d_out, d_vec):
    d_out[...] += mm_tn(act, low)
    d_vec[1:2, : low.shape[1]] += col(low.astype(F32))
    d_vec[0:1, :] += col(g_pre.astype(F32))
    at = 0
    for u in us:
        d_in[at : at + u.shape[1], :] += mm_tn(u, g_pre)
        at += u.shape[1]


def pack_matrix(packed, ref, rows, at):
    for j in range(4):
        packed[pl.ds(at + j, rows, stride=4), :] = ref[:rows, 128 * j : 128 * (j + 1)]
    return at + 4 * rows


def pack(packed, lead, rows_in, d_in, d_out, d_vec):
    def vector(i, at):
        for j in range(4):
            packed[at + j : at + j + 1, :] = d_vec[i : i + 1, 128 * j : 128 * (j + 1)]
        return at + 4
    at = pack_matrix(packed, d_in, rows_in, lead)
    at = vector(0, at)
    at = pack_matrix(packed, d_out, d_out.shape[0], at)
    for i in (1, 2, 3):
        at = vector(i, at)


def clear(*refs):
    for ref in refs:
        ref[...] = jnp.zeros_like(ref)


def spec(shape, fixed=True):
    if fixed:
        return pl.BlockSpec(shape, lambda i: (0,) * len(shape))
    return pl.BlockSpec(shape, lambda i: (i,) + (0,) * (len(shape) - 1))


def params(**more):
    return pltpu.CompilerParams(vmem_limit_bytes=VMEM_LIMIT, **more)


def shaped(*shape, dtype=F32):
    return jax.ShapeDtypeStruct(shape, dtype)


def send_rows(i, bm, low, want, out, acc):
    @pl.when(i == 0)
    def _():
        clear(acc)
    acc[...] += mm(pick(want[...], i * bm, bm), low)
    @pl.when(i == pl.num_programs(0) - 1)
    def _():
        out[...] = acc[...].astype(BF16)


def store_flat(packed, flat, at, sem):
    copy = pltpu.make_async_copy(packed, flat.at[pl.ds(at, packed.shape[0])], sem)
    copy.start()
    return copy


def mlp_sums(rows_in, wide=LATENT):
    return [pltpu.VMEM((rows_in, LATENT), F32), pltpu.VMEM((LATENT, wide), F32), pltpu.VMEM((8, LATENT), F32)]


def packed_rows(rows_in, lead=0):
    return pltpu.VMEM((lead + 4 * rows_in + 4 * LATENT + 16, 128), F32)


def encode_kernel(bm, x, w_in, w_out, vec, want, node, low, out, acc):
    i = pl.program_id(0)
    _, act = activate(first_half([x[...]], w_in, vec))
    hat, _ = second_half(act, w_out, vec)
    r = scale_shift(hat, vec)
    node[...] = r
    rounded = r.astype(BF16)
    low[...] = rounded
    send_rows(i, bm, rounded, want, out, acc)


def encode(x, block, want, bm=512):
    rows, k = x.shape
    slots = want.shape[0]
    w_in, w_out, vec = block
    return pl.pallas_call(
        functools.partial(encode_kernel, bm),
        grid=(rows // bm,),
        out_shape=(shaped(rows, LATENT), shaped(rows, LATENT, dtype=BF16), shaped(slots, LATENT, dtype=BF16)),
        in_specs=[spec((bm, k), False), spec(w_in.shape), spec(w_out.shape), spec(vec.shape), spec((slots, 1))],
        out_specs=(spec((bm, LATENT), False), spec((bm, LATENT), False), spec((slots, LATENT))),
        scratch_shapes=[pltpu.VMEM((slots, LATENT), F32)],
        compiler_params=params(),
        name="encode",
    )(x, w_in, w_out, vec, want)


def node_kernel(bm, served, want, landed, node, w_in, w_out, vec, node_new, low_new, sums, out, acc):
    i = pl.program_id(0)
    got = mm(place(served[...], i * bm, bm), landed[...]).astype(BF16)
    sums[...] = got
    old = node[...]
    _, act = activate(first_half([old.astype(BF16), got], w_in, vec))
    hat, _ = second_half(act, w_out, vec)
    r = old + scale_shift(hat, vec)
    node_new[...] = r
    rounded = r.astype(BF16)
    low_new[...] = rounded
    send_rows(i, bm, rounded, want, out, acc)


def node_forward(served, want, landed, node, block, bm=512):
    rows = node.shape[0]
    slots = want.shape[0]
    w_in, w_out, vec = block
    b = lambda: spec((bm, LATENT), False)
    return pl.pallas_call(
        functools.partial(node_kernel, bm),
        grid=(rows // bm,),
        out_shape=(shaped(rows, LATENT), shaped(rows, LATENT, dtype=BF16), shaped(rows, LATENT, dtype=BF16), shaped(slots, LATENT, dtype=BF16)),
        in_specs=[spec((1, slots)), spec((slots, 1)), spec((slots, LATENT)), b(), spec(w_in.shape), spec(w_out.shape), spec(vec.shape)],
        out_specs=(b(), b(), b(), spec((slots, LATENT))),
        scratch_shapes=[pltpu.VMEM((slots, LATENT), F32)],
        compiler_params=params(),
        name="node_forward",
    )(served, want, landed, node, w_in, w_out, vec)


def swap_start(n, me, src, dst, own, ssem, rsem):
    pltpu.make_async_copy(src.at[me], dst.at[me], own).start()
    def go(j, c):
        t = lax.rem(me + j, n)
        remote(src.at[t], dst.at[me], ssem.at[j], rsem.at[j], t).start()
        return c
    lax.fori_loop(1, n, go, 0)


def swap_wait(n, me, src, dst, own, ssem, rsem):
    def end(j, c):
        t = lax.rem(me + j, n)
        remote(src.at[t], dst.at[me], ssem.at[j], rsem.at[j], t).wait()
        return c
    lax.fori_loop(1, n, end, 0)
    pltpu.make_async_copy(src.at[me], dst.at[me], own).wait()


def flat_rows_of(ref):
    return ref[...].reshape(ref.shape[0] * ref.shape[1], ref.shape[2])


def edge_kernel(n, first, outgoing, source, pos, pos_r, *rest):
    rest = list(rest)
    blocks = rest[:3]
    geo_blocks = rest[3:6] if first else []
    rest = rest[6 if first else 3 :]
    edge_new, edge_low, sent, recv, landed, arrived, buffer, w_in, w_out, vec, own, s1, r1, s2, r2, wsem = rest[:16]
    held = [w_in, w_out, vec] + rest[16:]
    loads = [pltpu.make_async_copy(a, b, wsem.at[i]) for i, (a, b) in enumerate(zip(blocks + geo_blocks, held))]
    for load in loads:
        load.start()
    me = lax.axis_index("dev")
    greet(n, me)
    swap_start(n, me, outgoing, arrived, own.at[0], s1, r1)
    for load in loads:
        load.wait()
    if first:
        g_in, g_out, g_vec = held[3:]
        _, act = activate(first_half([source[...]], g_in, g_vec))
        hat, _ = second_half(act, g_out, g_vec)
        edge = scale_shift(hat, g_vec)
    else:
        edge = source[...]
    e = edge.astype(BF16)
    edge_low[...] = e
    slots = n * arrived.shape[1]
    pre = first_half([e], w_in, vec)
    pick_s, pick_r = pick(pos[:, 0:1], 0, slots), pick(pos[:, 1:2], 0, slots)
    put_r = place(pos_r[...], 0, slots)
    swap_wait(n, me, outgoing, arrived, own.at[0], s1, r1)
    rows = flat_rows_of(arrived)
    s = mm(pick_s, rows).astype(BF16)
    r = mm(pick_r, rows).astype(BF16)
    pre = pre + mm(s, w_in[LATENT : 2 * LATENT, :]) + mm(r, w_in[2 * LATENT :, :])
    _, act = activate(pre)
    hat, _ = second_half(act, w_out, vec)
    new = edge + scale_shift(hat, vec)
    buffer[...] = mm(put_r, new.astype(BF16)).astype(BF16).reshape(buffer.shape)
    swap_start(n, me, buffer, landed, own.at[1], s2, r2)
    edge_new[...] = new
    sent[...], recv[...] = s, r
    swap_wait(n, me, buffer, landed, own.at[1], s2, r2)


def held_scratch(block):
    return [pltpu.VMEM(a.shape, a.dtype) for a in block]


def edge_forward(n, outgoing, source, pos, pos_r, block, cid, geo=None):
    rows = source.shape[0]
    slots = outgoing.shape[0]
    outgoing = outgoing.reshape(n, slots // n, LATENT)
    V = pl.BlockSpec(memory_space=pltpu.VMEM)
    weights = list(block) + list(geo or ())
    low = lambda r: shaped(r, LATENT, dtype=BF16)
    return pl.pallas_call(
        functools.partial(edge_kernel, n, geo is not None),
        out_shape=(shaped(rows, LATENT), low(rows), low(rows), low(rows), shaped(*outgoing.shape, dtype=BF16)),
        in_specs=[ANY, V, V, V] + [ANY] * len(weights),
        out_specs=(V, V, V, V, ANY),
        scratch_shapes=[pltpu.VMEM(outgoing.shape, BF16), pltpu.VMEM(outgoing.shape, BF16)]
        + held_scratch(block)
        + [DMA((2,)), DMA((n,)), DMA((n,)), DMA((n,)), DMA((n,)), DMA((6,))]
        + held_scratch(geo or ()),
        compiler_params=params(collective_id=cid, has_side_effects=True),
        name="edge_forward",
    )(outgoing, source, pos, pos_r, *weights)


def turn_kernel(bm, at, dec_at, served, want, landed, node, x, target, level, land, count, w_in, w_out, vec, c_in, c_out, c_vec, flat, g_prev, out, d_out_o, d_vec_o, err_o, packed, packed2, d_in, d_out, d_vec, e_in, e_out, e_vec, err, acc, sem):
    i = pl.program_id(0)
    @pl.when(i == 0)
    def _():
        clear(d_in, d_out, d_vec, e_in, e_out, e_vec, err)
    got = mm(place(served[...], i * bm, bm), landed[...]).astype(BF16)
    old = node[...]
    low = old.astype(BF16)
    pre = first_half([low, got], w_in, vec)
    sigma, act = activate(pre)
    hat, inv = second_half(act, w_out, vec)
    u = (old + scale_shift(hat, vec)).astype(BF16)
    c_pre = first_half([u], c_in, c_vec)
    c_sigma, c_act = activate(c_pre)
    wide = c_out.shape[1]
    post = mm(c_act, c_out[...]) + c_vec[1:2, :wide]
    sea = (lax.broadcasted_iota(jnp.int32, (1, VARS), 1) < SEA_VARS).astype(F32)
    mask = level[...].astype(F32) * (1.0 - land[...].astype(F32) * sea)
    residual = x[...].astype(F32) + post[:, :VARS] - target[...]
    divisor = jnp.maximum(count[...], 1.0)
    err[:, :VARS] += col(mask * residual * residual)
    g = 2.0 * mask * residual / divisor
    g_low = jnp.concatenate([g, jnp.zeros((bm, wide - VARS), F32)], axis=1).astype(BF16)
    c_g = act_back(g_low, c_pre, c_sigma, c_out)
    weight_sums([u], c_act, g_low, c_g, e_in, e_out, e_vec)
    g_node = mm_nt(c_g, c_in[...])
    g_post = norm_back(g_node, hat, inv, vec, d_vec)
    g_pre = act_back(g_post, pre, sigma, w_out)
    weight_sums([low, got], act, g_post, g_pre, d_in, d_out, d_vec)
    g_prev[...] = g_node + mm_nt(g_pre, w_in[:LATENT, :])
    send_rows(i, bm, mm_nt(g_pre, w_in[LATENT:, :]).astype(BF16), want, out, acc)
    @pl.when(i == pl.num_programs(0) - 1)
    def _():
        d_out_o[...] = e_out[...]
        d_vec_o[...] = e_vec[...]
        err_o[...] = err[...]
        pack_matrix(packed2, e_in, LATENT, 0)
        one = store_flat(packed2, flat, dec_at, sem.at[0])
        pack(packed, 0, 2 * LATENT, d_in, d_out, d_vec)
        two = store_flat(packed, flat, at, sem.at[1])
        one.wait()
        two.wait()


def turn(served, want, landed, node, x, target, level, land, count, block, dec, flat_rows, at, dec_at, bm=512):
    rows = node.shape[0]
    slots = want.shape[0]
    wide = dec[1].shape[1]
    v = lambda: spec((bm, VARS), False)
    return pl.pallas_call(
        functools.partial(turn_kernel, bm, at, dec_at),
        grid=(rows // bm,),
        out_shape=(shaped(flat_rows, 128), shaped(rows, LATENT), shaped(slots, LATENT, dtype=BF16), shaped(LATENT, wide), shaped(8, LATENT), shaped(1, wide)),
        in_specs=[spec((1, slots)), spec((slots, 1)), spec((slots, LATENT)), spec((bm, LATENT), False), v(), v(), v(), spec((bm, 1), False), spec((1, 1))] + [spec(a.shape) for a in (*block, *dec)],
        out_specs=(ANY, spec((bm, LATENT), False), spec((slots, LATENT)), spec((LATENT, wide)), spec((8, LATENT)), spec((1, wide))),
        scratch_shapes=[packed_rows(2 * LATENT), pltpu.VMEM((4 * LATENT, 128), F32)] + mlp_sums(2 * LATENT) + mlp_sums(LATENT, wide) + [pltpu.VMEM((1, wide), F32), pltpu.VMEM((slots, LATENT), F32), DMA((2,))],
        compiler_params=params(),
        name="turn",
    )(served, want, landed, node, x, target, level, land, count, *block, *dec)


def edge_back_kernel(n, at, has_edge, geo_at, tail_at, outgoing, edge_low, sent, recv, pos, pos_s, pos_r, *rest):
    rest = list(rest)
    blocks = [rest.pop(0) for _ in range(3)]
    geo_blocks = [rest.pop(0) for _ in range(3)] if geo_at is not None else []
    rest.pop(0)
    g_edge = rest.pop(0) if has_edge else None
    geo = rest.pop(0) if geo_at is not None else None
    tail = rest.pop(0) if tail_at is not None else None
    flat, edge_prev, landed, returned, buffer, packed, d_in, d_out, d_vec, own, s1, r1, s2, r2, wsem, fsem, w_in, w_out, vec = rest[:19]
    rest = rest[19:]
    held = [w_in, w_out, vec] + rest[:3]
    loads = [pltpu.make_async_copy(a, b, wsem.at[i]) for i, (a, b) in enumerate(zip(blocks + geo_blocks, held))]
    for load in loads:
        load.start()
    stores = []
    if tail is not None:
        stores.append(store_flat(tail, flat, tail_at, fsem.at[2]))
    me = lax.axis_index("dev")
    greet(n, me)
    swap_start(n, me, outgoing, returned, own.at[0], s1, r1)
    for load in loads:
        load.wait()
    clear(d_in, d_out, d_vec)
    us = [edge_low[...], sent[...], recv[...]]
    slots = n * returned.shape[1]
    pre = first_half(us, w_in, vec)
    sigma, act = activate(pre)
    hat, inv = second_half(act, w_out, vec)
    pick_r = pick(pos[:, 1:2], 0, slots)
    put_s, put_r = place(pos_s[...], 0, slots), place(pos_r[...], 0, slots)
    if geo is not None:
        g_in, g_out, g_vec = rest[:3]
        c_pre = first_half([geo[...]], g_in, g_vec)
        c_sigma, c_act = activate(c_pre)
        c_hat, c_inv = second_half(c_act, g_out, g_vec)
    swap_wait(n, me, outgoing, returned, own.at[0], s1, r1)
    g = mm(pick_r, flat_rows_of(returned))
    if has_edge:
        g = g_edge[...] + g
    low = norm_back(g, hat, inv, vec, d_vec)
    g_pre = act_back(low, pre, sigma, w_out)
    s = mm_nt(g_pre, w_in[LATENT : 2 * LATENT, :]).astype(BF16)
    r = mm_nt(g_pre, w_in[2 * LATENT :, :]).astype(BF16)
    buffer[...] = (mm(put_s, s) + mm(put_r, r)).astype(BF16).reshape(buffer.shape)
    swap_start(n, me, buffer, landed, own.at[1], s2, r2)
    prev = g + mm_nt(g_pre, w_in[:LATENT, :])
    edge_prev[...] = prev
    weight_sums(us, act, low, g_pre, d_in, d_out, d_vec)
    pack(packed, 0, 3 * LATENT, d_in, d_out, d_vec)
    stores.append(store_flat(packed, flat, at, fsem.at[0]))
    if geo is not None:
        packed2, e_in, e_out, e_vec = rest[3:]
        clear(e_in, e_out, e_vec)
        c_low = norm_back(prev, c_hat, c_inv, g_vec, e_vec)
        c_g = act_back(c_low, c_pre, c_sigma, g_out)
        weight_sums([geo[...]], c_act, c_low, c_g, e_in, e_out, e_vec)
        pack(packed2, 0, GEO, e_in, e_out, e_vec)
        stores.append(store_flat(packed2, flat, geo_at, fsem.at[1]))
    swap_wait(n, me, buffer, landed, own.at[1], s2, r2)
    for store in stores:
        store.wait()


def edge_backward(n, outgoing, ins, pos, pos_s, pos_r, block, flat, at, cid, g_edge=None, geo=None, geo_at=None, tail=None, tail_at=None):
    rows = pos.shape[0]
    slots = outgoing.shape[0]
    outgoing = outgoing.reshape(n, slots // n, LATENT)
    V = pl.BlockSpec(memory_space=pltpu.VMEM)
    geo_block = geo[1] if geo is not None else ()
    args = [outgoing, *ins, pos, pos_s, pos_r, *block, *geo_block, flat]
    specs = [ANY] + [V] * 6 + [ANY] * (4 + len(geo_block))
    which = len(args) - 1
    scratch = [pltpu.VMEM(outgoing.shape, BF16), pltpu.VMEM(outgoing.shape, BF16), packed_rows(3 * LATENT)] + mlp_sums(3 * LATENT)
    scratch += [DMA((2,)), DMA((n,)), DMA((n,)), DMA((n,)), DMA((n,)), DMA((6,)), DMA((3,))] + held_scratch(block)
    for more in (g_edge, geo[0] if geo is not None else None, tail):
        if more is not None:
            args.append(more)
            specs.append(V)
    if geo is not None:
        scratch += held_scratch(geo_block) + [packed_rows(GEO)] + mlp_sums(geo[0].shape[1])
    return pl.pallas_call(
        functools.partial(edge_back_kernel, n, at, g_edge is not None, geo_at, tail_at),
        out_shape=(shaped(*flat.shape), shaped(rows, LATENT), shaped(*outgoing.shape, dtype=BF16)),
        in_specs=specs,
        out_specs=(ANY, V, ANY),
        scratch_shapes=scratch,
        input_output_aliases={which: 0},
        compiler_params=params(collective_id=cid, has_side_effects=True),
        name="edge_backward",
    )(*args)


def node_back_kernel(bm, at, served, want, landed, g_node, low, sums, w_in, w_out, vec, flat_in, flat, g_prev, out, packed, d_in, d_out, d_vec, acc, sem):
    i = pl.program_id(0)
    @pl.when(i == 0)
    def _():
        clear(d_in, d_out, d_vec)
    us = [low[...], sums[...]]
    pre = first_half(us, w_in, vec)
    sigma, act = activate(pre)
    hat, inv = second_half(act, w_out, vec)
    g = g_node[...] + mm(place(served[...], i * bm, bm), landed[...])
    g_post = norm_back(g, hat, inv, vec, d_vec)
    g_pre = act_back(g_post, pre, sigma, w_out)
    weight_sums(us, act, g_post, g_pre, d_in, d_out, d_vec)
    g_prev[...] = g + mm_nt(g_pre, w_in[:LATENT, :])
    send_rows(i, bm, mm_nt(g_pre, w_in[LATENT:, :]).astype(BF16), want, out, acc)
    @pl.when(i == pl.num_programs(0) - 1)
    def _():
        pack(packed, 0, 2 * LATENT, d_in, d_out, d_vec)
        store_flat(packed, flat, at, sem).wait()


def node_backward(served, want, landed, g_node, low, sums, block, flat, at, bm=512):
    rows = low.shape[0]
    slots = want.shape[0]
    b = lambda: spec((bm, LATENT), False)
    return pl.pallas_call(
        functools.partial(node_back_kernel, bm, at),
        grid=(rows // bm,),
        out_shape=(shaped(*flat.shape), shaped(rows, LATENT), shaped(slots, LATENT, dtype=BF16)),
        in_specs=[spec((1, slots)), spec((slots, 1)), spec((slots, LATENT)), b(), b(), b()] + [spec(a.shape) for a in block] + [ANY],
        out_specs=(ANY, b(), spec((slots, LATENT))),
        scratch_shapes=[packed_rows(2 * LATENT)] + mlp_sums(2 * LATENT) + [pltpu.VMEM((slots, LATENT), F32), DMA],
        input_output_aliases={9: 0},
        compiler_params=params(),
        name="node_backward",
    )(served, want, landed, g_node, low, sums, *block, flat)


def encode_back_kernel(bm, served, landed, g_node, x, w_in, w_out, vec, flat_in, flat, packed, d_in, d_out, d_vec, sem):
    i = pl.program_id(0)
    @pl.when(i == 0)
    def _():
        clear(d_in, d_out, d_vec)
    us = [x[...]]
    pre = first_half(us, w_in, vec)
    sigma, act = activate(pre)
    hat, inv = second_half(act, w_out, vec)
    g = g_node[...] + mm(place(served[...], i * bm, bm), landed[...])
    g_post = norm_back(g, hat, inv, vec, d_vec)
    g_pre = act_back(g_post, pre, sigma, w_out)
    weight_sums(us, act, g_post, g_pre, d_in, d_out, d_vec)
    @pl.when(i == pl.num_programs(0) - 1)
    def _():
        packed[0:4, :] = jnp.zeros((4, 128), F32)
        pack(packed, 4, VARS, d_in, d_out, d_vec)
        store_flat(packed, flat, 0, sem).wait()


def encode_backward(served, landed, g_node, x, block, flat, bm=512):
    rows, k = x.shape
    slots = landed.shape[0]
    return pl.pallas_call(
        functools.partial(encode_back_kernel, bm),
        grid=(rows // bm,),
        out_shape=shaped(*flat.shape),
        in_specs=[spec((1, slots)), spec((slots, LATENT)), spec((bm, LATENT), False), spec((bm, k), False)] + [spec(a.shape) for a in block] + [ANY],
        out_specs=ANY,
        scratch_shapes=[packed_rows(VARS, 4)] + mlp_sums(k) + [DMA],
        input_output_aliases={7: 0},
        compiler_params=params(),
        name="encode_backward",
    )(served, landed, g_node, x, *block, flat)


def relay_plan(segments, share_rows):
    jobs = []
    for block_id, part_name, part_shape, offset, entries in segments:
        if part_name not in ("w_in", "w_out") or part_shape[1] != LATENT:
            continue
        for first in range(0, part_shape[0], LATENT):
            rows = min(LATENT, part_shape[0] - first)
            follow = 0
            if first + rows == part_shape[0]:
                follow = 1 if part_name == "w_in" else 3
            begin = offset // 128 + 4 * first
            end = begin + 4 * (rows + follow)
            parts = []
            at = begin
            while at < end:
                owner, low = divmod(at, share_rows)
                size = min(end - at, share_rows - low)
                base = low // 16 * 16
                span = (low + size - base + 15) // 16 * 16
                parts.append((owner, base, span, low - base, at - begin))
                at += size
            jobs.append((block_id, part_name, first, rows, follow, parts))
    return jobs


def relay_kernel(jobs, shapes, shares, *rest):
    count = sum(len(s) for s in shapes)
    outs = rest[:count]
    stage, lines, made, vecs, isem, osem, vsem = rest[count:]
    index = {}
    for b, s in enumerate(shapes):
        for name, _ in s:
            index[b, name] = len(index)
    loads, at = [], 0
    for number, (b, name, first, rows, follow, parts) in enumerate(jobs):
        mine = []
        for owner, base, span, skip, to in parts:
            copy = pltpu.make_async_copy(shares.at[owner, pl.ds(base, span)], stage.at[pl.ds(at, span)], isem.at[len(loads) * 0 + number * 4 + len(mine)])
            copy.start()
            mine.append((copy, at, span, skip, to))
            at += span
        loads.append(mine)
    vecs[...] = jnp.zeros_like(vecs)
    stores = []
    for number, ((b, name, first, rows, follow, parts), mine) in enumerate(zip(jobs, loads)):
        for copy, where, span, skip, to in mine:
            copy.wait()
            lines[pl.ds(16 + to - skip, span), :] = stage[pl.ds(where, span), :].astype(F32)
        full = (rows + 15) // 16 * 16
        for j in range(4):
            made[number, :rows, 128 * j : 128 * (j + 1)] = lines[pl.ds(16 + j, rows, stride=4), :].astype(BF16)
        if rows < LATENT:
            made[number, rows:, :] = jnp.zeros((LATENT - rows, LATENT), BF16)
        for i in range(follow):
            row = i if name == "w_in" else i + 1
            for j in range(4):
                p = 16 + 4 * (rows + i) + j
                vecs[b, row : row + 1, 128 * j : 128 * (j + 1)] = lines[p : p + 1, :]
        out = outs[index[b, name]]
        size = min(LATENT, out.shape[0] - first)
        store = pltpu.make_async_copy(made.at[number, pl.ds(0, size)], out.at[pl.ds(first, size)], osem.at[number])
        store.start()
        stores.append(store)
    for b in range(len(shapes)):
        store = pltpu.make_async_copy(vecs.at[b], outs[index[b, "vec"]], vsem.at[b])
        store.start()
        stores.append(store)
    for store in stores:
        store.wait()


def relay(shares, segments, share_rows):
    jobs = relay_plan(segments, share_rows)
    blocks = segments[-1][0] + 1
    shapes = [[] for _ in range(blocks)]
    for b, name, shape, _, _ in segments:
        if name in ("w_in", "w_out") and shape[1] == LATENT:
            shapes[b].append((name, (-(-shape[0] // 128) * 128, LATENT)))
    for s in shapes:
        s.append(("vec", (8, LATENT)))
    stage = sum(span for job in jobs for _, _, span, _, _ in job[5])
    out_shape = [shaped(*shape, dtype=F32 if name == "vec" else BF16) for s in shapes for name, shape in s]
    outs = pl.pallas_call(
        functools.partial(relay_kernel, jobs, shapes),
        out_shape=out_shape,
        in_specs=[ANY],
        out_specs=[ANY] * len(out_shape),
        scratch_shapes=[pltpu.VMEM((stage, 128), BF16), pltpu.VMEM((16 + 4 * LATENT + 64, 128), F32), pltpu.VMEM((len(jobs), LATENT, LATENT), BF16), pltpu.VMEM((blocks, 8, LATENT), F32), DMA((4 * len(jobs),)), DMA((len(jobs),)), DMA((blocks,))],
        compiler_params=params(),
        name="relay",
    )(shares)
    made = [{} for _ in shapes]
    for (b, name), value in zip([(b, name) for b, s in enumerate(shapes) for name, _ in s], outs):
        made[b][name] = value
    return made


def make_asks(edge_owners, edge_local, devices):
    edges_here = edge_owners.shape[0]
    capacity = (5 * edges_here // (2 * devices) + 7) // 8 * 8
    owner = edge_owners.reshape(-1)
    local = edge_local.reshape(-1)
    wants = owner.shape[0]
    order = jnp.arange(wants, dtype=jnp.int32)
    before = (owner[:, None] == owner[None, :]) & (order[None, :] < order[:, None])
    ranking = jnp.sum(before.astype(jnp.int32), axis=1)
    position = owner * capacity + ranking
    slots = jnp.arange(devices * capacity, dtype=jnp.int32)
    asking = jnp.sum(jnp.where(slots[:, None] == position[None, :], local[None, :] + 1, 0), axis=1) - 1
    return (position, asking, capacity)


def widen(values, width):
    return jnp.pad(values, ((0, 0), (0, width - values.shape[1])))


def make_block(params):
    rows = params["w_in"].shape[0]
    w_in = jnp.pad(params["w_in"], ((0, -rows % 128), (0, 0)))
    w_out = widen(params["w_out"], (params["w_out"].shape[1] + 127) // 128 * 128)
    names = [name for name in ("b_in", "b_out", "gain", "shift") if name in params]
    vectors = [widen(params[name][None], LATENT) for name in names]
    vectors.append(jnp.zeros((8 - len(vectors), LATENT), jnp.bfloat16))
    return (w_in, w_out, jnp.concatenate(vectors).astype(jnp.float32))


def relaid_blocks(shares, segments, share_rows):
    def rows_of(first, last):
        parts = []
        while first < last:
            owner, low = divmod(first, share_rows)
            size = min(last - first, share_rows - low)
            parts.append(shares[owner, low : low + size])
            first += size
        return jnp.concatenate(parts) if len(parts) > 1 else parts[0]
    made = relay(shares, segments, share_rows)
    [(shape, begin, size)] = [(s, o, e) for _, name, s, o, e in segments if name == "w_out" and s[1] != LATENT]
    wide = shape[1]
    lines = rows_of(begin // 128, -(-(begin + size + wide) // 128)).reshape(-1)
    made[-1]["w_out"] = widen(lines[:size].reshape(shape), (wide + 127) // 128 * 128)
    bias = lines[size : size + wide].astype(jnp.float32)
    made[-1]["vec"] = made[-1]["vec"].at[1, :wide].set(bias)
    return [(m["w_in"], m["w_out"], m["vec"]) for m in made]


def local(
    inputs,
    targets,
    geometry,
    land_sea,
    level_mask,
    edge_owners,
    edge_local,
    step_count,
    master,
    first_moment,
    second_moment,
    ema,
):
    segments, total = layout(LATENT, VARS, GEO, LAYERS)
    devices = lax.axis_size("dev")
    share = master.shape[0]
    mine = devices == 32 and share % 128 == 0
    ocean = (jnp.arange(VARS) < SEA_VARS).astype(jnp.float32)
    position, asking, capacity = make_asks(edge_owners, edge_local, devices)
    slots = devices * capacity
    counted = jnp.sum(level_mask * (1 - land_sea[:, None] * ocean.astype(jnp.int32)[None, :])).astype(jnp.float32)
    if mine:
        share_rows = share // 128
        pad_rows = (share_rows + 31) // 32 * 32
        low = jnp.pad(master.astype(jnp.bfloat16).reshape(share_rows, 128), ((0, pad_rows - share_rows), (0, 0)))
        ask = jnp.pad(asking.reshape(devices, 1, capacity), ((0, 0), (0, 0), (0, 128 - capacity)))
        number = jnp.zeros((8, 128), jnp.float32).at[0, 0].set(counted)
        gathered, served, numbers = gather_weights(low, ask, number, 1)
        blocks = relaid_blocks(gathered, segments, share_rows)
        served = served[:, 0, :capacity].reshape(-1)
        count = jnp.sum(numbers)
    else:
        full_weights = lax.all_gather(master.astype(jnp.bfloat16), "dev", axis=0, tiled=True)
        blocks = [make_block(b) for b in unpack(full_weights, segments)]
        served = lax.all_to_all(asking.reshape(devices, capacity), "dev", 0, 0, tiled=True).reshape(-1)
        count = lax.psum(counted, "dev")
    want = served[:, None]
    served = served[None, :]
    pos = position.reshape(-1, 2)
    pos_s, pos_r = pos[:, 0][None, :], pos[:, 1][None, :]
    x = widen(inputs, 256)
    geo = widen(geometry, 128)
    land = land_sea[:, None]
    node, low, outgoing = encode(x, blocks[0], want)
    node_kept, edge_kept = [], []
    edge = geo
    for k in range(LAYERS):
        edge, *kept, landed = edge_forward(
            devices, outgoing, edge, pos, pos_r, blocks[2 + 2 * k], 3 + min(k, 1), blocks[1] if k == 0 else None
        )
        edge_kept.append(kept)
        landed = landed.reshape(slots, LATENT)
        if k < LAYERS - 1:
            before = low
            node, low, sums, outgoing = node_forward(served, want, landed, node, blocks[3 + 2 * k])
            node_kept.append((before, sums))
    pieces = [4 * s for s in (VARS + LATENT + 4, GEO + LATENT + 4) + (3 * LATENT + LATENT + 4, 2 * LATENT + LATENT + 4) * LAYERS]
    lead = 4
    places = [0] + [lead + sum(pieces[: i + 1]) for i in range(len(pieces))]
    flat_rows = (lead + PARAMS // 128 + 15) // 16 * 16 + 8
    dec_at = places[-1]
    tail_at = dec_at + 4 * LATENT
    k = LAYERS - 1
    flat, g_node, outgoing, d_out, d_vec, errors = turn(
        served, want, landed, node, inputs, targets, level_mask, land, count.reshape(1, 1),
        blocks[3 + 2 * k], blocks[-1], flat_rows, places[3 + 2 * k], dec_at,
    )
    error_here = jnp.sum(errors)
    tail = jnp.concatenate([d_vec[0], d_out[:, :VARS].reshape(-1), d_vec[1, :VARS]])
    tail_rows = flat_rows - tail_at
    tail = jnp.pad(tail, (0, tail_rows * 128 - tail.shape[0])).reshape(tail_rows, 128)
    g_edge = None
    for k in reversed(range(LAYERS)):
        more = {}
        if k == LAYERS - 1:
            more = dict(tail=tail, tail_at=tail_at)
        if k == 0:
            more = dict(geo=(geo, blocks[1]), geo_at=places[1])
        flat, g_edge, landed = edge_backward(
            devices, outgoing, edge_kept[k], pos, pos_s, pos_r, blocks[2 + 2 * k], flat, places[2 + 2 * k],
            5 + (LAYERS - 1 - k), g_edge=g_edge, **more,
        )
        landed = landed.reshape(slots, LATENT)
        if k > 0:
            before, sums = node_kept[k - 1]
            flat, g_node, outgoing = node_backward(
                served, want, landed, g_node, before, sums, blocks[1 + 2 * k], flat, places[1 + 2 * k]
            )
    flat = encode_backward(served, landed, g_node, x, blocks[0], flat)
    if mine:
        rows = (share_rows + 6 + 15) // 16 * 16
        error = jnp.zeros((8, 128), jnp.float32).at[0, 0].set(error_here)
        summed, squares, errors = reduce_gradient(flat, error, share_rows, lead, rows, 2)
        skip = lax.rem(lead + share_rows * lax.axis_index("dev"), 8)
        own_grad = lax.dynamic_slice_in_dim(summed, skip, share_rows).reshape(-1)
        grad_norm = jnp.sqrt(jnp.sum(squares))
        error_sum = jnp.sum(errors)
    else:
        own_grad = lax.psum_scatter(flat[lead : lead + PARAMS // 128].reshape(-1), "dev", scatter_dimension=0, tiled=True)
        error_sum, squares = lax.psum((error_here, jnp.sum(own_grad * own_grad)), "dev")
        grad_norm = jnp.sqrt(squares)
    loss = error_sum / jnp.maximum(count, 1.0)
    clipped = own_grad * jnp.minimum(1.0, clip_limit / grad_norm)
    step = step_count[0].astype(jnp.float32)
    new_first = beta_one * first_moment + (1.0 - beta_one) * clipped
    new_second = beta_two * second_moment + (1.0 - beta_two) * clipped * clipped
    first_hat = new_first / (1.0 - beta_one**step)
    second_hat = new_second / (1.0 - beta_two**step)
    new_master = master - learn_rate * (
        first_hat / (jnp.sqrt(second_hat) + adam_eps) + decay_rate * master
    )
    new_ema = ema_keep * ema + (1.0 - ema_keep) * new_master
    return (new_master, new_first, new_second, new_ema, loss, grad_norm)


def solution(mesh):
    in_specs = (
        P("dev", None),
        P("dev", None),
        P("dev", None),
        P("dev"),
        P("dev", None),
        P("dev", None),
        P("dev", None),
        P(),
        P("dev"),
        P("dev"),
        P("dev"),
        P("dev"),
    )
    out_specs = (P("dev"), P("dev"), P("dev"), P("dev"), P(), P())
    return jax.shard_map(local, mesh=mesh, in_specs=in_specs, out_specs=out_specs, check_vma=False)
```

```python
import functools
import types

import jax
import jax.numpy as jnp
import numpy as np
from jax import lax
from jax.experimental import pallas as pl
from jax.experimental.pallas import tpu as pltpu
from jax.sharding import PartitionSpec as P

LATENT = 512
VARS = 227
GEO = 4
SEA_VARS = 4
LAYERS = 3
PARAMS = 6545408


norm_eps = 1e-05
clip_limit = 0.01
beta_one = 0.9
beta_two = 0.999
adam_eps = 1e-08
learn_rate = 0.03
decay_rate = 0.1
ema_keep = 0.9


def layout(width, variables, geometry, layers):
    shapes = [(variables, width, True), (geometry, width, True)]
    for k in range(layers):
        shapes.append((3 * width, width, True))
        shapes.append((2 * width, width, True))
    shapes.append((width, variables, False))
    segments = []
    offset = 0
    for block_id, (fan_in, fan_out, normed) in enumerate(shapes):
        members = [
            ("w_in", (fan_in, width)),
            ("b_in", (width,)),
            ("w_out", (width, fan_out)),
            ("b_out", (fan_out,)),
        ]
        if normed:
            members = members + [("gain", (fan_out,)), ("shift", (fan_out,))]
        for part_name, part_shape in members:
            entries = int(np.prod(part_shape))
            segments.append((block_id, part_name, part_shape, offset, entries))
            offset += entries
    return (segments, offset)


def unpack(flat, segments):
    blocks = [dict() for k in range(segments[-1][0] + 1)]
    for block_id, part_name, part_shape, offset, entries in segments:
        blocks[block_id][part_name] = flat[offset : offset + entries].reshape(part_shape)
    return blocks


MESH = pl.DeviceIdType.MESH

def remote(src, dst, send, recv, target):
    return pltpu.make_async_remote_copy(src, dst, send, recv, device_id=(target,), device_id_type=MESH)

def greet(n, me):
    barrier = pltpu.get_barrier_semaphore()
    def hello(j, c):
        pl.semaphore_signal(barrier, inc=1, device_id=(lax.rem(me + j, n),), device_id_type=MESH)
        return c
    lax.fori_loop(1, n, hello, 0)
    pl.semaphore_wait(barrier, n - 1)

def a2a_kernel(n, a_ref, o_ref, own, ssem, rsem):
    me = lax.axis_index('dev')
    greet(n, me)
    here = pltpu.make_async_copy(a_ref.at[me], o_ref.at[me], own)
    here.start()
    def go(j, c):
        t = lax.rem(me + j, n)
        remote(a_ref.at[t], o_ref.at[me], ssem.at[j], rsem.at[j], t).start()
        return c
    lax.fori_loop(1, n, go, 0)
    def end(j, c):
        t = lax.rem(me + j, n)
        remote(a_ref.at[t], o_ref.at[me], ssem.at[j], rsem.at[j], t).wait()
        return c
    lax.fori_loop(1, n, end, 0)
    here.wait()

def a2a(x, cid, space=pl.ANY):
    n = x.shape[0]
    return pl.pallas_call(
        functools.partial(a2a_kernel, n),
        out_shape=jax.ShapeDtypeStruct(x.shape, x.dtype),
        in_specs=[pl.BlockSpec(memory_space=space)],
        out_specs=pl.BlockSpec(memory_space=space),
        scratch_shapes=[pltpu.SemaphoreType.DMA, pltpu.SemaphoreType.DMA((n,)), pltpu.SemaphoreType.DMA((n,))],
        compiler_params=pltpu.CompilerParams(collective_id=cid, has_side_effects=True),
    )(x)

def gather_kernel(w_ref, ask_ref, num_ref, o_ref, served_ref, nums_ref, own, small_s, small_r, zs, zr, hs, hr, cs, cr, ds, dr, bs, br):
    n = 32
    me = lax.axis_index('dev')
    c, x, y, z = lax.rem(me, 2), lax.rem(me // 2, 2), lax.rem(me // 4, 2), me // 8
    rows = w_ref.shape[0]
    half = rows // 2
    A, B = pl.ds(0, half), pl.ds(half, half)
    def dev(z, y, x, c):
        return ((z * 2 + y) * 2 + x) * 2 + c
    greet(n, me)
    tx, ty, tc = dev(z, y, 1 - x, c), dev(z, 1 - y, x, c), dev(z, y, x, 1 - c)
    up, down = dev(lax.rem(z + 1, 4), y, x, c), dev(lax.rem(z + 3, 4), y, x, c)
    pend = []
    def start(cp):
        cp.start(); pend.append(cp)
    mine = pltpu.make_async_copy(w_ref, o_ref.at[me], own.at[0])
    mine.start()
    planes = [z, z + 1 - 2 * lax.rem(z, 2), 2 - z // 2, 3 - 3 * (z // 2)]
    def on_up(i, wait):
        src = w_ref if i == 0 else o_ref.at[dev(planes[i], y, x, c)]
        slot = dev(planes[i], y, x, c)
        @pl.when((planes[i] <= z) & (z < 3))
        def _():
            cp = remote(src, o_ref.at[slot], zs.at[0, i], zr.at[planes[i]], up)
            cp.wait_send() if wait else cp.start()
    def on_down(i, wait):
        src = w_ref if i == 0 else o_ref.at[dev(planes[i], y, x, c)]
        slot = dev(planes[i], y, x, c)
        @pl.when((planes[i] >= z) & (z > 0))
        def _():
            cp = remote(src, o_ref.at[slot], zs.at[1, i], zr.at[planes[i]], down)
            cp.wait_send() if wait else cp.start()
    start(remote(w_ref.at[A], o_ref.at[me, A], hs.at[0, 0], hr.at[0, 0], tx))
    start(remote(w_ref.at[B], o_ref.at[me, B], hs.at[0, 1], hr.at[0, 1], ty))
    on_up(0, False)
    on_down(0, False)
    start(remote(w_ref, o_ref.at[me], bs.at[0], br.at[0], tc))
    mine2 = pltpu.make_async_copy(ask_ref.at[me], served_ref.at[me], own.at[1])
    mine2.start()
    mine3 = pltpu.make_async_copy(num_ref, nums_ref.at[me], own.at[2])
    mine3.start()
    def go(j, carry):
        t = lax.rem(me + j, n)
        remote(ask_ref.at[t], served_ref.at[me], small_s.at[0, j], small_r.at[0, j], t).start()
        remote(num_ref, nums_ref.at[me], small_s.at[1, j], small_r.at[1, j], t).start()
        return carry
    lax.fori_loop(1, n, go, 0)
    nb = [1]
    def sib(slot, part):
        i = nb[0]; nb[0] += 1
        ref = o_ref.at[slot] if part is None else o_ref.at[slot, part]
        start(remote(ref, ref, bs.at[i], br.at[i], tc))
    def first(k):
        s = dev(planes[k], y, x, c)
        remote(w_ref, o_ref.at[s], zs.at[0, k], zr.at[planes[k]], tc).wait_recv()
        start(remote(o_ref.at[s, A], o_ref.at[s, A], hs.at[k, 0], hr.at[k, 0], tx))
        start(remote(o_ref.at[s, B], o_ref.at[s, B], hs.at[k, 1], hr.at[k, 1], ty))
        on_up(k, False)
        on_down(k, False)
        sib(s, None)
    def second(k):
        zz = planes[k]
        s = dev(zz, y, x, c)
        sx, sy = dev(zz, y, 1 - x, c), dev(zz, 1 - y, x, c)
        own_a = w_ref.at[A] if k == 0 else o_ref.at[s, A]
        own_b = w_ref.at[B] if k == 0 else o_ref.at[s, B]
        start(remote(own_a, o_ref.at[s, A], cs.at[k, 0], cr.at[k, 0], ty))
        start(remote(own_b, o_ref.at[s, B], ds.at[k, 0], dr.at[k, 0], tx))
        remote(own_a, o_ref.at[sx, A], hs.at[k, 0], hr.at[k, 0], tx).wait_recv()
        start(remote(o_ref.at[sx, A], o_ref.at[sx, A], cs.at[k, 1], cr.at[k, 1], ty))
        remote(own_b, o_ref.at[sy, B], hs.at[k, 1], hr.at[k, 1], ty).wait_recv()
        start(remote(o_ref.at[sy, B], o_ref.at[sy, B], ds.at[k, 1], dr.at[k, 1], tx))
        sib(sx, A)
        sib(sy, B)
    def third(k):
        zz = planes[k]
        sx, sy, sd = dev(zz, y, 1 - x, c), dev(zz, 1 - y, x, c), dev(zz, 1 - y, 1 - x, c)
        w = w_ref.at[A]
        remote(w, o_ref.at[sy, A], cs.at[k, 0], cr.at[k, 0], ty).wait_recv()
        sib(sy, A)
        remote(w, o_ref.at[sx, B], ds.at[k, 0], dr.at[k, 0], tx).wait_recv()
        sib(sx, B)
        remote(w, o_ref.at[sd, A], cs.at[k, 1], cr.at[k, 1], ty).wait_recv()
        sib(sd, A)
        remote(w, o_ref.at[sd, B], ds.at[k, 1], dr.at[k, 1], tx).wait_recv()
        sib(sd, B)
    second(0)
    first(1)
    third(0)
    second(1)
    first(2)
    third(1)
    second(2)
    first(3)
    third(2)
    second(3)
    third(3)
    nb2 = [0]
    def got(*parts):
        for part in parts:
            i = nb2[0]; nb2[0] += 1
            ref = w_ref if part is None else w_ref.at[part]
            o = o_ref.at[me] if part is None else o_ref.at[me, part]
            remote(ref, o, bs.at[i], br.at[i], tc).wait_recv()
    g1, g2, g3 = (None,), (A, B), (A, B, A, B)
    for g in (g1, g2, g1, g3, g2, g1, g3, g2, g1, g3, g2, g3):
        got(*g)
    def end(j, carry):
        t = lax.rem(me + j, n)
        remote(ask_ref.at[t], served_ref.at[me], small_s.at[0, j], small_r.at[0, j], t).wait()
        remote(num_ref, nums_ref.at[me], small_s.at[1, j], small_r.at[1, j], t).wait()
        return carry
    lax.fori_loop(1, n, end, 0)
    for i in range(4):
        on_up(i, True)
        on_down(i, True)
    for cp in pend:
        cp.wait_send()
    mine.wait(); mine2.wait(); mine3.wait()


def gather_weights(w, ask, num, cid):
    n = 32
    rows = w.shape[0]
    D = pltpu.SemaphoreType.DMA
    sib = 1 + 4 * 2 + 3 + 4 * 4
    anyspec = pl.BlockSpec(memory_space=pl.ANY)
    return pl.pallas_call(
        gather_kernel,
        out_shape=(jax.ShapeDtypeStruct((n, rows, 128), w.dtype), jax.ShapeDtypeStruct(ask.shape, ask.dtype), jax.ShapeDtypeStruct((n,) + num.shape, num.dtype)),
        in_specs=[anyspec] * 3, out_specs=(anyspec,) * 3,
        scratch_shapes=[D((3,)), D((2, n)), D((2, n)), D((2, 4)), D((4,)), D((4, 2)), D((4, 2)), D((4, 2)), D((4, 2)), D((4, 2)), D((4, 2)), D((sib,)), D((sib,))],
        compiler_params=pltpu.CompilerParams(collective_id=cid, has_side_effects=True),
    )(w, ask, num)


def accumulate(dst, src, rows):
    step = 80
    whole = rows // step
    def body(i, carry):
        at = pl.ds(pl.multiple_of(i * step, 8), step)
        dst[at] = dst[at] + src[at]
        return carry
    lax.fori_loop(0, whole, body, 0)
    if rows % step:
        at = pl.ds(whole * step, rows % step)
        dst[at] = dst[at] + src[at]

SCHEDULE = ['g0', 'g1', 's0', 'm0', 'g2', 's1', 'f0', 'm1', 'g3', 's2', 'f1', 'm2', 's3', 'f2', 'm3', 'f3']


def reduce_kernel(share_rows, lead, g_ref, err_ref, o_ref, sq_ref, errs_ref, L, R, YA, XA, XB, YB, Z, sq, own, ls, rs0_s, rs0_r, as1, ar1, as2, ar2, bs1, br1, bs2, br2, zs, zr, es, er, qs, qr):
    n = 32
    me = lax.axis_index('dev')
    c, x, y, z = lax.rem(me, 2), lax.rem(me // 2, 2), lax.rem(me // 4, 2), me // 8
    rows = L.shape[2]
    half = rows // 2
    A, B = pl.ds(0, half), pl.ds(half, half)
    def dev(z, y, x, c):
        return ((z * 2 + y) * 2 + x) * 2 + c
    def begin(d):
        return pl.multiple_of((lead + share_rows * d) // 8 * 8, 8)
    greet(n, me)
    tx, ty, tc = dev(z, y, 1 - x, c), dev(z, 1 - y, x, c), dev(z, y, x, 1 - c)
    pend = []
    def start(cp):
        cp.start(); pend.append(cp)
    order = [2, 1, 3, 0]
    zz = [lax.rem(z + k, 4) for k in range(4)]
    def fetch(k):
        for i in range(4):
            ys, xs = i // 2, i % 2
            start(remote(g_ref.at[pl.ds(begin(dev(zz[k], ys, xs, 1 - c)), rows)], R.at[k, i], rs0_s.at[k, i], rs0_r.at[k, i], tc))
            pltpu.make_async_copy(g_ref.at[pl.ds(begin(dev(zz[k], ys, xs, c)), rows)], L.at[k, i], ls.at[k, i]).start()
    e_own = pltpu.make_async_copy(err_ref, errs_ref.at[me], own.at[0])
    e_own.start()
    def go(j, carry):
        t = lax.rem(me + j, n)
        remote(err_ref, errs_ref.at[me], es.at[j], er.at[j], t).start()
        return carry
    lax.fori_loop(1, n, go, 0)
    i_own, i_x, i_y = y * 2 + x, y * 2 + 1 - x, (1 - y) * 2 + x
    def s0(k):
        for i in range(4):
            pltpu.make_async_copy(g_ref.at[pl.ds(0, rows)], L.at[k, i], ls.at[k, i]).wait()
            remote(L.at[k, i], R.at[k, i], rs0_s.at[k, i], rs0_r.at[k, i], tc).wait_recv()
            accumulate(L.at[k, i], R.at[k, i], rows)
        for j in range(2):
            start(remote(L.at[k, (1 - y) * 2 + j, A], YA.at[k, j], as1.at[k, j], ar1.at[k, j], ty))
            start(remote(L.at[k, j * 2 + 1 - x, B], XB.at[k, j], bs1.at[k, j], br1.at[k, j], tx))
    def mid(k):
        for j in range(2):
            remote(L.at[k, 0, A], YA.at[k, j], as1.at[k, j], ar1.at[k, j], ty).wait_recv()
            accumulate(L.at[k, y * 2 + j, A], YA.at[k, j], half)
        start(remote(L.at[k, i_x, A], XA.at[k], as2.at[k], ar2.at[k], tx))
        for j in range(2):
            remote(L.at[k, 0, B], XB.at[k, j], bs1.at[k, j], br1.at[k, j], tx).wait_recv()
            accumulate(L.at[k, j * 2 + x, B], XB.at[k, j], half)
        start(remote(L.at[k, i_y, B], YB.at[k], bs2.at[k], br2.at[k], ty))
    def fin(k):
        remote(L.at[k, 0, A], XA.at[k], as2.at[k], ar2.at[k], tx).wait_recv()
        accumulate(L.at[k, i_own, A], XA.at[k], half)
        remote(L.at[k, 0, B], YB.at[k], bs2.at[k], br2.at[k], ty).wait_recv()
        accumulate(L.at[k, i_own, B], YB.at[k], half)
        if k:
            start(remote(L.at[k, i_own], Z.at[k - 1], zs.at[k - 1], zr.at[k - 1], dev(zz[k], y, x, c)))
    for step in SCHEDULE:
        {"g": fetch, "s": s0, "m": mid, "f": fin}[step[0]](order[int(step[1])])
    for k in range(3):
        remote(L.at[0, 0], Z.at[k], zs.at[k], zr.at[k], tc).wait_recv()
    first = lax.rem(lead + share_rows * me, 8)
    sq[...] = jnp.zeros_like(sq)
    mine = L.at[0, i_own]
    def total(r, size):
        at = pl.ds(r, size)
        v = mine[at] + Z[0, at] + (Z[1, at] + Z[2, at])
        o_ref[at] = v
        row = r + lax.broadcasted_iota(jnp.int32, (size, 128), 0)
        inside = (row >= first) & (row < first + share_rows)
        v = jnp.where(inside, v, 0.0)
        v = v * v
        sq[...] += jnp.sum(v.reshape(size // 8, 8, 128), axis=0)
    step = 80
    def several(i, carry):
        total(pl.multiple_of(i * step, 8), step)
        return carry
    lax.fori_loop(0, rows // step, several, 0)
    if rows % step:
        total(rows // step * step, rows % step)
    q_own = pltpu.make_async_copy(sq, sq_ref.at[me], own.at[1])
    q_own.start()
    def go2(j, carry):
        t = lax.rem(me + j, n)
        remote(sq, sq_ref.at[me], qs.at[j], qr.at[j], t).start()
        return carry
    lax.fori_loop(1, n, go2, 0)
    for cp in pend:
        cp.wait_send()
    def end(j, carry):
        t = lax.rem(me + j, n)
        remote(err_ref, errs_ref.at[me], es.at[j], er.at[j], t).wait()
        remote(sq, sq_ref.at[me], qs.at[j], qr.at[j], t).wait()
        return carry
    lax.fori_loop(1, n, end, 0)
    e_own.wait()
    q_own.wait()

def reduce_gradient(g, err, share_rows, lead, rows, cid):
    n = 32
    D = pltpu.SemaphoreType.DMA
    anyspec = pl.BlockSpec(memory_space=pl.ANY)
    vm = pl.BlockSpec(memory_space=pltpu.VMEM)
    half = rows // 2
    F = lambda *s: pltpu.VMEM(s + (128,), jnp.float32)
    return pl.pallas_call(
        functools.partial(reduce_kernel, share_rows, lead),
        out_shape=(jax.ShapeDtypeStruct((rows, 128), jnp.float32), jax.ShapeDtypeStruct((n, 8, 128), jnp.float32), jax.ShapeDtypeStruct((n, 8, 128), jnp.float32)),
        in_specs=[anyspec, vm], out_specs=(vm, vm, vm),
        scratch_shapes=[F(4, 4, rows), F(4, 4, rows), F(4, 2, half), F(4, half), F(4, 2, half), F(4, half), F(3, rows), F(8),
            D((2,)), D((4, 4)), D((4, 4)), D((4, 4)), D((4, 2)), D((4, 2)), D((4,)), D((4,)), D((4, 2)), D((4, 2)), D((4,)), D((4,)), D((3,)), D((3,)), D((n,)), D((n,)), D((n,)), D((n,))],
        compiler_params=pltpu.CompilerParams(collective_id=cid, has_side_effects=True, vmem_limit_bytes=48 << 20),
    )(g, err)


F32, BF16 = jnp.float32, jnp.bfloat16
VMEM_LIMIT = 56 << 20
ANY = pl.BlockSpec(memory_space=pl.ANY)
DMA = pltpu.SemaphoreType.DMA


def mm(a, b):
    return jnp.dot(a, b, preferred_element_type=F32)


def mm_nt(a, b):
    return lax.dot_general(a, b, (((1,), (1,)), ((), ())), preferred_element_type=F32)


def mm_tn(a, b):
    return lax.dot_general(a, b, (((0,), (0,)), ((), ())), preferred_element_type=F32)


def col(v):
    return jnp.sum(v, axis=0, keepdims=True)


def pick(slots, first, rows):
    r = first + lax.broadcasted_iota(jnp.int32, (slots.shape[0], rows), 1)
    return jnp.where(slots == r, 1.0, 0.0).astype(BF16)


def place(slots, first, rows):
    r = first + lax.broadcasted_iota(jnp.int32, (rows, slots.shape[1]), 0)
    return jnp.where(slots == r, 1.0, 0.0).astype(BF16)


def first_half(us, w_in, vec):
    pre = vec[0:1, :]
    at = 0
    for u in us:
        pre = pre + mm(u, w_in[at : at + u.shape[1], :])
        at += u.shape[1]
    return pre


def activate(pre):
    sigma = jax.nn.sigmoid(pre)
    return sigma, (pre * sigma).astype(BF16)


def normalize(post):
    centred = post - jnp.mean(post, axis=-1, keepdims=True)
    inv = lax.rsqrt(jnp.mean(centred * centred, axis=-1, keepdims=True) + norm_eps)
    return centred * inv, inv


def second_half(act, w_out, vec):
    return normalize(mm(act, w_out[...]) + vec[1:2, :])


def scale_shift(hat, vec):
    return hat * vec[2:3, :] + vec[3:4, :]


def norm_back(g, hat, inv, vec, d_vec):
    if d_vec is not None:
        d_vec[2:3, :] += col(g * hat)
        d_vec[3:4, :] += col(g)
    s = g * vec[2:3, :]
    post = inv * (
        s - jnp.mean(s, axis=-1, keepdims=True) - hat * jnp.mean(s * hat, axis=-1, keepdims=True)
    )
    return post.astype(BF16)


def act_back(low, pre, sigma, w_out):
    g_act = mm_nt(low, w_out[...])
    return (g_act * sigma * (1.0 + pre * (1.0 - sigma))).astype(BF16)


def weight_sums(us, act, low, g_pre, d_in, d_out, d_vec):
    d_out[...] += mm_tn(act, low)
    d_vec[1:2, : low.shape[1]] += col(low.astype(F32))
    d_vec[0:1, :] += col(g_pre.astype(F32))
    at = 0
    for u in us:
        d_in[at : at + u.shape[1], :] += mm_tn(u, g_pre)
        at += u.shape[1]


def pack_matrix(packed, ref, rows, at):
    for j in range(4):
        packed[pl.ds(at + j, rows, stride=4), :] = ref[:rows, 128 * j : 128 * (j + 1)]
    return at + 4 * rows


def pack(packed, lead, rows_in, d_in, d_out, d_vec):
    def vector(i, at):
        for j in range(4):
            packed[at + j : at + j + 1, :] = d_vec[i : i + 1, 128 * j : 128 * (j + 1)]
        return at + 4
    at = pack_matrix(packed, d_in, rows_in, lead)
    at = vector(0, at)
    at = pack_matrix(packed, d_out, d_out.shape[0], at)
    for i in (1, 2, 3):
        at = vector(i, at)


def clear(*refs):
    for ref in refs:
        ref[...] = jnp.zeros_like(ref)


def spec(shape, fixed=True):
    if fixed:
        return pl.BlockSpec(shape, lambda i: (0,) * len(shape))
    return pl.BlockSpec(shape, lambda i: (i,) + (0,) * (len(shape) - 1))


def params(**more):
    return pltpu.CompilerParams(vmem_limit_bytes=VMEM_LIMIT, **more)


def shaped(*shape, dtype=F32):
    return jax.ShapeDtypeStruct(shape, dtype)


def store_flat(packed, flat, at, sem):
    copy = pltpu.make_async_copy(packed, flat.at[pl.ds(at, packed.shape[0])], sem)
    copy.start()
    return copy


def mlp_sums(rows_in, wide=LATENT):
    return [pltpu.VMEM((rows_in, LATENT), F32), pltpu.VMEM((LATENT, wide), F32), pltpu.VMEM((8, LATENT), F32)]


def packed_rows(rows_in, lead=0):
    return pltpu.VMEM((lead + 4 * rows_in + 4 * LATENT + 16, 128), F32)


def named_call(body, name, inputs, outputs, scratch, aliases=None, cid=None):
    names = [*inputs, *outputs, *scratch]
    aliases = {list(inputs).index(i): list(outputs).index(o) for i, o in (aliases or {}).items()}
    def kernel(*refs):
        body(types.SimpleNamespace(**dict(zip(names, refs))))
    more = {} if cid is None else dict(collective_id=cid, has_side_effects=True)
    values = pl.pallas_call(
        kernel,
        out_shape=tuple(shape for shape, _ in outputs.values()),
        in_specs=[s for _, s in inputs.values()],
        out_specs=tuple(s for _, s in outputs.values()),
        scratch_shapes=list(scratch.values()),
        input_output_aliases=aliases,
        compiler_params=params(**more),
        name=name,
    )(*[v for v, _ in inputs.values()])
    return types.SimpleNamespace(**dict(zip(outputs, values)))


def swap_start(n, me, src, dst, own, ssem, rsem):
    pltpu.make_async_copy(src.at[me], dst.at[me], own).start()
    def go(j, c):
        t = lax.rem(me + j, n)
        remote(src.at[t], dst.at[me], ssem.at[j], rsem.at[j], t).start()
        return c
    lax.fori_loop(1, n, go, 0)


def swap_wait(n, me, src, dst, own, ssem, rsem):
    def end(j, c):
        t = lax.rem(me + j, n)
        remote(src.at[t], dst.at[me], ssem.at[j], rsem.at[j], t).wait()
        return c
    lax.fori_loop(1, n, end, 0)
    pltpu.make_async_copy(src.at[me], dst.at[me], own).wait()


def flat_rows_of(ref):
    return ref[...].reshape(ref.shape[0] * ref.shape[1], ref.shape[2])


def greet_start(n, me):
    barrier = pltpu.get_barrier_semaphore()
    def hello(j, c):
        pl.semaphore_signal(barrier, inc=1, device_id=(lax.rem(me + j, n),), device_id_type=MESH)
        return c
    lax.fori_loop(1, n, hello, 0)


def greet_wait(n):
    pl.semaphore_wait(pltpu.get_barrier_semaphore(), n - 1)


class Loads:
    def __init__(self, r, sem):
        self.r, self.sem, self.copies = r, sem, {}

    def start(self, *names):
        for name in names:
            copy = pltpu.make_async_copy(getattr(self.r, name), getattr(self.r, "_" + name), self.sem.at[len(self.copies)])
            copy.start()
            self.copies[name] = copy

    def wait(self, *names):
        for name in names:
            self.copies[name].wait()


def store_all(r, sem, *names):
    copies = [pltpu.make_async_copy(getattr(r, "_" + name), getattr(r, name), sem.at[i]) for i, name in enumerate(names)]
    for copy in copies:
        copy.start()
    return copies


def same_rows(want, served):
    return jnp.where((want[...] == served[...]) & (want[...] >= 0), 1.0, 0.0).astype(BF16)


def swap_scratch(shape, n):
    return dict(away=pltpu.VMEM(shape, BF16), here=pltpu.VMEM(shape, BF16), back=pltpu.VMEM(shape, BF16), own=DMA((2,)), s1=DMA((n,)), r1=DMA((n,)), s2=DMA((n,)), r2=DMA((n,)))


def held(prefix, block):
    return {prefix + part: pltpu.VMEM(a.shape, a.dtype) for part, a in zip(("_in", "_out", "_vec"), block)}


def weights(prefix, block):
    return {prefix + part: (a, ANY) for part, a in zip(("_in", "_out", "_vec"), block)}


def rows_block(bm, width=LATENT):
    return pl.BlockSpec((bm, width), lambda i: (i, 0))


def edge_kernel(n, first, bm, r):
    me = lax.axis_index("dev")
    greet_start(n, me)
    loads = Loads(r, r.lsem)
    node_weights = ["p_in", "p_out", "p_vec"]
    early = node_weights + ([] if first else ["landed_in", "slots_in"])
    late = ["e_in", "e_out", "e_vec"] + (["g_in", "g_out", "g_vec"] if first else [])
    loads.start(*early)
    loads.start(*late)
    loads.wait(*early)
    count = r.want.shape[0]
    if first:
        rows = r.x.shape[0]
        us = [mm(pick(r.want[...], 0, rows), r.x[...]).astype(BF16)]
    else:
        landed = flat_rows_of(r._landed_in)
        got = mm(same_rows(r.want, r.served), landed).astype(BF16)
        r._sums_s[...] = got
        old = r._slots_in[...]
        us = [old.astype(BF16), got]
    _, act = activate(first_half(us, r._p_in, r._p_vec))
    hat, _ = second_half(act, r._p_out, r._p_vec)
    slots = scale_shift(hat, r._p_vec)
    if not first:
        slots = old + slots
    r._slots[...] = slots
    r.away[...] = slots.astype(BF16).reshape(r.away.shape)
    greet_wait(n)
    swap_start(n, me, r.away, r.here, r.own.at[0], r.s1, r.r1)
    stores = store_all(r, r.ssem, *(["slots"] if first else ["slots", "sums_s"]))
    loads.wait(*late)
    if first:
        _, act = activate(first_half([r.source[...]], r._g_in, r._g_vec))
        hat, _ = second_half(act, r._g_out, r._g_vec)
        r._edge[...] = scale_shift(hat, r._g_vec)
    else:
        r._edge[...] = r.source[...]
    e = r._edge[...].astype(BF16)
    r.edge_low[...] = e
    r._pre[...] = first_half([e], r._e_in, r._e_vec)
    if first:
        def body(node, low):
            i = pl.program_id(0)
            u = r.x[pl.ds(pl.multiple_of(i * bm, bm), bm), :]
            _, act = activate(first_half([u], r._p_in, r._p_vec))
            hat, _ = second_half(act, r._p_out, r._p_vec)
            new = scale_shift(hat, r._p_vec)
            node[...] = new
            low[...] = new.astype(BF16)
        pltpu.emit_pipeline(body, grid=(r.node.shape[0] // bm,), in_specs=[], out_specs=[rows_block(bm)] * 2)(r.node, r.low)
    else:
        def body(node_in, node, low, sums):
            i = pl.program_id(0)
            got = mm(place(r.served[...], i * bm, bm), flat_rows_of(r._landed_in)).astype(BF16)
            sums[...] = got
            old = node_in[...]
            _, act = activate(first_half([old.astype(BF16), got], r._p_in, r._p_vec))
            hat, _ = second_half(act, r._p_out, r._p_vec)
            new = old + scale_shift(hat, r._p_vec)
            node[...] = new
            low[...] = new.astype(BF16)
        pltpu.emit_pipeline(body, grid=(r.node.shape[0] // bm,), in_specs=[rows_block(bm)], out_specs=[rows_block(bm)] * 3)(r.node_in, r.node, r.low, r.sums)
    pick_s, pick_r = pick(r.pos[:, 0:1], 0, count), pick(r.pos[:, 1:2], 0, count)
    put_r = place(r.pos_r[...], 0, count)
    swap_wait(n, me, r.away, r.here, r.own.at[0], r.s1, r.r1)
    rows = flat_rows_of(r.here)
    s = mm(pick_s, rows).astype(BF16)
    v = mm(pick_r, rows).astype(BF16)
    pre = r._pre[...] + mm(s, r._e_in[LATENT : 2 * LATENT, :]) + mm(v, r._e_in[2 * LATENT :, :])
    _, act = activate(pre)
    hat, _ = second_half(act, r._e_out, r._e_vec)
    new = r._edge[...] + scale_shift(hat, r._e_vec)
    r.back[...] = mm(put_r, new.astype(BF16)).astype(BF16).reshape(r.back.shape)
    swap_start(n, me, r.back, r.landed, r.own.at[1], r.s2, r.r2)
    r.edge[...] = new
    r.sent[...], r.recv[...] = s, v
    for store in stores:
        store.wait()
    swap_wait(n, me, r.back, r.landed, r.own.at[1], r.s2, r.r2)


def edge_forward(n, cid, source, routes, edge_block, node_block, rows, x=None, geo_block=None, landed=None, node=None, slots=None, bm=512):
    first = x is not None
    want, served, pos, pos_s, pos_r = routes
    count = want.shape[0]
    edges = source.shape[0]
    shape = (n, count // n, LATENT)
    V = pl.BlockSpec(memory_space=pltpu.VMEM)
    inputs = dict(source=(source, V), want=(want, V), served=(served, V), pos=(pos, V), pos_r=(pos_r, V))
    inputs |= weights("p", node_block) | weights("e", edge_block)
    scratch = held("_p", node_block) | held("_e", edge_block) | swap_scratch(shape, n)
    scratch |= dict(_slots=pltpu.VMEM((count, LATENT), F32), _edge=pltpu.VMEM((edges, LATENT), F32), _pre=pltpu.VMEM((edges, LATENT), F32), lsem=DMA((12,)), ssem=DMA((2,)))
    low = lambda r: shaped(r, LATENT, dtype=BF16)
    outputs = dict(edge=(shaped(edges, LATENT), V), edge_low=(low(edges), V), sent=(low(edges), V), recv=(low(edges), V), landed=(shaped(*shape, dtype=BF16), ANY))
    outputs |= dict(node=(shaped(rows, LATENT), ANY), low=(low(rows), ANY), slots=(shaped(count, LATENT), ANY))
    if first:
        inputs |= dict(x=(x, V)) | weights("g", geo_block)
        scratch |= held("_g", geo_block)
    else:
        inputs |= dict(landed_in=(landed, ANY), node_in=(node, ANY), slots_in=(slots, ANY))
        scratch |= dict(_landed_in=pltpu.VMEM(shape, BF16), _slots_in=pltpu.VMEM((count, LATENT), F32), _sums_s=pltpu.VMEM((count, LATENT), BF16))
        outputs |= dict(sums=(low(rows), ANY), sums_s=(low(count), ANY))
    return named_call(functools.partial(edge_kernel, n, first, bm), "edge_forward", inputs, outputs, scratch, cid=cid)


def turn_kernel(bm, at, dec_at, served, want, landed, node, x, target, level, land, count, w_in, w_out, vec, c_in, c_out, c_vec, flat, g_prev, g_slots, out, d_out_o, d_vec_o, err_o, packed, packed2, d_in, d_out, d_vec, e_in, e_out, e_vec, err, acc, sem):
    i = pl.program_id(0)
    @pl.when(i == 0)
    def _():
        clear(d_in, d_out, d_vec, e_in, e_out, e_vec, err, acc, g_slots)
    got = mm(place(served[...], i * bm, bm), landed[...]).astype(BF16)
    old = node[...]
    low = old.astype(BF16)
    pre = first_half([low, got], w_in, vec)
    sigma, act = activate(pre)
    hat, inv = second_half(act, w_out, vec)
    u = (old + scale_shift(hat, vec)).astype(BF16)
    c_pre = first_half([u], c_in, c_vec)
    c_sigma, c_act = activate(c_pre)
    wide = c_out.shape[1]
    post = mm(c_act, c_out[...]) + c_vec[1:2, :wide]
    sea = (lax.broadcasted_iota(jnp.int32, (1, VARS), 1) < SEA_VARS).astype(F32)
    mask = level[...].astype(F32) * (1.0 - land[...].astype(F32) * sea)
    residual = x[...].astype(F32) + post[:, :VARS] - target[...]
    divisor = jnp.maximum(count[...], 1.0)
    err[:, :VARS] += col(mask * residual * residual)
    g = 2.0 * mask * residual / divisor
    g_low = jnp.concatenate([g, jnp.zeros((bm, wide - VARS), F32)], axis=1).astype(BF16)
    c_g = act_back(g_low, c_pre, c_sigma, c_out)
    weight_sums([u], c_act, g_low, c_g, e_in, e_out, e_vec)
    g_node = mm_nt(c_g, c_in[...])
    g_post = norm_back(g_node, hat, inv, vec, d_vec)
    g_pre = act_back(g_post, pre, sigma, w_out)
    weight_sums([low, got], act, g_post, g_pre, d_in, d_out, d_vec)
    g = g_node + mm_nt(g_pre, w_in[:LATENT, :])
    g_prev[...] = g
    chosen = pick(want[...], i * bm, bm)
    acc[...] += mm(chosen, mm_nt(g_pre, w_in[LATENT:, :]).astype(BF16))
    high = g.astype(BF16)
    rest = g - high.astype(F32)
    middle = rest.astype(BF16)
    small = (rest - middle.astype(F32)).astype(BF16)
    g_slots[...] += mm(chosen, high) + (mm(chosen, middle) + mm(chosen, small))
    @pl.when(i == pl.num_programs(0) - 1)
    def _():
        out[...] = acc[...].astype(BF16)
        d_out_o[...] = e_out[...]
        d_vec_o[...] = e_vec[...]
        err_o[...] = err[...]
        pack_matrix(packed2, e_in, LATENT, 0)
        one = store_flat(packed2, flat, dec_at, sem.at[0])
        pack(packed, 0, 2 * LATENT, d_in, d_out, d_vec)
        two = store_flat(packed, flat, at, sem.at[1])
        one.wait()
        two.wait()


def turn(served, want, landed, node, x, target, level, land, count, block, dec, flat_rows, at, dec_at, bm=512):
    rows = node.shape[0]
    slots = want.shape[0]
    wide = dec[1].shape[1]
    v = lambda: spec((bm, VARS), False)
    return pl.pallas_call(
        functools.partial(turn_kernel, bm, at, dec_at),
        grid=(rows // bm,),
        out_shape=(shaped(flat_rows, 128), shaped(rows, LATENT), shaped(slots, LATENT), shaped(slots, LATENT, dtype=BF16), shaped(LATENT, wide), shaped(8, LATENT), shaped(1, wide)),
        in_specs=[spec((1, slots)), spec((slots, 1)), spec((slots, LATENT)), spec((bm, LATENT), False), v(), v(), v(), spec((bm, 1), False), spec((1, 1))] + [spec(a.shape) for a in (*block, *dec)],
        out_specs=(ANY, spec((bm, LATENT), False), spec((slots, LATENT)), spec((slots, LATENT)), spec((LATENT, wide)), spec((8, LATENT)), spec((1, wide))),
        scratch_shapes=[packed_rows(2 * LATENT), pltpu.VMEM((4 * LATENT, 128), F32)] + mlp_sums(2 * LATENT) + mlp_sums(LATENT, wide) + [pltpu.VMEM((1, wide), F32), pltpu.VMEM((slots, LATENT), F32), DMA((2,))],
        compiler_params=params(),
        name="turn",
    )(served, want, landed, node, x, target, level, land, count, *block, *dec)


def edge_back_kernel(n, at, node_at, geo_at, tail_at, bm, r):
    me = lax.axis_index("dev")
    greet_start(n, me)
    loads = Loads(r, r.lsem)
    nodes = node_at is not None
    early = ["p_in", "p_out", "p_vec", "landed_in", "g_slots_in", "slots_in", "sums_s"] if nodes else []
    late = ["e_in", "e_out", "e_vec"] + (["g_in", "g_out", "g_vec"] if geo_at is not None else [])
    loads.start(*early)
    loads.start(*late)
    stores = []
    if tail_at is not None:
        stores.append(store_flat(r.tail, r.flat, tail_at, r.fsem.at[2]))
    count = r.want.shape[0]
    if nodes:
        loads.wait(*early)
        us = [r._slots_in[...].astype(BF16), r._sums_s[...]]
        pre = first_half(us, r._p_in, r._p_vec)
        sigma, act = activate(pre)
        hat, inv = second_half(act, r._p_out, r._p_vec)
        g = r._g_slots_in[...] + mm(same_rows(r.want, r.served), flat_rows_of(r._landed_in))
        low = norm_back(g, hat, inv, r._p_vec, None)
        g_pre = act_back(low, pre, sigma, r._p_out)
        r.away[...] = mm_nt(g_pre, r._p_in[LATENT:, :]).astype(BF16).reshape(r.away.shape)
        source = r.away
    else:
        source = r.outgoing
    greet_wait(n)
    swap_start(n, me, source, r.here, r.own.at[0], r.s1, r.r1)
    if nodes:
        r._g_slots[...] = g + mm_nt(g_pre, r._p_in[:LATENT, :])
        stores += store_all(r, r.ssem, "g_slots")
        clear(r.n_in, r.n_out, r.n_vec)
    clear(r.d_in, r.d_out, r.d_vec)
    def node_rows(first, last):
        if not nodes:
            return
        def body(g_node, low_in, sums_in, g_prev):
            i = first + pl.program_id(0)
            us = [low_in[...], sums_in[...]]
            pre = first_half(us, r._p_in, r._p_vec)
            sigma, act = activate(pre)
            hat, inv = second_half(act, r._p_out, r._p_vec)
            g = g_node[...] + mm(place(r.served[...], i * bm, bm), flat_rows_of(r._landed_in))
            low = norm_back(g, hat, inv, r._p_vec, r.n_vec)
            g_pre = act_back(low, pre, sigma, r._p_out)
            weight_sums(us, act, low, g_pre, r.n_in, r.n_out, r.n_vec)
            g_prev[...] = g + mm_nt(g_pre, r._p_in[:LATENT, :])
        block = pl.BlockSpec((bm, LATENT), lambda i: (first + i, 0))
        pltpu.emit_pipeline(body, grid=(last - first,), in_specs=[block] * 3, out_specs=[block])(r.g_node, r.low, r.sums, r.g_prev)
    blocks = r.g_node.shape[0] // bm if nodes else 0
    node_rows(0, blocks // 2)
    loads.wait(*late)
    us = [r.edge_low[...], r.sent[...], r.recv[...]]
    pre = first_half(us, r._e_in, r._e_vec)
    sigma, act = activate(pre)
    hat, inv = second_half(act, r._e_out, r._e_vec)
    pick_r = pick(r.pos[:, 1:2], 0, count)
    put_s, put_r = place(r.pos_s[...], 0, count), place(r.pos_r[...], 0, count)
    swap_wait(n, me, source, r.here, r.own.at[0], r.s1, r.r1)
    g = mm(pick_r, flat_rows_of(r.here))
    if hasattr(r, "g_edge"):
        g = r.g_edge[...] + g
    low = norm_back(g, hat, inv, r._e_vec, r.d_vec)
    g_pre = act_back(low, pre, sigma, r._e_out)
    s = mm_nt(g_pre, r._e_in[LATENT : 2 * LATENT, :]).astype(BF16)
    v = mm_nt(g_pre, r._e_in[2 * LATENT :, :]).astype(BF16)
    r.back[...] = (mm(put_s, s) + mm(put_r, v)).astype(BF16).reshape(r.back.shape)
    swap_start(n, me, r.back, r.landed, r.own.at[1], r.s2, r.r2)
    prev = g + mm_nt(g_pre, r._e_in[:LATENT, :])
    r.edge_prev[...] = prev
    weight_sums(us, act, low, g_pre, r.d_in, r.d_out, r.d_vec)
    pack(r.packed, 0, 3 * LATENT, r.d_in, r.d_out, r.d_vec)
    stores.append(store_flat(r.packed, r.flat, at, r.fsem.at[0]))
    if geo_at is not None:
        c_us = [r.geo[...]]
        c_pre = first_half(c_us, r._g_in, r._g_vec)
        c_sigma, c_act = activate(c_pre)
        c_hat, c_inv = second_half(c_act, r._g_out, r._g_vec)
        clear(r.c_in, r.c_out, r.c_vec)
        c_low = norm_back(prev, c_hat, c_inv, r._g_vec, r.c_vec)
        c_g = act_back(c_low, c_pre, c_sigma, r._g_out)
        weight_sums(c_us, c_act, c_low, c_g, r.c_in, r.c_out, r.c_vec)
        pack(r.c_packed, 0, GEO, r.c_in, r.c_out, r.c_vec)
        stores.append(store_flat(r.c_packed, r.flat, geo_at, r.fsem.at[1]))
    node_rows(blocks // 2, blocks)
    if nodes:
        pack(r.n_packed, 0, 2 * LATENT, r.n_in, r.n_out, r.n_vec)
        stores.append(store_flat(r.n_packed, r.flat, node_at, r.fsem.at[3]))
    swap_wait(n, me, r.back, r.landed, r.own.at[1], r.s2, r.r2)
    for store in stores:
        store.wait()


def sums_scratch(prefix, rows_in):
    return dict(zip((prefix + "_in", prefix + "_out", prefix + "_vec"), mlp_sums(rows_in)))


def edge_backward(n, cid, ins, routes, edge_block, flat, at, g_edge=None, outgoing=None, tail=None, tail_at=None, node=None, node_at=None, geo=None, geo_at=None, bm=512):
    want, served, pos, pos_s, pos_r = routes
    count = want.shape[0]
    edges = pos.shape[0]
    shape = (n, count // n, LATENT)
    V = pl.BlockSpec(memory_space=pltpu.VMEM)
    inputs = dict(want=(want, V), served=(served, V), pos=(pos, V), pos_s=(pos_s, V), pos_r=(pos_r, V), flat_in=(flat, ANY))
    inputs |= {name: (value, V) for name, value in zip(("edge_low", "sent", "recv"), ins)} | weights("e", edge_block)
    scratch = held("_e", edge_block) | swap_scratch(shape, n) | sums_scratch("d", 3 * LATENT)
    scratch |= dict(packed=packed_rows(3 * LATENT), lsem=DMA((16,)), ssem=DMA((1,)), fsem=DMA((4,)))
    outputs = dict(flat=(shaped(*flat.shape), ANY), edge_prev=(shaped(edges, LATENT), V), landed=(shaped(*shape, dtype=BF16), ANY))
    if g_edge is not None:
        inputs |= dict(g_edge=(g_edge, V))
    if outgoing is not None:
        inputs |= dict(outgoing=(outgoing.reshape(shape), ANY))
    if tail is not None:
        inputs |= dict(tail=(tail, V))
    if node is not None:
        for name, value in zip(("landed_in", "g_slots_in", "slots_in", "sums_s", "g_node", "low", "sums"), node):
            inputs[name] = (value, ANY)
        inputs |= weights("p", node[7])
        scratch |= held("_p", node[7]) | sums_scratch("n", 2 * LATENT)
        f = pltpu.VMEM((count, LATENT), F32)
        scratch |= dict(n_packed=packed_rows(2 * LATENT), _landed_in=pltpu.VMEM(shape, BF16), _g_slots_in=f, _slots_in=f, _g_slots=f, _sums_s=pltpu.VMEM((count, LATENT), BF16))
        rows = node[4].shape[0]
        outputs |= dict(g_prev=(shaped(rows, LATENT), ANY), g_slots=(shaped(count, LATENT), ANY))
    if geo is not None:
        inputs |= dict(geo=(geo[0], V)) | weights("g", geo[1])
        scratch |= held("_g", geo[1]) | sums_scratch("c", geo[0].shape[1]) | dict(c_packed=packed_rows(GEO))
    body = functools.partial(edge_back_kernel, n, at, node_at, geo_at, tail_at, bm)
    return named_call(body, "edge_backward", inputs, outputs, scratch, aliases=dict(flat_in="flat"), cid=cid)


def encode_back_kernel(bm, served, landed, g_node, x, w_in, w_out, vec, flat_in, flat, packed, d_in, d_out, d_vec, sem):
    i = pl.program_id(0)
    @pl.when(i == 0)
    def _():
        clear(d_in, d_out, d_vec)
    us = [x[...]]
    pre = first_half(us, w_in, vec)
    sigma, act = activate(pre)
    hat, inv = second_half(act, w_out, vec)
    g = g_node[...] + mm(place(served[...], i * bm, bm), landed[...])
    g_post = norm_back(g, hat, inv, vec, d_vec)
    g_pre = act_back(g_post, pre, sigma, w_out)
    weight_sums(us, act, g_post, g_pre, d_in, d_out, d_vec)
    @pl.when(i == pl.num_programs(0) - 1)
    def _():
        packed[0:4, :] = jnp.zeros((4, 128), F32)
        pack(packed, 4, VARS, d_in, d_out, d_vec)
        store_flat(packed, flat, 0, sem).wait()


def encode_backward(served, landed, g_node, x, block, flat, bm=512):
    rows, k = x.shape
    slots = landed.shape[0]
    return pl.pallas_call(
        functools.partial(encode_back_kernel, bm),
        grid=(rows // bm,),
        out_shape=shaped(*flat.shape),
        in_specs=[spec((1, slots)), spec((slots, LATENT)), spec((bm, LATENT), False), spec((bm, k), False)] + [spec(a.shape) for a in block] + [ANY],
        out_specs=ANY,
        scratch_shapes=[packed_rows(VARS, 4)] + mlp_sums(k) + [DMA],
        input_output_aliases={7: 0},
        compiler_params=params(),
        name="encode_backward",
    )(served, landed, g_node, x, *block, flat)


def relay_plan(segments, share_rows):
    jobs = []
    for block_id, part_name, part_shape, offset, entries in segments:
        if part_name not in ("w_in", "w_out") or part_shape[1] != LATENT:
            continue
        for first in range(0, part_shape[0], LATENT):
            rows = min(LATENT, part_shape[0] - first)
            follow = 0
            if first + rows == part_shape[0]:
                follow = 1 if part_name == "w_in" else 3
            begin = offset // 128 + 4 * first
            end = begin + 4 * (rows + follow)
            parts = []
            at = begin
            while at < end:
                owner, low = divmod(at, share_rows)
                size = min(end - at, share_rows - low)
                base = low // 16 * 16
                span = (low + size - base + 15) // 16 * 16
                parts.append((owner, base, span, low - base, at - begin))
                at += size
            jobs.append((block_id, part_name, first, rows, follow, parts))
    return jobs


def relay_kernel(jobs, shapes, shares, *rest):
    count = sum(len(s) for s in shapes)
    outs = rest[:count]
    stage, lines, made, vecs, isem, osem, vsem = rest[count:]
    index = {}
    for b, s in enumerate(shapes):
        for name, _ in s:
            index[b, name] = len(index)
    loads, at = [], 0
    for number, (b, name, first, rows, follow, parts) in enumerate(jobs):
        mine = []
        for owner, base, span, skip, to in parts:
            copy = pltpu.make_async_copy(shares.at[owner, pl.ds(base, span)], stage.at[pl.ds(at, span)], isem.at[len(loads) * 0 + number * 4 + len(mine)])
            copy.start()
            mine.append((copy, at, span, skip, to))
            at += span
        loads.append(mine)
    vecs[...] = jnp.zeros_like(vecs)
    stores = []
    for number, ((b, name, first, rows, follow, parts), mine) in enumerate(zip(jobs, loads)):
        for copy, where, span, skip, to in mine:
            copy.wait()
            lines[pl.ds(16 + to - skip, span), :] = stage[pl.ds(where, span), :].astype(F32)
        full = (rows + 15) // 16 * 16
        for j in range(4):
            made[number, :rows, 128 * j : 128 * (j + 1)] = lines[pl.ds(16 + j, rows, stride=4), :].astype(BF16)
        if rows < LATENT:
            made[number, rows:, :] = jnp.zeros((LATENT - rows, LATENT), BF16)
        for i in range(follow):
            row = i if name == "w_in" else i + 1
            for j in range(4):
                p = 16 + 4 * (rows + i) + j
                vecs[b, row : row + 1, 128 * j : 128 * (j + 1)] = lines[p : p + 1, :]
        out = outs[index[b, name]]
        size = min(LATENT, out.shape[0] - first)
        store = pltpu.make_async_copy(made.at[number, pl.ds(0, size)], out.at[pl.ds(first, size)], osem.at[number])
        store.start()
        stores.append(store)
    for b in range(len(shapes)):
        store = pltpu.make_async_copy(vecs.at[b], outs[index[b, "vec"]], vsem.at[b])
        store.start()
        stores.append(store)
    for store in stores:
        store.wait()


def relay(shares, segments, share_rows):
    jobs = relay_plan(segments, share_rows)
    blocks = segments[-1][0] + 1
    shapes = [[] for _ in range(blocks)]
    for b, name, shape, _, _ in segments:
        if name in ("w_in", "w_out") and shape[1] == LATENT:
            shapes[b].append((name, (-(-shape[0] // 128) * 128, LATENT)))
    for s in shapes:
        s.append(("vec", (8, LATENT)))
    stage = sum(span for job in jobs for _, _, span, _, _ in job[5])
    out_shape = [shaped(*shape, dtype=F32 if name == "vec" else BF16) for s in shapes for name, shape in s]
    outs = pl.pallas_call(
        functools.partial(relay_kernel, jobs, shapes),
        out_shape=out_shape,
        in_specs=[ANY],
        out_specs=[ANY] * len(out_shape),
        scratch_shapes=[pltpu.VMEM((stage, 128), BF16), pltpu.VMEM((16 + 4 * LATENT + 64, 128), F32), pltpu.VMEM((len(jobs), LATENT, LATENT), BF16), pltpu.VMEM((blocks, 8, LATENT), F32), DMA((4 * len(jobs),)), DMA((len(jobs),)), DMA((blocks,))],
        compiler_params=params(),
        name="relay",
    )(shares)
    made = [{} for _ in shapes]
    for (b, name), value in zip([(b, name) for b, s in enumerate(shapes) for name, _ in s], outs):
        made[b][name] = value
    return made


def make_asks(edge_owners, edge_local, devices):
    edges_here = edge_owners.shape[0]
    capacity = (5 * edges_here // (2 * devices) + 7) // 8 * 8
    owner = edge_owners.reshape(-1)
    local = edge_local.reshape(-1)
    wants = owner.shape[0]
    order = jnp.arange(wants, dtype=jnp.int32)
    before = (owner[:, None] == owner[None, :]) & (order[None, :] < order[:, None])
    ranking = jnp.sum(before.astype(jnp.int32), axis=1)
    position = owner * capacity + ranking
    slots = jnp.arange(devices * capacity, dtype=jnp.int32)
    asking = jnp.sum(jnp.where(slots[:, None] == position[None, :], local[None, :] + 1, 0), axis=1) - 1
    return (position, asking, capacity)


def widen(values, width):
    return jnp.pad(values, ((0, 0), (0, width - values.shape[1])))


def make_block(params):
    rows = params["w_in"].shape[0]
    w_in = jnp.pad(params["w_in"], ((0, -rows % 128), (0, 0)))
    w_out = widen(params["w_out"], (params["w_out"].shape[1] + 127) // 128 * 128)
    names = [name for name in ("b_in", "b_out", "gain", "shift") if name in params]
    vectors = [widen(params[name][None], LATENT) for name in names]
    vectors.append(jnp.zeros((8 - len(vectors), LATENT), jnp.bfloat16))
    return (w_in, w_out, jnp.concatenate(vectors).astype(jnp.float32))


def relaid_blocks(shares, segments, share_rows):
    def rows_of(first, last):
        parts = []
        while first < last:
            owner, low = divmod(first, share_rows)
            size = min(last - first, share_rows - low)
            parts.append(shares[owner, low : low + size])
            first += size
        return jnp.concatenate(parts) if len(parts) > 1 else parts[0]
    made = relay(shares, segments, share_rows)
    [(shape, begin, size)] = [(s, o, e) for _, name, s, o, e in segments if name == "w_out" and s[1] != LATENT]
    wide = shape[1]
    lines = rows_of(begin // 128, -(-(begin + size + wide) // 128)).reshape(-1)
    made[-1]["w_out"] = widen(lines[:size].reshape(shape), (wide + 127) // 128 * 128)
    bias = lines[size : size + wide].astype(jnp.float32)
    made[-1]["vec"] = made[-1]["vec"].at[1, :wide].set(bias)
    return [(m["w_in"], m["w_out"], m["vec"]) for m in made]


def local(
    inputs,
    targets,
    geometry,
    land_sea,
    level_mask,
    edge_owners,
    edge_local,
    step_count,
    master,
    first_moment,
    second_moment,
    ema,
):
    segments, total = layout(LATENT, VARS, GEO, LAYERS)
    devices = lax.axis_size("dev")
    share = master.shape[0]
    mine = devices == 32 and share % 128 == 0
    ocean = (jnp.arange(VARS) < SEA_VARS).astype(jnp.float32)
    position, asking, capacity = make_asks(edge_owners, edge_local, devices)
    slots = devices * capacity
    counted = jnp.sum(level_mask * (1 - land_sea[:, None] * ocean.astype(jnp.int32)[None, :])).astype(jnp.float32)
    if mine:
        share_rows = share // 128
        pad_rows = (share_rows + 31) // 32 * 32
        low = jnp.pad(master.astype(jnp.bfloat16).reshape(share_rows, 128), ((0, pad_rows - share_rows), (0, 0)))
        ask = jnp.pad(asking.reshape(devices, 1, capacity), ((0, 0), (0, 0), (0, 128 - capacity)))
        number = jnp.zeros((8, 128), jnp.float32).at[0, 0].set(counted)
        gathered, served, numbers = gather_weights(low, ask, number, 1)
        blocks = relaid_blocks(gathered, segments, share_rows)
        served = served[:, 0, :capacity].reshape(-1)
        count = jnp.sum(numbers)
    else:
        full_weights = lax.all_gather(master.astype(jnp.bfloat16), "dev", axis=0, tiled=True)
        blocks = [make_block(b) for b in unpack(full_weights, segments)]
        served = lax.all_to_all(asking.reshape(devices, capacity), "dev", 0, 0, tiled=True).reshape(-1)
        count = lax.psum(counted, "dev")
    want = served[:, None]
    served = served[None, :]
    pos = position.reshape(-1, 2)
    pos_s, pos_r = pos[:, 0][None, :], pos[:, 1][None, :]
    x = widen(inputs, 256)
    geo = widen(geometry, 128)
    land = land_sea[:, None]
    routes = (want, served, pos, pos_s, pos_r)
    done = [edge_forward(devices, 3, geo, routes, blocks[2], blocks[0], inputs.shape[0], x=x, geo_block=blocks[1])]
    for k in range(1, LAYERS):
        f = done[-1]
        done.append(
            edge_forward(
                devices, 4, f.edge, routes, blocks[2 + 2 * k], blocks[1 + 2 * k], inputs.shape[0],
                landed=f.landed, node=f.node, slots=f.slots,
            )
        )
    pieces = [4 * s for s in (VARS + LATENT + 4, GEO + LATENT + 4) + (3 * LATENT + LATENT + 4, 2 * LATENT + LATENT + 4) * LAYERS]
    lead = 4
    places = [0] + [lead + sum(pieces[: i + 1]) for i in range(len(pieces))]
    flat_rows = (lead + PARAMS // 128 + 15) // 16 * 16 + 8
    dec_at = places[-1]
    tail_at = dec_at + 4 * LATENT
    k = LAYERS - 1
    flat, g_node, g_slots, outgoing, d_out, d_vec, errors = turn(
        served, want, done[k].landed.reshape(slots, LATENT), done[k].node, inputs, targets, level_mask, land, count.reshape(1, 1),
        blocks[3 + 2 * k], blocks[-1], flat_rows, places[3 + 2 * k], dec_at,
    )
    error_here = jnp.sum(errors)
    tail = jnp.concatenate([d_vec[0], d_out[:, :VARS].reshape(-1), d_vec[1, :VARS]])
    tail_rows = flat_rows - tail_at
    tail = jnp.pad(tail, (0, tail_rows * 128 - tail.shape[0])).reshape(tail_rows, 128)
    g_edge, landed = None, None
    for k in reversed(range(LAYERS)):
        more = {}
        if k == LAYERS - 1:
            more |= dict(outgoing=outgoing, tail=tail, tail_at=tail_at)
        else:
            more |= dict(
                node=(landed, g_slots, done[k].slots, done[k + 1].sums_s, g_node, done[k].low, done[k + 1].sums, blocks[3 + 2 * k]),
                node_at=places[3 + 2 * k],
            )
        if k == 0:
            more |= dict(geo=(geo, blocks[1]), geo_at=places[1])
        f = done[k]
        b = edge_backward(
            devices, 5 + (LAYERS - 1 - k), (f.edge_low, f.sent, f.recv), routes, blocks[2 + 2 * k], flat, places[2 + 2 * k],
            g_edge=g_edge, **more,
        )
        flat, g_edge, landed = b.flat, b.edge_prev, b.landed
        if k < LAYERS - 1:
            g_node, g_slots = b.g_prev, b.g_slots
    flat = encode_backward(served, landed.reshape(slots, LATENT), g_node, x, blocks[0], flat)
    if mine:
        rows = (share_rows + 6 + 15) // 16 * 16
        error = jnp.zeros((8, 128), jnp.float32).at[0, 0].set(error_here)
        summed, squares, errors = reduce_gradient(flat, error, share_rows, lead, rows, 2)
        skip = lax.rem(lead + share_rows * lax.axis_index("dev"), 8)
        own_grad = lax.dynamic_slice_in_dim(summed, skip, share_rows).reshape(-1)
        grad_norm = jnp.sqrt(jnp.sum(squares))
        error_sum = jnp.sum(errors)
    else:
        own_grad = lax.psum_scatter(flat[lead : lead + PARAMS // 128].reshape(-1), "dev", scatter_dimension=0, tiled=True)
        error_sum, squares = lax.psum((error_here, jnp.sum(own_grad * own_grad)), "dev")
        grad_norm = jnp.sqrt(squares)
    loss = error_sum / jnp.maximum(count, 1.0)
    clipped = own_grad * jnp.minimum(1.0, clip_limit / grad_norm)
    step = step_count[0].astype(jnp.float32)
    new_first = beta_one * first_moment + (1.0 - beta_one) * clipped
    new_second = beta_two * second_moment + (1.0 - beta_two) * clipped * clipped
    first_hat = new_first / (1.0 - beta_one**step)
    second_hat = new_second / (1.0 - beta_two**step)
    new_master = master - learn_rate * (
        first_hat / (jnp.sqrt(second_hat) + adam_eps) + decay_rate * master
    )
    new_ema = ema_keep * ema + (1.0 - ema_keep) * new_master
    return (new_master, new_first, new_second, new_ema, loss, grad_norm)


def solution(mesh):
    in_specs = (
        P("dev", None),
        P("dev", None),
        P("dev", None),
        P("dev"),
        P("dev", None),
        P("dev", None),
        P("dev", None),
        P(),
        P("dev"),
        P("dev"),
        P("dev"),
        P("dev"),
    )
    out_specs = (P("dev"), P("dev"), P("dev"), P("dev"), P(), P())
    return jax.shard_map(local, mesh=mesh, in_specs=in_specs, out_specs=out_specs, check_vma=False)
```

```python
import functools
import types

import jax
import jax.numpy as jnp
import numpy as np
from jax import lax
from jax.experimental import pallas as pl
from jax.experimental.pallas import tpu as pltpu
from jax.sharding import PartitionSpec as P

LATENT = 512
VARS = 227
GEO = 4
SEA_VARS = 4
LAYERS = 3
PARAMS = 6545408


norm_eps = 1e-05
clip_limit = 0.01
beta_one = 0.9
beta_two = 0.999
adam_eps = 1e-08
learn_rate = 0.03
decay_rate = 0.1
ema_keep = 0.9


def layout(width, variables, geometry, layers):
    shapes = [(variables, width, True), (geometry, width, True)]
    for k in range(layers):
        shapes.append((3 * width, width, True))
        shapes.append((2 * width, width, True))
    shapes.append((width, variables, False))
    segments = []
    offset = 0
    for block_id, (fan_in, fan_out, normed) in enumerate(shapes):
        members = [
            ("w_in", (fan_in, width)),
            ("b_in", (width,)),
            ("w_out", (width, fan_out)),
            ("b_out", (fan_out,)),
        ]
        if normed:
            members = members + [("gain", (fan_out,)), ("shift", (fan_out,))]
        for part_name, part_shape in members:
            entries = int(np.prod(part_shape))
            segments.append((block_id, part_name, part_shape, offset, entries))
            offset += entries
    return (segments, offset)


def unpack(flat, segments):
    blocks = [dict() for k in range(segments[-1][0] + 1)]
    for block_id, part_name, part_shape, offset, entries in segments:
        blocks[block_id][part_name] = flat[offset : offset + entries].reshape(part_shape)
    return blocks


MESH = pl.DeviceIdType.MESH

def remote(src, dst, send, recv, target):
    return pltpu.make_async_remote_copy(src, dst, send, recv, device_id=(target,), device_id_type=MESH)

def greet(n, me):
    barrier = pltpu.get_barrier_semaphore()
    def hello(j, c):
        pl.semaphore_signal(barrier, inc=1, device_id=(lax.rem(me + j, n),), device_id_type=MESH)
        return c
    lax.fori_loop(1, n, hello, 0)
    pl.semaphore_wait(barrier, n - 1)

def a2a_kernel(n, a_ref, o_ref, own, ssem, rsem):
    me = lax.axis_index('dev')
    greet(n, me)
    here = pltpu.make_async_copy(a_ref.at[me], o_ref.at[me], own)
    here.start()
    def go(j, c):
        t = lax.rem(me + j, n)
        remote(a_ref.at[t], o_ref.at[me], ssem.at[j], rsem.at[j], t).start()
        return c
    lax.fori_loop(1, n, go, 0)
    def end(j, c):
        t = lax.rem(me + j, n)
        remote(a_ref.at[t], o_ref.at[me], ssem.at[j], rsem.at[j], t).wait()
        return c
    lax.fori_loop(1, n, end, 0)
    here.wait()

def a2a(x, cid, space=pl.ANY):
    n = x.shape[0]
    return pl.pallas_call(
        functools.partial(a2a_kernel, n),
        out_shape=jax.ShapeDtypeStruct(x.shape, x.dtype),
        in_specs=[pl.BlockSpec(memory_space=space)],
        out_specs=pl.BlockSpec(memory_space=space),
        scratch_shapes=[pltpu.SemaphoreType.DMA, pltpu.SemaphoreType.DMA((n,)), pltpu.SemaphoreType.DMA((n,))],
        compiler_params=pltpu.CompilerParams(collective_id=cid, has_side_effects=True),
    )(x)

def gather_kernel(w_ref, ask_ref, num_ref, o_ref, served_ref, nums_ref, own, small_s, small_r, zs, zr, hs, hr, cs, cr, ds, dr, bs, br):
    n = 32
    me = lax.axis_index('dev')
    c, x, y, z = lax.rem(me, 2), lax.rem(me // 2, 2), lax.rem(me // 4, 2), me // 8
    rows = w_ref.shape[0]
    half = rows // 2
    A, B = pl.ds(0, half), pl.ds(half, half)
    def dev(z, y, x, c):
        return ((z * 2 + y) * 2 + x) * 2 + c
    greet(n, me)
    tx, ty, tc = dev(z, y, 1 - x, c), dev(z, 1 - y, x, c), dev(z, y, x, 1 - c)
    up, down = dev(lax.rem(z + 1, 4), y, x, c), dev(lax.rem(z + 3, 4), y, x, c)
    pend = []
    def start(cp):
        cp.start(); pend.append(cp)
    mine = pltpu.make_async_copy(w_ref, o_ref.at[me], own.at[0])
    mine.start()
    planes = [z, z + 1 - 2 * lax.rem(z, 2), 2 - z // 2, 3 - 3 * (z // 2)]
    def on_up(i, wait):
        src = w_ref if i == 0 else o_ref.at[dev(planes[i], y, x, c)]
        slot = dev(planes[i], y, x, c)
        @pl.when((planes[i] <= z) & (z < 3))
        def _():
            cp = remote(src, o_ref.at[slot], zs.at[0, i], zr.at[planes[i]], up)
            cp.wait_send() if wait else cp.start()
    def on_down(i, wait):
        src = w_ref if i == 0 else o_ref.at[dev(planes[i], y, x, c)]
        slot = dev(planes[i], y, x, c)
        @pl.when((planes[i] >= z) & (z > 0))
        def _():
            cp = remote(src, o_ref.at[slot], zs.at[1, i], zr.at[planes[i]], down)
            cp.wait_send() if wait else cp.start()
    start(remote(w_ref.at[A], o_ref.at[me, A], hs.at[0, 0], hr.at[0, 0], tx))
    start(remote(w_ref.at[B], o_ref.at[me, B], hs.at[0, 1], hr.at[0, 1], ty))
    on_up(0, False)
    on_down(0, False)
    start(remote(w_ref, o_ref.at[me], bs.at[0], br.at[0], tc))
    mine2 = pltpu.make_async_copy(ask_ref.at[me], served_ref.at[me], own.at[1])
    mine2.start()
    mine3 = pltpu.make_async_copy(num_ref, nums_ref.at[me], own.at[2])
    mine3.start()
    def go(j, carry):
        t = lax.rem(me + j, n)
        remote(ask_ref.at[t], served_ref.at[me], small_s.at[0, j], small_r.at[0, j], t).start()
        remote(num_ref, nums_ref.at[me], small_s.at[1, j], small_r.at[1, j], t).start()
        return carry
    lax.fori_loop(1, n, go, 0)
    nb = [1]
    def sib(slot, part):
        i = nb[0]; nb[0] += 1
        ref = o_ref.at[slot] if part is None else o_ref.at[slot, part]
        start(remote(ref, ref, bs.at[i], br.at[i], tc))
    def first(k):
        s = dev(planes[k], y, x, c)
        remote(w_ref, o_ref.at[s], zs.at[0, k], zr.at[planes[k]], tc).wait_recv()
        start(remote(o_ref.at[s, A], o_ref.at[s, A], hs.at[k, 0], hr.at[k, 0], tx))
        start(remote(o_ref.at[s, B], o_ref.at[s, B], hs.at[k, 1], hr.at[k, 1], ty))
        on_up(k, False)
        on_down(k, False)
        sib(s, None)
    def second(k):
        zz = planes[k]
        s = dev(zz, y, x, c)
        sx, sy = dev(zz, y, 1 - x, c), dev(zz, 1 - y, x, c)
        own_a = w_ref.at[A] if k == 0 else o_ref.at[s, A]
        own_b = w_ref.at[B] if k == 0 else o_ref.at[s, B]
        start(remote(own_a, o_ref.at[s, A], cs.at[k, 0], cr.at[k, 0], ty))
        start(remote(own_b, o_ref.at[s, B], ds.at[k, 0], dr.at[k, 0], tx))
        remote(own_a, o_ref.at[sx, A], hs.at[k, 0], hr.at[k, 0], tx).wait_recv()
        start(remote(o_ref.at[sx, A], o_ref.at[sx, A], cs.at[k, 1], cr.at[k, 1], ty))
        remote(own_b, o_ref.at[sy, B], hs.at[k, 1], hr.at[k, 1], ty).wait_recv()
        start(remote(o_ref.at[sy, B], o_ref.at[sy, B], ds.at[k, 1], dr.at[k, 1], tx))
        sib(sx, A)
        sib(sy, B)
    def third(k):
        zz = planes[k]
        sx, sy, sd = dev(zz, y, 1 - x, c), dev(zz, 1 - y, x, c), dev(zz, 1 - y, 1 - x, c)
        w = w_ref.at[A]
        remote(w, o_ref.at[sy, A], cs.at[k, 0], cr.at[k, 0], ty).wait_recv()
        sib(sy, A)
        remote(w, o_ref.at[sx, B], ds.at[k, 0], dr.at[k, 0], tx).wait_recv()
        sib(sx, B)
        remote(w, o_ref.at[sd, A], cs.at[k, 1], cr.at[k, 1], ty).wait_recv()
        sib(sd, A)
        remote(w, o_ref.at[sd, B], ds.at[k, 1], dr.at[k, 1], tx).wait_recv()
        sib(sd, B)
    second(0)
    first(1)
    third(0)
    second(1)
    first(2)
    third(1)
    second(2)
    first(3)
    third(2)
    second(3)
    third(3)
    nb2 = [0]
    def got(*parts):
        for part in parts:
            i = nb2[0]; nb2[0] += 1
            ref = w_ref if part is None else w_ref.at[part]
            o = o_ref.at[me] if part is None else o_ref.at[me, part]
            remote(ref, o, bs.at[i], br.at[i], tc).wait_recv()
    g1, g2, g3 = (None,), (A, B), (A, B, A, B)
    for g in (g1, g2, g1, g3, g2, g1, g3, g2, g1, g3, g2, g3):
        got(*g)
    def end(j, carry):
        t = lax.rem(me + j, n)
        remote(ask_ref.at[t], served_ref.at[me], small_s.at[0, j], small_r.at[0, j], t).wait()
        remote(num_ref, nums_ref.at[me], small_s.at[1, j], small_r.at[1, j], t).wait()
        return carry
    lax.fori_loop(1, n, end, 0)
    for i in range(4):
        on_up(i, True)
        on_down(i, True)
    for cp in pend:
        cp.wait_send()
    mine.wait(); mine2.wait(); mine3.wait()


def gather_weights(w, ask, num, cid):
    n = 32
    rows = w.shape[0]
    D = pltpu.SemaphoreType.DMA
    sib = 1 + 4 * 2 + 3 + 4 * 4
    anyspec = pl.BlockSpec(memory_space=pl.ANY)
    return pl.pallas_call(
        gather_kernel,
        out_shape=(jax.ShapeDtypeStruct((n, rows, 128), w.dtype), jax.ShapeDtypeStruct(ask.shape, ask.dtype), jax.ShapeDtypeStruct((n,) + num.shape, num.dtype)),
        in_specs=[anyspec] * 3, out_specs=(anyspec,) * 3,
        scratch_shapes=[D((3,)), D((2, n)), D((2, n)), D((2, 4)), D((4,)), D((4, 2)), D((4, 2)), D((4, 2)), D((4, 2)), D((4, 2)), D((4, 2)), D((sib,)), D((sib,))],
        compiler_params=pltpu.CompilerParams(collective_id=cid, has_side_effects=True),
    )(w, ask, num)


F32, BF16 = jnp.float32, jnp.bfloat16
VMEM_LIMIT = 60 << 20
ANY = pl.BlockSpec(memory_space=pl.ANY)
DMA = pltpu.SemaphoreType.DMA


def mm(a, b):
    return jnp.dot(a, b, preferred_element_type=F32)


def mm_nt(a, b):
    return lax.dot_general(a, b, (((1,), (1,)), ((), ())), preferred_element_type=F32)


def mm_tn(a, b):
    return lax.dot_general(a, b, (((0,), (0,)), ((), ())), preferred_element_type=F32)


def contract(a, b, left, right):
    return lax.dot_general(a, b, (((left,), (right,)), ((), ())), preferred_element_type=F32)


def col(v):
    return jnp.sum(v, axis=0, keepdims=True)


def pick(slots, first, rows):
    r = first + lax.broadcasted_iota(jnp.int32, (slots.shape[0], rows), 1)
    return jnp.where(slots == r, 1.0, 0.0).astype(BF16)


def place(slots, first, rows):
    r = first + lax.broadcasted_iota(jnp.int32, (rows, slots.shape[1]), 0)
    return jnp.where(slots == r, 1.0, 0.0).astype(BF16)


def first_half(us, w_in, vec):
    pre = vec[0:1, :]
    at = 0
    for u in us:
        pre = pre + mm(u, w_in[at : at + u.shape[1], :])
        at += u.shape[1]
    return pre


def activate(pre):
    sigma = jax.nn.sigmoid(pre)
    return sigma, (pre * sigma).astype(BF16)


def normalize(post):
    centred = post - jnp.mean(post, axis=-1, keepdims=True)
    inv = lax.rsqrt(jnp.mean(centred * centred, axis=-1, keepdims=True) + norm_eps)
    return centred * inv, inv


def second_half(act, w_out, vec):
    return normalize(mm(act, w_out[...]) + vec[1:2, :])


def scale_shift(hat, vec):
    return hat * vec[2:3, :] + vec[3:4, :]


def norm_back(g, hat, inv, vec, d_vec):
    if d_vec is not None:
        d_vec[2:3, :] += col(g * hat)
        d_vec[3:4, :] += col(g)
    s = g * vec[2:3, :]
    post = inv * (
        s - jnp.mean(s, axis=-1, keepdims=True) - hat * jnp.mean(s * hat, axis=-1, keepdims=True)
    )
    return post.astype(BF16)


def act_back(low, pre, sigma, w_out):
    g_act = mm_nt(low, w_out[...])
    return (g_act * sigma * (1.0 + pre * (1.0 - sigma))).astype(BF16)


def weight_sums(us, act, low, g_pre, d_in, d_out, d_vec):
    d_out[...] += mm_tn(act, low)
    d_vec[1:2, : low.shape[1]] += col(low.astype(F32))
    d_vec[0:1, :] += col(g_pre.astype(F32))
    at = 0
    for u in us:
        d_in[at : at + u.shape[1], :] += mm_tn(u, g_pre)
        at += u.shape[1]


def pack_matrix(packed, ref, rows, at):
    for j in range(4):
        packed[pl.ds(at + j, rows, stride=4), :] = ref[:rows, 128 * j : 128 * (j + 1)]
    return at + 4 * rows


def pack(packed, lead, rows_in, d_in, d_out, d_vec):
    def vector(i, at):
        for j in range(4):
            packed[at + j : at + j + 1, :] = d_vec[i : i + 1, 128 * j : 128 * (j + 1)]
        return at + 4
    at = pack_matrix(packed, d_in, rows_in, lead)
    at = vector(0, at)
    at = pack_matrix(packed, d_out, d_out.shape[0], at)
    for i in (1, 2, 3):
        at = vector(i, at)


def clear(*refs):
    for ref in refs:
        ref[...] = jnp.zeros_like(ref)


def spec(shape, fixed=True):
    if fixed:
        return pl.BlockSpec(shape, lambda i: (0,) * len(shape))
    return pl.BlockSpec(shape, lambda i: (i,) + (0,) * (len(shape) - 1))


def params(**more):
    return pltpu.CompilerParams(vmem_limit_bytes=VMEM_LIMIT, **more)


def shaped(*shape, dtype=F32):
    return jax.ShapeDtypeStruct(shape, dtype)


class Chunks:
    def __init__(self, begins, rows, cuts):
        self.begins, self.rows, self.cuts = begins, rows, cuts

    def shape(self, group):
        return (self.cuts[group + 1] - self.cuts[group], self.rows, 128)

    def pieces(self, at, size):
        found = []
        for group in range(len(self.cuts) - 1):
            for owner in range(self.cuts[group], self.cuts[group + 1]):
                begin = self.begins[owner]
                low, high = max(at, begin), min(at + size, begin + self.rows)
                if low < high:
                    found.append((group, owner - self.cuts[group], low - begin, low - at, high - low))
        return found

    def groups(self, *places):
        return sorted({p[0] for at, size in places for p in self.pieces(at, size)})


class Stores:
    def __init__(self, refs, chunks, sem):
        self.refs, self.chunks, self.sem, self.copies = refs, chunks, sem, []

    def put(self, packed, at):
        for group, owner, row, skip, size in self.chunks.pieces(at, packed.shape[0]):
            source = packed.at[pl.ds(skip, size)]
            copy = pltpu.make_async_copy(source, self.refs[group].at[owner, pl.ds(row, size)], self.sem.at[len(self.copies)])
            copy.start()
            self.copies.append(copy)

    def wait(self):
        for copy in self.copies:
            copy.wait()


STORES = 48


def flat_refs(r, groups):
    return {group: getattr(r, f"flat{group}") for group in groups}


def mlp_sums(rows_in, wide=LATENT):
    return [pltpu.VMEM((rows_in, LATENT), F32), pltpu.VMEM((LATENT, wide), F32), pltpu.VMEM((8, LATENT), F32)]


def packed_rows(rows_in, lead=0):
    return pltpu.VMEM((lead + 4 * rows_in + 4 * LATENT + 16, 128), F32)


def named_call(body, name, inputs, outputs, scratch, aliases=None, cid=None):
    names = [*inputs, *outputs, *scratch]
    aliases = {list(inputs).index(i): list(outputs).index(o) for i, o in (aliases or {}).items()}
    def kernel(*refs):
        body(types.SimpleNamespace(**dict(zip(names, refs))))
    more = {} if cid is None else dict(collective_id=cid, has_side_effects=True)
    values = pl.pallas_call(
        kernel,
        out_shape=tuple(shape for shape, _ in outputs.values()),
        in_specs=[s for _, s in inputs.values()],
        out_specs=tuple(s for _, s in outputs.values()),
        scratch_shapes=list(scratch.values()),
        input_output_aliases=aliases,
        compiler_params=params(**more),
        name=name,
    )(*[v for v, _ in inputs.values()])
    return types.SimpleNamespace(**dict(zip(outputs, values)))


def swap_start(n, me, srcs, dsts, own, ssem, rsem):
    for i, (src, dst) in enumerate(zip(srcs, dsts)):
        pltpu.make_async_copy(src.at[me], dst.at[me], own.at[i]).start()
    def go(j, c):
        t = lax.rem(me + j, n)
        for i, (src, dst) in enumerate(zip(srcs, dsts)):
            remote(src.at[t], dst.at[me], ssem.at[i, j], rsem.at[i, j], t).start()
        return c
    lax.fori_loop(1, n, go, 0)


def swap_wait(n, me, srcs, dsts, own, ssem, rsem):
    def end(j, c):
        t = lax.rem(me + j, n)
        for i, (src, dst) in enumerate(zip(srcs, dsts)):
            remote(src.at[t], dst.at[me], ssem.at[i, j], rsem.at[i, j], t).wait()
        return c
    lax.fori_loop(1, n, end, 0)
    for i, (src, dst) in enumerate(zip(srcs, dsts)):
        pltpu.make_async_copy(src.at[me], dst.at[me], own.at[i]).wait()


def several(r, name):
    return [getattr(r, f"{name}{i}") for i in range(4) if hasattr(r, f"{name}{i}")]


def numbered(name, values):
    return {f"{name}{i}": value for i, value in enumerate(values)}


def slot_rows(refs):
    rows = [ref[...].reshape(ref.shape[0] * ref.shape[1], ref.shape[2]) for ref in refs]
    return rows[0] if len(rows) == 1 else jnp.concatenate(rows, axis=0)


def put_slot_rows(refs, rows):
    at = 0
    for ref in refs:
        size = ref.shape[0] * ref.shape[1]
        ref[...] = rows[at : at + size, :].reshape(ref.shape)
        at += size


def greet_start(n, me):
    barrier = pltpu.get_barrier_semaphore()
    def hello(j, c):
        pl.semaphore_signal(barrier, inc=1, device_id=(lax.rem(me + j, n),), device_id_type=MESH)
        return c
    lax.fori_loop(1, n, hello, 0)


def greet_wait(n):
    pl.semaphore_wait(pltpu.get_barrier_semaphore(), n - 1)


class Loads:
    def __init__(self, r, sem):
        self.r, self.sem, self.copies = r, sem, {}

    def start(self, *names):
        for name in names:
            copy = pltpu.make_async_copy(getattr(self.r, name), getattr(self.r, "_" + name), self.sem.at[len(self.copies)])
            copy.start()
            self.copies[name] = copy

    def wait(self, *names):
        for name in names:
            self.copies[name].wait()


def store_all(r, sem, *names):
    copies = [pltpu.make_async_copy(getattr(r, "_" + name), getattr(r, name), sem.at[i]) for i, name in enumerate(names)]
    for copy in copies:
        copy.start()
    return copies


def same_rows(want, served):
    return jnp.where((want[...] == served[...]) & (want[...] >= 0), 1.0, 0.0).astype(BF16)


def swap_scratch(shapes, n):
    parts = len(shapes)
    scratch = dict(own=DMA((2, parts)), s1=DMA((parts, n)), r1=DMA((parts, n)), s2=DMA((parts, n)), r2=DMA((parts, n)))
    for name in ("away", "here", "back"):
        scratch |= numbered(name, [pltpu.VMEM(shape, BF16) for shape in shapes])
    return scratch


def held(prefix, block):
    return {prefix + part: pltpu.VMEM(a.shape, a.dtype) for part, a in zip(("_in", "_out", "_vec"), block)}


def weights(prefix, block):
    return {prefix + part: (a, ANY) for part, a in zip(("_in", "_out", "_vec"), block)}


def rows_block(bm, width=LATENT):
    return pl.BlockSpec((bm, width), lambda i: (i, 0))


def edge_kernel(n, first, bm, r):
    me = lax.axis_index("dev")
    greet_start(n, me)
    loads = Loads(r, r.lsem)
    node_weights = ["p_in", "p_out", "p_vec"]
    landing = [name for name in vars(r) if name.startswith("landed_in")]
    early = node_weights + ([] if first else [*landing, "slots_in"])
    late = ["e_in", "e_out", "e_vec"] + (["g_in", "g_out", "g_vec"] if first else [])
    loads.start(*early)
    loads.start(*late)
    loads.wait(*early)
    count = r.want.shape[0]
    if first:
        asked = contract(pick(r.want[...], 0, r.x.shape[1]), r.x[...], 1, 1).astype(BF16)
        pre = contract(asked, r._p_in[:VARS, :], 1, 0) + r._p_vec[0:1, :]
    else:
        landed = slot_rows(several(r, "_landed_in"))
        got = mm(same_rows(r.want, r.served), landed).astype(BF16)
        r._sums_s[...] = got
        old = r._slots_in[...]
        pre = first_half([old.astype(BF16), got], r._p_in, r._p_vec)
    _, act = activate(pre)
    hat, _ = second_half(act, r._p_out, r._p_vec)
    slots = scale_shift(hat, r._p_vec)
    if not first:
        slots = old + slots
    r._slots[...] = slots
    away, here, back, out = (several(r, name) for name in ("away", "here", "back", "landed"))
    put_slot_rows(away, slots.astype(BF16))
    greet_wait(n)
    swap_start(n, me, away, here, r.own.at[0], r.s1, r.r1)
    stores = store_all(r, r.ssem, *(["slots"] if first else ["slots", "sums_s"]))
    loads.wait(*late)
    if first:
        _, act = activate(first_half([r.source[...]], r._g_in, r._g_vec))
        hat, _ = second_half(act, r._g_out, r._g_vec)
        r._edge[...] = scale_shift(hat, r._g_vec)
    else:
        r._edge[...] = r.source[...]
    e = r._edge[...].astype(BF16)
    r.edge_low[...] = e
    r._pre[...] = first_half([e], r._e_in, r._e_vec)
    if first:
        def body(node, low):
            i = pl.program_id(0)
            u = r.x[:, pl.ds(pl.multiple_of(i * bm, bm), bm)]
            _, act = activate(contract(u, r._p_in[:VARS, :], 0, 0) + r._p_vec[0:1, :])
            hat, _ = second_half(act, r._p_out, r._p_vec)
            new = scale_shift(hat, r._p_vec)
            node[...] = new
            low[...] = new.astype(BF16)
        pltpu.emit_pipeline(body, grid=(r.node.shape[0] // bm,), in_specs=[], out_specs=[rows_block(bm)] * 2)(r.node, r.low)
    else:
        def body(node_in, node, low, sums):
            i = pl.program_id(0)
            got = mm(place(r.served[...], i * bm, bm), slot_rows(several(r, "_landed_in"))).astype(BF16)
            sums[...] = got
            old = node_in[...]
            _, act = activate(first_half([old.astype(BF16), got], r._p_in, r._p_vec))
            hat, _ = second_half(act, r._p_out, r._p_vec)
            new = old + scale_shift(hat, r._p_vec)
            node[...] = new
            low[...] = new.astype(BF16)
        pltpu.emit_pipeline(body, grid=(r.node.shape[0] // bm,), in_specs=[rows_block(bm)], out_specs=[rows_block(bm)] * 3)(r.node_in, r.node, r.low, r.sums)
    pick_s, pick_r = pick(r.pos[:, 0:1], 0, count), pick(r.pos[:, 1:2], 0, count)
    put_r = place(r.pos_r[...], 0, count)
    swap_wait(n, me, away, here, r.own.at[0], r.s1, r.r1)
    rows = slot_rows(here)
    s = mm(pick_s, rows).astype(BF16)
    v = mm(pick_r, rows).astype(BF16)
    pre = r._pre[...] + mm(s, r._e_in[LATENT : 2 * LATENT, :]) + mm(v, r._e_in[2 * LATENT :, :])
    _, act = activate(pre)
    hat, _ = second_half(act, r._e_out, r._e_vec)
    new = r._edge[...] + scale_shift(hat, r._e_vec)
    put_slot_rows(back, mm(put_r, new.astype(BF16)).astype(BF16))
    swap_start(n, me, back, out, r.own.at[1], r.s2, r.r2)
    r.edge[...] = new
    r.sent[...], r.recv[...] = s, v
    for store in stores:
        store.wait()
    swap_wait(n, me, back, out, r.own.at[1], r.s2, r.r2)


def edge_forward(n, parts, cid, source, routes, edge_block, node_block, rows, x=None, geo_block=None, landed=None, node=None, slots=None, bm=512):
    first = x is not None
    want, served, pos, pos_s, pos_r = routes
    count = want.shape[0]
    edges = source.shape[0]
    shapes = [(n, p, LATENT) for p in parts]
    V = pl.BlockSpec(memory_space=pltpu.VMEM)
    inputs = dict(source=(source, V), want=(want, V), served=(served, V), pos=(pos, V), pos_r=(pos_r, V))
    inputs |= weights("p", node_block) | weights("e", edge_block)
    scratch = held("_p", node_block) | held("_e", edge_block) | swap_scratch(shapes, n)
    scratch |= dict(_slots=pltpu.VMEM((count, LATENT), F32), _edge=pltpu.VMEM((edges, LATENT), F32), _pre=pltpu.VMEM((edges, LATENT), F32), lsem=DMA((12,)), ssem=DMA((2,)))
    low = lambda r: shaped(r, LATENT, dtype=BF16)
    outputs = dict(edge=(shaped(edges, LATENT), V), edge_low=(low(edges), V), sent=(low(edges), V), recv=(low(edges), V)) | numbered("landed", [(shaped(*s, dtype=BF16), ANY) for s in shapes])
    outputs |= dict(node=(shaped(rows, LATENT), ANY), low=(low(rows), ANY), slots=(shaped(count, LATENT), ANY))
    if first:
        inputs |= dict(x=(x, V)) | weights("g", geo_block)
        scratch |= held("_g", geo_block)
    else:
        inputs |= numbered("landed_in", [(v, ANY) for v in landed]) | dict(node_in=(node, ANY), slots_in=(slots, ANY))
        scratch |= numbered("_landed_in", [pltpu.VMEM(s, BF16) for s in shapes]) | dict(_slots_in=pltpu.VMEM((count, LATENT), F32), _sums_s=pltpu.VMEM((count, LATENT), BF16))
        outputs |= dict(sums=(low(rows), ANY), sums_s=(low(count), ANY))
    return named_call(functools.partial(edge_kernel, n, first, bm), "edge_forward", inputs, outputs, scratch, cid=cid)


def turn_kernel(parts, bm, chunks, group, at, dec_at, served, want, *refs):
    landed, refs = refs[:parts], refs[parts:]
    flat, g_prev, *outs = refs[13 : 15 + parts]
    node, x, target, level, land, count, w_in, w_out, vec, c_in, c_out, c_vec, c_bias = refs[:13]
    d_out_o, d_first_o, d_bias_o, err_o, packed, packed2, d_in, d_out, d_vec, e_in, e_out, e_vec, e_bias, err, acc, sem = refs[13 + 2 + parts:]
    i = pl.program_id(0)
    @pl.when(i == 0)
    def _():
        clear(d_in, d_out, d_vec, e_in, e_out, e_vec, e_bias, err, acc)
    got = mm(place(served[...], i * bm, bm), slot_rows(landed)).astype(BF16)
    old = node[...]
    low = old.astype(BF16)
    pre = first_half([low, got], w_in, vec)
    sigma, act = activate(pre)
    hat, inv = second_half(act, w_out, vec)
    u = (old + scale_shift(hat, vec)).astype(BF16)
    c_pre = first_half([u], c_in, c_vec)
    c_sigma, c_act = activate(c_pre)
    wide = c_out.shape[1]
    post = contract(c_out[...], c_act, 0, 1)
    sea = (lax.broadcasted_iota(jnp.int32, (VARS, 1), 0) < SEA_VARS).astype(F32)
    mask = level[...].astype(F32) * (1.0 - sea * land[...].astype(F32))
    residual = x[...].astype(F32) + (post[:VARS, :] + c_bias[...]) - target[...]
    divisor = jnp.maximum(count[...], 1.0)
    err[...] += jnp.sum(mask * residual * residual, axis=0, keepdims=True)
    g = 2.0 * mask * residual / divisor
    g_low = jnp.concatenate([g, jnp.zeros((wide - VARS, bm), F32)], axis=0).astype(BF16)
    e_bias[...] += jnp.sum(g_low.astype(F32), axis=1, keepdims=True)
    e_out[...] += contract(c_act, g_low, 0, 1)
    g_act = contract(g_low, c_out[...], 0, 1)
    c_g = (g_act * c_sigma * (1.0 + c_pre * (1.0 - c_sigma))).astype(BF16)
    e_vec[0:1, :] += col(c_g.astype(F32))
    e_in[...] += mm_tn(u, c_g)
    g_node = mm_nt(c_g, c_in[...])
    g_post = norm_back(g_node, hat, inv, vec, d_vec)
    g_pre = act_back(g_post, pre, sigma, w_out)
    weight_sums([low, got], act, g_post, g_pre, d_in, d_out, d_vec)
    g_prev[...] = g_node + mm_nt(g_pre, w_in[:LATENT, :])
    acc[...] += mm(pick(want[...], i * bm, bm), mm_nt(g_pre, w_in[LATENT:, :]).astype(BF16))
    @pl.when(i == pl.num_programs(0) - 1)
    def _():
        put_slot_rows(outs, acc[...].astype(BF16))
        d_out_o[...] = e_out[...]
        d_first_o[...] = e_vec[0:1, :]
        d_bias_o[...] = e_bias[...]
        err_o[...] = err[...]
        stores = Stores({group: flat}, chunks, sem)
        pack_matrix(packed2, e_in, LATENT, 0)
        stores.put(packed2, dec_at)
        pack(packed, 0, 2 * LATENT, d_in, d_out, d_vec)
        stores.put(packed, at)
        stores.wait()


def turn(served, want, landed, node, x, target, level, land, count, block, dec, bias, chunks, at, dec_at, bm=512):
    rows = node.shape[0]
    slots = want.shape[0]
    wide = dec[1].shape[1]
    [group] = chunks.groups((at, dec_at + 4 * LATENT - at))
    v = lambda height: pl.BlockSpec((height, bm), lambda i: (0, i))
    part = [spec(p.shape) for p in landed]
    return pl.pallas_call(
        functools.partial(turn_kernel, len(landed), bm, chunks, group, at, dec_at),
        grid=(rows // bm,),
        out_shape=(shaped(*chunks.shape(group)), shaped(rows, LATENT), *(shaped(*p.shape, dtype=BF16) for p in landed), shaped(LATENT, wide), shaped(1, LATENT), shaped(wide, 1), shaped(1, bm)),
        in_specs=[spec((1, slots)), spec((slots, 1)), *part, spec((bm, LATENT), False), v(VARS), v(VARS), v(VARS), v(1), spec((1, 1))] + [spec(a.shape) for a in (*block, *dec, bias)],
        out_specs=(ANY, spec((bm, LATENT), False), *part, spec((LATENT, wide)), spec((1, LATENT)), spec((wide, 1)), spec((1, bm))),
        scratch_shapes=[packed_rows(2 * LATENT), pltpu.VMEM((4 * LATENT, 128), F32)] + mlp_sums(2 * LATENT) + mlp_sums(LATENT, wide) + [pltpu.VMEM((wide, 1), F32), pltpu.VMEM((1, bm), F32), pltpu.VMEM((slots, LATENT), F32), DMA((STORES,))],
        compiler_params=params(),
        name="turn",
    )(served, want, *landed, node, x, target, level, land, count, *block, *dec, bias)


def gather_slots(r, bm):
    clear(r._g_slots)
    def body(g_node):
        chosen = pick(r.want[...], pl.program_id(0) * bm, bm)
        g = g_node[...]
        high = g.astype(BF16)
        rest = g - high.astype(F32)
        middle = rest.astype(BF16)
        small = (rest - middle.astype(F32)).astype(BF16)
        r._g_slots[...] += mm(chosen, high) + (mm(chosen, middle) + mm(chosen, small))
    pltpu.emit_pipeline(body, grid=(r.g_node.shape[0] // bm,), in_specs=[rows_block(bm)], out_specs=[])(r.g_node)


def edge_back_kernel(n, chunks, groups, at, node_at, geo_at, tail_at, bm, r):
    me = lax.axis_index("dev")
    greet_start(n, me)
    loads = Loads(r, r.lsem)
    nodes = node_at is not None
    landing = [name for name in vars(r) if name.startswith("landed_in")]
    early = ["p_in", "p_out", "p_vec", *landing, "g_slots_in", "slots_in", "sums_s"] if nodes else []
    late = ["e_in", "e_out", "e_vec"] + (["g_in", "g_out", "g_vec"] if geo_at is not None else [])
    loads.start(*early)
    loads.start(*late)
    flats = Stores(flat_refs(r, groups), chunks, r.fsem)
    stores = [flats]
    if tail_at is not None:
        flats.put(r.tail, tail_at)
    count = r.want.shape[0]
    here, back, out = (several(r, name) for name in ("here", "back", "landed"))
    if nodes:
        loads.wait(*early)
        us = [r._slots_in[...].astype(BF16), r._sums_s[...]]
        pre = first_half(us, r._p_in, r._p_vec)
        sigma, act = activate(pre)
        hat, inv = second_half(act, r._p_out, r._p_vec)
        g = r._g_slots_in[...] + mm(same_rows(r.want, r.served), slot_rows(several(r, "_landed_in")))
        low = norm_back(g, hat, inv, r._p_vec, None)
        g_pre = act_back(low, pre, sigma, r._p_out)
        source = several(r, "away")
        put_slot_rows(source, mm_nt(g_pre, r._p_in[LATENT:, :]).astype(BF16))
    else:
        source = several(r, "outgoing")
    greet_wait(n)
    swap_start(n, me, source, here, r.own.at[0], r.s1, r.r1)
    if nodes:
        r._g_slots[...] = g + mm_nt(g_pre, r._p_in[:LATENT, :])
        stores += store_all(r, r.ssem, "g_slots")
        clear(r.n_in, r.n_out, r.n_vec)
    clear(r.d_in, r.d_out, r.d_vec)
    def node_rows(first, last):
        if not nodes:
            return
        def body(g_node, low_in, sums_in, g_prev):
            i = first + pl.program_id(0)
            us = [low_in[...], sums_in[...]]
            pre = first_half(us, r._p_in, r._p_vec)
            sigma, act = activate(pre)
            hat, inv = second_half(act, r._p_out, r._p_vec)
            g = g_node[...] + mm(place(r.served[...], i * bm, bm), slot_rows(several(r, "_landed_in")))
            low = norm_back(g, hat, inv, r._p_vec, r.n_vec)
            g_pre = act_back(low, pre, sigma, r._p_out)
            weight_sums(us, act, low, g_pre, r.n_in, r.n_out, r.n_vec)
            g_prev[...] = g + mm_nt(g_pre, r._p_in[:LATENT, :])
        block = pl.BlockSpec((bm, LATENT), lambda i: (first + i, 0))
        pltpu.emit_pipeline(body, grid=(last - first,), in_specs=[block] * 3, out_specs=[block])(r.g_node, r.low, r.sums, r.g_prev)
    blocks = r.g_node.shape[0] // bm if nodes else 0
    node_rows(0, blocks // 2)
    if not nodes:
        gather_slots(r, bm)
    loads.wait(*late)
    us = [r.edge_low[...], r.sent[...], r.recv[...]]
    pre = first_half(us, r._e_in, r._e_vec)
    sigma, act = activate(pre)
    hat, inv = second_half(act, r._e_out, r._e_vec)
    pick_r = pick(r.pos[:, 1:2], 0, count)
    put_s, put_r = place(r.pos_s[...], 0, count), place(r.pos_r[...], 0, count)
    swap_wait(n, me, source, here, r.own.at[0], r.s1, r.r1)
    g = mm(pick_r, slot_rows(here))
    if hasattr(r, "g_edge"):
        g = r.g_edge[...] + g
    low = norm_back(g, hat, inv, r._e_vec, r.d_vec)
    g_pre = act_back(low, pre, sigma, r._e_out)
    s = mm_nt(g_pre, r._e_in[LATENT : 2 * LATENT, :]).astype(BF16)
    v = mm_nt(g_pre, r._e_in[2 * LATENT :, :]).astype(BF16)
    put_slot_rows(back, (mm(put_s, s) + mm(put_r, v)).astype(BF16))
    swap_start(n, me, back, out, r.own.at[1], r.s2, r.r2)
    prev = g + mm_nt(g_pre, r._e_in[:LATENT, :])
    r.edge_prev[...] = prev
    weight_sums(us, act, low, g_pre, r.d_in, r.d_out, r.d_vec)
    pack(r.packed, 0, 3 * LATENT, r.d_in, r.d_out, r.d_vec)
    flats.put(r.packed, at)
    if geo_at is not None:
        c_us = [r.geo[...]]
        c_pre = first_half(c_us, r._g_in, r._g_vec)
        c_sigma, c_act = activate(c_pre)
        c_hat, c_inv = second_half(c_act, r._g_out, r._g_vec)
        clear(r.c_in, r.c_out, r.c_vec)
        c_low = norm_back(prev, c_hat, c_inv, r._g_vec, r.c_vec)
        c_g = act_back(c_low, c_pre, c_sigma, r._g_out)
        weight_sums(c_us, c_act, c_low, c_g, r.c_in, r.c_out, r.c_vec)
        pack(r.c_packed, 0, GEO, r.c_in, r.c_out, r.c_vec)
        flats.put(r.c_packed, geo_at)
    node_rows(blocks // 2, blocks)
    if nodes:
        pack(r.n_packed, 0, 2 * LATENT, r.n_in, r.n_out, r.n_vec)
        flats.put(r.n_packed, node_at)
    if not nodes:
        stores += store_all(r, r.ssem, "g_slots")
    swap_wait(n, me, back, out, r.own.at[1], r.s2, r.r2)
    for store in stores:
        store.wait()


def sums_scratch(prefix, rows_in):
    return dict(zip((prefix + "_in", prefix + "_out", prefix + "_vec"), mlp_sums(rows_in)))


def edge_backward(n, parts, cid, ins, routes, edge_block, chunks, flats, at, g_edge=None, outgoing=None, g_node=None, tail=None, tail_at=None, node=None, node_at=None, geo=None, geo_at=None, bm=512):
    want, served, pos, pos_s, pos_r = routes
    count = want.shape[0]
    edges = pos.shape[0]
    shapes = [(n, p, LATENT) for p in parts]
    V = pl.BlockSpec(memory_space=pltpu.VMEM)
    inputs = dict(want=(want, V), served=(served, V), pos=(pos, V), pos_s=(pos_s, V), pos_r=(pos_r, V))
    inputs |= {name: (value, V) for name, value in zip(("edge_low", "sent", "recv"), ins)} | weights("e", edge_block)
    scratch = held("_e", edge_block) | swap_scratch(shapes, n) | sums_scratch("d", 3 * LATENT)
    scratch |= dict(packed=packed_rows(3 * LATENT), lsem=DMA((16,)), ssem=DMA((2,)), fsem=DMA((STORES,)))
    outputs = dict(edge_prev=(shaped(edges, LATENT), V)) | numbered("landed", [(shaped(*s, dtype=BF16), ANY) for s in shapes])
    places = [(at, scratch["packed"].shape[0])]
    if g_edge is not None:
        inputs |= dict(g_edge=(g_edge, V))
    if outgoing is not None:
        inputs |= numbered("outgoing", [(v, ANY) for v in outgoing]) | dict(g_node=(g_node, ANY))
        outputs |= dict(g_slots=(shaped(count, LATENT), ANY))
        scratch |= dict(_g_slots=pltpu.VMEM((count, LATENT), F32))
    if tail is not None:
        inputs |= dict(tail=(tail, V))
        places.append((tail_at, tail.shape[0]))
    if node is not None:
        inputs |= numbered("landed_in", [(v, ANY) for v in node[0]])
        for name, value in zip(("g_slots_in", "slots_in", "sums_s", "g_node", "low", "sums"), node[1:]):
            inputs[name] = (value, ANY)
        inputs |= weights("p", node[7])
        scratch |= held("_p", node[7]) | sums_scratch("n", 2 * LATENT)
        f = pltpu.VMEM((count, LATENT), F32)
        scratch |= numbered("_landed_in", [pltpu.VMEM(s, BF16) for s in shapes]) | dict(n_packed=packed_rows(2 * LATENT), _g_slots_in=f, _slots_in=f, _g_slots=f, _sums_s=pltpu.VMEM((count, LATENT), BF16))
        rows = node[4].shape[0]
        places.append((node_at, scratch["n_packed"].shape[0]))
        outputs |= dict(g_prev=(shaped(rows, LATENT), ANY), g_slots=(shaped(count, LATENT), ANY))
    if geo is not None:
        inputs |= dict(geo=(geo[0], V)) | weights("g", geo[1])
        scratch |= held("_g", geo[1]) | sums_scratch("c", geo[0].shape[1]) | dict(c_packed=packed_rows(GEO))
        places.append((geo_at, scratch["c_packed"].shape[0]))
    groups = chunks.groups(*places)
    aliases = {}
    for group in groups:
        outputs[f"flat{group}"] = (shaped(*chunks.shape(group)), ANY)
        if group in flats:
            inputs[f"flat{group}_in"] = (flats[group], ANY)
            aliases[f"flat{group}_in"] = f"flat{group}"
    body = functools.partial(edge_back_kernel, n, chunks, groups, at, node_at, geo_at, tail_at, bm)
    made = named_call(body, "edge_backward", inputs, outputs, scratch, aliases=aliases, cid=cid)
    flats.update(flat_refs(made, groups))
    return made


def encode_back_kernel(parts, bm, chunks, served, *refs):
    landed, refs = refs[:parts], refs[parts:]
    g_node, x, w_in, w_out, vec, flat_in, flat, packed, d_in, d_out, d_vec, sem = refs
    i = pl.program_id(0)
    @pl.when(i == 0)
    def _():
        clear(d_in, d_out, d_vec)
    pre = contract(x[...], w_in[:VARS, :], 0, 0) + vec[0:1, :]
    sigma, act = activate(pre)
    hat, inv = second_half(act, w_out, vec)
    g = g_node[...] + mm(place(served[...], i * bm, bm), slot_rows(landed))
    g_post = norm_back(g, hat, inv, vec, d_vec)
    g_pre = act_back(g_post, pre, sigma, w_out)
    weight_sums([], act, g_post, g_pre, d_in, d_out, d_vec)
    d_in[:VARS, :] += mm(x[...], g_pre)
    @pl.when(i == pl.num_programs(0) - 1)
    def _():
        packed[0:4, :] = jnp.zeros((4, 128), F32)
        pack(packed, 4, VARS, d_in, d_out, d_vec)
        stores = Stores({0: flat}, chunks, sem)
        stores.put(packed, 0)
        stores.wait()


def encode_backward(served, landed, g_node, x, block, chunks, flat, bm=512):
    k, rows = block[0].shape[0], x.shape[1]
    slots = served.shape[1]
    return pl.pallas_call(
        functools.partial(encode_back_kernel, len(landed), bm, chunks),
        grid=(rows // bm,),
        out_shape=shaped(*flat.shape),
        in_specs=[spec((1, slots)), *(spec(p.shape) for p in landed), spec((bm, LATENT), False), pl.BlockSpec((VARS, bm), lambda i: (0, i))] + [spec(a.shape) for a in block] + [ANY],
        out_specs=ANY,
        scratch_shapes=[packed_rows(VARS, 4)] + mlp_sums(k) + [DMA((STORES,))],
        input_output_aliases={6 + len(landed): 0},
        compiler_params=params(),
        name="encode_backward",
    )(served, *landed, g_node, x, *block, flat)


def relay_plan(segments, share_rows):
    jobs = []
    for block_id, part_name, part_shape, offset, entries in segments:
        if part_name not in ("w_in", "w_out") or part_shape[1] != LATENT:
            continue
        for first in range(0, part_shape[0], LATENT):
            rows = min(LATENT, part_shape[0] - first)
            follow = 0
            if first + rows == part_shape[0]:
                follow = 1 if part_name == "w_in" else 3
            begin = offset // 128 + 4 * first
            end = begin + 4 * (rows + follow)
            parts = []
            at = begin
            while at < end:
                owner, low = divmod(at, share_rows)
                size = min(end - at, share_rows - low)
                base = low // 16 * 16
                span = (low + size - base + 15) // 16 * 16
                parts.append((owner, base, span, low - base, at - begin))
                at += size
            jobs.append((block_id, part_name, first, rows, follow, parts))
    return jobs


def relay_kernel(jobs, shapes, shares, *rest):
    count = sum(len(s) for s in shapes)
    outs = rest[:count]
    stage, lines, made, vecs, isem, osem, vsem = rest[count:]
    index = {}
    for b, s in enumerate(shapes):
        for name, _ in s:
            index[b, name] = len(index)
    loads, at = [], 0
    for number, (b, name, first, rows, follow, parts) in enumerate(jobs):
        mine = []
        for owner, base, span, skip, to in parts:
            copy = pltpu.make_async_copy(shares.at[owner, pl.ds(base, span)], stage.at[pl.ds(at, span)], isem.at[len(loads) * 0 + number * 4 + len(mine)])
            copy.start()
            mine.append((copy, at, span, skip, to))
            at += span
        loads.append(mine)
    vecs[...] = jnp.zeros_like(vecs)
    stores = []
    for number, ((b, name, first, rows, follow, parts), mine) in enumerate(zip(jobs, loads)):
        for copy, where, span, skip, to in mine:
            copy.wait()
            lines[pl.ds(16 + to - skip, span), :] = stage[pl.ds(where, span), :].astype(F32)
        full = (rows + 15) // 16 * 16
        for j in range(4):
            made[number, :rows, 128 * j : 128 * (j + 1)] = lines[pl.ds(16 + j, rows, stride=4), :].astype(BF16)
        if rows < LATENT:
            made[number, rows:, :] = jnp.zeros((LATENT - rows, LATENT), BF16)
        for i in range(follow):
            row = i if name == "w_in" else i + 1
            for j in range(4):
                p = 16 + 4 * (rows + i) + j
                vecs[b, row : row + 1, 128 * j : 128 * (j + 1)] = lines[p : p + 1, :]
        out = outs[index[b, name]]
        size = min(LATENT, out.shape[0] - first)
        store = pltpu.make_async_copy(made.at[number, pl.ds(0, size)], out.at[pl.ds(first, size)], osem.at[number])
        store.start()
        stores.append(store)
    for b in range(len(shapes)):
        store = pltpu.make_async_copy(vecs.at[b], outs[index[b, "vec"]], vsem.at[b])
        store.start()
        stores.append(store)
    for store in stores:
        store.wait()


def relay(shares, segments, share_rows):
    jobs = relay_plan(segments, share_rows)
    blocks = segments[-1][0] + 1
    shapes = [[] for _ in range(blocks)]
    for b, name, shape, _, _ in segments:
        if name in ("w_in", "w_out") and shape[1] == LATENT:
            shapes[b].append((name, (-(-shape[0] // 128) * 128, LATENT)))
    for s in shapes:
        s.append(("vec", (8, LATENT)))
    stage = sum(span for job in jobs for _, _, span, _, _ in job[5])
    out_shape = [shaped(*shape, dtype=F32 if name == "vec" else BF16) for s in shapes for name, shape in s]
    outs = pl.pallas_call(
        functools.partial(relay_kernel, jobs, shapes),
        out_shape=out_shape,
        in_specs=[ANY],
        out_specs=[ANY] * len(out_shape),
        scratch_shapes=[pltpu.VMEM((stage, 128), BF16), pltpu.VMEM((16 + 4 * LATENT + 64, 128), F32), pltpu.VMEM((len(jobs), LATENT, LATENT), BF16), pltpu.VMEM((blocks, 8, LATENT), F32), DMA((4 * len(jobs),)), DMA((len(jobs),)), DMA((blocks,))],
        compiler_params=params(),
        name="relay",
    )(shares)
    made = [{} for _ in shapes]
    for (b, name), value in zip([(b, name) for b, s in enumerate(shapes) for name, _ in s], outs):
        made[b][name] = value
    return made


def accumulate(dst, src, rows):
    step = 80
    whole = rows // step
    def body(i, carry):
        at = pl.ds(pl.multiple_of(i * step, 8), step)
        dst[at] = dst[at] + src[at]
        return carry
    lax.fori_loop(0, whole, body, 0)
    if rows % step:
        at = pl.ds(whole * step, rows % step)
        dst[at] = dst[at] + src[at]


def where_am_i():
    me = lax.axis_index("dev")
    return me, me // 8, lax.rem(me // 4, 2), lax.rem(me // 2, 2), lax.rem(me, 2)


def device_at(z, y, x, c):
    return ((z * 2 + y) * 2 + x) * 2 + c


def plane_scratch(units, rows):
    upper = rows // 16 * 8
    lower = rows - upper
    F = lambda *s: pltpu.VMEM((units,) + s + (128,), F32)
    refs = dict(pL=F(4, rows), pR=F(4, rows), pYA=F(2, upper), pXA=F(upper), pXB=F(2, lower), pYB=F(lower))
    sems = {}
    for name, count in (("c", 4), ("a1", 2), ("a2", 1), ("b1", 2), ("b2", 1)):
        sems["p" + name + "s"] = DMA((units, count))
        sems["p" + name + "r"] = DMA((units, count))
    return refs | sems | dict(pl=DMA((units, 4)))


class PlaneSum:
    def __init__(self, r, rows):
        self.r, self.rows = r, rows
        self.upper = rows // 16 * 8
        self.A, self.B = pl.ds(0, self.upper), pl.ds(self.upper, rows - self.upper)
        _, z, y, x, c = where_am_i()
        self.y, self.x, self.c = y, x, c
        self.tx, self.ty, self.tc = device_at(z, y, 1 - x, c), device_at(z, 1 - y, x, c), device_at(z, y, x, 1 - c)
        self.own = y * 2 + x
        self.sends = []

    def send(self, *args):
        copy = remote(*args)
        copy.start()
        self.sends.append(copy)

    def fetch(self, u, source):
        r = self.r
        self.example = source(0, 0)
        for i in range(4):
            self.send(source(i, 1 - self.c), r.pR.at[u, i], r.pcs.at[u, i], r.pcr.at[u, i], self.tc)
            pltpu.make_async_copy(source(i, self.c), r.pL.at[u, i], r.pl.at[u, i]).start()

    def pair(self, u):
        r, L = self.r, self.r.pL
        for i in range(4):
            pltpu.make_async_copy(self.example, L.at[u, i], r.pl.at[u, i]).wait()
            remote(L.at[u, i], r.pR.at[u, i], r.pcs.at[u, i], r.pcr.at[u, i], self.tc).wait_recv()
            accumulate(L.at[u, i], r.pR.at[u, i], self.rows)
        for j in range(2):
            self.send(L.at[u, (1 - self.y) * 2 + j, self.A], r.pYA.at[u, j], r.pa1s.at[u, j], r.pa1r.at[u, j], self.ty)
            self.send(L.at[u, j * 2 + 1 - self.x, self.B], r.pXB.at[u, j], r.pb1s.at[u, j], r.pb1r.at[u, j], self.tx)

    def middle(self, u):
        r, L = self.r, self.r.pL
        up, low = self.upper, self.rows - self.upper
        for j in range(2):
            remote(L.at[u, 0, self.A], r.pYA.at[u, j], r.pa1s.at[u, j], r.pa1r.at[u, j], self.ty).wait_recv()
            accumulate(L.at[u, self.y * 2 + j, self.A], r.pYA.at[u, j], up)
        self.send(L.at[u, self.y * 2 + 1 - self.x, self.A], r.pXA.at[u], r.pa2s.at[u, 0], r.pa2r.at[u, 0], self.tx)
        for j in range(2):
            remote(L.at[u, 0, self.B], r.pXB.at[u, j], r.pb1s.at[u, j], r.pb1r.at[u, j], self.tx).wait_recv()
            accumulate(L.at[u, j * 2 + self.x, self.B], r.pXB.at[u, j], low)
        self.send(L.at[u, (1 - self.y) * 2 + self.x, self.B], r.pYB.at[u], r.pb2s.at[u, 0], r.pb2r.at[u, 0], self.ty)

    def last(self, u):
        r, L = self.r, self.r.pL
        remote(L.at[u, 0, self.A], r.pXA.at[u], r.pa2s.at[u, 0], r.pa2r.at[u, 0], self.tx).wait_recv()
        accumulate(L.at[u, self.own, self.A], r.pXA.at[u], self.upper)
        remote(L.at[u, 0, self.B], r.pYB.at[u], r.pb2s.at[u, 0], r.pb2r.at[u, 0], self.ty).wait_recv()
        accumulate(L.at[u, self.own, self.B], r.pYB.at[u], self.rows - self.upper)

    def result(self, u):
        return self.r.pL.at[u, self.own]

    def finish(self):
        for copy in self.sends:
            copy.wait_send()


PARTS = 1


def reduce_kernel(n, share_rows, lead, rows, r):
    me, z, y, x, c = where_am_i()
    greet(n, me)
    size = rows // PARTS
    plane = PlaneSum(r, size)
    units = [(away, part) for away in (2, 1, 3, 0) for part in range(PARTS)]
    goal = [lax.rem(z + away, 4) for away, _ in units]
    rows_of = [pl.ds(part * size, size) for _, part in units]

    def fetch(u):
        if u < len(units):
            plane.fetch(u, lambda i, core: r.flat.at[goal[u] * 8 + i * 2 + core, rows_of[u]])

    def along(u):
        away, part = units[u]
        at = 3 - away
        return remote(plane.result(u), r.zq.at[at, rows_of[u]], r.zqs.at[at, part], r.zqr.at[at, part], device_at(goal[u], y, x, c))

    def last(u):
        plane.last(u)
        if units[u][0]:
            along(u).start()

    fetch(0)
    fetch(1)
    e_own = pltpu.make_async_copy(r.err, r.errs.at[me], r.own.at[0])
    e_own.start()
    def go(j, carry):
        t = lax.rem(me + j, n)
        remote(r.err, r.errs.at[me], r.es.at[j], r.er.at[j], t).start()
        return carry
    lax.fori_loop(1, n, go, 0)
    plane.pair(0)
    plane.middle(0)
    for u in range(1, len(units)):
        fetch(u + 1)
        plane.pair(u)
        last(u - 1)
        plane.middle(u)
    last(len(units) - 1)
    first = lax.rem(lead + share_rows * me, 8)
    r.sq[...] = jnp.zeros_like(r.sq)

    def piece(ref, base, at, count):
        here, there = pl.ds(at, count), pl.ds(base + at, count)
        v = ref[here] + r.zq[0, there] + (r.zq[1, there] + r.zq[2, there])
        r.out[there] = v
        row = base + at + lax.broadcasted_iota(jnp.int32, v.shape, 0)
        v = jnp.where((row >= first) & (row < first + share_rows), v, 0.0)
        v = v * v
        r.sq[...] += jnp.sum(v.reshape(count // 8, 8, 128), axis=0)

    for u in range(len(units) - PARTS, len(units)):
        part = units[u][1]
        for at in range(3):
            remote(plane.result(u), r.zq.at[at, rows_of[u]], r.zqs.at[at, part], r.zqr.at[at, part], plane.tc).wait_recv()
        step = 80
        def several(i, carry):
            piece(plane.result(u), part * size, pl.multiple_of(i * step, 8), step)
            return carry
        lax.fori_loop(0, size // step, several, 0)
        if size % step:
            piece(plane.result(u), part * size, size // step * step, size % step)
    q_own = pltpu.make_async_copy(r.sq, r.squares.at[me], r.own.at[1])
    q_own.start()
    def go2(j, carry):
        t = lax.rem(me + j, n)
        remote(r.sq, r.squares.at[me], r.qs.at[j], r.qr.at[j], t).start()
        return carry
    lax.fori_loop(1, n, go2, 0)
    plane.finish()
    for u in range(len(units)):
        if units[u][0]:
            along(u).wait_send()
    def end(j, carry):
        t = lax.rem(me + j, n)
        remote(r.err, r.errs.at[me], r.es.at[j], r.er.at[j], t).wait()
        remote(r.sq, r.squares.at[me], r.qs.at[j], r.qr.at[j], t).wait()
        return carry
    lax.fori_loop(1, n, end, 0)
    e_own.wait()
    q_own.wait()


def reduce_gradient(n, flat, err, share_rows, lead, rows, cid):
    V = pl.BlockSpec(memory_space=pltpu.VMEM)
    F = lambda *s: pltpu.VMEM(s + (128,), F32)
    inputs = dict(flat=(flat, ANY), err=(err, V))
    small = (shaped(n, 8, 128), V)
    outputs = dict(out=(shaped(rows, 128), V), squares=small, errs=small)
    scratch = plane_scratch(4 * PARTS, rows // PARTS) | dict(zq=F(3, rows), sq=F(8), zqs=DMA((3, PARTS)), zqr=DMA((3, PARTS)))
    scratch |= dict(own=DMA((2,)), es=DMA((n,)), er=DMA((n,)), qs=DMA((n,)), qr=DMA((n,)))
    out = named_call(functools.partial(reduce_kernel, n, share_rows, lead, rows), "reduce_gradient", inputs, outputs, scratch, cid=cid)
    return out.out, out.squares, out.errs


def make_parts(capacity):
    whole = capacity // 16 * 16
    rest = (capacity - whole + 3) // 4 * 4
    return [rows for rows in (whole, rest) if rows]


def make_asks(edge_owners, edge_local, devices, parts):
    owner = edge_owners.reshape(-1)
    local = edge_local.reshape(-1)
    wants = owner.shape[0]
    order = jnp.arange(wants, dtype=jnp.int32)
    before = (owner[:, None] == owner[None, :]) & (order[None, :] < order[:, None])
    ranking = jnp.sum(before.astype(jnp.int32), axis=1)
    capacity = sum(parts)
    slots = jnp.arange(devices * capacity, dtype=jnp.int32)
    place = owner * capacity + ranking
    asking = jnp.sum(jnp.where(slots[:, None] == place[None, :], local[None, :] + 1, 0), axis=1) - 1
    position = owner * parts[0] + ranking
    if len(parts) > 1:
        position = jnp.where(ranking < parts[0], position, devices * parts[0] + owner * parts[1] + ranking - parts[0])
    return (position, asking.reshape(devices, capacity))


def widen(values, width):
    return jnp.pad(values, ((0, 0), (0, width - values.shape[1])))


def make_block(params):
    rows = params["w_in"].shape[0]
    w_in = jnp.pad(params["w_in"], ((0, -rows % 128), (0, 0)))
    w_out = widen(params["w_out"], (params["w_out"].shape[1] + 127) // 128 * 128)
    names = [name for name in ("b_in", "b_out", "gain", "shift") if name in params]
    vectors = [widen(params[name][None], LATENT) for name in names]
    vectors.append(jnp.zeros((8 - len(vectors), LATENT), jnp.bfloat16))
    return (w_in, w_out, jnp.concatenate(vectors).astype(jnp.float32))


def relaid_blocks(shares, segments, share_rows):
    def rows_of(first, last):
        parts = []
        while first < last:
            owner, low = divmod(first, share_rows)
            size = min(last - first, share_rows - low)
            parts.append(shares[owner, low : low + size])
            first += size
        return jnp.concatenate(parts) if len(parts) > 1 else parts[0]
    made = relay(shares, segments, share_rows)
    [(shape, begin, size)] = [(s, o, e) for _, name, s, o, e in segments if name == "w_out" and s[1] != LATENT]
    wide = shape[1]
    first, end = begin // 128, (begin + size) // 128
    made[-1]["w_out"] = widen(rows_of(first, end).reshape(shape), (wide + 127) // 128 * 128)
    bias = rows_of(end, end + (wide + 127) // 128).reshape(-1)[:wide, None].astype(jnp.float32)
    return [(m["w_in"], m["w_out"], m["vec"]) for m in made], bias


def local(
    inputs,
    targets,
    geometry,
    land_sea,
    level_mask,
    edge_owners,
    edge_local,
    step_count,
    master,
    first_moment,
    second_moment,
    ema,
):
    segments, total = layout(LATENT, VARS, GEO, LAYERS)
    devices = lax.axis_size("dev")
    share = master.shape[0]
    mine = devices == 32 and share % 128 == 0
    ocean = (jnp.arange(VARS) < SEA_VARS).astype(jnp.float32)
    parts = make_parts(5 * edge_owners.shape[0] // (2 * devices))
    capacity = sum(parts)
    position, asking = make_asks(edge_owners, edge_local, devices, parts)
    counted = jnp.sum(level_mask * (1 - land_sea[:, None] * ocean.astype(jnp.int32)[None, :])).astype(jnp.float32)
    if mine:
        share_rows = share // 128
        pad_rows = (share_rows + 31) // 32 * 32
        low = jnp.pad(master.astype(jnp.bfloat16).reshape(share_rows, 128), ((0, pad_rows - share_rows), (0, 0)))
        ask = jnp.pad(asking.reshape(devices, 1, capacity), ((0, 0), (0, 0), (0, 128 - capacity)))
        number = jnp.zeros((8, 128), jnp.float32).at[0, 0].set(counted)
        gathered, served, numbers = gather_weights(low, ask, number, 1)
        blocks, bias = relaid_blocks(gathered, segments, share_rows)
        served = served[:, 0, :capacity]
        count = jnp.sum(numbers)
    else:
        full_weights = lax.all_gather(master.astype(jnp.bfloat16), "dev", axis=0, tiled=True)
        whole = unpack(full_weights, segments)
        blocks = [make_block(b) for b in whole]
        bias = whole[-1]["b_out"][:, None].astype(jnp.float32)
        served = lax.all_to_all(asking, "dev", 0, 0, tiled=True)
        count = lax.psum(counted, "dev")
    served = jnp.concatenate([served[:, sum(parts[:i]) : sum(parts[: i + 1])].reshape(-1) for i in range(len(parts))])
    want = served[:, None]
    served = served[None, :]
    pos = position.reshape(-1, 2)
    pos_s, pos_r = pos[:, 0][None, :], pos[:, 1][None, :]
    x = inputs.T
    geo = widen(geometry, 128)
    land = land_sea[None, :]
    routes = (want, served, pos, pos_s, pos_r)
    done = [edge_forward(devices, parts, 3, geo, routes, blocks[2], blocks[0], inputs.shape[0], x=x, geo_block=blocks[1])]
    for k in range(1, LAYERS):
        f = done[-1]
        done.append(
            edge_forward(
                devices, parts, 4, f.edge, routes, blocks[2 + 2 * k], blocks[1 + 2 * k], inputs.shape[0],
                landed=several(f, "landed"), node=f.node, slots=f.slots,
            )
        )
    pieces = [4 * s for s in (VARS + LATENT + 4, GEO + LATENT + 4) + (3 * LATENT + LATENT + 4, 2 * LATENT + LATENT + 4) * LAYERS]
    lead = 4
    places = [0] + [lead + sum(pieces[: i + 1]) for i in range(len(pieces))]
    flat_rows = (lead + PARAMS // 128 + 15) // 16 * 16 + 8
    if mine:
        begins = [(lead + share_rows * d) // 8 * 8 for d in range(devices)]
        chunks = Chunks(begins, (share_rows + 6 + 15) // 16 * 16, [0, 32])
    else:
        chunks = Chunks([0], flat_rows, [0, 1])
    dec_at = places[-1]
    tail_at = dec_at + 4 * LATENT
    k = LAYERS - 1
    flat, g_node, *outgoing, d_out, d_first, d_bias, errors = turn(
        served, want, several(done[k], "landed"), done[k].node, x, targets.T, level_mask.T, land, count.reshape(1, 1),
        blocks[3 + 2 * k], blocks[-1], bias, chunks, places[3 + 2 * k], dec_at,
    )
    flats = {len(chunks.cuts) - 2: flat}
    error_here = jnp.sum(errors)
    tail = jnp.concatenate([d_first[0], d_out[:, :VARS].reshape(-1), d_bias[:VARS, 0]])
    tail_rows = flat_rows - tail_at
    tail = jnp.pad(tail, (0, tail_rows * 128 - tail.shape[0])).reshape(tail_rows, 128)
    g_edge, landed = None, None
    for k in reversed(range(LAYERS)):
        more = {}
        if k == LAYERS - 1:
            more |= dict(outgoing=outgoing, g_node=g_node, tail=tail, tail_at=tail_at)
        else:
            more |= dict(
                node=(landed, g_slots, done[k].slots, done[k + 1].sums_s, g_node, done[k].low, done[k + 1].sums, blocks[3 + 2 * k]),
                node_at=places[3 + 2 * k],
            )
        if k == 0:
            more |= dict(geo=(geo, blocks[1]), geo_at=places[1])
        f = done[k]
        b = edge_backward(
            devices, parts, 5 + (LAYERS - 1 - k), (f.edge_low, f.sent, f.recv), routes, blocks[2 + 2 * k], chunks, flats, places[2 + 2 * k],
            g_edge=g_edge, **more,
        )
        g_edge, landed = b.edge_prev, several(b, "landed")
        g_slots = b.g_slots
        if k < LAYERS - 1:
            g_node = b.g_prev
    flat = encode_backward(served, landed, g_node, x, blocks[0], chunks, flats[0])
    if mine:
        error = jnp.zeros((8, 128), jnp.float32).at[0, 0].set(error_here)
        summed, squares, errors = reduce_gradient(devices, flat, error, share_rows, lead, chunks.rows, 2)
        skip = lax.rem(lead + share_rows * lax.axis_index("dev"), 8)
        own_grad = lax.dynamic_slice_in_dim(summed, skip, share_rows).reshape(-1)
        grad_norm = jnp.sqrt(jnp.sum(squares))
        error_sum = jnp.sum(errors)
    else:
        own_grad = lax.psum_scatter(flat[0, lead : lead + PARAMS // 128].reshape(-1), "dev", scatter_dimension=0, tiled=True)
        error_sum, squares = lax.psum((error_here, jnp.sum(own_grad * own_grad)), "dev")
        grad_norm = jnp.sqrt(squares)
    loss = error_sum / jnp.maximum(count, 1.0)
    clipped = own_grad * jnp.minimum(1.0, clip_limit / grad_norm)
    step = step_count[0].astype(jnp.float32)
    new_first = beta_one * first_moment + (1.0 - beta_one) * clipped
    new_second = beta_two * second_moment + (1.0 - beta_two) * clipped * clipped
    first_hat = new_first / (1.0 - beta_one**step)
    second_hat = new_second / (1.0 - beta_two**step)
    new_master = master - learn_rate * (
        first_hat / (jnp.sqrt(second_hat) + adam_eps) + decay_rate * master
    )
    new_ema = ema_keep * ema + (1.0 - ema_keep) * new_master
    return (new_master, new_first, new_second, new_ema, loss, grad_norm)


def solution(mesh):
    in_specs = (
        P("dev", None),
        P("dev", None),
        P("dev", None),
        P("dev"),
        P("dev", None),
        P("dev", None),
        P("dev", None),
        P(),
        P("dev"),
        P("dev"),
        P("dev"),
        P("dev"),
    )
    out_specs = (P("dev"), P("dev"), P("dev"), P("dev"), P(), P())
    return jax.shard_map(local, mesh=mesh, in_specs=in_specs, out_specs=out_specs, check_vma=False)
```

```python
import functools
import types

import jax
import jax.numpy as jnp
import numpy as np
from jax import lax
from jax.experimental import pallas as pl
from jax.experimental.pallas import tpu as pltpu
from jax.sharding import PartitionSpec as P

LATENT = 512
VARS = 227
GEO = 4
SEA_VARS = 4
LAYERS = 3
PARAMS = 6545408


norm_eps = 1e-05
clip_limit = 0.01
beta_one = 0.9
beta_two = 0.999
adam_eps = 1e-08
learn_rate = 0.03
decay_rate = 0.1
ema_keep = 0.9


def layout(width, variables, geometry, layers):
    shapes = [(variables, width, True), (geometry, width, True)]
    for k in range(layers):
        shapes.append((3 * width, width, True))
        shapes.append((2 * width, width, True))
    shapes.append((width, variables, False))
    segments = []
    offset = 0
    for block_id, (fan_in, fan_out, normed) in enumerate(shapes):
        members = [
            ("w_in", (fan_in, width)),
            ("b_in", (width,)),
            ("w_out", (width, fan_out)),
            ("b_out", (fan_out,)),
        ]
        if normed:
            members = members + [("gain", (fan_out,)), ("shift", (fan_out,))]
        for part_name, part_shape in members:
            entries = int(np.prod(part_shape))
            segments.append((block_id, part_name, part_shape, offset, entries))
            offset += entries
    return (segments, offset)


def unpack(flat, segments):
    blocks = [dict() for k in range(segments[-1][0] + 1)]
    for block_id, part_name, part_shape, offset, entries in segments:
        blocks[block_id][part_name] = flat[offset : offset + entries].reshape(part_shape)
    return blocks


MESH = pl.DeviceIdType.MESH

def remote(src, dst, send, recv, target):
    return pltpu.make_async_remote_copy(src, dst, send, recv, device_id=(target,), device_id_type=MESH)

def greet(n, me):
    barrier = pltpu.get_barrier_semaphore()
    def hello(j, c):
        pl.semaphore_signal(barrier, inc=1, device_id=(lax.rem(me + j, n),), device_id_type=MESH)
        return c
    lax.fori_loop(1, n, hello, 0)
    pl.semaphore_wait(barrier, n - 1)

def a2a_kernel(n, a_ref, o_ref, own, ssem, rsem):
    me = lax.axis_index('dev')
    greet(n, me)
    here = pltpu.make_async_copy(a_ref.at[me], o_ref.at[me], own)
    here.start()
    def go(j, c):
        t = lax.rem(me + j, n)
        remote(a_ref.at[t], o_ref.at[me], ssem.at[j], rsem.at[j], t).start()
        return c
    lax.fori_loop(1, n, go, 0)
    def end(j, c):
        t = lax.rem(me + j, n)
        remote(a_ref.at[t], o_ref.at[me], ssem.at[j], rsem.at[j], t).wait()
        return c
    lax.fori_loop(1, n, end, 0)
    here.wait()

def a2a(x, cid, space=pl.ANY):
    n = x.shape[0]
    return pl.pallas_call(
        functools.partial(a2a_kernel, n),
        out_shape=jax.ShapeDtypeStruct(x.shape, x.dtype),
        in_specs=[pl.BlockSpec(memory_space=space)],
        out_specs=pl.BlockSpec(memory_space=space),
        scratch_shapes=[pltpu.SemaphoreType.DMA, pltpu.SemaphoreType.DMA((n,)), pltpu.SemaphoreType.DMA((n,))],
        compiler_params=pltpu.CompilerParams(collective_id=cid, has_side_effects=True),
    )(x)

def gather_kernel(w_ref, ask_ref, num_ref, o_ref, served_ref, nums_ref, own, small_s, small_r, zs, zr, hs, hr, cs, cr, ds, dr, bs, br):
    n = 32
    me = lax.axis_index('dev')
    c, x, y, z = lax.rem(me, 2), lax.rem(me // 2, 2), lax.rem(me // 4, 2), me // 8
    rows = w_ref.shape[0]
    half = rows // 2
    A, B = pl.ds(0, half), pl.ds(half, half)
    def dev(z, y, x, c):
        return ((z * 2 + y) * 2 + x) * 2 + c
    greet(n, me)
    tx, ty, tc = dev(z, y, 1 - x, c), dev(z, 1 - y, x, c), dev(z, y, x, 1 - c)
    up, down = dev(lax.rem(z + 1, 4), y, x, c), dev(lax.rem(z + 3, 4), y, x, c)
    pend = []
    def start(cp):
        cp.start(); pend.append(cp)
    mine = pltpu.make_async_copy(w_ref, o_ref.at[me], own.at[0])
    mine.start()
    planes = [z, z + 1 - 2 * lax.rem(z, 2), 2 - z // 2, 3 - 3 * (z // 2)]
    def on_up(i, wait):
        src = w_ref if i == 0 else o_ref.at[dev(planes[i], y, x, c)]
        slot = dev(planes[i], y, x, c)
        @pl.when((planes[i] <= z) & (z < 3))
        def _():
            cp = remote(src, o_ref.at[slot], zs.at[0, i], zr.at[planes[i]], up)
            cp.wait_send() if wait else cp.start()
    def on_down(i, wait):
        src = w_ref if i == 0 else o_ref.at[dev(planes[i], y, x, c)]
        slot = dev(planes[i], y, x, c)
        @pl.when((planes[i] >= z) & (z > 0))
        def _():
            cp = remote(src, o_ref.at[slot], zs.at[1, i], zr.at[planes[i]], down)
            cp.wait_send() if wait else cp.start()
    start(remote(w_ref.at[A], o_ref.at[me, A], hs.at[0, 0], hr.at[0, 0], tx))
    start(remote(w_ref.at[B], o_ref.at[me, B], hs.at[0, 1], hr.at[0, 1], ty))
    on_up(0, False)
    on_down(0, False)
    start(remote(w_ref, o_ref.at[me], bs.at[0], br.at[0], tc))
    mine2 = pltpu.make_async_copy(ask_ref.at[me], served_ref.at[me], own.at[1])
    mine2.start()
    mine3 = pltpu.make_async_copy(num_ref, nums_ref.at[me], own.at[2])
    mine3.start()
    def go(j, carry):
        t = lax.rem(me + j, n)
        remote(ask_ref.at[t], served_ref.at[me], small_s.at[0, j], small_r.at[0, j], t).start()
        remote(num_ref, nums_ref.at[me], small_s.at[1, j], small_r.at[1, j], t).start()
        return carry
    lax.fori_loop(1, n, go, 0)
    nb = [1]
    def sib(slot, part):
        i = nb[0]; nb[0] += 1
        ref = o_ref.at[slot] if part is None else o_ref.at[slot, part]
        start(remote(ref, ref, bs.at[i], br.at[i], tc))
    def first(k):
        s = dev(planes[k], y, x, c)
        remote(w_ref, o_ref.at[s], zs.at[0, k], zr.at[planes[k]], tc).wait_recv()
        start(remote(o_ref.at[s, A], o_ref.at[s, A], hs.at[k, 0], hr.at[k, 0], tx))
        start(remote(o_ref.at[s, B], o_ref.at[s, B], hs.at[k, 1], hr.at[k, 1], ty))
        on_up(k, False)
        on_down(k, False)
        sib(s, None)
    def second(k):
        zz = planes[k]
        s = dev(zz, y, x, c)
        sx, sy = dev(zz, y, 1 - x, c), dev(zz, 1 - y, x, c)
        own_a = w_ref.at[A] if k == 0 else o_ref.at[s, A]
        own_b = w_ref.at[B] if k == 0 else o_ref.at[s, B]
        start(remote(own_a, o_ref.at[s, A], cs.at[k, 0], cr.at[k, 0], ty))
        start(remote(own_b, o_ref.at[s, B], ds.at[k, 0], dr.at[k, 0], tx))
        remote(own_a, o_ref.at[sx, A], hs.at[k, 0], hr.at[k, 0], tx).wait_recv()
        start(remote(o_ref.at[sx, A], o_ref.at[sx, A], cs.at[k, 1], cr.at[k, 1], ty))
        remote(own_b, o_ref.at[sy, B], hs.at[k, 1], hr.at[k, 1], ty).wait_recv()
        start(remote(o_ref.at[sy, B], o_ref.at[sy, B], ds.at[k, 1], dr.at[k, 1], tx))
        sib(sx, A)
        sib(sy, B)
    def third(k):
        zz = planes[k]
        sx, sy, sd = dev(zz, y, 1 - x, c), dev(zz, 1 - y, x, c), dev(zz, 1 - y, 1 - x, c)
        w = w_ref.at[A]
        remote(w, o_ref.at[sy, A], cs.at[k, 0], cr.at[k, 0], ty).wait_recv()
        sib(sy, A)
        remote(w, o_ref.at[sx, B], ds.at[k, 0], dr.at[k, 0], tx).wait_recv()
        sib(sx, B)
        remote(w, o_ref.at[sd, A], cs.at[k, 1], cr.at[k, 1], ty).wait_recv()
        sib(sd, A)
        remote(w, o_ref.at[sd, B], ds.at[k, 1], dr.at[k, 1], tx).wait_recv()
        sib(sd, B)
    second(0)
    first(1)
    third(0)
    second(1)
    first(2)
    third(1)
    second(2)
    first(3)
    third(2)
    second(3)
    third(3)
    nb2 = [0]
    def got(*parts):
        for part in parts:
            i = nb2[0]; nb2[0] += 1
            ref = w_ref if part is None else w_ref.at[part]
            o = o_ref.at[me] if part is None else o_ref.at[me, part]
            remote(ref, o, bs.at[i], br.at[i], tc).wait_recv()
    g1, g2, g3 = (None,), (A, B), (A, B, A, B)
    for g in (g1, g2, g1, g3, g2, g1, g3, g2, g1, g3, g2, g3):
        got(*g)
    def end(j, carry):
        t = lax.rem(me + j, n)
        remote(ask_ref.at[t], served_ref.at[me], small_s.at[0, j], small_r.at[0, j], t).wait()
        remote(num_ref, nums_ref.at[me], small_s.at[1, j], small_r.at[1, j], t).wait()
        return carry
    lax.fori_loop(1, n, end, 0)
    for i in range(4):
        on_up(i, True)
        on_down(i, True)
    for cp in pend:
        cp.wait_send()
    mine.wait(); mine2.wait(); mine3.wait()


def gather_weights(w, ask, num, cid):
    n = 32
    rows = w.shape[0]
    D = pltpu.SemaphoreType.DMA
    sib = 1 + 4 * 2 + 3 + 4 * 4
    anyspec = pl.BlockSpec(memory_space=pl.ANY)
    return pl.pallas_call(
        gather_kernel,
        out_shape=(jax.ShapeDtypeStruct((n, rows, 128), w.dtype), jax.ShapeDtypeStruct(ask.shape, ask.dtype), jax.ShapeDtypeStruct((n,) + num.shape, num.dtype)),
        in_specs=[anyspec] * 3, out_specs=(anyspec,) * 3,
        scratch_shapes=[D((3,)), D((2, n)), D((2, n)), D((2, 4)), D((4,)), D((4, 2)), D((4, 2)), D((4, 2)), D((4, 2)), D((4, 2)), D((4, 2)), D((sib,)), D((sib,))],
        compiler_params=pltpu.CompilerParams(collective_id=cid, has_side_effects=True),
    )(w, ask, num)


F32, BF16 = jnp.float32, jnp.bfloat16
VMEM_LIMIT = 60 << 20
ANY = pl.BlockSpec(memory_space=pl.ANY)
DMA = pltpu.SemaphoreType.DMA


def mm(a, b):
    return jnp.dot(a, b, preferred_element_type=F32)


def mm_nt(a, b):
    return lax.dot_general(a, b, (((1,), (1,)), ((), ())), preferred_element_type=F32)


def mm_tn(a, b):
    return lax.dot_general(a, b, (((0,), (0,)), ((), ())), preferred_element_type=F32)


def contract(a, b, left, right):
    return lax.dot_general(a, b, (((left,), (right,)), ((), ())), preferred_element_type=F32)


def col(v):
    return jnp.sum(v, axis=0, keepdims=True)


def pick(slots, first, rows):
    r = first + lax.broadcasted_iota(jnp.int32, (slots.shape[0], rows), 1)
    return jnp.where(slots == r, 1.0, 0.0).astype(BF16)


def place(slots, first, rows):
    r = first + lax.broadcasted_iota(jnp.int32, (rows, slots.shape[1]), 0)
    return jnp.where(slots == r, 1.0, 0.0).astype(BF16)


def first_half(us, w_in, vec):
    pre = vec[0:1, :]
    at = 0
    for u in us:
        pre = pre + mm(u, w_in[at : at + u.shape[1], :])
        at += u.shape[1]
    return pre


def activate(pre):
    sigma = jax.nn.sigmoid(pre)
    return sigma, (pre * sigma).astype(BF16)


def normalize(post):
    centred = post - jnp.mean(post, axis=-1, keepdims=True)
    inv = lax.rsqrt(jnp.mean(centred * centred, axis=-1, keepdims=True) + norm_eps)
    return centred * inv, inv


def second_half(act, w_out, vec):
    return normalize(mm(act, w_out[...]) + vec[1:2, :])


def scale_shift(hat, vec):
    return hat * vec[2:3, :] + vec[3:4, :]


def norm_back(g, hat, inv, vec, d_vec):
    if d_vec is not None:
        d_vec[2:3, :] += col(g * hat)
        d_vec[3:4, :] += col(g)
    s = g * vec[2:3, :]
    post = inv * (
        s - jnp.mean(s, axis=-1, keepdims=True) - hat * jnp.mean(s * hat, axis=-1, keepdims=True)
    )
    return post.astype(BF16)


def act_back(low, pre, sigma, w_out):
    g_act = mm_nt(low, w_out[...])
    return (g_act * sigma * (1.0 + pre * (1.0 - sigma))).astype(BF16)


def weight_sums(us, act, low, g_pre, d_in, d_out, d_vec):
    d_out[...] += mm_tn(act, low)
    d_vec[1:2, : low.shape[1]] += col(low.astype(F32))
    d_vec[0:1, :] += col(g_pre.astype(F32))
    at = 0
    for u in us:
        d_in[at : at + u.shape[1], :] += mm_tn(u, g_pre)
        at += u.shape[1]


def pack_matrix(packed, ref, rows, at):
    for j in range(4):
        packed[pl.ds(at + j, rows, stride=4), :] = ref[:rows, 128 * j : 128 * (j + 1)]
    return at + 4 * rows


def pack(packed, lead, rows_in, d_in, d_out, d_vec):
    def vector(i, at):
        for j in range(4):
            packed[at + j : at + j + 1, :] = d_vec[i : i + 1, 128 * j : 128 * (j + 1)]
        return at + 4
    at = pack_matrix(packed, d_in, rows_in, lead)
    at = vector(0, at)
    at = pack_matrix(packed, d_out, d_out.shape[0], at)
    for i in (1, 2, 3):
        at = vector(i, at)


def clear(*refs):
    for ref in refs:
        ref[...] = jnp.zeros_like(ref)


def spec(shape, fixed=True):
    if fixed:
        return pl.BlockSpec(shape, lambda i: (0,) * len(shape))
    return pl.BlockSpec(shape, lambda i: (i,) + (0,) * (len(shape) - 1))


def params(**more):
    return pltpu.CompilerParams(vmem_limit_bytes=VMEM_LIMIT, **more)


def shaped(*shape, dtype=F32):
    return jax.ShapeDtypeStruct(shape, dtype)


class Chunks:
    def __init__(self, begins, rows, cuts):
        self.begins, self.rows, self.cuts = begins, rows, cuts

    def shape(self, group):
        return (self.cuts[group + 1] - self.cuts[group], self.rows, 128)

    def pieces(self, at, size):
        found = []
        for group in range(len(self.cuts) - 1):
            for owner in range(self.cuts[group], self.cuts[group + 1]):
                begin = self.begins[owner]
                low, high = max(at, begin), min(at + size, begin + self.rows)
                if low < high:
                    found.append((group, owner - self.cuts[group], low - begin, low - at, high - low))
        return found

    def groups(self, *places):
        return sorted({p[0] for at, size in places for p in self.pieces(at, size)})


class Stores:
    def __init__(self, refs, chunks, sem):
        self.refs, self.chunks, self.sem, self.copies = refs, chunks, sem, []

    def put(self, packed, at):
        for group, owner, row, skip, size in self.chunks.pieces(at, packed.shape[0]):
            source = packed.at[pl.ds(skip, size)]
            copy = pltpu.make_async_copy(source, self.refs[group].at[owner, pl.ds(row, size)], self.sem.at[len(self.copies)])
            copy.start()
            self.copies.append(copy)

    def wait(self):
        for copy in self.copies:
            copy.wait()


STORES = 48


def flat_refs(r, groups):
    return {group: getattr(r, f"flat{group}") for group in groups}


def mlp_sums(rows_in, wide=LATENT):
    return [pltpu.VMEM((rows_in, LATENT), F32), pltpu.VMEM((LATENT, wide), F32), pltpu.VMEM((8, LATENT), F32)]


def packed_rows(rows_in, lead=0):
    return pltpu.VMEM((lead + 4 * rows_in + 4 * LATENT + 16, 128), F32)


def named_call(body, name, inputs, outputs, scratch, aliases=None, cid=None):
    names = [*inputs, *outputs, *scratch]
    aliases = {list(inputs).index(i): list(outputs).index(o) for i, o in (aliases or {}).items()}
    def kernel(*refs):
        body(types.SimpleNamespace(**dict(zip(names, refs))))
    more = {} if cid is None else dict(collective_id=cid, has_side_effects=True)
    values = pl.pallas_call(
        kernel,
        out_shape=tuple(shape for shape, _ in outputs.values()),
        in_specs=[s for _, s in inputs.values()],
        out_specs=tuple(s for _, s in outputs.values()),
        scratch_shapes=list(scratch.values()),
        input_output_aliases=aliases,
        compiler_params=params(**more),
        name=name,
    )(*[v for v, _ in inputs.values()])
    return types.SimpleNamespace(**dict(zip(outputs, values)))


def swap_start(n, me, srcs, dsts, own, ssem, rsem):
    for i, (src, dst) in enumerate(zip(srcs, dsts)):
        pltpu.make_async_copy(src.at[me], dst.at[me], own.at[i]).start()
    def go(j, c):
        t = lax.rem(me + j, n)
        for i, (src, dst) in enumerate(zip(srcs, dsts)):
            remote(src.at[t], dst.at[me], ssem.at[i, j], rsem.at[i, j], t).start()
        return c
    lax.fori_loop(1, n, go, 0)


def swap_wait(n, me, srcs, dsts, own, ssem, rsem):
    def end(j, c):
        t = lax.rem(me + j, n)
        for i, (src, dst) in enumerate(zip(srcs, dsts)):
            remote(src.at[t], dst.at[me], ssem.at[i, j], rsem.at[i, j], t).wait()
        return c
    lax.fori_loop(1, n, end, 0)
    for i, (src, dst) in enumerate(zip(srcs, dsts)):
        pltpu.make_async_copy(src.at[me], dst.at[me], own.at[i]).wait()


def several(r, name):
    return [getattr(r, f"{name}{i}") for i in range(4) if hasattr(r, f"{name}{i}")]


def numbered(name, values):
    return {f"{name}{i}": value for i, value in enumerate(values)}


def slot_rows(refs):
    rows = [ref[...].reshape(ref.shape[0] * ref.shape[1], ref.shape[2]) for ref in refs]
    return rows[0] if len(rows) == 1 else jnp.concatenate(rows, axis=0)


def put_slot_rows(refs, rows):
    at = 0
    for ref in refs:
        size = ref.shape[0] * ref.shape[1]
        ref[...] = rows[at : at + size, :].reshape(ref.shape)
        at += size


def greet_start(n, me):
    barrier = pltpu.get_barrier_semaphore()
    def hello(j, c):
        pl.semaphore_signal(barrier, inc=1, device_id=(lax.rem(me + j, n),), device_id_type=MESH)
        return c
    lax.fori_loop(1, n, hello, 0)


def greet_wait(n):
    pl.semaphore_wait(pltpu.get_barrier_semaphore(), n - 1)


class Loads:
    def __init__(self, r, sem):
        self.r, self.sem, self.copies = r, sem, {}

    def start(self, *names):
        for name in names:
            copy = pltpu.make_async_copy(getattr(self.r, name), getattr(self.r, "_" + name), self.sem.at[len(self.copies)])
            copy.start()
            self.copies[name] = copy

    def wait(self, *names):
        for name in names:
            self.copies[name].wait()


def store_all(r, sem, *names):
    copies = [pltpu.make_async_copy(getattr(r, "_" + name), getattr(r, name), sem.at[i]) for i, name in enumerate(names)]
    for copy in copies:
        copy.start()
    return copies


def same_rows(want, served):
    return jnp.where((want[...] == served[...]) & (want[...] >= 0), 1.0, 0.0).astype(BF16)


def swap_scratch(shapes, n):
    parts = len(shapes)
    scratch = dict(own=DMA((2, parts)), s1=DMA((parts, n)), r1=DMA((parts, n)), s2=DMA((parts, n)), r2=DMA((parts, n)))
    for name in ("away", "here", "back"):
        scratch |= numbered(name, [pltpu.VMEM(shape, BF16) for shape in shapes])
    return scratch


def held(prefix, block):
    return {prefix + part: pltpu.VMEM(a.shape, a.dtype) for part, a in zip(("_in", "_out", "_vec"), block)}


def weights(prefix, block):
    return {prefix + part: (a, ANY) for part, a in zip(("_in", "_out", "_vec"), block)}


def rows_block(bm, width=LATENT):
    return pl.BlockSpec((bm, width), lambda i: (i, 0))


def edge_kernel(n, first, bm, r):
    me = lax.axis_index("dev")
    greet_start(n, me)
    loads = Loads(r, r.lsem)
    node_weights = ["p_in", "p_out", "p_vec"]
    landing = [name for name in vars(r) if name.startswith("landed_in")]
    early = node_weights + ([] if first else [*landing, "slots_in"])
    late = ["e_in", "e_out", "e_vec"] + (["g_in", "g_out", "g_vec"] if first else [])
    loads.start(*early)
    loads.start(*late)
    loads.wait(*early)
    count = r.want.shape[0]
    if first:
        asked = contract(pick(r.want[...], 0, r.x.shape[1]), r.x[...], 1, 1).astype(BF16)
        pre = contract(asked, r._p_in[:VARS, :], 1, 0) + r._p_vec[0:1, :]
    else:
        landed = slot_rows(several(r, "_landed_in"))
        got = mm(same_rows(r.want, r.served), landed).astype(BF16)
        r._sums_s[...] = got
        old = r._slots_in[...]
        pre = first_half([old.astype(BF16), got], r._p_in, r._p_vec)
    _, act = activate(pre)
    hat, _ = second_half(act, r._p_out, r._p_vec)
    slots = scale_shift(hat, r._p_vec)
    if not first:
        slots = old + slots
    r._slots[...] = slots
    away, here, back, out = (several(r, name) for name in ("away", "here", "back", "landed"))
    put_slot_rows(away, slots.astype(BF16))
    greet_wait(n)
    swap_start(n, me, away, here, r.own.at[0], r.s1, r.r1)
    stores = store_all(r, r.ssem, *(["slots"] if first else ["slots", "sums_s"]))
    loads.wait(*late)
    if first:
        _, act = activate(first_half([r.source[...]], r._g_in, r._g_vec))
        hat, _ = second_half(act, r._g_out, r._g_vec)
        r._edge[...] = scale_shift(hat, r._g_vec)
    else:
        r._edge[...] = r.source[...]
    e = r._edge[...].astype(BF16)
    r.edge_low[...] = e
    r._pre[...] = first_half([e], r._e_in, r._e_vec)
    if first:
        def body(node, low):
            i = pl.program_id(0)
            u = r.x[:, pl.ds(pl.multiple_of(i * bm, bm), bm)]
            _, act = activate(contract(u, r._p_in[:VARS, :], 0, 0) + r._p_vec[0:1, :])
            hat, _ = second_half(act, r._p_out, r._p_vec)
            new = scale_shift(hat, r._p_vec)
            node[...] = new
            low[...] = new.astype(BF16)
        pltpu.emit_pipeline(body, grid=(r.node.shape[0] // bm,), in_specs=[], out_specs=[rows_block(bm)] * 2)(r.node, r.low)
    else:
        def body(node_in, node, low, sums):
            i = pl.program_id(0)
            got = mm(place(r.served[...], i * bm, bm), slot_rows(several(r, "_landed_in"))).astype(BF16)
            sums[...] = got
            old = node_in[...]
            _, act = activate(first_half([old.astype(BF16), got], r._p_in, r._p_vec))
            hat, _ = second_half(act, r._p_out, r._p_vec)
            new = old + scale_shift(hat, r._p_vec)
            node[...] = new
            low[...] = new.astype(BF16)
        pltpu.emit_pipeline(body, grid=(r.node.shape[0] // bm,), in_specs=[rows_block(bm)], out_specs=[rows_block(bm)] * 3)(r.node_in, r.node, r.low, r.sums)
    pick_s, pick_r = pick(r.pos[:, 0:1], 0, count), pick(r.pos[:, 1:2], 0, count)
    put_r = place(r.pos_r[...], 0, count)
    swap_wait(n, me, away, here, r.own.at[0], r.s1, r.r1)
    rows = slot_rows(here)
    s = mm(pick_s, rows).astype(BF16)
    v = mm(pick_r, rows).astype(BF16)
    pre = r._pre[...] + mm(s, r._e_in[LATENT : 2 * LATENT, :]) + mm(v, r._e_in[2 * LATENT :, :])
    _, act = activate(pre)
    hat, _ = second_half(act, r._e_out, r._e_vec)
    new = r._edge[...] + scale_shift(hat, r._e_vec)
    put_slot_rows(back, mm(put_r, new.astype(BF16)).astype(BF16))
    swap_start(n, me, back, out, r.own.at[1], r.s2, r.r2)
    r.edge[...] = new
    r.sent[...], r.recv[...] = s, v
    for store in stores:
        store.wait()
    swap_wait(n, me, back, out, r.own.at[1], r.s2, r.r2)


def edge_forward(n, parts, cid, source, routes, edge_block, node_block, rows, x=None, geo_block=None, landed=None, node=None, slots=None, bm=512):
    first = x is not None
    want, served, pos, pos_s, pos_r = routes
    count = want.shape[0]
    edges = source.shape[0]
    shapes = [(n, p, LATENT) for p in parts]
    V = pl.BlockSpec(memory_space=pltpu.VMEM)
    inputs = dict(source=(source, V), want=(want, V), served=(served, V), pos=(pos, V), pos_r=(pos_r, V))
    inputs |= weights("p", node_block) | weights("e", edge_block)
    scratch = held("_p", node_block) | held("_e", edge_block) | swap_scratch(shapes, n)
    scratch |= dict(_slots=pltpu.VMEM((count, LATENT), F32), _edge=pltpu.VMEM((edges, LATENT), F32), _pre=pltpu.VMEM((edges, LATENT), F32), lsem=DMA((12,)), ssem=DMA((2,)))
    low = lambda r: shaped(r, LATENT, dtype=BF16)
    outputs = dict(edge=(shaped(edges, LATENT), V), edge_low=(low(edges), V), sent=(low(edges), V), recv=(low(edges), V)) | numbered("landed", [(shaped(*s, dtype=BF16), ANY) for s in shapes])
    outputs |= dict(node=(shaped(rows, LATENT), ANY), low=(low(rows), ANY), slots=(shaped(count, LATENT), ANY))
    if first:
        inputs |= dict(x=(x, V)) | weights("g", geo_block)
        scratch |= held("_g", geo_block)
    else:
        inputs |= numbered("landed_in", [(v, ANY) for v in landed]) | dict(node_in=(node, ANY), slots_in=(slots, ANY))
        scratch |= numbered("_landed_in", [pltpu.VMEM(s, BF16) for s in shapes]) | dict(_slots_in=pltpu.VMEM((count, LATENT), F32), _sums_s=pltpu.VMEM((count, LATENT), BF16))
        outputs |= dict(sums=(low(rows), ANY), sums_s=(low(count), ANY))
    return named_call(functools.partial(edge_kernel, n, first, bm), "edge_forward", inputs, outputs, scratch, cid=cid)


def turn_kernel(parts, bm, chunks, group, at, dec_at, served, want, *refs):
    landed, refs = refs[:parts], refs[parts:]
    flat, g_prev, *outs = refs[13 : 15 + parts]
    node, x, target, level, land, count, w_in, w_out, vec, c_in, c_out, c_vec, c_bias = refs[:13]
    d_out_o, d_first_o, d_bias_o, err_o, packed, packed2, d_in, d_out, d_vec, e_in, e_out, e_vec, e_bias, err, acc, sem = refs[13 + 2 + parts:]
    i = pl.program_id(0)
    @pl.when(i == 0)
    def _():
        clear(d_in, d_out, d_vec, e_in, e_out, e_vec, e_bias, err, acc)
    got = mm(place(served[...], i * bm, bm), slot_rows(landed)).astype(BF16)
    old = node[...]
    low = old.astype(BF16)
    pre = first_half([low, got], w_in, vec)
    sigma, act = activate(pre)
    hat, inv = second_half(act, w_out, vec)
    u = (old + scale_shift(hat, vec)).astype(BF16)
    c_pre = first_half([u], c_in, c_vec)
    c_sigma, c_act = activate(c_pre)
    wide = c_out.shape[1]
    post = contract(c_out[...], c_act, 0, 1)
    sea = (lax.broadcasted_iota(jnp.int32, (VARS, 1), 0) < SEA_VARS).astype(F32)
    mask = level[...].astype(F32) * (1.0 - sea * land[...].astype(F32))
    residual = x[...].astype(F32) + (post[:VARS, :] + c_bias[...]) - target[...]
    divisor = jnp.maximum(count[...], 1.0)
    err[...] += jnp.sum(mask * residual * residual, axis=0, keepdims=True)
    g = 2.0 * mask * residual / divisor
    g_low = jnp.concatenate([g, jnp.zeros((wide - VARS, bm), F32)], axis=0).astype(BF16)
    e_bias[...] += jnp.sum(g_low.astype(F32), axis=1, keepdims=True)
    e_out[...] += contract(c_act, g_low, 0, 1)
    g_act = contract(g_low, c_out[...], 0, 1)
    c_g = (g_act * c_sigma * (1.0 + c_pre * (1.0 - c_sigma))).astype(BF16)
    e_vec[0:1, :] += col(c_g.astype(F32))
    e_in[...] += mm_tn(u, c_g)
    g_node = mm_nt(c_g, c_in[...])
    g_post = norm_back(g_node, hat, inv, vec, d_vec)
    g_pre = act_back(g_post, pre, sigma, w_out)
    weight_sums([low, got], act, g_post, g_pre, d_in, d_out, d_vec)
    g_prev[...] = g_node + mm_nt(g_pre, w_in[:LATENT, :])
    acc[...] += mm(pick(want[...], i * bm, bm), mm_nt(g_pre, w_in[LATENT:, :]).astype(BF16))
    @pl.when(i == pl.num_programs(0) - 1)
    def _():
        put_slot_rows(outs, acc[...].astype(BF16))
        d_out_o[...] = e_out[...]
        d_first_o[...] = e_vec[0:1, :]
        d_bias_o[...] = e_bias[...]
        err_o[...] = err[...]
        stores = Stores({group: flat}, chunks, sem)
        pack_matrix(packed2, e_in, LATENT, 0)
        stores.put(packed2, dec_at)
        pack(packed, 0, 2 * LATENT, d_in, d_out, d_vec)
        stores.put(packed, at)
        stores.wait()


def turn(served, want, landed, node, x, target, level, land, count, block, dec, bias, chunks, at, dec_at, bm=512):
    rows = node.shape[0]
    slots = want.shape[0]
    wide = dec[1].shape[1]
    [group] = chunks.groups((at, dec_at + 4 * LATENT - at))
    v = lambda height: pl.BlockSpec((height, bm), lambda i: (0, i))
    part = [spec(p.shape) for p in landed]
    return pl.pallas_call(
        functools.partial(turn_kernel, len(landed), bm, chunks, group, at, dec_at),
        grid=(rows // bm,),
        out_shape=(shaped(*chunks.shape(group)), shaped(rows, LATENT), *(shaped(*p.shape, dtype=BF16) for p in landed), shaped(LATENT, wide), shaped(1, LATENT), shaped(wide, 1), shaped(1, bm)),
        in_specs=[spec((1, slots)), spec((slots, 1)), *part, spec((bm, LATENT), False), v(VARS), v(VARS), v(VARS), v(1), spec((1, 1))] + [spec(a.shape) for a in (*block, *dec, bias)],
        out_specs=(ANY, spec((bm, LATENT), False), *part, spec((LATENT, wide)), spec((1, LATENT)), spec((wide, 1)), spec((1, bm))),
        scratch_shapes=[packed_rows(2 * LATENT), pltpu.VMEM((4 * LATENT, 128), F32)] + mlp_sums(2 * LATENT) + mlp_sums(LATENT, wide) + [pltpu.VMEM((wide, 1), F32), pltpu.VMEM((1, bm), F32), pltpu.VMEM((slots, LATENT), F32), DMA((STORES,))],
        compiler_params=params(),
        name="turn",
    )(served, want, *landed, node, x, target, level, land, count, *block, *dec, bias)


def gather_slots(r, bm):
    clear(r._g_slots)
    def body(g_node):
        chosen = pick(r.want[...], pl.program_id(0) * bm, bm)
        g = g_node[...]
        high = g.astype(BF16)
        rest = g - high.astype(F32)
        middle = rest.astype(BF16)
        small = (rest - middle.astype(F32)).astype(BF16)
        r._g_slots[...] += mm(chosen, high) + (mm(chosen, middle) + mm(chosen, small))
    pltpu.emit_pipeline(body, grid=(r.g_node.shape[0] // bm,), in_specs=[rows_block(bm)], out_specs=[])(r.g_node)


def edge_back_kernel(n, chunks, groups, at, node_at, geo_at, tail_at, bm, r):
    me = lax.axis_index("dev")
    greet_start(n, me)
    loads = Loads(r, r.lsem)
    nodes = node_at is not None
    landing = [name for name in vars(r) if name.startswith("landed_in")]
    early = ["p_in", "p_out", "p_vec", *landing, "g_slots_in", "slots_in", "sums_s"] if nodes else []
    late = ["e_in", "e_out", "e_vec"] + (["g_in", "g_out", "g_vec"] if geo_at is not None else [])
    loads.start(*early)
    loads.start(*late)
    flats = Stores(flat_refs(r, groups), chunks, r.fsem)
    stores = [flats]
    if tail_at is not None:
        flats.put(r.tail, tail_at)
    count = r.want.shape[0]
    here, back, out = (several(r, name) for name in ("here", "back", "landed"))
    if nodes:
        loads.wait(*early)
        us = [r._slots_in[...].astype(BF16), r._sums_s[...]]
        pre = first_half(us, r._p_in, r._p_vec)
        sigma, act = activate(pre)
        hat, inv = second_half(act, r._p_out, r._p_vec)
        g = r._g_slots_in[...] + mm(same_rows(r.want, r.served), slot_rows(several(r, "_landed_in")))
        low = norm_back(g, hat, inv, r._p_vec, None)
        g_pre = act_back(low, pre, sigma, r._p_out)
        source = several(r, "away")
        put_slot_rows(source, mm_nt(g_pre, r._p_in[LATENT:, :]).astype(BF16))
    else:
        source = several(r, "outgoing")
    greet_wait(n)
    swap_start(n, me, source, here, r.own.at[0], r.s1, r.r1)
    if nodes:
        r._g_slots[...] = g + mm_nt(g_pre, r._p_in[:LATENT, :])
        stores += store_all(r, r.ssem, "g_slots")
        clear(r.n_in, r.n_out, r.n_vec)
    clear(r.d_in, r.d_out, r.d_vec)
    def node_rows(first, last):
        if not nodes:
            return
        def body(g_node, low_in, sums_in, g_prev):
            i = first + pl.program_id(0)
            us = [low_in[...], sums_in[...]]
            pre = first_half(us, r._p_in, r._p_vec)
            sigma, act = activate(pre)
            hat, inv = second_half(act, r._p_out, r._p_vec)
            g = g_node[...] + mm(place(r.served[...], i * bm, bm), slot_rows(several(r, "_landed_in")))
            low = norm_back(g, hat, inv, r._p_vec, r.n_vec)
            g_pre = act_back(low, pre, sigma, r._p_out)
            weight_sums(us, act, low, g_pre, r.n_in, r.n_out, r.n_vec)
            g_prev[...] = g + mm_nt(g_pre, r._p_in[:LATENT, :])
        block = pl.BlockSpec((bm, LATENT), lambda i: (first + i, 0))
        pltpu.emit_pipeline(body, grid=(last - first,), in_specs=[block] * 3, out_specs=[block])(r.g_node, r.low, r.sums, r.g_prev)
    blocks = r.g_node.shape[0] // bm if nodes else 0
    node_rows(0, blocks // 2)
    if not nodes:
        gather_slots(r, bm)
    loads.wait(*late)
    us = [r.edge_low[...], r.sent[...], r.recv[...]]
    pre = first_half(us, r._e_in, r._e_vec)
    sigma, act = activate(pre)
    hat, inv = second_half(act, r._e_out, r._e_vec)
    pick_r = pick(r.pos[:, 1:2], 0, count)
    put_s, put_r = place(r.pos_s[...], 0, count), place(r.pos_r[...], 0, count)
    swap_wait(n, me, source, here, r.own.at[0], r.s1, r.r1)
    g = mm(pick_r, slot_rows(here))
    if hasattr(r, "g_edge"):
        g = r.g_edge[...] + g
    low = norm_back(g, hat, inv, r._e_vec, r.d_vec)
    g_pre = act_back(low, pre, sigma, r._e_out)
    s = mm_nt(g_pre, r._e_in[LATENT : 2 * LATENT, :]).astype(BF16)
    v = mm_nt(g_pre, r._e_in[2 * LATENT :, :]).astype(BF16)
    put_slot_rows(back, (mm(put_s, s) + mm(put_r, v)).astype(BF16))
    swap_start(n, me, back, out, r.own.at[1], r.s2, r.r2)
    prev = g + mm_nt(g_pre, r._e_in[:LATENT, :])
    r.edge_prev[...] = prev
    weight_sums(us, act, low, g_pre, r.d_in, r.d_out, r.d_vec)
    pack(r.packed, 0, 3 * LATENT, r.d_in, r.d_out, r.d_vec)
    flats.put(r.packed, at)
    if geo_at is not None:
        c_us = [r.geo[...]]
        c_pre = first_half(c_us, r._g_in, r._g_vec)
        c_sigma, c_act = activate(c_pre)
        c_hat, c_inv = second_half(c_act, r._g_out, r._g_vec)
        clear(r.c_in, r.c_out, r.c_vec)
        c_low = norm_back(prev, c_hat, c_inv, r._g_vec, r.c_vec)
        c_g = act_back(c_low, c_pre, c_sigma, r._g_out)
        weight_sums(c_us, c_act, c_low, c_g, r.c_in, r.c_out, r.c_vec)
        pack(r.c_packed, 0, GEO, r.c_in, r.c_out, r.c_vec)
        flats.put(r.c_packed, geo_at)
    node_rows(blocks // 2, blocks)
    if nodes:
        pack(r.n_packed, 0, 2 * LATENT, r.n_in, r.n_out, r.n_vec)
        flats.put(r.n_packed, node_at)
    if not nodes:
        stores += store_all(r, r.ssem, "g_slots")
    swap_wait(n, me, back, out, r.own.at[1], r.s2, r.r2)
    for store in stores:
        store.wait()


def sums_scratch(prefix, rows_in):
    return dict(zip((prefix + "_in", prefix + "_out", prefix + "_vec"), mlp_sums(rows_in)))


def edge_backward(n, parts, cid, ins, routes, edge_block, chunks, flats, at, g_edge=None, outgoing=None, g_node=None, tail=None, tail_at=None, node=None, node_at=None, geo=None, geo_at=None, bm=512):
    want, served, pos, pos_s, pos_r = routes
    count = want.shape[0]
    edges = pos.shape[0]
    shapes = [(n, p, LATENT) for p in parts]
    V = pl.BlockSpec(memory_space=pltpu.VMEM)
    inputs = dict(want=(want, V), served=(served, V), pos=(pos, V), pos_s=(pos_s, V), pos_r=(pos_r, V))
    inputs |= {name: (value, V) for name, value in zip(("edge_low", "sent", "recv"), ins)} | weights("e", edge_block)
    scratch = held("_e", edge_block) | swap_scratch(shapes, n) | sums_scratch("d", 3 * LATENT)
    scratch |= dict(packed=packed_rows(3 * LATENT), lsem=DMA((16,)), ssem=DMA((2,)), fsem=DMA((STORES,)))
    outputs = dict(edge_prev=(shaped(edges, LATENT), V)) | numbered("landed", [(shaped(*s, dtype=BF16), ANY) for s in shapes])
    places = [(at, scratch["packed"].shape[0])]
    if g_edge is not None:
        inputs |= dict(g_edge=(g_edge, V))
    if outgoing is not None:
        inputs |= numbered("outgoing", [(v, ANY) for v in outgoing]) | dict(g_node=(g_node, ANY))
        outputs |= dict(g_slots=(shaped(count, LATENT), ANY))
        scratch |= dict(_g_slots=pltpu.VMEM((count, LATENT), F32))
    if tail is not None:
        inputs |= dict(tail=(tail, V))
        places.append((tail_at, tail.shape[0]))
    if node is not None:
        inputs |= numbered("landed_in", [(v, ANY) for v in node[0]])
        for name, value in zip(("g_slots_in", "slots_in", "sums_s", "g_node", "low", "sums"), node[1:]):
            inputs[name] = (value, ANY)
        inputs |= weights("p", node[7])
        scratch |= held("_p", node[7]) | sums_scratch("n", 2 * LATENT)
        f = pltpu.VMEM((count, LATENT), F32)
        scratch |= numbered("_landed_in", [pltpu.VMEM(s, BF16) for s in shapes]) | dict(n_packed=packed_rows(2 * LATENT), _g_slots_in=f, _slots_in=f, _g_slots=f, _sums_s=pltpu.VMEM((count, LATENT), BF16))
        rows = node[4].shape[0]
        places.append((node_at, scratch["n_packed"].shape[0]))
        outputs |= dict(g_prev=(shaped(rows, LATENT), ANY), g_slots=(shaped(count, LATENT), ANY))
    if geo is not None:
        inputs |= dict(geo=(geo[0], V)) | weights("g", geo[1])
        scratch |= held("_g", geo[1]) | sums_scratch("c", geo[0].shape[1]) | dict(c_packed=packed_rows(GEO))
        places.append((geo_at, scratch["c_packed"].shape[0]))
    groups = chunks.groups(*places)
    aliases = {}
    for group in groups:
        outputs[f"flat{group}"] = (shaped(*chunks.shape(group)), ANY)
        if group in flats:
            inputs[f"flat{group}_in"] = (flats[group], ANY)
            aliases[f"flat{group}_in"] = f"flat{group}"
    body = functools.partial(edge_back_kernel, n, chunks, groups, at, node_at, geo_at, tail_at, bm)
    made = named_call(body, "edge_backward", inputs, outputs, scratch, aliases=aliases, cid=cid)
    flats.update(flat_refs(made, groups))
    return made


def encode_back_rows(first, bm, served, landed, g_node, x, w_in, w_out, vec, d_in, d_out, d_vec):
    pre = contract(x[...], w_in[:VARS, :], 0, 0) + vec[0:1, :]
    sigma, act = activate(pre)
    hat, inv = second_half(act, w_out, vec)
    g = g_node[...] + mm(place(served[...], first, bm), slot_rows(landed))
    g_post = norm_back(g, hat, inv, vec, d_vec)
    g_pre = act_back(g_post, pre, sigma, w_out)
    weight_sums([], act, g_post, g_pre, d_in, d_out, d_vec)
    d_in[:VARS, :] += mm(x[...], g_pre)


def encode_pack(packed, d_in, d_out, d_vec):
    packed[0:4, :] = jnp.zeros((4, 128), F32)
    pack(packed, 4, VARS, d_in, d_out, d_vec)


def encode_back_kernel(parts, bm, chunks, served, *refs):
    landed, refs = refs[:parts], refs[parts:]
    g_node, x, w_in, w_out, vec, flat_in, flat, packed, d_in, d_out, d_vec, sem = refs
    i = pl.program_id(0)
    @pl.when(i == 0)
    def _():
        clear(d_in, d_out, d_vec)
    encode_back_rows(i * bm, bm, served, landed, g_node, x, w_in, w_out, vec, d_in, d_out, d_vec)
    @pl.when(i == pl.num_programs(0) - 1)
    def _():
        encode_pack(packed, d_in, d_out, d_vec)
        stores = Stores({0: flat}, chunks, sem)
        stores.put(packed, 0)
        stores.wait()


def encode_backward(served, landed, g_node, x, block, chunks, flat, bm=512):
    k, rows = block[0].shape[0], x.shape[1]
    slots = served.shape[1]
    return pl.pallas_call(
        functools.partial(encode_back_kernel, len(landed), bm, chunks),
        grid=(rows // bm,),
        out_shape=shaped(*flat.shape),
        in_specs=[spec((1, slots)), *(spec(p.shape) for p in landed), spec((bm, LATENT), False), pl.BlockSpec((VARS, bm), lambda i: (0, i))] + [spec(a.shape) for a in block] + [ANY],
        out_specs=ANY,
        scratch_shapes=[packed_rows(VARS, 4)] + mlp_sums(k) + [DMA((STORES,))],
        input_output_aliases={6 + len(landed): 0},
        compiler_params=params(),
        name="encode_backward",
    )(served, *landed, g_node, x, *block, flat)


def relay_plan(segments, share_rows):
    jobs = []
    for block_id, part_name, part_shape, offset, entries in segments:
        if part_name not in ("w_in", "w_out") or part_shape[1] != LATENT:
            continue
        for first in range(0, part_shape[0], LATENT):
            rows = min(LATENT, part_shape[0] - first)
            follow = 0
            if first + rows == part_shape[0]:
                follow = 1 if part_name == "w_in" else 3
            begin = offset // 128 + 4 * first
            end = begin + 4 * (rows + follow)
            parts = []
            at = begin
            while at < end:
                owner, low = divmod(at, share_rows)
                size = min(end - at, share_rows - low)
                base = low // 16 * 16
                span = (low + size - base + 15) // 16 * 16
                parts.append((owner, base, span, low - base, at - begin))
                at += size
            jobs.append((block_id, part_name, first, rows, follow, parts))
    return jobs


def relay_kernel(jobs, shapes, shares, *rest):
    count = sum(len(s) for s in shapes)
    outs = rest[:count]
    stage, lines, made, vecs, isem, osem, vsem = rest[count:]
    index = {}
    for b, s in enumerate(shapes):
        for name, _ in s:
            index[b, name] = len(index)
    loads, at = [], 0
    for number, (b, name, first, rows, follow, parts) in enumerate(jobs):
        mine = []
        for owner, base, span, skip, to in parts:
            copy = pltpu.make_async_copy(shares.at[owner, pl.ds(base, span)], stage.at[pl.ds(at, span)], isem.at[len(loads) * 0 + number * 4 + len(mine)])
            copy.start()
            mine.append((copy, at, span, skip, to))
            at += span
        loads.append(mine)
    vecs[...] = jnp.zeros_like(vecs)
    stores = []
    for number, ((b, name, first, rows, follow, parts), mine) in enumerate(zip(jobs, loads)):
        for copy, where, span, skip, to in mine:
            copy.wait()
            lines[pl.ds(16 + to - skip, span), :] = stage[pl.ds(where, span), :].astype(F32)
        full = (rows + 15) // 16 * 16
        for j in range(4):
            made[number, :rows, 128 * j : 128 * (j + 1)] = lines[pl.ds(16 + j, rows, stride=4), :].astype(BF16)
        if rows < LATENT:
            made[number, rows:, :] = jnp.zeros((LATENT - rows, LATENT), BF16)
        for i in range(follow):
            row = i if name == "w_in" else i + 1
            for j in range(4):
                p = 16 + 4 * (rows + i) + j
                vecs[b, row : row + 1, 128 * j : 128 * (j + 1)] = lines[p : p + 1, :]
        out = outs[index[b, name]]
        size = min(LATENT, out.shape[0] - first)
        store = pltpu.make_async_copy(made.at[number, pl.ds(0, size)], out.at[pl.ds(first, size)], osem.at[number])
        store.start()
        stores.append(store)
    for b in range(len(shapes)):
        store = pltpu.make_async_copy(vecs.at[b], outs[index[b, "vec"]], vsem.at[b])
        store.start()
        stores.append(store)
    for store in stores:
        store.wait()


def relay(shares, segments, share_rows):
    jobs = relay_plan(segments, share_rows)
    blocks = segments[-1][0] + 1
    shapes = [[] for _ in range(blocks)]
    for b, name, shape, _, _ in segments:
        if name in ("w_in", "w_out") and shape[1] == LATENT:
            shapes[b].append((name, (-(-shape[0] // 128) * 128, LATENT)))
    for s in shapes:
        s.append(("vec", (8, LATENT)))
    stage = sum(span for job in jobs for _, _, span, _, _ in job[5])
    out_shape = [shaped(*shape, dtype=F32 if name == "vec" else BF16) for s in shapes for name, shape in s]
    outs = pl.pallas_call(
        functools.partial(relay_kernel, jobs, shapes),
        out_shape=out_shape,
        in_specs=[ANY],
        out_specs=[ANY] * len(out_shape),
        scratch_shapes=[pltpu.VMEM((stage, 128), BF16), pltpu.VMEM((16 + 4 * LATENT + 64, 128), F32), pltpu.VMEM((len(jobs), LATENT, LATENT), BF16), pltpu.VMEM((blocks, 8, LATENT), F32), DMA((4 * len(jobs),)), DMA((len(jobs),)), DMA((blocks,))],
        compiler_params=params(),
        name="relay",
    )(shares)
    made = [{} for _ in shapes]
    for (b, name), value in zip([(b, name) for b, s in enumerate(shapes) for name, _ in s], outs):
        made[b][name] = value
    return made


def accumulate(dst, src, rows):
    step = 80
    whole = rows // step
    def body(i, carry):
        at = pl.ds(pl.multiple_of(i * step, 8), step)
        dst[at] = dst[at] + src[at]
        return carry
    lax.fori_loop(0, whole, body, 0)
    if rows % step:
        at = pl.ds(whole * step, rows % step)
        dst[at] = dst[at] + src[at]


def where_am_i():
    me = lax.axis_index("dev")
    return me, me // 8, lax.rem(me // 4, 2), lax.rem(me // 2, 2), lax.rem(me, 2)


def device_at(z, y, x, c):
    return ((z * 2 + y) * 2 + x) * 2 + c


def plane_scratch(units, rows):
    upper = rows // 16 * 8
    lower = rows - upper
    F = lambda *s: pltpu.VMEM((units,) + s + (128,), F32)
    refs = dict(pL=F(4, rows), pR=F(4, rows), pYA=F(2, upper), pXA=F(upper), pXB=F(2, lower), pYB=F(lower))
    sems = {}
    for name, count in (("c", 4), ("a1", 2), ("a2", 1), ("b1", 2), ("b2", 1)):
        sems["p" + name + "s"] = DMA((units, count))
        sems["p" + name + "r"] = DMA((units, count))
    return refs | sems | dict(pl=DMA((units, 4)))


class PlaneSum:
    def __init__(self, r, rows):
        self.r, self.rows = r, rows
        self.upper = rows // 16 * 8
        self.A, self.B = pl.ds(0, self.upper), pl.ds(self.upper, rows - self.upper)
        _, z, y, x, c = where_am_i()
        self.y, self.x, self.c = y, x, c
        self.tx, self.ty, self.tc = device_at(z, y, 1 - x, c), device_at(z, 1 - y, x, c), device_at(z, y, x, 1 - c)
        self.own = y * 2 + x
        self.sends = []

    def send(self, *args):
        copy = remote(*args)
        copy.start()
        self.sends.append(copy)

    def fetch(self, u, source):
        r = self.r
        self.example = source(0, 0)
        for i in range(4):
            self.send(source(i, 1 - self.c), r.pR.at[u, i], r.pcs.at[u, i], r.pcr.at[u, i], self.tc)
            pltpu.make_async_copy(source(i, self.c), r.pL.at[u, i], r.pl.at[u, i]).start()

    def pair(self, u):
        r, L = self.r, self.r.pL
        for i in range(4):
            pltpu.make_async_copy(self.example, L.at[u, i], r.pl.at[u, i]).wait()
            remote(L.at[u, i], r.pR.at[u, i], r.pcs.at[u, i], r.pcr.at[u, i], self.tc).wait_recv()
            accumulate(L.at[u, i], r.pR.at[u, i], self.rows)
        for j in range(2):
            self.send(L.at[u, (1 - self.y) * 2 + j, self.A], r.pYA.at[u, j], r.pa1s.at[u, j], r.pa1r.at[u, j], self.ty)
            self.send(L.at[u, j * 2 + 1 - self.x, self.B], r.pXB.at[u, j], r.pb1s.at[u, j], r.pb1r.at[u, j], self.tx)

    def middle(self, u):
        r, L = self.r, self.r.pL
        up, low = self.upper, self.rows - self.upper
        for j in range(2):
            remote(L.at[u, 0, self.A], r.pYA.at[u, j], r.pa1s.at[u, j], r.pa1r.at[u, j], self.ty).wait_recv()
            accumulate(L.at[u, self.y * 2 + j, self.A], r.pYA.at[u, j], up)
        self.send(L.at[u, self.y * 2 + 1 - self.x, self.A], r.pXA.at[u], r.pa2s.at[u, 0], r.pa2r.at[u, 0], self.tx)
        for j in range(2):
            remote(L.at[u, 0, self.B], r.pXB.at[u, j], r.pb1s.at[u, j], r.pb1r.at[u, j], self.tx).wait_recv()
            accumulate(L.at[u, j * 2 + self.x, self.B], r.pXB.at[u, j], low)
        self.send(L.at[u, (1 - self.y) * 2 + self.x, self.B], r.pYB.at[u], r.pb2s.at[u, 0], r.pb2r.at[u, 0], self.ty)

    def last(self, u):
        r, L = self.r, self.r.pL
        remote(L.at[u, 0, self.A], r.pXA.at[u], r.pa2s.at[u, 0], r.pa2r.at[u, 0], self.tx).wait_recv()
        accumulate(L.at[u, self.own, self.A], r.pXA.at[u], self.upper)
        remote(L.at[u, 0, self.B], r.pYB.at[u], r.pb2s.at[u, 0], r.pb2r.at[u, 0], self.ty).wait_recv()
        accumulate(L.at[u, self.own, self.B], r.pYB.at[u], self.rows - self.upper)

    def result(self, u):
        return self.r.pL.at[u, self.own]

    def finish(self):
        for copy in self.sends:
            copy.wait_send()


def reduce_kernel(n, chunks, share_rows, lead, bm, r):
    me, z, y, x, c = where_am_i()
    greet(n, me)
    rows = chunks.rows
    plane = PlaneSum(r, rows)
    def by_plane(*goals):
        return jnp.where(z == 0, goals[0], jnp.where(z == 1, goals[1], jnp.where(z == 2, goals[2], goals[3])))
    goal = [by_plane(2, 3, 3, 1), by_plane(1, 2, 0, 0), by_plane(3, 0, 1, 2), z]

    def fetch(u):
        if u < 4:
            plane.fetch(u, lambda i, core: r.flat0.at[goal[u] * 8 + i * 2 + core])

    def along(u):
        at = lax.rem(z - goal[u] + 4, 4) - 1
        return remote(plane.result(u), r.zq.at[at], r.zqs.at[u], r.zqr.at[at], device_at(goal[u], y, x, c))

    fetch(0)
    clear(r.d_in, r.d_out, r.d_vec)
    plane.pair(0)
    def body(g_node, x_rows):
        encode_back_rows(pl.program_id(0) * bm, bm, r.served, several(r, "landed"), g_node, x_rows, r.p_in, r.p_out, r.p_vec, r.d_in, r.d_out, r.d_vec)
    pltpu.emit_pipeline(body, grid=(r.g_node.shape[0] // bm,), in_specs=[rows_block(bm), pl.BlockSpec((VARS, bm), lambda i: (0, i))], out_specs=[])(r.g_node, r.x)
    encode_pack(r.packed, r.d_in, r.d_out, r.d_vec)
    stores = Stores({0: r.flat0}, chunks, r.fsem)
    stores.put(r.packed, 0)
    stores.wait()
    fetch(1)
    plane.middle(0)
    for u in (1, 2, 3):
        fetch(u + 1)
        plane.pair(u)
        plane.last(u - 1)
        along(u - 1).start()
        plane.middle(u)
    plane.last(3)
    first = lax.rem(lead + share_rows * me, 8)
    r.both[0:8, :] = jnp.zeros((8, 128), F32)
    width = r.err.shape[1] // 128
    for j in range(8):
        r.both[8 + j : 9 + j, :] = r.err[:, 128 * j : 128 * (j + 1)] if j < width else jnp.zeros((1, 128), F32)
    own = plane.result(3)

    def piece(at, count):
        rows_here = pl.ds(at, count)
        v = own[rows_here] + r.zq[0, rows_here] + (r.zq[1, rows_here] + r.zq[2, rows_here])
        r.out[rows_here] = v
        row = at + lax.broadcasted_iota(jnp.int32, v.shape, 0)
        v = jnp.where((row >= first) & (row < first + share_rows), v, 0.0)
        v = v * v
        r.both[0:8, :] += jnp.sum(v.reshape(count // 8, 8, 128), axis=0)

    for at in range(3):
        remote(own, r.zq.at[at], r.zqs.at[at], r.zqr.at[at], plane.tc).wait_recv()
    step = 80
    def several_tiles(i, carry):
        piece(pl.multiple_of(i * step, 8), step)
        return carry
    lax.fori_loop(0, rows // step, several_tiles, 0)
    if rows % step:
        piece(rows // step * step, rows % step)
    q_own = pltpu.make_async_copy(r.both, r.all.at[me], r.own)
    q_own.start()
    def go(j, carry):
        t = lax.rem(me + j, n)
        remote(r.both, r.all.at[me], r.qs.at[j], r.qr.at[j], t).start()
        return carry
    lax.fori_loop(1, n, go, 0)
    plane.finish()
    for u in range(3):
        along(u).wait_send()
    def end(j, carry):
        t = lax.rem(me + j, n)
        remote(r.both, r.all.at[me], r.qs.at[j], r.qr.at[j], t).wait()
        return carry
    lax.fori_loop(1, n, end, 0)
    q_own.wait()
    r.sums[...] = jnp.sum(r.all[...], axis=0)


def reduce_gradient(n, chunks, flat, errors, share_rows, lead, encoder, cid, bm=512):
    served, landed, g_node, x, block = encoder
    V = pl.BlockSpec(memory_space=pltpu.VMEM)
    F = lambda *s: pltpu.VMEM(s + (128,), F32)
    rows = chunks.rows
    inputs = dict(flat_in=(flat, ANY), err=(errors, V), served=(served, V), g_node=(g_node, ANY), x=(x, ANY))
    inputs |= numbered("landed", [(v, V) for v in landed])
    inputs |= {name: (v, V) for name, v in zip(("p_in", "p_out", "p_vec"), block)}
    outputs = dict(flat0=(shaped(*flat.shape), ANY), out=(shaped(rows, 128), V), sums=(shaped(16, 128), V))
    scratch = plane_scratch(4, rows) | dict(zq=F(3, rows), zqs=DMA((3,)), zqr=DMA((3,)))
    scratch |= dict(both=F(16), all=F(n, 16), own=DMA, qs=DMA((n,)), qr=DMA((n,)), packed=packed_rows(VARS, 4), fsem=DMA((STORES,)))
    scratch |= sums_scratch("d", block[0].shape[0])
    body = functools.partial(reduce_kernel, n, chunks, share_rows, lead, bm)
    made = named_call(body, "reduce_gradient", inputs, outputs, scratch, aliases=dict(flat_in="flat0"), cid=cid)
    return made.out, jnp.sum(made.sums[:8]), jnp.sum(made.sums[8:])


def make_parts(capacity):
    whole = capacity // 16 * 16
    rest = (capacity - whole + 3) // 4 * 4
    return [rows for rows in (whole, rest) if rows]


def make_asks(edge_owners, edge_local, devices, parts):
    owner = edge_owners.reshape(-1)
    local = edge_local.reshape(-1)
    wants = owner.shape[0]
    order = jnp.arange(wants, dtype=jnp.int32)
    before = (owner[:, None] == owner[None, :]) & (order[None, :] < order[:, None])
    ranking = jnp.sum(before.astype(jnp.int32), axis=1)
    capacity = sum(parts)
    slots = jnp.arange(devices * capacity, dtype=jnp.int32)
    place = owner * capacity + ranking
    asking = jnp.sum(jnp.where(slots[:, None] == place[None, :], local[None, :] + 1, 0), axis=1) - 1
    position = owner * parts[0] + ranking
    if len(parts) > 1:
        position = jnp.where(ranking < parts[0], position, devices * parts[0] + owner * parts[1] + ranking - parts[0])
    return (position, asking.reshape(devices, capacity))


def widen(values, width):
    return jnp.pad(values, ((0, 0), (0, width - values.shape[1])))


def make_block(params):
    rows = params["w_in"].shape[0]
    w_in = jnp.pad(params["w_in"], ((0, -rows % 128), (0, 0)))
    w_out = widen(params["w_out"], (params["w_out"].shape[1] + 127) // 128 * 128)
    names = [name for name in ("b_in", "b_out", "gain", "shift") if name in params]
    vectors = [widen(params[name][None], LATENT) for name in names]
    vectors.append(jnp.zeros((8 - len(vectors), LATENT), jnp.bfloat16))
    return (w_in, w_out, jnp.concatenate(vectors).astype(jnp.float32))


def relaid_blocks(shares, segments, share_rows):
    def rows_of(first, last):
        parts = []
        while first < last:
            owner, low = divmod(first, share_rows)
            size = min(last - first, share_rows - low)
            parts.append(shares[owner, low : low + size])
            first += size
        return jnp.concatenate(parts) if len(parts) > 1 else parts[0]
    made = relay(shares, segments, share_rows)
    [(shape, begin, size)] = [(s, o, e) for _, name, s, o, e in segments if name == "w_out" and s[1] != LATENT]
    wide = shape[1]
    first, end = begin // 128, (begin + size) // 128
    made[-1]["w_out"] = widen(rows_of(first, end).reshape(shape), (wide + 127) // 128 * 128)
    bias = rows_of(end, end + (wide + 127) // 128).reshape(-1)[:wide, None].astype(jnp.float32)
    return [(m["w_in"], m["w_out"], m["vec"]) for m in made], bias


def local(
    inputs,
    targets,
    geometry,
    land_sea,
    level_mask,
    edge_owners,
    edge_local,
    step_count,
    master,
    first_moment,
    second_moment,
    ema,
):
    segments, total = layout(LATENT, VARS, GEO, LAYERS)
    devices = lax.axis_size("dev")
    share = master.shape[0]
    mine = devices == 32 and share % 128 == 0
    ocean = (jnp.arange(VARS) < SEA_VARS).astype(jnp.float32)
    parts = make_parts(5 * edge_owners.shape[0] // (2 * devices))
    capacity = sum(parts)
    position, asking = make_asks(edge_owners, edge_local, devices, parts)
    counted = jnp.sum(level_mask * (1 - land_sea[:, None] * ocean.astype(jnp.int32)[None, :])).astype(jnp.float32)
    if mine:
        share_rows = share // 128
        pad_rows = (share_rows + 31) // 32 * 32
        low = jnp.pad(master.astype(jnp.bfloat16).reshape(share_rows, 128), ((0, pad_rows - share_rows), (0, 0)))
        ask = jnp.pad(asking.reshape(devices, 1, capacity), ((0, 0), (0, 0), (0, 128 - capacity)))
        number = jnp.zeros((8, 128), jnp.float32).at[0, 0].set(counted)
        gathered, served, numbers = gather_weights(low, ask, number, 1)
        blocks, bias = relaid_blocks(gathered, segments, share_rows)
        served = served[:, 0, :capacity]
        count = jnp.sum(numbers)
    else:
        full_weights = lax.all_gather(master.astype(jnp.bfloat16), "dev", axis=0, tiled=True)
        whole = unpack(full_weights, segments)
        blocks = [make_block(b) for b in whole]
        bias = whole[-1]["b_out"][:, None].astype(jnp.float32)
        served = lax.all_to_all(asking, "dev", 0, 0, tiled=True)
        count = lax.psum(counted, "dev")
    served = jnp.concatenate([served[:, sum(parts[:i]) : sum(parts[: i + 1])].reshape(-1) for i in range(len(parts))])
    want = served[:, None]
    served = served[None, :]
    pos = position.reshape(-1, 2)
    pos_s, pos_r = pos[:, 0][None, :], pos[:, 1][None, :]
    x = inputs.T
    geo = widen(geometry, 128)
    land = land_sea[None, :]
    routes = (want, served, pos, pos_s, pos_r)
    done = [edge_forward(devices, parts, 3, geo, routes, blocks[2], blocks[0], inputs.shape[0], x=x, geo_block=blocks[1])]
    for k in range(1, LAYERS):
        f = done[-1]
        done.append(
            edge_forward(
                devices, parts, 4, f.edge, routes, blocks[2 + 2 * k], blocks[1 + 2 * k], inputs.shape[0],
                landed=several(f, "landed"), node=f.node, slots=f.slots,
            )
        )
    pieces = [4 * s for s in (VARS + LATENT + 4, GEO + LATENT + 4) + (3 * LATENT + LATENT + 4, 2 * LATENT + LATENT + 4) * LAYERS]
    lead = 4
    places = [0] + [lead + sum(pieces[: i + 1]) for i in range(len(pieces))]
    flat_rows = (lead + PARAMS // 128 + 15) // 16 * 16 + 8
    if mine:
        begins = [(lead + share_rows * d) // 8 * 8 for d in range(devices)]
        chunks = Chunks(begins, (share_rows + 6 + 15) // 16 * 16, [0, 32])
    else:
        chunks = Chunks([0], flat_rows, [0, 1])
    dec_at = places[-1]
    tail_at = dec_at + 4 * LATENT
    k = LAYERS - 1
    flat, g_node, *outgoing, d_out, d_first, d_bias, errors = turn(
        served, want, several(done[k], "landed"), done[k].node, x, targets.T, level_mask.T, land, count.reshape(1, 1),
        blocks[3 + 2 * k], blocks[-1], bias, chunks, places[3 + 2 * k], dec_at,
    )
    flats = {len(chunks.cuts) - 2: flat}
    tail = jnp.concatenate([d_first[0], d_out[:, :VARS].reshape(-1), d_bias[:VARS, 0]])
    tail_rows = flat_rows - tail_at
    tail = jnp.pad(tail, (0, tail_rows * 128 - tail.shape[0])).reshape(tail_rows, 128)
    g_edge, landed = None, None
    for k in reversed(range(LAYERS)):
        more = {}
        if k == LAYERS - 1:
            more |= dict(outgoing=outgoing, g_node=g_node, tail=tail, tail_at=tail_at)
        else:
            more |= dict(
                node=(landed, g_slots, done[k].slots, done[k + 1].sums_s, g_node, done[k].low, done[k + 1].sums, blocks[3 + 2 * k]),
                node_at=places[3 + 2 * k],
            )
        if k == 0:
            more |= dict(geo=(geo, blocks[1]), geo_at=places[1])
        f = done[k]
        b = edge_backward(
            devices, parts, 5 + (LAYERS - 1 - k), (f.edge_low, f.sent, f.recv), routes, blocks[2 + 2 * k], chunks, flats, places[2 + 2 * k],
            g_edge=g_edge, **more,
        )
        g_edge, landed = b.edge_prev, several(b, "landed")
        g_slots = b.g_slots
        if k < LAYERS - 1:
            g_node = b.g_prev
    if mine:
        encoder = (served, landed, g_node, x, blocks[0])
        summed, squares, error_sum = reduce_gradient(devices, chunks, flats[0], errors, share_rows, lead, encoder, 2)
        skip = lax.rem(lead + share_rows * lax.axis_index("dev"), 8)
        own_grad = lax.dynamic_slice_in_dim(summed, skip, share_rows).reshape(-1)
    else:
        flat = encode_backward(served, landed, g_node, x, blocks[0], chunks, flats[0])
        own_grad = lax.psum_scatter(flat[0, lead : lead + PARAMS // 128].reshape(-1), "dev", scatter_dimension=0, tiled=True)
        error_sum, squares = lax.psum((jnp.sum(errors), jnp.sum(own_grad * own_grad)), "dev")
    grad_norm = jnp.sqrt(squares)
    loss = error_sum / jnp.maximum(count, 1.0)
    clipped = own_grad * jnp.minimum(1.0, clip_limit / grad_norm)
    step = step_count[0].astype(jnp.float32)
    new_first = beta_one * first_moment + (1.0 - beta_one) * clipped
    new_second = beta_two * second_moment + (1.0 - beta_two) * clipped * clipped
    first_hat = new_first / (1.0 - beta_one**step)
    second_hat = new_second / (1.0 - beta_two**step)
    new_master = master - learn_rate * (
        first_hat / (jnp.sqrt(second_hat) + adam_eps) + decay_rate * master
    )
    new_ema = ema_keep * ema + (1.0 - ema_keep) * new_master
    return (new_master, new_first, new_second, new_ema, loss, grad_norm)


def solution(mesh):
    in_specs = (
        P("dev", None),
        P("dev", None),
        P("dev", None),
        P("dev"),
        P("dev", None),
        P("dev", None),
        P("dev", None),
        P(),
        P("dev"),
        P("dev"),
        P("dev"),
        P("dev"),
    )
    out_specs = (P("dev"), P("dev"), P("dev"), P("dev"), P(), P())
    return jax.shard_map(local, mesh=mesh, in_specs=in_specs, out_specs=out_specs, check_vma=False)
```

```python
import functools
import types

import jax
import jax.numpy as jnp
import numpy as np
from jax import lax
from jax.experimental import pallas as pl
from jax.experimental.pallas import tpu as pltpu
from jax.sharding import PartitionSpec as P

LATENT = 512
VARS = 227
GEO = 4
SEA_VARS = 4
LAYERS = 3
PARAMS = 6545408


norm_eps = 1e-05
clip_limit = 0.01
beta_one = 0.9
beta_two = 0.999
adam_eps = 1e-08
learn_rate = 0.03
decay_rate = 0.1
ema_keep = 0.9


def layout(width, variables, geometry, layers):
    shapes = [(variables, width, True), (geometry, width, True)]
    for k in range(layers):
        shapes.append((3 * width, width, True))
        shapes.append((2 * width, width, True))
    shapes.append((width, variables, False))
    segments = []
    offset = 0
    for block_id, (fan_in, fan_out, normed) in enumerate(shapes):
        members = [
            ("w_in", (fan_in, width)),
            ("b_in", (width,)),
            ("w_out", (width, fan_out)),
            ("b_out", (fan_out,)),
        ]
        if normed:
            members = members + [("gain", (fan_out,)), ("shift", (fan_out,))]
        for part_name, part_shape in members:
            entries = int(np.prod(part_shape))
            segments.append((block_id, part_name, part_shape, offset, entries))
            offset += entries
    return (segments, offset)


def unpack(flat, segments):
    blocks = [dict() for k in range(segments[-1][0] + 1)]
    for block_id, part_name, part_shape, offset, entries in segments:
        blocks[block_id][part_name] = flat[offset : offset + entries].reshape(part_shape)
    return blocks


MESH = pl.DeviceIdType.MESH

def remote(src, dst, send, recv, target):
    return pltpu.make_async_remote_copy(src, dst, send, recv, device_id=(target,), device_id_type=MESH)

def greet(n, me):
    barrier = pltpu.get_barrier_semaphore()
    def hello(j, c):
        pl.semaphore_signal(barrier, inc=1, device_id=(lax.rem(me + j, n),), device_id_type=MESH)
        return c
    lax.fori_loop(1, n, hello, 0)
    pl.semaphore_wait(barrier, n - 1)


F32, BF16 = jnp.float32, jnp.bfloat16
VMEM_LIMIT = 60 << 20
ANY = pl.BlockSpec(memory_space=pl.ANY)
DMA = pltpu.SemaphoreType.DMA


def mm(a, b):
    return jnp.dot(a, b, preferred_element_type=F32)


def mm_nt(a, b):
    return lax.dot_general(a, b, (((1,), (1,)), ((), ())), preferred_element_type=F32)


def mm_tn(a, b):
    return lax.dot_general(a, b, (((0,), (0,)), ((), ())), preferred_element_type=F32)


def contract(a, b, left, right):
    return lax.dot_general(a, b, (((left,), (right,)), ((), ())), preferred_element_type=F32)


def col(v):
    return jnp.sum(v, axis=0, keepdims=True)


def pick(slots, first, rows):
    r = first + lax.broadcasted_iota(jnp.int32, (slots.shape[0], rows), 1)
    return jnp.where(slots == r, 1.0, 0.0).astype(BF16)


def place(slots, first, rows):
    r = first + lax.broadcasted_iota(jnp.int32, (rows, slots.shape[1]), 0)
    return jnp.where(slots == r, 1.0, 0.0).astype(BF16)


def first_half(us, w_in, vec):
    pre = vec[0:1, :]
    at = 0
    for u in us:
        pre = pre + mm(u, w_in[at : at + u.shape[1], :])
        at += u.shape[1]
    return pre


def activate(pre):
    sigma = jax.nn.sigmoid(pre)
    return sigma, (pre * sigma).astype(BF16)


def normalize(post):
    centred = post - jnp.mean(post, axis=-1, keepdims=True)
    inv = lax.rsqrt(jnp.mean(centred * centred, axis=-1, keepdims=True) + norm_eps)
    return centred * inv, inv


def second_half(act, w_out, vec):
    return normalize(mm(act, w_out[...]) + vec[1:2, :])


def scale_shift(hat, vec):
    return hat * vec[2:3, :] + vec[3:4, :]


def norm_back(g, hat, inv, vec, d_vec):
    if d_vec is not None:
        d_vec[2:3, :] += col(g * hat)
        d_vec[3:4, :] += col(g)
    s = g * vec[2:3, :]
    post = inv * (
        s - jnp.mean(s, axis=-1, keepdims=True) - hat * jnp.mean(s * hat, axis=-1, keepdims=True)
    )
    return post.astype(BF16)


def act_back(low, pre, sigma, w_out):
    g_act = mm_nt(low, w_out[...])
    return (g_act * sigma * (1.0 + pre * (1.0 - sigma))).astype(BF16)


def weight_sums(us, act, low, g_pre, d_in, d_out, d_vec):
    d_out[...] += mm_tn(act, low)
    d_vec[1:2, : low.shape[1]] += col(low.astype(F32))
    d_vec[0:1, :] += col(g_pre.astype(F32))
    at = 0
    for u in us:
        d_in[at : at + u.shape[1], :] += mm_tn(u, g_pre)
        at += u.shape[1]


def pack_matrix(packed, ref, rows, at):
    for j in range(4):
        packed[pl.ds(at + j, rows, stride=4), :] = ref[:rows, 128 * j : 128 * (j + 1)]
    return at + 4 * rows


def pack(packed, lead, rows_in, d_in, d_out, d_vec):
    def vector(i, at):
        for j in range(4):
            packed[at + j : at + j + 1, :] = d_vec[i : i + 1, 128 * j : 128 * (j + 1)]
        return at + 4
    at = pack_matrix(packed, d_in, rows_in, lead)
    at = vector(0, at)
    at = pack_matrix(packed, d_out, d_out.shape[0], at)
    for i in (1, 2, 3):
        at = vector(i, at)


def clear(*refs):
    for ref in refs:
        ref[...] = jnp.zeros_like(ref)


def spec(shape, fixed=True):
    if fixed:
        return pl.BlockSpec(shape, lambda i: (0,) * len(shape))
    return pl.BlockSpec(shape, lambda i: (i,) + (0,) * (len(shape) - 1))


def params(**more):
    return pltpu.CompilerParams(vmem_limit_bytes=VMEM_LIMIT, **more)


def shaped(*shape, dtype=F32):
    return jax.ShapeDtypeStruct(shape, dtype)


class Chunks:
    def __init__(self, begins, rows, cuts):
        self.begins, self.rows, self.cuts = begins, rows, cuts

    def shape(self, group):
        return (self.cuts[group + 1] - self.cuts[group], self.rows, 128)

    def pieces(self, at, size):
        found = []
        for group in range(len(self.cuts) - 1):
            for owner in range(self.cuts[group], self.cuts[group + 1]):
                begin = self.begins[owner]
                low, high = max(at, begin), min(at + size, begin + self.rows)
                if low < high:
                    found.append((group, owner - self.cuts[group], low - begin, low - at, high - low))
        return found

    def groups(self, *places):
        return sorted({p[0] for at, size in places for p in self.pieces(at, size)})


class Stores:
    def __init__(self, refs, chunks, sem):
        self.refs, self.chunks, self.sem, self.copies = refs, chunks, sem, []

    def put(self, packed, at):
        for group, owner, row, skip, size in self.chunks.pieces(at, packed.shape[0]):
            source = packed.at[pl.ds(skip, size)]
            copy = pltpu.make_async_copy(source, self.refs[group].at[owner, pl.ds(row, size)], self.sem.at[len(self.copies)])
            copy.start()
            self.copies.append(copy)

    def wait(self):
        for copy in self.copies:
            copy.wait()


STORES = 48


def flat_refs(r, groups):
    return {group: getattr(r, f"flat{group}") for group in groups}


def mlp_sums(rows_in, wide=LATENT):
    return [pltpu.VMEM((rows_in, LATENT), F32), pltpu.VMEM((LATENT, wide), F32), pltpu.VMEM((8, LATENT), F32)]


def packed_rows(rows_in, lead=0):
    return pltpu.VMEM((lead + 4 * rows_in + 4 * LATENT + 16, 128), F32)


def named_call(body, name, inputs, outputs, scratch, aliases=None, cid=None):
    names = [*inputs, *outputs, *scratch]
    aliases = {list(inputs).index(i): list(outputs).index(o) for i, o in (aliases or {}).items()}
    def kernel(*refs):
        body(types.SimpleNamespace(**dict(zip(names, refs))))
    more = {} if cid is None else dict(collective_id=cid, has_side_effects=True)
    values = pl.pallas_call(
        kernel,
        out_shape=tuple(shape for shape, _ in outputs.values()),
        in_specs=[s for _, s in inputs.values()],
        out_specs=tuple(s for _, s in outputs.values()),
        scratch_shapes=list(scratch.values()),
        input_output_aliases=aliases,
        compiler_params=params(**more),
        name=name,
    )(*[v for v, _ in inputs.values()])
    return types.SimpleNamespace(**dict(zip(outputs, values)))


def swap_start(n, me, srcs, dsts, own, ssem, rsem):
    for i, (src, dst) in enumerate(zip(srcs, dsts)):
        pltpu.make_async_copy(src.at[me], dst.at[me], own.at[i]).start()
    def go(j, c):
        t = lax.rem(me + j, n)
        for i, (src, dst) in enumerate(zip(srcs, dsts)):
            remote(src.at[t], dst.at[me], ssem.at[i, j], rsem.at[i, j], t).start()
        return c
    lax.fori_loop(1, n, go, 0)


def swap_wait(n, me, srcs, dsts, own, ssem, rsem):
    def end(j, c):
        t = lax.rem(me + j, n)
        for i, (src, dst) in enumerate(zip(srcs, dsts)):
            remote(src.at[t], dst.at[me], ssem.at[i, j], rsem.at[i, j], t).wait()
        return c
    lax.fori_loop(1, n, end, 0)
    for i, (src, dst) in enumerate(zip(srcs, dsts)):
        pltpu.make_async_copy(src.at[me], dst.at[me], own.at[i]).wait()


def several(r, name):
    return [getattr(r, f"{name}{i}") for i in range(4) if hasattr(r, f"{name}{i}")]


def numbered(name, values):
    return {f"{name}{i}": value for i, value in enumerate(values)}


def slot_rows(refs):
    rows = [ref[...].reshape(ref.shape[0] * ref.shape[1], ref.shape[2]) for ref in refs]
    return rows[0] if len(rows) == 1 else jnp.concatenate(rows, axis=0)


def put_slot_rows(refs, rows):
    at = 0
    for ref in refs:
        size = ref.shape[0] * ref.shape[1]
        ref[...] = rows[at : at + size, :].reshape(ref.shape)
        at += size


def greet_start(n, me):
    barrier = pltpu.get_barrier_semaphore()
    def hello(j, c):
        pl.semaphore_signal(barrier, inc=1, device_id=(lax.rem(me + j, n),), device_id_type=MESH)
        return c
    lax.fori_loop(1, n, hello, 0)


def greet_wait(n):
    pl.semaphore_wait(pltpu.get_barrier_semaphore(), n - 1)


class Loads:
    def __init__(self, r, sem):
        self.r, self.sem, self.copies = r, sem, {}

    def start(self, *names):
        for name in names:
            copy = pltpu.make_async_copy(getattr(self.r, name), getattr(self.r, "_" + name), self.sem.at[len(self.copies)])
            copy.start()
            self.copies[name] = copy

    def wait(self, *names):
        for name in names:
            self.copies[name].wait()


def store_all(r, sem, *names):
    copies = [pltpu.make_async_copy(getattr(r, "_" + name), getattr(r, name), sem.at[i]) for i, name in enumerate(names)]
    for copy in copies:
        copy.start()
    return copies


def same_rows(want, served):
    return jnp.where((want[...] == served[...]) & (want[...] >= 0), 1.0, 0.0).astype(BF16)


def swap_scratch(shapes, n):
    parts = len(shapes)
    scratch = dict(own=DMA((2, parts)), s1=DMA((parts, n)), r1=DMA((parts, n)), s2=DMA((parts, n)), r2=DMA((parts, n)))
    for name in ("away", "here", "back"):
        scratch |= numbered(name, [pltpu.VMEM(shape, BF16) for shape in shapes])
    return scratch


def held(prefix, block):
    return {prefix + part: pltpu.VMEM(a.shape, a.dtype) for part, a in zip(("_in", "_out", "_vec"), block)}


def weights(prefix, block):
    return {prefix + part: (a, ANY) for part, a in zip(("_in", "_out", "_vec"), block)}


def rows_block(bm, width=LATENT):
    return pl.BlockSpec((bm, width), lambda i: (i, 0))


def edge_kernel(n, first, bm, r):
    me = lax.axis_index("dev")
    greet_start(n, me)
    loads = Loads(r, r.lsem)
    node_weights = ["p_in", "p_out", "p_vec"]
    landing = [name for name in vars(r) if name.startswith("landed_in")]
    early = node_weights + ([] if first else [*landing, "slots_in"])
    late = ["e_in", "e_out", "e_vec"] + (["g_in", "g_out", "g_vec"] if first else [])
    loads.start(*early)
    loads.start(*late)
    loads.wait(*early)
    count = r.want.shape[0]
    if first:
        asked = contract(pick(r.want[...], 0, r.x.shape[1]), r.x[...], 1, 1).astype(BF16)
        pre = contract(asked, r._p_in[:VARS, :], 1, 0) + r._p_vec[0:1, :]
    else:
        landed = slot_rows(several(r, "_landed_in"))
        got = mm(same_rows(r.want, r.served), landed).astype(BF16)
        r._sums_s[...] = got
        old = r._slots_in[...]
        pre = first_half([old.astype(BF16), got], r._p_in, r._p_vec)
    _, act = activate(pre)
    hat, _ = second_half(act, r._p_out, r._p_vec)
    slots = scale_shift(hat, r._p_vec)
    if not first:
        slots = old + slots
    r._slots[...] = slots
    away, here, back, out = (several(r, name) for name in ("away", "here", "back", "landed"))
    put_slot_rows(away, slots.astype(BF16))
    greet_wait(n)
    swap_start(n, me, away, here, r.own.at[0], r.s1, r.r1)
    stores = store_all(r, r.ssem, *(["slots"] if first else ["slots", "sums_s"]))
    loads.wait(*late)
    if first:
        _, act = activate(first_half([r.source[...]], r._g_in, r._g_vec))
        hat, _ = second_half(act, r._g_out, r._g_vec)
        r._edge[...] = scale_shift(hat, r._g_vec)
    else:
        r._edge[...] = r.source[...]
    e = r._edge[...].astype(BF16)
    r.edge_low[...] = e
    r._pre[...] = first_half([e], r._e_in, r._e_vec)
    if first:
        def body(node, low):
            i = pl.program_id(0)
            u = r.x[:, pl.ds(pl.multiple_of(i * bm, bm), bm)]
            _, act = activate(contract(u, r._p_in[:VARS, :], 0, 0) + r._p_vec[0:1, :])
            hat, _ = second_half(act, r._p_out, r._p_vec)
            new = scale_shift(hat, r._p_vec)
            node[...] = new
            low[...] = new.astype(BF16)
        pltpu.emit_pipeline(body, grid=(r.node.shape[0] // bm,), in_specs=[], out_specs=[rows_block(bm)] * 2)(r.node, r.low)
    else:
        def body(node_in, node, low, sums):
            i = pl.program_id(0)
            got = mm(place(r.served[...], i * bm, bm), slot_rows(several(r, "_landed_in"))).astype(BF16)
            sums[...] = got
            old = node_in[...]
            _, act = activate(first_half([old.astype(BF16), got], r._p_in, r._p_vec))
            hat, _ = second_half(act, r._p_out, r._p_vec)
            new = old + scale_shift(hat, r._p_vec)
            node[...] = new
            low[...] = new.astype(BF16)
        pltpu.emit_pipeline(body, grid=(r.node.shape[0] // bm,), in_specs=[rows_block(bm)], out_specs=[rows_block(bm)] * 3)(r.node_in, r.node, r.low, r.sums)
    pick_s, pick_r = pick(r.pos[:, 0:1], 0, count), pick(r.pos[:, 1:2], 0, count)
    put_r = place(r.pos_r[...], 0, count)
    swap_wait(n, me, away, here, r.own.at[0], r.s1, r.r1)
    rows = slot_rows(here)
    s = mm(pick_s, rows).astype(BF16)
    v = mm(pick_r, rows).astype(BF16)
    pre = r._pre[...] + mm(s, r._e_in[LATENT : 2 * LATENT, :]) + mm(v, r._e_in[2 * LATENT :, :])
    _, act = activate(pre)
    hat, _ = second_half(act, r._e_out, r._e_vec)
    new = r._edge[...] + scale_shift(hat, r._e_vec)
    put_slot_rows(back, mm(put_r, new.astype(BF16)).astype(BF16))
    swap_start(n, me, back, out, r.own.at[1], r.s2, r.r2)
    r.edge[...] = new
    r.sent[...], r.recv[...] = s, v
    for store in stores:
        store.wait()
    swap_wait(n, me, back, out, r.own.at[1], r.s2, r.r2)


def edge_forward(n, parts, cid, source, routes, edge_block, node_block, rows, x=None, geo_block=None, landed=None, node=None, slots=None, bm=512):
    first = x is not None
    want, served, pos, pos_s, pos_r = routes
    count = want.shape[0]
    edges = source.shape[0]
    shapes = [(n, p, LATENT) for p in parts]
    V = pl.BlockSpec(memory_space=pltpu.VMEM)
    inputs = dict(source=(source, V), want=(want, V), served=(served, V), pos=(pos, V), pos_r=(pos_r, V))
    inputs |= weights("p", node_block) | weights("e", edge_block)
    scratch = held("_p", node_block) | held("_e", edge_block) | swap_scratch(shapes, n)
    scratch |= dict(_slots=pltpu.VMEM((count, LATENT), F32), _edge=pltpu.VMEM((edges, LATENT), F32), _pre=pltpu.VMEM((edges, LATENT), F32), lsem=DMA((12,)), ssem=DMA((2,)))
    low = lambda r: shaped(r, LATENT, dtype=BF16)
    outputs = dict(edge=(shaped(edges, LATENT), V), edge_low=(low(edges), V), sent=(low(edges), V), recv=(low(edges), V)) | numbered("landed", [(shaped(*s, dtype=BF16), ANY) for s in shapes])
    outputs |= dict(node=(shaped(rows, LATENT), ANY), low=(low(rows), ANY), slots=(shaped(count, LATENT), ANY))
    if first:
        inputs |= dict(x=(x, V)) | weights("g", geo_block)
        scratch |= held("_g", geo_block)
    else:
        inputs |= numbered("landed_in", [(v, ANY) for v in landed]) | dict(node_in=(node, ANY), slots_in=(slots, ANY))
        scratch |= numbered("_landed_in", [pltpu.VMEM(s, BF16) for s in shapes]) | dict(_slots_in=pltpu.VMEM((count, LATENT), F32), _sums_s=pltpu.VMEM((count, LATENT), BF16))
        outputs |= dict(sums=(low(rows), ANY), sums_s=(low(count), ANY))
    return named_call(functools.partial(edge_kernel, n, first, bm), "edge_forward", inputs, outputs, scratch, cid=cid)


def turn_kernel(parts, bm, chunks, group, at, dec_at, served, want, *refs):
    landed, refs = refs[:parts], refs[parts:]
    flat, g_prev, *outs = refs[13 : 15 + parts]
    node, x, target, level, land, count, w_in, w_out, vec, c_in, c_out, c_vec, c_bias = refs[:13]
    d_out_o, d_first_o, d_bias_o, err_o, packed, packed2, d_in, d_out, d_vec, e_in, e_out, e_vec, e_bias, err, acc, sem = refs[13 + 2 + parts:]
    i = pl.program_id(0)
    @pl.when(i == 0)
    def _():
        clear(d_in, d_out, d_vec, e_in, e_out, e_vec, e_bias, err, acc)
    got = mm(place(served[...], i * bm, bm), slot_rows(landed)).astype(BF16)
    old = node[...]
    low = old.astype(BF16)
    pre = first_half([low, got], w_in, vec)
    sigma, act = activate(pre)
    hat, inv = second_half(act, w_out, vec)
    u = (old + scale_shift(hat, vec)).astype(BF16)
    c_pre = first_half([u], c_in, c_vec)
    c_sigma, c_act = activate(c_pre)
    wide = c_out.shape[1]
    post = contract(c_out[...], c_act, 0, 1)
    sea = (lax.broadcasted_iota(jnp.int32, (VARS, 1), 0) < SEA_VARS).astype(F32)
    mask = level[...].astype(F32) * (1.0 - sea * land[...].astype(F32))
    residual = x[...].astype(F32) + (post[:VARS, :] + c_bias[...]) - target[...]
    divisor = jnp.maximum(count[...], 1.0)
    err[...] += jnp.sum(mask * residual * residual, axis=0, keepdims=True)
    g = 2.0 * mask * residual / divisor
    g_low = jnp.concatenate([g, jnp.zeros((wide - VARS, bm), F32)], axis=0).astype(BF16)
    e_bias[...] += jnp.sum(g_low.astype(F32), axis=1, keepdims=True)
    e_out[...] += contract(c_act, g_low, 0, 1)
    g_act = contract(g_low, c_out[...], 0, 1)
    c_g = (g_act * c_sigma * (1.0 + c_pre * (1.0 - c_sigma))).astype(BF16)
    e_vec[0:1, :] += col(c_g.astype(F32))
    e_in[...] += mm_tn(u, c_g)
    g_node = mm_nt(c_g, c_in[...])
    g_post = norm_back(g_node, hat, inv, vec, d_vec)
    g_pre = act_back(g_post, pre, sigma, w_out)
    weight_sums([low, got], act, g_post, g_pre, d_in, d_out, d_vec)
    g_prev[...] = g_node + mm_nt(g_pre, w_in[:LATENT, :])
    acc[...] += mm(pick(want[...], i * bm, bm), mm_nt(g_pre, w_in[LATENT:, :]).astype(BF16))
    @pl.when(i == pl.num_programs(0) - 1)
    def _():
        put_slot_rows(outs, acc[...].astype(BF16))
        d_out_o[...] = e_out[...]
        d_first_o[...] = e_vec[0:1, :]
        d_bias_o[...] = e_bias[...]
        err_o[...] = err[...]
        stores = Stores({group: flat}, chunks, sem)
        pack_matrix(packed2, e_in, LATENT, 0)
        stores.put(packed2, dec_at)
        pack(packed, 0, 2 * LATENT, d_in, d_out, d_vec)
        stores.put(packed, at)
        stores.wait()


def turn(served, want, landed, node, x, target, level, land, count, block, dec, bias, chunks, at, dec_at, bm=512):
    rows = node.shape[0]
    slots = want.shape[0]
    wide = dec[1].shape[1]
    [group] = chunks.groups((at, dec_at + 4 * LATENT - at))
    v = lambda height: pl.BlockSpec((height, bm), lambda i: (0, i))
    part = [spec(p.shape) for p in landed]
    return pl.pallas_call(
        functools.partial(turn_kernel, len(landed), bm, chunks, group, at, dec_at),
        grid=(rows // bm,),
        out_shape=(shaped(*chunks.shape(group)), shaped(rows, LATENT), *(shaped(*p.shape, dtype=BF16) for p in landed), shaped(LATENT, wide), shaped(1, LATENT), shaped(wide, 1), shaped(1, bm)),
        in_specs=[spec((1, slots)), spec((slots, 1)), *part, spec((bm, LATENT), False), v(VARS), v(VARS), v(VARS), v(1), spec((1, 1))] + [spec(a.shape) for a in (*block, *dec, bias)],
        out_specs=(ANY, spec((bm, LATENT), False), *part, spec((LATENT, wide)), spec((1, LATENT)), spec((wide, 1)), spec((1, bm))),
        scratch_shapes=[packed_rows(2 * LATENT), pltpu.VMEM((4 * LATENT, 128), F32)] + mlp_sums(2 * LATENT) + mlp_sums(LATENT, wide) + [pltpu.VMEM((wide, 1), F32), pltpu.VMEM((1, bm), F32), pltpu.VMEM((slots, LATENT), F32), DMA((STORES,))],
        compiler_params=params(),
        name="turn",
    )(served, want, *landed, node, x, target, level, land, count, *block, *dec, bias)


def gather_slots(r, bm):
    clear(r._g_slots)
    def body(g_node):
        chosen = pick(r.want[...], pl.program_id(0) * bm, bm)
        g = g_node[...]
        high = g.astype(BF16)
        rest = g - high.astype(F32)
        middle = rest.astype(BF16)
        small = (rest - middle.astype(F32)).astype(BF16)
        r._g_slots[...] += mm(chosen, high) + (mm(chosen, middle) + mm(chosen, small))
    pltpu.emit_pipeline(body, grid=(r.g_node.shape[0] // bm,), in_specs=[rows_block(bm)], out_specs=[])(r.g_node)


def edge_back_kernel(n, chunks, groups, at, node_at, geo_at, tail_at, bm, r):
    me = lax.axis_index("dev")
    greet_start(n, me)
    loads = Loads(r, r.lsem)
    nodes = node_at is not None
    landing = [name for name in vars(r) if name.startswith("landed_in")]
    early = ["p_in", "p_out", "p_vec", *landing, "g_slots_in", "slots_in", "sums_s"] if nodes else []
    late = ["e_in", "e_out", "e_vec"] + (["g_in", "g_out", "g_vec"] if geo_at is not None else [])
    loads.start(*early)
    loads.start(*late)
    flats = Stores(flat_refs(r, groups), chunks, r.fsem)
    stores = [flats]
    if tail_at is not None:
        flats.put(r.tail, tail_at)
    count = r.want.shape[0]
    here, back, out = (several(r, name) for name in ("here", "back", "landed"))
    if nodes:
        loads.wait(*early)
        us = [r._slots_in[...].astype(BF16), r._sums_s[...]]
        pre = first_half(us, r._p_in, r._p_vec)
        sigma, act = activate(pre)
        hat, inv = second_half(act, r._p_out, r._p_vec)
        g = r._g_slots_in[...] + mm(same_rows(r.want, r.served), slot_rows(several(r, "_landed_in")))
        low = norm_back(g, hat, inv, r._p_vec, None)
        g_pre = act_back(low, pre, sigma, r._p_out)
        source = several(r, "away")
        put_slot_rows(source, mm_nt(g_pre, r._p_in[LATENT:, :]).astype(BF16))
    else:
        source = several(r, "outgoing")
    greet_wait(n)
    swap_start(n, me, source, here, r.own.at[0], r.s1, r.r1)
    if nodes:
        r._g_slots[...] = g + mm_nt(g_pre, r._p_in[:LATENT, :])
        stores += store_all(r, r.ssem, "g_slots")
        clear(r.n_in, r.n_out, r.n_vec)
    clear(r.d_in, r.d_out, r.d_vec)
    def node_rows(first, last):
        if not nodes:
            return
        def body(g_node, low_in, sums_in, g_prev):
            i = first + pl.program_id(0)
            us = [low_in[...], sums_in[...]]
            pre = first_half(us, r._p_in, r._p_vec)
            sigma, act = activate(pre)
            hat, inv = second_half(act, r._p_out, r._p_vec)
            g = g_node[...] + mm(place(r.served[...], i * bm, bm), slot_rows(several(r, "_landed_in")))
            low = norm_back(g, hat, inv, r._p_vec, r.n_vec)
            g_pre = act_back(low, pre, sigma, r._p_out)
            weight_sums(us, act, low, g_pre, r.n_in, r.n_out, r.n_vec)
            g_prev[...] = g + mm_nt(g_pre, r._p_in[:LATENT, :])
        block = pl.BlockSpec((bm, LATENT), lambda i: (first + i, 0))
        pltpu.emit_pipeline(body, grid=(last - first,), in_specs=[block] * 3, out_specs=[block])(r.g_node, r.low, r.sums, r.g_prev)
    blocks = r.g_node.shape[0] // bm if nodes else 0
    node_rows(0, blocks // 2)
    if not nodes:
        gather_slots(r, bm)
    loads.wait(*late)
    us = [r.edge_low[...], r.sent[...], r.recv[...]]
    pre = first_half(us, r._e_in, r._e_vec)
    sigma, act = activate(pre)
    hat, inv = second_half(act, r._e_out, r._e_vec)
    pick_r = pick(r.pos[:, 1:2], 0, count)
    put_s, put_r = place(r.pos_s[...], 0, count), place(r.pos_r[...], 0, count)
    swap_wait(n, me, source, here, r.own.at[0], r.s1, r.r1)
    g = mm(pick_r, slot_rows(here))
    if hasattr(r, "g_edge"):
        g = r.g_edge[...] + g
    low = norm_back(g, hat, inv, r._e_vec, r.d_vec)
    g_pre = act_back(low, pre, sigma, r._e_out)
    s = mm_nt(g_pre, r._e_in[LATENT : 2 * LATENT, :]).astype(BF16)
    v = mm_nt(g_pre, r._e_in[2 * LATENT :, :]).astype(BF16)
    put_slot_rows(back, (mm(put_s, s) + mm(put_r, v)).astype(BF16))
    swap_start(n, me, back, out, r.own.at[1], r.s2, r.r2)
    prev = g + mm_nt(g_pre, r._e_in[:LATENT, :])
    r.edge_prev[...] = prev
    weight_sums(us, act, low, g_pre, r.d_in, r.d_out, r.d_vec)
    pack(r.packed, 0, 3 * LATENT, r.d_in, r.d_out, r.d_vec)
    flats.put(r.packed, at)
    if geo_at is not None:
        c_us = [r.geo[...]]
        c_pre = first_half(c_us, r._g_in, r._g_vec)
        c_sigma, c_act = activate(c_pre)
        c_hat, c_inv = second_half(c_act, r._g_out, r._g_vec)
        clear(r.c_in, r.c_out, r.c_vec)
        c_low = norm_back(prev, c_hat, c_inv, r._g_vec, r.c_vec)
        c_g = act_back(c_low, c_pre, c_sigma, r._g_out)
        weight_sums(c_us, c_act, c_low, c_g, r.c_in, r.c_out, r.c_vec)
        pack(r.c_packed, 0, GEO, r.c_in, r.c_out, r.c_vec)
        flats.put(r.c_packed, geo_at)
    node_rows(blocks // 2, blocks)
    if nodes:
        pack(r.n_packed, 0, 2 * LATENT, r.n_in, r.n_out, r.n_vec)
        flats.put(r.n_packed, node_at)
    if not nodes:
        stores += store_all(r, r.ssem, "g_slots")
    swap_wait(n, me, back, out, r.own.at[1], r.s2, r.r2)
    for store in stores:
        store.wait()


def sums_scratch(prefix, rows_in):
    return dict(zip((prefix + "_in", prefix + "_out", prefix + "_vec"), mlp_sums(rows_in)))


def edge_backward(n, parts, cid, ins, routes, edge_block, chunks, flats, at, g_edge=None, outgoing=None, g_node=None, tail=None, tail_at=None, node=None, node_at=None, geo=None, geo_at=None, bm=512):
    want, served, pos, pos_s, pos_r = routes
    count = want.shape[0]
    edges = pos.shape[0]
    shapes = [(n, p, LATENT) for p in parts]
    V = pl.BlockSpec(memory_space=pltpu.VMEM)
    inputs = dict(want=(want, V), served=(served, V), pos=(pos, V), pos_s=(pos_s, V), pos_r=(pos_r, V))
    inputs |= {name: (value, V) for name, value in zip(("edge_low", "sent", "recv"), ins)} | weights("e", edge_block)
    scratch = held("_e", edge_block) | swap_scratch(shapes, n) | sums_scratch("d", 3 * LATENT)
    scratch |= dict(packed=packed_rows(3 * LATENT), lsem=DMA((16,)), ssem=DMA((2,)), fsem=DMA((STORES,)))
    outputs = dict(edge_prev=(shaped(edges, LATENT), V)) | numbered("landed", [(shaped(*s, dtype=BF16), ANY) for s in shapes])
    places = [(at, scratch["packed"].shape[0])]
    if g_edge is not None:
        inputs |= dict(g_edge=(g_edge, V))
    if outgoing is not None:
        inputs |= numbered("outgoing", [(v, ANY) for v in outgoing]) | dict(g_node=(g_node, ANY))
        outputs |= dict(g_slots=(shaped(count, LATENT), ANY))
        scratch |= dict(_g_slots=pltpu.VMEM((count, LATENT), F32))
    if tail is not None:
        inputs |= dict(tail=(tail, V))
        places.append((tail_at, tail.shape[0]))
    if node is not None:
        inputs |= numbered("landed_in", [(v, ANY) for v in node[0]])
        for name, value in zip(("g_slots_in", "slots_in", "sums_s", "g_node", "low", "sums"), node[1:]):
            inputs[name] = (value, ANY)
        inputs |= weights("p", node[7])
        scratch |= held("_p", node[7]) | sums_scratch("n", 2 * LATENT)
        f = pltpu.VMEM((count, LATENT), F32)
        scratch |= numbered("_landed_in", [pltpu.VMEM(s, BF16) for s in shapes]) | dict(n_packed=packed_rows(2 * LATENT), _g_slots_in=f, _slots_in=f, _g_slots=f, _sums_s=pltpu.VMEM((count, LATENT), BF16))
        rows = node[4].shape[0]
        places.append((node_at, scratch["n_packed"].shape[0]))
        outputs |= dict(g_prev=(shaped(rows, LATENT), ANY), g_slots=(shaped(count, LATENT), ANY))
    if geo is not None:
        inputs |= dict(geo=(geo[0], V)) | weights("g", geo[1])
        scratch |= held("_g", geo[1]) | sums_scratch("c", geo[0].shape[1]) | dict(c_packed=packed_rows(GEO))
        places.append((geo_at, scratch["c_packed"].shape[0]))
    groups = chunks.groups(*places)
    aliases = {}
    for group in groups:
        outputs[f"flat{group}"] = (shaped(*chunks.shape(group)), ANY)
        if group in flats:
            inputs[f"flat{group}_in"] = (flats[group], ANY)
            aliases[f"flat{group}_in"] = f"flat{group}"
    body = functools.partial(edge_back_kernel, n, chunks, groups, at, node_at, geo_at, tail_at, bm)
    made = named_call(body, "edge_backward", inputs, outputs, scratch, aliases=aliases, cid=cid)
    flats.update(flat_refs(made, groups))
    return made


def encode_back_rows(first, bm, served, landed, g_node, x, w_in, w_out, vec, d_in, d_out, d_vec):
    pre = contract(x[...], w_in[:VARS, :], 0, 0) + vec[0:1, :]
    sigma, act = activate(pre)
    hat, inv = second_half(act, w_out, vec)
    g = g_node[...] + mm(place(served[...], first, bm), slot_rows(landed))
    g_post = norm_back(g, hat, inv, vec, d_vec)
    g_pre = act_back(g_post, pre, sigma, w_out)
    weight_sums([], act, g_post, g_pre, d_in, d_out, d_vec)
    d_in[:VARS, :] += mm(x[...], g_pre)


def encode_pack(packed, d_in, d_out, d_vec):
    packed[0:4, :] = jnp.zeros((4, 128), F32)
    pack(packed, 4, VARS, d_in, d_out, d_vec)


def encode_back_kernel(parts, bm, chunks, served, *refs):
    landed, refs = refs[:parts], refs[parts:]
    g_node, x, w_in, w_out, vec, flat_in, flat, packed, d_in, d_out, d_vec, sem = refs
    i = pl.program_id(0)
    @pl.when(i == 0)
    def _():
        clear(d_in, d_out, d_vec)
    encode_back_rows(i * bm, bm, served, landed, g_node, x, w_in, w_out, vec, d_in, d_out, d_vec)
    @pl.when(i == pl.num_programs(0) - 1)
    def _():
        encode_pack(packed, d_in, d_out, d_vec)
        stores = Stores({0: flat}, chunks, sem)
        stores.put(packed, 0)
        stores.wait()


def encode_backward(served, landed, g_node, x, block, chunks, flat, bm=512):
    k, rows = block[0].shape[0], x.shape[1]
    slots = served.shape[1]
    return pl.pallas_call(
        functools.partial(encode_back_kernel, len(landed), bm, chunks),
        grid=(rows // bm,),
        out_shape=shaped(*flat.shape),
        in_specs=[spec((1, slots)), *(spec(p.shape) for p in landed), spec((bm, LATENT), False), pl.BlockSpec((VARS, bm), lambda i: (0, i))] + [spec(a.shape) for a in block] + [ANY],
        out_specs=ANY,
        scratch_shapes=[packed_rows(VARS, 4)] + mlp_sums(k) + [DMA((STORES,))],
        input_output_aliases={6 + len(landed): 0},
        compiler_params=params(),
        name="encode_backward",
    )(served, *landed, g_node, x, *block, flat)


def relay_plan(segments, share_rows):
    jobs = []
    for block_id, part_name, part_shape, offset, entries in segments:
        if part_name not in ("w_in", "w_out") or part_shape[1] != LATENT:
            continue
        for first in range(0, part_shape[0], LATENT):
            rows = min(LATENT, part_shape[0] - first)
            follow = 0
            if first + rows == part_shape[0]:
                follow = 1 if part_name == "w_in" else 3
            begin = offset // 128 + 4 * first
            end = begin + 4 * (rows + follow)
            parts = []
            at = begin
            while at < end:
                owner, low = divmod(at, share_rows)
                size = min(end - at, share_rows - low)
                base = low // 16 * 16
                span = (low + size - base + 15) // 16 * 16
                parts.append((owner, base, span, low - base, at - begin))
                at += size
            jobs.append((block_id, part_name, first, rows, follow, parts))
    return jobs


class Relay:
    def __init__(self, r, shares):
        self.r, self.shares, self.loads, self.at, self.count = r, shares, {}, 0, 0

    def load(self, job):
        r, mine = self.r, []
        for owner, base, span, skip, to in job[5]:
            place = pl.ds(self.at, span)
            copy = pltpu.make_async_copy(self.shares.at[owner, pl.ds(base, span)], r.stage.at[place], r.isem.at[self.count])
            copy.start()
            mine.append((copy, place, span, skip, to))
            self.at += span
            self.count += 1
        self.loads[job[:3]] = mine

    def run(self, job, target, vec):
        _, name, _, rows, follow, _ = job
        lines = self.r.lines
        for copy, place, span, skip, to in self.loads[job[:3]]:
            copy.wait()
            lines[pl.ds(16 + to - skip, span), :] = self.r.stage[place, :].astype(F32)
        for j in range(4):
            target[:rows, 128 * j : 128 * (j + 1)] = lines[pl.ds(16 + j, rows, stride=4), :].astype(BF16)
        if rows < target.shape[0]:
            target[rows:, :] = jnp.zeros((target.shape[0] - rows, LATENT), BF16)
        for i in range(follow):
            row = i if name == "w_in" else i + 1
            for j in range(4):
                p = 16 + 4 * (rows + i) + j
                vec[row : row + 1, 128 * j : 128 * (j + 1)] = lines[p : p + 1, :]


class Gather:
    def __init__(self, r, w, o):
        self.r, self.w, self.o = r, w, o
        self.me, z, y, x, c = where_am_i()
        self.z = z
        half = w.shape[0] // 2
        self.A, self.B = pl.ds(0, half), pl.ds(half, half)
        self.dev = lambda zz, fy=0, fx=0: device_at(zz, y + fy * (1 - 2 * y), x + fx * (1 - 2 * x), c)
        self.tx, self.ty, self.tc = self.dev(z, 0, 1), self.dev(z, 1, 0), device_at(z, y, x, 1 - c)
        self.up, self.down = self.dev(jnp.minimum(z + 1, 3)), self.dev(jnp.maximum(z - 1, 0))
        def by_plane(*v):
            return jnp.where(z == 0, v[0], jnp.where(z == 1, v[1], jnp.where(z == 2, v[2], v[3])))
        self.come = [z, by_plane(1, 0, 1, 2), by_plane(2, 2, 3, 1), by_plane(3, 3, 0, 0)]
        self.go = [z, by_plane(1, 0, 1, 2), by_plane(2, 2, 0, 0), by_plane(3, 3, 3, 1)]
        self.sends, self.sibling, self.seen = [], [], 0

    def send(self, *args):
        copy = remote(*args)
        copy.start()
        self.sends.append(copy)

    def share(self, k, part=None):
        ref = self.w if k == 0 else self.o.at[self.dev(self.go[k])]
        return ref if part is None else ref.at[part]

    def to_sibling(self, slot, part=None, source=None):
        r, i = self.r, len(self.sibling)
        ref = self.o.at[slot] if part is None else self.o.at[slot, part]
        self.send(ref if source is None else source, ref, r.bs.at[i], r.br.at[i], self.tc)
        self.sibling.append(part)

    def from_sibling(self, count):
        r = self.r
        for i in range(self.seen, count):
            part = self.sibling[i]
            ref = self.o.at[self.me] if part is None else self.o.at[self.me, part]
            remote(ref, ref, r.bs.at[i], r.br.at[i], self.tc).wait_recv()
        self.seen = count

    def onward(self, i, wait=False):
        r, z, plane = self.r, self.z, self.come[i]
        slot = self.dev(plane)
        source = self.w if i == 0 else self.o.at[slot]
        for d, target, here in ((0, self.up, (plane <= z) & (z < 3)), (1, self.down, (plane >= z) & (z > 0))):
            @pl.when(here)
            def _():
                copy = remote(source, self.o.at[slot], r.zs.at[d, i], r.zr.at[plane], target)
                if wait:
                    copy.wait_send()
                else:
                    copy.start()

    def begin(self):
        r = self.r
        self.mine = pltpu.make_async_copy(self.w, self.o.at[self.me], r.gown.at[0])
        self.mine.start()
        self.spread(0)
        self.onward(0)
        self.to_sibling(self.me, None, self.w)

    def arrive(self, i):
        slot = self.dev(self.come[i])
        remote(self.w, self.o.at[slot], self.r.zs.at[0, i], self.r.zr.at[self.come[i]], self.tc).wait_recv()
        self.onward(i)
        self.to_sibling(slot)

    def spread(self, k):
        r, slot = self.r, self.dev(self.go[k])
        self.send(self.share(k, self.A), self.o.at[slot, self.A], r.hs.at[k, 0], r.hr.at[k, 0], self.tx)
        self.send(self.share(k, self.B), self.o.at[slot, self.B], r.hs.at[k, 1], r.hr.at[k, 1], self.ty)

    def second(self, k):
        r, o, zz = self.r, self.o, self.go[k]
        s, sx, sy = self.dev(zz), self.dev(zz, 0, 1), self.dev(zz, 1, 0)
        self.send(self.share(k, self.A), o.at[s, self.A], r.cs.at[k, 0], r.cr.at[k, 0], self.ty)
        self.send(self.share(k, self.B), o.at[s, self.B], r.ds.at[k, 0], r.dr.at[k, 0], self.tx)
        remote(o.at[sx, self.A], o.at[sx, self.A], r.hs.at[k, 0], r.hr.at[k, 0], self.tx).wait_recv()
        self.send(o.at[sx, self.A], o.at[sx, self.A], r.cs.at[k, 1], r.cr.at[k, 1], self.ty)
        remote(o.at[sy, self.B], o.at[sy, self.B], r.hs.at[k, 1], r.hr.at[k, 1], self.ty).wait_recv()
        self.send(o.at[sy, self.B], o.at[sy, self.B], r.ds.at[k, 1], r.dr.at[k, 1], self.tx)
        self.to_sibling(sx, self.A)
        self.to_sibling(sy, self.B)

    def third(self, k):
        r, o, zz = self.r, self.o, self.go[k]
        for slot, part, ss, rr, i, target in (
            (self.dev(zz, 1, 0), self.A, r.cs, r.cr, 0, self.ty),
            (self.dev(zz, 0, 1), self.B, r.ds, r.dr, 0, self.tx),
            (self.dev(zz, 1, 1), self.A, r.cs, r.cr, 1, self.ty),
            (self.dev(zz, 1, 1), self.B, r.ds, r.dr, 1, self.tx),
        ):
            remote(o.at[slot, part], o.at[slot, part], ss.at[k, i], rr.at[k, i], target).wait_recv()
            self.to_sibling(slot, part)

    def finish(self):
        for i in range(4):
            self.onward(i, True)
        for copy in self.sends:
            copy.wait_send()


def start_kernel(n, jobs, bm, r):
    me = lax.axis_index("dev")
    gather = Gather(r, r.w, r.shares)
    greet(n, me)
    gather.begin()
    asks, asked = several(r, "ask"), several(r, "asked")
    swap_start(n, me, asks, asked, r.aown, r.a1, r.b1)
    number = pltpu.make_async_copy(r.number, r.numbers.at[me], r.gown.at[1])
    number.start()
    def go(j, carry):
        t = lax.rem(me + j, n)
        remote(r.number, r.numbers.at[me], r.ns.at[j], r.nr.at[j], t).start()
        return carry
    lax.fori_loop(1, n, go, 0)
    gather.second(0)
    gather.arrive(1)
    gather.spread(1)
    gather.third(0)
    gather.second(1)
    gather.arrive(2)
    gather.arrive(3)
    gather.spread(2)
    gather.third(1)
    gather.second(2)
    swap_wait(n, me, asks, asked, r.aown, r.a1, r.b1)
    columns = slot_rows(asked)
    r.want[...] = columns[:, 0:1]
    r.served[...] = jnp.transpose(columns)[0:1, :]
    chosen = pick(r.want[...], 0, r.x.shape[1])
    rows = contract(chosen, r.x[...], 1, 1).astype(BF16)
    gather.spread(3)
    gather.third(2)
    plane_0 = len(gather.sibling)
    gather.second(3)
    gather.from_sibling(plane_0)
    gather.mine.wait()
    relay = Relay(r, r.shares)
    block = [[job for job in jobs if job[0] == b] for b in range(jobs[-1][0] + 1)]
    names = ["p", "g", "e"]
    def into(b):
        for job in block[b]:
            target = getattr(r, "_" + names[b] + job[1][1:])
            relay.run(job, target.at[pl.ds(job[2], min(LATENT, target.shape[0] - job[2]))], getattr(r, "_" + names[b] + "_vec"))
    for vec in (r._p_vec, r._g_vec, r._e_vec, r.vecs):
        vec[...] = jnp.zeros_like(vec)
    for job in block[0]:
        relay.load(job)
    into(0)
    for job in block[1]:
        relay.load(job)
    _, act = activate(contract(rows, r._p_in[:VARS, :], 1, 0) + r._p_vec[0:1, :])
    hat, _ = second_half(act, r._p_out, r._p_vec)
    r._slots[...] = scale_shift(hat, r._p_vec)
    away, here, back, out = (several(r, name) for name in ("away", "here", "back", "landed"))
    put_slot_rows(away, r._slots[...].astype(BF16))
    swap_start(n, me, away, here, r.own.at[0], r.s1, r.r1)
    stores = store_all(r, r.ssem, "slots")
    def body(node, low):
        i = pl.program_id(0)
        u = r.x[:, pl.ds(pl.multiple_of(i * bm, bm), bm)]
        _, act = activate(contract(u, r._p_in[:VARS, :], 0, 0) + r._p_vec[0:1, :])
        hat, _ = second_half(act, r._p_out, r._p_vec)
        new = scale_shift(hat, r._p_vec)
        node[...] = new
        low[...] = new.astype(BF16)
    pltpu.emit_pipeline(body, grid=(r.node.shape[0] // bm,), in_specs=[], out_specs=[rows_block(bm)] * 2)(r.node, r.low)
    gather.third(3)
    gather.from_sibling(len(gather.sibling))
    for b in range(2, len(block)):
        for job in block[b]:
            relay.load(job)
    into(1)
    into(2)
    _, act = activate(first_half([r.source[...]], r._g_in, r._g_vec))
    hat, _ = second_half(act, r._g_out, r._g_vec)
    r._edge[...] = scale_shift(hat, r._g_vec)
    e = r._edge[...].astype(BF16)
    r.edge_low[...] = e
    count = r.want.shape[0]
    pre = first_half([e], r._e_in, r._e_vec)
    pick_s, pick_r = pick(r.pos[:, 0:1], 0, count), pick(r.pos[:, 1:2], 0, count)
    put_r = place(r.pos_r[...], 0, count)
    kept = [f"m{b}{part}" for b in range(3) for part in ("_in", "_out", "_vec")]
    for i, name in enumerate(kept):
        b, part = int(name[1]), name[2:]
        copy = pltpu.make_async_copy(getattr(r, "_" + names[b] + part), getattr(r, name), r.osem.at[i])
        copy.start()
        stores.append(copy)
    swap_wait(n, me, away, here, r.own.at[0], r.s1, r.r1)
    rows = slot_rows(here)
    s = mm(pick_s, rows).astype(BF16)
    v = mm(pick_r, rows).astype(BF16)
    pre = pre + mm(s, r._e_in[LATENT : 2 * LATENT, :]) + mm(v, r._e_in[2 * LATENT :, :])
    _, act = activate(pre)
    hat, _ = second_half(act, r._e_out, r._e_vec)
    new = r._edge[...] + scale_shift(hat, r._e_vec)
    put_slot_rows(back, mm(put_r, new.astype(BF16)).astype(BF16))
    swap_start(n, me, back, out, r.own.at[1], r.s2, r.r2)
    r.edge[...] = new
    r.sent[...], r.recv[...] = s, v
    at = len(kept)
    late = [job for b in range(3, len(block)) for job in block[b]]
    for i, job in enumerate(late):
        b, name, first = job[:3]
        relay.run(job, r.made.at[i], r.vecs.at[b])
        copy = pltpu.make_async_copy(r.made.at[i], getattr(r, f"m{b}{name[1:]}").at[pl.ds(first, LATENT)], r.osem.at[at + i])
        copy.start()
        stores.append(copy)
    at += len(late)
    for b in range(3, len(block)):
        copy = pltpu.make_async_copy(r.vecs.at[b], getattr(r, f"m{b}_vec"), r.osem.at[at + b])
        copy.start()
        stores.append(copy)
    gather.finish()
    def end(j, carry):
        t = lax.rem(me + j, n)
        remote(r.number, r.numbers.at[me], r.ns.at[j], r.nr.at[j], t).wait()
        return carry
    lax.fori_loop(1, n, end, 0)
    number.wait()
    for store in stores:
        store.wait()
    swap_wait(n, me, back, out, r.own.at[1], r.s2, r.r2)


def start(n, parts, cid, w, number, asks, source, pos, pos_r, x, segments, share_rows, bm=512):
    jobs = relay_plan(segments, share_rows)
    blocks = segments[-1][0] + 1
    count, edges, rows = n * sum(parts), source.shape[0], x.shape[1]
    V = pl.BlockSpec(memory_space=pltpu.VMEM)
    tables = [(n, p, 128) for p in parts]
    shapes = [(n, p, LATENT) for p in parts]
    inputs = dict(w=(w, ANY), number=(number, V), source=(source, V), pos=(pos, V), pos_r=(pos_r, V), x=(x, V)) | numbered("ask", [(a, V) for a in asks])
    low = lambda r: shaped(r, LATENT, dtype=BF16)
    outputs = dict(shares=(shaped(n, *w.shape, dtype=BF16), ANY), numbers=(shaped(n, *number.shape), ANY))
    outputs |= dict(want=(shaped(count, 1, dtype=jnp.int32), V), served=(shaped(1, count, dtype=jnp.int32), V))
    outputs |= dict(edge=(shaped(edges, LATENT), V), edge_low=(low(edges), V), sent=(low(edges), V), recv=(low(edges), V))
    outputs |= numbered("landed", [(shaped(*s, dtype=BF16), ANY) for s in shapes])
    outputs |= dict(node=(shaped(rows, LATENT), ANY), low=(low(rows), ANY), slots=(shaped(count, LATENT), ANY))
    made = {}
    for b, name, shape, _, _ in segments:
        if name in ("w_in", "w_out") and shape[1] == LATENT:
            made[f"m{b}{name[1:]}"] = (-(-shape[0] // 128) * 128, LATENT)
    outputs |= {name: (shaped(*shape, dtype=BF16), ANY) for name, shape in made.items()}
    outputs |= {f"m{b}_vec": (shaped(8, LATENT), ANY) for b in range(blocks)}
    scratch = swap_scratch(shapes, n) | numbered("asked", [pltpu.VMEM(s, jnp.int32) for s in tables])
    scratch |= dict(aown=DMA((len(parts),)), a1=DMA((len(parts), n)), b1=DMA((len(parts), n)), ns=DMA((n,)), nr=DMA((n,)), gown=DMA((2,)))
    for b, name in enumerate(("_p", "_g", "_e")):
        scratch |= {name + "_in": pltpu.VMEM(made[f"m{b}_in"], BF16), name + "_out": pltpu.VMEM(made[f"m{b}_out"], BF16), name + "_vec": pltpu.VMEM((8, LATENT), F32)}
    stage = sum(part[2] for job in jobs for part in job[5])
    late = sum(1 for job in jobs if job[0] > 2)
    scratch |= dict(_slots=pltpu.VMEM((count, LATENT), F32), _edge=pltpu.VMEM((edges, LATENT), F32), ssem=DMA((1,)))
    scratch |= dict(stage=pltpu.VMEM((stage, 128), BF16), lines=pltpu.VMEM((16 + 4 * LATENT + 64, 128), F32), made=pltpu.VMEM((late, LATENT, LATENT), BF16))
    scratch |= dict(vecs=pltpu.VMEM((blocks, 8, LATENT), F32), isem=DMA((sum(len(job[5]) for job in jobs),)), osem=DMA((9 + late + blocks,)))
    scratch |= dict(zs=DMA((2, 4)), zr=DMA((4,)), bs=DMA((28,)), br=DMA((28,)))
    for name in ("h", "c", "d"):
        scratch |= {name + "s": DMA((4, 2)), name + "r": DMA((4, 2))}
    return named_call(functools.partial(start_kernel, n, jobs, bm), "start", inputs, outputs, scratch, cid=cid)


def accumulate(dst, src, rows):
    step = 80
    whole = rows // step
    def body(i, carry):
        at = pl.ds(pl.multiple_of(i * step, 8), step)
        dst[at] = dst[at] + src[at]
        return carry
    lax.fori_loop(0, whole, body, 0)
    if rows % step:
        at = pl.ds(whole * step, rows % step)
        dst[at] = dst[at] + src[at]


def where_am_i():
    me = lax.axis_index("dev")
    return me, me // 8, lax.rem(me // 4, 2), lax.rem(me // 2, 2), lax.rem(me, 2)


def device_at(z, y, x, c):
    return ((z * 2 + y) * 2 + x) * 2 + c


def plane_scratch(units, rows):
    upper = rows // 16 * 8
    lower = rows - upper
    F = lambda *s: pltpu.VMEM((units,) + s + (128,), F32)
    refs = dict(pL=F(4, rows), pR=F(4, rows), pYA=F(2, upper), pXA=F(upper), pXB=F(2, lower), pYB=F(lower))
    sems = {}
    for name, count in (("c", 4), ("a1", 2), ("a2", 1), ("b1", 2), ("b2", 1)):
        sems["p" + name + "s"] = DMA((units, count))
        sems["p" + name + "r"] = DMA((units, count))
    return refs | sems | dict(pl=DMA((units, 4)))


class PlaneSum:
    def __init__(self, r, rows):
        self.r, self.rows = r, rows
        self.upper = rows // 16 * 8
        self.A, self.B = pl.ds(0, self.upper), pl.ds(self.upper, rows - self.upper)
        _, z, y, x, c = where_am_i()
        self.y, self.x, self.c = y, x, c
        self.tx, self.ty, self.tc = device_at(z, y, 1 - x, c), device_at(z, 1 - y, x, c), device_at(z, y, x, 1 - c)
        self.own = y * 2 + x
        self.sends = []

    def send(self, *args):
        copy = remote(*args)
        copy.start()
        self.sends.append(copy)

    def fetch(self, u, source):
        r = self.r
        self.example = source(0, 0)
        for i in range(4):
            self.send(source(i, 1 - self.c), r.pR.at[u, i], r.pcs.at[u, i], r.pcr.at[u, i], self.tc)
            pltpu.make_async_copy(source(i, self.c), r.pL.at[u, i], r.pl.at[u, i]).start()

    def pair(self, u):
        r, L = self.r, self.r.pL
        for i in range(4):
            pltpu.make_async_copy(self.example, L.at[u, i], r.pl.at[u, i]).wait()
            remote(L.at[u, i], r.pR.at[u, i], r.pcs.at[u, i], r.pcr.at[u, i], self.tc).wait_recv()
            accumulate(L.at[u, i], r.pR.at[u, i], self.rows)
        for j in range(2):
            self.send(L.at[u, (1 - self.y) * 2 + j, self.A], r.pYA.at[u, j], r.pa1s.at[u, j], r.pa1r.at[u, j], self.ty)
            self.send(L.at[u, j * 2 + 1 - self.x, self.B], r.pXB.at[u, j], r.pb1s.at[u, j], r.pb1r.at[u, j], self.tx)

    def middle(self, u):
        r, L = self.r, self.r.pL
        up, low = self.upper, self.rows - self.upper
        for j in range(2):
            remote(L.at[u, 0, self.A], r.pYA.at[u, j], r.pa1s.at[u, j], r.pa1r.at[u, j], self.ty).wait_recv()
            accumulate(L.at[u, self.y * 2 + j, self.A], r.pYA.at[u, j], up)
        self.send(L.at[u, self.y * 2 + 1 - self.x, self.A], r.pXA.at[u], r.pa2s.at[u, 0], r.pa2r.at[u, 0], self.tx)
        for j in range(2):
            remote(L.at[u, 0, self.B], r.pXB.at[u, j], r.pb1s.at[u, j], r.pb1r.at[u, j], self.tx).wait_recv()
            accumulate(L.at[u, j * 2 + self.x, self.B], r.pXB.at[u, j], low)
        self.send(L.at[u, (1 - self.y) * 2 + self.x, self.B], r.pYB.at[u], r.pb2s.at[u, 0], r.pb2r.at[u, 0], self.ty)

    def last(self, u):
        r, L = self.r, self.r.pL
        remote(L.at[u, 0, self.A], r.pXA.at[u], r.pa2s.at[u, 0], r.pa2r.at[u, 0], self.tx).wait_recv()
        accumulate(L.at[u, self.own, self.A], r.pXA.at[u], self.upper)
        remote(L.at[u, 0, self.B], r.pYB.at[u], r.pb2s.at[u, 0], r.pb2r.at[u, 0], self.ty).wait_recv()
        accumulate(L.at[u, self.own, self.B], r.pYB.at[u], self.rows - self.upper)

    def result(self, u):
        return self.r.pL.at[u, self.own]

    def finish(self):
        for copy in self.sends:
            copy.wait_send()


def reduce_kernel(n, chunks, share_rows, lead, bm, r):
    me, z, y, x, c = where_am_i()
    greet(n, me)
    rows = chunks.rows
    plane = PlaneSum(r, rows)
    def by_plane(*goals):
        return jnp.where(z == 0, goals[0], jnp.where(z == 1, goals[1], jnp.where(z == 2, goals[2], goals[3])))
    goal = [by_plane(2, 3, 3, 1), by_plane(1, 2, 0, 0), by_plane(3, 0, 1, 2), z]

    def fetch(u):
        if u < 4:
            plane.fetch(u, lambda i, core: r.flat0.at[goal[u] * 8 + i * 2 + core])

    def along(u):
        at = lax.rem(z - goal[u] + 4, 4) - 1
        return remote(plane.result(u), r.zq.at[at], r.zqs.at[u], r.zqr.at[at], device_at(goal[u], y, x, c))

    fetch(0)
    clear(r.d_in, r.d_out, r.d_vec)
    plane.pair(0)
    def body(g_node, x_rows):
        encode_back_rows(pl.program_id(0) * bm, bm, r.served, several(r, "landed"), g_node, x_rows, r.p_in, r.p_out, r.p_vec, r.d_in, r.d_out, r.d_vec)
    pltpu.emit_pipeline(body, grid=(r.g_node.shape[0] // bm,), in_specs=[rows_block(bm), pl.BlockSpec((VARS, bm), lambda i: (0, i))], out_specs=[])(r.g_node, r.x)
    encode_pack(r.packed, r.d_in, r.d_out, r.d_vec)
    stores = Stores({0: r.flat0}, chunks, r.fsem)
    stores.put(r.packed, 0)
    stores.wait()
    fetch(1)
    plane.middle(0)
    for u in (1, 2, 3):
        fetch(u + 1)
        plane.pair(u)
        plane.last(u - 1)
        along(u - 1).start()
        plane.middle(u)
    plane.last(3)
    first = lax.rem(lead + share_rows * me, 8)
    r.both[0:8, :] = jnp.zeros((8, 128), F32)
    width = r.err.shape[1] // 128
    for j in range(8):
        r.both[8 + j : 9 + j, :] = r.err[:, 128 * j : 128 * (j + 1)] if j < width else jnp.zeros((1, 128), F32)
    own = plane.result(3)

    def piece(at, count):
        rows_here = pl.ds(at, count)
        v = own[rows_here] + r.zq[0, rows_here] + (r.zq[1, rows_here] + r.zq[2, rows_here])
        r.out[rows_here] = v
        row = at + lax.broadcasted_iota(jnp.int32, v.shape, 0)
        v = jnp.where((row >= first) & (row < first + share_rows), v, 0.0)
        v = v * v
        r.both[0:8, :] += jnp.sum(v.reshape(count // 8, 8, 128), axis=0)

    for at in range(3):
        remote(own, r.zq.at[at], r.zqs.at[at], r.zqr.at[at], plane.tc).wait_recv()
    step = 80
    def several_tiles(i, carry):
        piece(pl.multiple_of(i * step, 8), step)
        return carry
    lax.fori_loop(0, rows // step, several_tiles, 0)
    if rows % step:
        piece(rows // step * step, rows % step)
    q_own = pltpu.make_async_copy(r.both, r.all.at[me], r.own)
    q_own.start()
    def go(j, carry):
        t = lax.rem(me + j, n)
        remote(r.both, r.all.at[me], r.qs.at[j], r.qr.at[j], t).start()
        return carry
    lax.fori_loop(1, n, go, 0)
    plane.finish()
    for u in range(3):
        along(u).wait_send()
    def end(j, carry):
        t = lax.rem(me + j, n)
        remote(r.both, r.all.at[me], r.qs.at[j], r.qr.at[j], t).wait()
        return carry
    lax.fori_loop(1, n, end, 0)
    q_own.wait()
    r.sums[...] = jnp.sum(r.all[...], axis=0)


def reduce_gradient(n, chunks, flat, errors, share_rows, lead, encoder, cid, bm=512):
    served, landed, g_node, x, block = encoder
    V = pl.BlockSpec(memory_space=pltpu.VMEM)
    F = lambda *s: pltpu.VMEM(s + (128,), F32)
    rows = chunks.rows
    inputs = dict(flat_in=(flat, ANY), err=(errors, V), served=(served, V), g_node=(g_node, ANY), x=(x, ANY))
    inputs |= numbered("landed", [(v, V) for v in landed])
    inputs |= {name: (v, V) for name, v in zip(("p_in", "p_out", "p_vec"), block)}
    outputs = dict(flat0=(shaped(*flat.shape), ANY), out=(shaped(rows, 128), V), sums=(shaped(16, 128), V))
    scratch = plane_scratch(4, rows) | dict(zq=F(3, rows), zqs=DMA((3,)), zqr=DMA((3,)))
    scratch |= dict(both=F(16), all=F(n, 16), own=DMA, qs=DMA((n,)), qr=DMA((n,)), packed=packed_rows(VARS, 4), fsem=DMA((STORES,)))
    scratch |= sums_scratch("d", block[0].shape[0])
    body = functools.partial(reduce_kernel, n, chunks, share_rows, lead, bm)
    made = named_call(body, "reduce_gradient", inputs, outputs, scratch, aliases=dict(flat_in="flat0"), cid=cid)
    return made.out, jnp.sum(made.sums[:8]), jnp.sum(made.sums[8:])


def make_parts(capacity):
    whole = capacity // 16 * 16
    rest = (capacity - whole + 3) // 4 * 4
    return [rows for rows in (whole, rest) if rows]


def make_asks(edge_owners, edge_local, devices, parts):
    owner = edge_owners.reshape(-1)
    local = edge_local.reshape(-1)
    wants = owner.shape[0]
    order = jnp.arange(wants, dtype=jnp.int32)
    before = (owner[:, None] == owner[None, :]) & (order[None, :] < order[:, None])
    ranking = jnp.sum(before.astype(jnp.int32), axis=1)
    capacity = sum(parts)
    slots = jnp.arange(devices * capacity, dtype=jnp.int32)
    place = owner * capacity + ranking
    asking = jnp.sum(jnp.where(slots[:, None] == place[None, :], local[None, :] + 1, 0), axis=1) - 1
    position = owner * parts[0] + ranking
    if len(parts) > 1:
        position = jnp.where(ranking < parts[0], position, devices * parts[0] + owner * parts[1] + ranking - parts[0])
    return (position, asking.reshape(devices, capacity))


def widen(values, width):
    return jnp.pad(values, ((0, 0), (0, width - values.shape[1])))


def make_block(params):
    rows = params["w_in"].shape[0]
    w_in = jnp.pad(params["w_in"], ((0, -rows % 128), (0, 0)))
    w_out = widen(params["w_out"], (params["w_out"].shape[1] + 127) // 128 * 128)
    names = [name for name in ("b_in", "b_out", "gain", "shift") if name in params]
    vectors = [widen(params[name][None], LATENT) for name in names]
    vectors.append(jnp.zeros((8 - len(vectors), LATENT), jnp.bfloat16))
    return (w_in, w_out, jnp.concatenate(vectors).astype(jnp.float32))


def relaid_blocks(made, segments, share_rows):
    shares = made.shares
    def rows_of(first, last):
        parts = []
        while first < last:
            owner, low = divmod(first, share_rows)
            size = min(last - first, share_rows - low)
            parts.append(shares[owner, low : low + size])
            first += size
        return jnp.concatenate(parts) if len(parts) > 1 else parts[0]
    [(shape, begin, size)] = [(s, o, e) for _, name, s, o, e in segments if name == "w_out" and s[1] != LATENT]
    wide = shape[1]
    first, end = begin // 128, (begin + size) // 128
    w_out = widen(rows_of(first, end).reshape(shape), (wide + 127) // 128 * 128)
    bias = rows_of(end, end + (wide + 127) // 128).reshape(-1)[:wide, None].astype(jnp.float32)
    blocks = []
    for b in range(segments[-1][0] + 1):
        get = lambda part: getattr(made, f"m{b}{part}", w_out)
        blocks.append((get("_in"), get("_out"), get("_vec")))
    return blocks, bias


def local(
    inputs,
    targets,
    geometry,
    land_sea,
    level_mask,
    edge_owners,
    edge_local,
    step_count,
    master,
    first_moment,
    second_moment,
    ema,
):
    segments, total = layout(LATENT, VARS, GEO, LAYERS)
    devices = lax.axis_size("dev")
    share = master.shape[0]
    mine = devices == 32 and share % 128 == 0
    ocean = (jnp.arange(VARS) < SEA_VARS).astype(jnp.float32)
    parts = make_parts(5 * edge_owners.shape[0] // (2 * devices))
    capacity = sum(parts)
    position, asking = make_asks(edge_owners, edge_local, devices, parts)
    counted = jnp.sum(level_mask * (1 - land_sea[:, None] * ocean.astype(jnp.int32)[None, :])).astype(jnp.float32)
    pos = position.reshape(-1, 2)
    pos_s, pos_r = pos[:, 0][None, :], pos[:, 1][None, :]
    x = inputs.T
    geo = widen(geometry, 128)
    if mine:
        share_rows = share // 128
        pad_rows = (share_rows + 31) // 32 * 32
        low = jnp.pad(master.astype(jnp.bfloat16).reshape(share_rows, 128), ((0, pad_rows - share_rows), (0, 0)))
        number = jnp.zeros((8, 128), jnp.float32).at[0, 0].set(counted)
        cuts = [sum(parts[:i]) for i in range(len(parts) + 1)]
        asks = [jnp.broadcast_to(asking[:, a:b, None], (devices, b - a, 128)) for a, b in zip(cuts, cuts[1:])]
        begun = start(devices, parts, 1, low, number, asks, geo, pos, pos_r, x, segments, share_rows)
        blocks, bias = relaid_blocks(begun, segments, share_rows)
        want, served = begun.want, begun.served
        count = jnp.sum(begun.numbers)
    else:
        full_weights = lax.all_gather(master.astype(jnp.bfloat16), "dev", axis=0, tiled=True)
        whole = unpack(full_weights, segments)
        blocks = [make_block(b) for b in whole]
        bias = whole[-1]["b_out"][:, None].astype(jnp.float32)
        served = lax.all_to_all(asking, "dev", 0, 0, tiled=True)
        count = lax.psum(counted, "dev")
        served = jnp.concatenate([served[:, sum(parts[:i]) : sum(parts[: i + 1])].reshape(-1) for i in range(len(parts))])
        want = served[:, None]
        served = served[None, :]
    land = land_sea[None, :]
    routes = (want, served, pos, pos_s, pos_r)
    if mine:
        done = [begun]
    else:
        done = [edge_forward(devices, parts, 3, geo, routes, blocks[2], blocks[0], inputs.shape[0], x=x, geo_block=blocks[1])]
    for k in range(1, LAYERS):
        f = done[-1]
        done.append(
            edge_forward(
                devices, parts, 4, f.edge, routes, blocks[2 + 2 * k], blocks[1 + 2 * k], inputs.shape[0],
                landed=several(f, "landed"), node=f.node, slots=f.slots,
            )
        )
    pieces = [4 * s for s in (VARS + LATENT + 4, GEO + LATENT + 4) + (3 * LATENT + LATENT + 4, 2 * LATENT + LATENT + 4) * LAYERS]
    lead = 4
    places = [0] + [lead + sum(pieces[: i + 1]) for i in range(len(pieces))]
    flat_rows = (lead + PARAMS // 128 + 15) // 16 * 16 + 8
    if mine:
        begins = [(lead + share_rows * d) // 8 * 8 for d in range(devices)]
        chunks = Chunks(begins, (share_rows + 6 + 15) // 16 * 16, [0, 32])
    else:
        chunks = Chunks([0], flat_rows, [0, 1])
    dec_at = places[-1]
    tail_at = dec_at + 4 * LATENT
    k = LAYERS - 1
    flat, g_node, *outgoing, d_out, d_first, d_bias, errors = turn(
        served, want, several(done[k], "landed"), done[k].node, x, targets.T, level_mask.T, land, count.reshape(1, 1),
        blocks[3 + 2 * k], blocks[-1], bias, chunks, places[3 + 2 * k], dec_at,
    )
    flats = {len(chunks.cuts) - 2: flat}
    tail = jnp.concatenate([d_first[0], d_out[:, :VARS].reshape(-1), d_bias[:VARS, 0]])
    tail_rows = flat_rows - tail_at
    tail = jnp.pad(tail, (0, tail_rows * 128 - tail.shape[0])).reshape(tail_rows, 128)
    g_edge, landed = None, None
    for k in reversed(range(LAYERS)):
        more = {}
        if k == LAYERS - 1:
            more |= dict(outgoing=outgoing, g_node=g_node, tail=tail, tail_at=tail_at)
        else:
            more |= dict(
                node=(landed, g_slots, done[k].slots, done[k + 1].sums_s, g_node, done[k].low, done[k + 1].sums, blocks[3 + 2 * k]),
                node_at=places[3 + 2 * k],
            )
        if k == 0:
            more |= dict(geo=(geo, blocks[1]), geo_at=places[1])
        f = done[k]
        b = edge_backward(
            devices, parts, 5 + (LAYERS - 1 - k), (f.edge_low, f.sent, f.recv), routes, blocks[2 + 2 * k], chunks, flats, places[2 + 2 * k],
            g_edge=g_edge, **more,
        )
        g_edge, landed = b.edge_prev, several(b, "landed")
        g_slots = b.g_slots
        if k < LAYERS - 1:
            g_node = b.g_prev
    if mine:
        encoder = (served, landed, g_node, x, blocks[0])
        summed, squares, error_sum = reduce_gradient(devices, chunks, flats[0], errors, share_rows, lead, encoder, 2)
        skip = lax.rem(lead + share_rows * lax.axis_index("dev"), 8)
        own_grad = lax.dynamic_slice_in_dim(summed, skip, share_rows).reshape(-1)
    else:
        flat = encode_backward(served, landed, g_node, x, blocks[0], chunks, flats[0])
        own_grad = lax.psum_scatter(flat[0, lead : lead + PARAMS // 128].reshape(-1), "dev", scatter_dimension=0, tiled=True)
        error_sum, squares = lax.psum((jnp.sum(errors), jnp.sum(own_grad * own_grad)), "dev")
    grad_norm = jnp.sqrt(squares)
    loss = error_sum / jnp.maximum(count, 1.0)
    clipped = own_grad * jnp.minimum(1.0, clip_limit / grad_norm)
    step = step_count[0].astype(jnp.float32)
    new_first = beta_one * first_moment + (1.0 - beta_one) * clipped
    new_second = beta_two * second_moment + (1.0 - beta_two) * clipped * clipped
    first_hat = new_first / (1.0 - beta_one**step)
    second_hat = new_second / (1.0 - beta_two**step)
    new_master = master - learn_rate * (
        first_hat / (jnp.sqrt(second_hat) + adam_eps) + decay_rate * master
    )
    new_ema = ema_keep * ema + (1.0 - ema_keep) * new_master
    return (new_master, new_first, new_second, new_ema, loss, grad_norm)


def solution(mesh):
    in_specs = (
        P("dev", None),
        P("dev", None),
        P("dev", None),
        P("dev"),
        P("dev", None),
        P("dev", None),
        P("dev", None),
        P(),
        P("dev"),
        P("dev"),
        P("dev"),
        P("dev"),
    )
    out_specs = (P("dev"), P("dev"), P("dev"), P("dev"), P(), P())
    return jax.shard_map(local, mesh=mesh, in_specs=in_specs, out_specs=out_specs, check_vma=False)
```

```python
import functools
import types

import jax
import jax.numpy as jnp
import numpy as np
from jax import lax
from jax.experimental import pallas as pl
from jax.experimental.pallas import tpu as pltpu
from jax.sharding import PartitionSpec as P

LATENT = 512
VARS = 227
GEO = 4
SEA_VARS = 4
LAYERS = 3
PARAMS = 6545408


norm_eps = 1e-05
clip_limit = 0.01
beta_one = 0.9
beta_two = 0.999
adam_eps = 1e-08
learn_rate = 0.03
decay_rate = 0.1
ema_keep = 0.9


def layout(width, variables, geometry, layers):
    shapes = [(variables, width, True), (geometry, width, True)]
    for k in range(layers):
        shapes.append((3 * width, width, True))
        shapes.append((2 * width, width, True))
    shapes.append((width, variables, False))
    segments = []
    offset = 0
    for block_id, (fan_in, fan_out, normed) in enumerate(shapes):
        members = [
            ("w_in", (fan_in, width)),
            ("b_in", (width,)),
            ("w_out", (width, fan_out)),
            ("b_out", (fan_out,)),
        ]
        if normed:
            members = members + [("gain", (fan_out,)), ("shift", (fan_out,))]
        for part_name, part_shape in members:
            entries = int(np.prod(part_shape))
            segments.append((block_id, part_name, part_shape, offset, entries))
            offset += entries
    return (segments, offset)


def unpack(flat, segments):
    blocks = [dict() for k in range(segments[-1][0] + 1)]
    for block_id, part_name, part_shape, offset, entries in segments:
        blocks[block_id][part_name] = flat[offset : offset + entries].reshape(part_shape)
    return blocks


MESH = pl.DeviceIdType.MESH

def remote(src, dst, send, recv, target):
    return pltpu.make_async_remote_copy(src, dst, send, recv, device_id=(target,), device_id_type=MESH)

def greet(n, me):
    barrier = pltpu.get_barrier_semaphore()
    def hello(j, c):
        pl.semaphore_signal(barrier, inc=1, device_id=(lax.rem(me + j, n),), device_id_type=MESH)
        return c
    lax.fori_loop(1, n, hello, 0)
    pl.semaphore_wait(barrier, n - 1)


F32, BF16 = jnp.float32, jnp.bfloat16
VMEM_LIMIT = 60 << 20
ANY = pl.BlockSpec(memory_space=pl.ANY)
DMA = pltpu.SemaphoreType.DMA


def mm(a, b):
    return jnp.dot(a, b, preferred_element_type=F32)


def mm_nt(a, b):
    return lax.dot_general(a, b, (((1,), (1,)), ((), ())), preferred_element_type=F32)


def mm_tn(a, b):
    return lax.dot_general(a, b, (((0,), (0,)), ((), ())), preferred_element_type=F32)


def contract(a, b, left, right):
    return lax.dot_general(a, b, (((left,), (right,)), ((), ())), preferred_element_type=F32)


def col(v):
    return jnp.sum(v, axis=0, keepdims=True)


def pick(slots, first, rows):
    r = first + lax.broadcasted_iota(jnp.int32, (slots.shape[0], rows), 1)
    return jnp.where(slots == r, 1.0, 0.0).astype(BF16)


def place(slots, first, rows):
    r = first + lax.broadcasted_iota(jnp.int32, (rows, slots.shape[1]), 0)
    return jnp.where(slots == r, 1.0, 0.0).astype(BF16)


def first_half(us, w_in, vec):
    pre = vec[0:1, :]
    at = 0
    for u in us:
        pre = pre + mm(u, w_in[at : at + u.shape[1], :])
        at += u.shape[1]
    return pre


def activate(pre):
    sigma = jax.nn.sigmoid(pre)
    return sigma, (pre * sigma).astype(BF16)


def normalize(post):
    centred = post - jnp.mean(post, axis=-1, keepdims=True)
    inv = lax.rsqrt(jnp.mean(centred * centred, axis=-1, keepdims=True) + norm_eps)
    return centred * inv, inv


def second_half(act, w_out, vec):
    return normalize(mm(act, w_out[...]) + vec[1:2, :])


def scale_shift(hat, vec):
    return hat * vec[2:3, :] + vec[3:4, :]


def norm_back(g, hat, inv, vec, d_vec):
    if d_vec is not None:
        d_vec[2:3, :] += col(g * hat)
        d_vec[3:4, :] += col(g)
    s = g * vec[2:3, :]
    post = inv * (
        s - jnp.mean(s, axis=-1, keepdims=True) - hat * jnp.mean(s * hat, axis=-1, keepdims=True)
    )
    return post.astype(BF16)


def act_back(low, pre, sigma, w_out):
    g_act = mm_nt(low, w_out[...])
    return (g_act * sigma * (1.0 + pre * (1.0 - sigma))).astype(BF16)


def weight_sums(us, act, low, g_pre, d_in, d_out, d_vec):
    d_out[...] += mm_tn(act, low)
    d_vec[1:2, : low.shape[1]] += col(low.astype(F32))
    d_vec[0:1, :] += col(g_pre.astype(F32))
    at = 0
    for u in us:
        d_in[at : at + u.shape[1], :] += mm_tn(u, g_pre)
        at += u.shape[1]


def pack_matrix(packed, ref, rows, at):
    for j in range(4):
        packed[pl.ds(at + j, rows, stride=4), :] = ref[:rows, 128 * j : 128 * (j + 1)]
    return at + 4 * rows


def pack(packed, lead, rows_in, d_in, d_out, d_vec):
    def vector(i, at):
        for j in range(4):
            packed[at + j : at + j + 1, :] = d_vec[i : i + 1, 128 * j : 128 * (j + 1)]
        return at + 4
    at = pack_matrix(packed, d_in, rows_in, lead)
    at = vector(0, at)
    at = pack_matrix(packed, d_out, d_out.shape[0], at)
    for i in (1, 2, 3):
        at = vector(i, at)


def clear(*refs):
    for ref in refs:
        ref[...] = jnp.zeros_like(ref)


def spec(shape, fixed=True):
    if fixed:
        return pl.BlockSpec(shape, lambda i: (0,) * len(shape))
    return pl.BlockSpec(shape, lambda i: (i,) + (0,) * (len(shape) - 1))


def params(**more):
    return pltpu.CompilerParams(vmem_limit_bytes=VMEM_LIMIT, **more)


def shaped(*shape, dtype=F32):
    return jax.ShapeDtypeStruct(shape, dtype)


class Chunks:
    def __init__(self, begins, rows, cuts):
        self.begins, self.rows, self.cuts = begins, rows, cuts

    def shape(self, group):
        return (self.cuts[group + 1] - self.cuts[group], self.rows, 128)

    def pieces(self, at, size):
        found = []
        for group in range(len(self.cuts) - 1):
            for owner in range(self.cuts[group], self.cuts[group + 1]):
                begin = self.begins[owner]
                low, high = max(at, begin), min(at + size, begin + self.rows)
                if low < high:
                    found.append((group, owner - self.cuts[group], low - begin, low - at, high - low))
        return found

    def groups(self, *places):
        return sorted({p[0] for at, size in places for p in self.pieces(at, size)})


class Stores:
    def __init__(self, refs, chunks, sem):
        self.refs, self.chunks, self.sem, self.copies = refs, chunks, sem, []

    def put(self, packed, at):
        for group, owner, row, skip, size in self.chunks.pieces(at, packed.shape[0]):
            source = packed.at[pl.ds(skip, size)]
            copy = pltpu.make_async_copy(source, self.refs[group].at[owner, pl.ds(row, size)], self.sem.at[len(self.copies)])
            copy.start()
            self.copies.append(copy)

    def wait(self):
        for copy in self.copies:
            copy.wait()


STORES = 48


def flat_refs(r, groups):
    return {group: getattr(r, f"flat{group}") for group in groups}


def mlp_sums(rows_in, wide=LATENT):
    return [pltpu.VMEM((rows_in, LATENT), F32), pltpu.VMEM((LATENT, wide), F32), pltpu.VMEM((8, LATENT), F32)]


def packed_rows(rows_in, lead=0):
    return pltpu.VMEM((lead + 4 * rows_in + 4 * LATENT + 16, 128), F32)


def named_call(body, name, inputs, outputs, scratch, aliases=None, cid=None):
    names = [*inputs, *outputs, *scratch]
    aliases = {list(inputs).index(i): list(outputs).index(o) for i, o in (aliases or {}).items()}
    def kernel(*refs):
        body(types.SimpleNamespace(**dict(zip(names, refs))))
    more = {} if cid is None else dict(collective_id=cid, has_side_effects=True)
    values = pl.pallas_call(
        kernel,
        out_shape=tuple(shape for shape, _ in outputs.values()),
        in_specs=[s for _, s in inputs.values()],
        out_specs=tuple(s for _, s in outputs.values()),
        scratch_shapes=list(scratch.values()),
        input_output_aliases=aliases,
        compiler_params=params(**more),
        name=name,
    )(*[v for v, _ in inputs.values()])
    return types.SimpleNamespace(**dict(zip(outputs, values)))


def swap_start(n, me, srcs, dsts, own, ssem, rsem):
    for i, (src, dst) in enumerate(zip(srcs, dsts)):
        pltpu.make_async_copy(src.at[me], dst.at[me], own.at[i]).start()
    def go(j, c):
        t = lax.rem(me + j, n)
        for i, (src, dst) in enumerate(zip(srcs, dsts)):
            remote(src.at[t], dst.at[me], ssem.at[i, j], rsem.at[i, j], t).start()
        return c
    lax.fori_loop(1, n, go, 0)


def swap_wait(n, me, srcs, dsts, own, ssem, rsem):
    def end(j, c):
        t = lax.rem(me + j, n)
        for i, (src, dst) in enumerate(zip(srcs, dsts)):
            remote(src.at[t], dst.at[me], ssem.at[i, j], rsem.at[i, j], t).wait()
        return c
    lax.fori_loop(1, n, end, 0)
    for i, (src, dst) in enumerate(zip(srcs, dsts)):
        pltpu.make_async_copy(src.at[me], dst.at[me], own.at[i]).wait()


def several(r, name):
    return [getattr(r, f"{name}{i}") for i in range(4) if hasattr(r, f"{name}{i}")]


def numbered(name, values):
    return {f"{name}{i}": value for i, value in enumerate(values)}


def slot_rows(refs):
    rows = [ref[...].reshape(ref.shape[0] * ref.shape[1], ref.shape[2]) for ref in refs]
    return rows[0] if len(rows) == 1 else jnp.concatenate(rows, axis=0)


def put_slot_rows(refs, rows):
    at = 0
    for ref in refs:
        size = ref.shape[0] * ref.shape[1]
        ref[...] = rows[at : at + size, :].reshape(ref.shape)
        at += size


def greet_start(n, me):
    barrier = pltpu.get_barrier_semaphore()
    def hello(j, c):
        pl.semaphore_signal(barrier, inc=1, device_id=(lax.rem(me + j, n),), device_id_type=MESH)
        return c
    lax.fori_loop(1, n, hello, 0)


def greet_wait(n):
    pl.semaphore_wait(pltpu.get_barrier_semaphore(), n - 1)


class Loads:
    def __init__(self, r, sem):
        self.r, self.sem, self.copies = r, sem, {}

    def start(self, *names):
        for name in names:
            copy = pltpu.make_async_copy(getattr(self.r, name), getattr(self.r, "_" + name), self.sem.at[len(self.copies)])
            copy.start()
            self.copies[name] = copy

    def wait(self, *names):
        for name in names:
            self.copies[name].wait()


def store_all(r, sem, *names):
    copies = [pltpu.make_async_copy(getattr(r, "_" + name), getattr(r, name), sem.at[i]) for i, name in enumerate(names)]
    for copy in copies:
        copy.start()
    return copies


def same_rows(want, served):
    return jnp.where((want[...] == served[...]) & (want[...] >= 0), 1.0, 0.0).astype(BF16)


def swap_scratch(shapes, n):
    parts = len(shapes)
    scratch = dict(own=DMA((2, parts)), s1=DMA((parts, n)), r1=DMA((parts, n)), s2=DMA((parts, n)), r2=DMA((parts, n)))
    for name in ("away", "here", "back"):
        scratch |= numbered(name, [pltpu.VMEM(shape, BF16) for shape in shapes])
    return scratch


def held(prefix, block):
    return {prefix + part: pltpu.VMEM(a.shape, a.dtype) for part, a in zip(("_in", "_out", "_vec"), block)}


def weights(prefix, block):
    return {prefix + part: (a, ANY) for part, a in zip(("_in", "_out", "_vec"), block)}


def rows_block(bm, width=LATENT):
    return pl.BlockSpec((bm, width), lambda i: (i, 0))


def edge_kernel(n, first, bm, r):
    me = lax.axis_index("dev")
    greet_start(n, me)
    loads = Loads(r, r.lsem)
    node_weights = ["p_in", "p_out", "p_vec"]
    landing = [name for name in vars(r) if name.startswith("landed_in")]
    early = node_weights + ([] if first else [*landing, "slots_in"])
    late = ["e_in", "e_out", "e_vec"] + (["g_in", "g_out", "g_vec"] if first else [])
    loads.start(*early)
    loads.start(*late)
    loads.wait(*early)
    count = r.want.shape[0]
    if first:
        asked = contract(pick(r.want[...], 0, r.x.shape[1]), r.x[...], 1, 1).astype(BF16)
        pre = contract(asked, r._p_in[:VARS, :], 1, 0) + r._p_vec[0:1, :]
    else:
        landed = slot_rows(several(r, "_landed_in"))
        got = mm(same_rows(r.want, r.served), landed).astype(BF16)
        r._sums_s[...] = got
        old = r._slots_in[...]
        pre = first_half([old.astype(BF16), got], r._p_in, r._p_vec)
    _, act = activate(pre)
    hat, _ = second_half(act, r._p_out, r._p_vec)
    slots = scale_shift(hat, r._p_vec)
    if not first:
        slots = old + slots
    r._slots[...] = slots
    away, here, back, out = (several(r, name) for name in ("away", "here", "back", "landed"))
    put_slot_rows(away, slots.astype(BF16))
    greet_wait(n)
    swap_start(n, me, away, here, r.own.at[0], r.s1, r.r1)
    stores = store_all(r, r.ssem, *(["slots"] if first else ["slots", "sums_s"]))
    loads.wait(*late)
    if first:
        _, act = activate(first_half([r.source[...]], r._g_in, r._g_vec))
        hat, _ = second_half(act, r._g_out, r._g_vec)
        r._edge[...] = scale_shift(hat, r._g_vec)
    else:
        r._edge[...] = r.source[...]
    e = r._edge[...].astype(BF16)
    r.edge_low[...] = e
    r._pre[...] = first_half([e], r._e_in, r._e_vec)
    if first:
        def body(node, low):
            i = pl.program_id(0)
            u = r.x[:, pl.ds(pl.multiple_of(i * bm, bm), bm)]
            _, act = activate(contract(u, r._p_in[:VARS, :], 0, 0) + r._p_vec[0:1, :])
            hat, _ = second_half(act, r._p_out, r._p_vec)
            new = scale_shift(hat, r._p_vec)
            node[...] = new
            low[...] = new.astype(BF16)
        pltpu.emit_pipeline(body, grid=(r.node.shape[0] // bm,), in_specs=[], out_specs=[rows_block(bm)] * 2)(r.node, r.low)
    else:
        def body(node_in, node, low, sums):
            i = pl.program_id(0)
            got = mm(place(r.served[...], i * bm, bm), slot_rows(several(r, "_landed_in"))).astype(BF16)
            sums[...] = got
            old = node_in[...]
            _, act = activate(first_half([old.astype(BF16), got], r._p_in, r._p_vec))
            hat, _ = second_half(act, r._p_out, r._p_vec)
            new = old + scale_shift(hat, r._p_vec)
            node[...] = new
            low[...] = new.astype(BF16)
        pltpu.emit_pipeline(body, grid=(r.node.shape[0] // bm,), in_specs=[rows_block(bm)], out_specs=[rows_block(bm)] * 3)(r.node_in, r.node, r.low, r.sums)
    pick_s, pick_r = pick(r.pos[:, 0:1], 0, count), pick(r.pos[:, 1:2], 0, count)
    put_r = place(r.pos_r[...], 0, count)
    swap_wait(n, me, away, here, r.own.at[0], r.s1, r.r1)
    rows = slot_rows(here)
    s = mm(pick_s, rows).astype(BF16)
    v = mm(pick_r, rows).astype(BF16)
    pre = r._pre[...] + mm(s, r._e_in[LATENT : 2 * LATENT, :]) + mm(v, r._e_in[2 * LATENT :, :])
    _, act = activate(pre)
    hat, _ = second_half(act, r._e_out, r._e_vec)
    new = r._edge[...] + scale_shift(hat, r._e_vec)
    put_slot_rows(back, mm(put_r, new.astype(BF16)).astype(BF16))
    swap_start(n, me, back, out, r.own.at[1], r.s2, r.r2)
    r.edge[...] = new
    r.sent[...], r.recv[...] = s, v
    for store in stores:
        store.wait()
    swap_wait(n, me, back, out, r.own.at[1], r.s2, r.r2)


def edge_forward(n, parts, cid, source, routes, edge_block, node_block, rows, x=None, geo_block=None, landed=None, node=None, slots=None, bm=512):
    first = x is not None
    want, served, pos, pos_s, pos_r = routes
    count = want.shape[0]
    edges = source.shape[0]
    shapes = [(n, p, LATENT) for p in parts]
    V = pl.BlockSpec(memory_space=pltpu.VMEM)
    inputs = dict(source=(source, V), want=(want, V), served=(served, V), pos=(pos, V), pos_r=(pos_r, V))
    inputs |= weights("p", node_block) | weights("e", edge_block)
    scratch = held("_p", node_block) | held("_e", edge_block) | swap_scratch(shapes, n)
    scratch |= dict(_slots=pltpu.VMEM((count, LATENT), F32), _edge=pltpu.VMEM((edges, LATENT), F32), _pre=pltpu.VMEM((edges, LATENT), F32), lsem=DMA((12,)), ssem=DMA((2,)))
    low = lambda r: shaped(r, LATENT, dtype=BF16)
    outputs = dict(edge=(shaped(edges, LATENT), V), edge_low=(low(edges), V), sent=(low(edges), V), recv=(low(edges), V)) | numbered("landed", [(shaped(*s, dtype=BF16), ANY) for s in shapes])
    outputs |= dict(node=(shaped(rows, LATENT), ANY), low=(low(rows), ANY), slots=(shaped(count, LATENT), ANY))
    if first:
        inputs |= dict(x=(x, V)) | weights("g", geo_block)
        scratch |= held("_g", geo_block)
    else:
        inputs |= numbered("landed_in", [(v, ANY) for v in landed]) | dict(node_in=(node, ANY), slots_in=(slots, ANY))
        scratch |= numbered("_landed_in", [pltpu.VMEM(s, BF16) for s in shapes]) | dict(_slots_in=pltpu.VMEM((count, LATENT), F32), _sums_s=pltpu.VMEM((count, LATENT), BF16))
        outputs |= dict(sums=(low(rows), ANY), sums_s=(low(count), ANY))
    return named_call(functools.partial(edge_kernel, n, first, bm), "edge_forward", inputs, outputs, scratch, cid=cid)


def turn_kernel(parts, bm, chunks, group, at, dec_at, served, want, *refs):
    landed, refs = refs[:parts], refs[parts:]
    flat, g_prev, *outs = refs[13 : 15 + parts]
    node, x, target, level, land, count, w_in, w_out, vec, c_in, c_out, c_vec, c_bias = refs[:13]
    d_out_o, d_first_o, d_bias_o, err_o, packed, packed2, d_in, d_out, d_vec, e_in, e_out, e_vec, e_bias, err, acc, sem = refs[13 + 2 + parts:]
    i = pl.program_id(0)
    @pl.when(i == 0)
    def _():
        clear(d_in, d_out, d_vec, e_in, e_out, e_vec, e_bias, err, acc)
    got = mm(place(served[...], i * bm, bm), slot_rows(landed)).astype(BF16)
    old = node[...]
    low = old.astype(BF16)
    pre = first_half([low, got], w_in, vec)
    sigma, act = activate(pre)
    hat, inv = second_half(act, w_out, vec)
    u = (old + scale_shift(hat, vec)).astype(BF16)
    c_pre = first_half([u], c_in, c_vec)
    c_sigma, c_act = activate(c_pre)
    wide = c_out.shape[1]
    post = contract(c_out[...], c_act, 0, 1)
    sea = (lax.broadcasted_iota(jnp.int32, (VARS, 1), 0) < SEA_VARS).astype(F32)
    mask = level[...].astype(F32) * (1.0 - sea * land[...].astype(F32))
    residual = x[...].astype(F32) + (post[:VARS, :] + c_bias[...]) - target[...]
    divisor = jnp.maximum(count[...], 1.0)
    err[...] += jnp.sum(mask * residual * residual, axis=0, keepdims=True)
    g = 2.0 * mask * residual / divisor
    g_low = jnp.concatenate([g, jnp.zeros((wide - VARS, bm), F32)], axis=0).astype(BF16)
    e_bias[...] += jnp.sum(g_low.astype(F32), axis=1, keepdims=True)
    e_out[...] += contract(c_act, g_low, 0, 1)
    g_act = contract(g_low, c_out[...], 0, 1)
    c_g = (g_act * c_sigma * (1.0 + c_pre * (1.0 - c_sigma))).astype(BF16)
    e_vec[0:1, :] += col(c_g.astype(F32))
    e_in[...] += mm_tn(u, c_g)
    g_node = mm_nt(c_g, c_in[...])
    g_post = norm_back(g_node, hat, inv, vec, d_vec)
    g_pre = act_back(g_post, pre, sigma, w_out)
    weight_sums([low, got], act, g_post, g_pre, d_in, d_out, d_vec)
    g_prev[...] = g_node + mm_nt(g_pre, w_in[:LATENT, :])
    acc[...] += mm(pick(want[...], i * bm, bm), mm_nt(g_pre, w_in[LATENT:, :]).astype(BF16))
    @pl.when(i == pl.num_programs(0) - 1)
    def _():
        put_slot_rows(outs, acc[...].astype(BF16))
        d_out_o[...] = e_out[...]
        d_first_o[...] = e_vec[0:1, :]
        d_bias_o[...] = e_bias[...]
        err_o[...] = err[...]
        stores = Stores({group: flat}, chunks, sem)
        pack_matrix(packed2, e_in, LATENT, 0)
        stores.put(packed2, dec_at)
        pack(packed, 0, 2 * LATENT, d_in, d_out, d_vec)
        stores.put(packed, at)
        stores.wait()


def turn(served, want, landed, node, x, target, level, land, count, block, dec, bias, chunks, at, dec_at, bm=512):
    rows = node.shape[0]
    slots = want.shape[0]
    wide = dec[1].shape[1]
    [group] = chunks.groups((at, dec_at + 4 * LATENT - at))
    v = lambda height: pl.BlockSpec((height, bm), lambda i: (0, i))
    part = [spec(p.shape) for p in landed]
    return pl.pallas_call(
        functools.partial(turn_kernel, len(landed), bm, chunks, group, at, dec_at),
        grid=(rows // bm,),
        out_shape=(shaped(*chunks.shape(group)), shaped(rows, LATENT), *(shaped(*p.shape, dtype=BF16) for p in landed), shaped(LATENT, wide), shaped(1, LATENT), shaped(wide, 1), shaped(1, bm)),
        in_specs=[spec((1, slots)), spec((slots, 1)), *part, spec((bm, LATENT), False), v(VARS), v(VARS), v(VARS), v(1), spec((1, 1))] + [spec(a.shape) for a in (*block, *dec, bias)],
        out_specs=(ANY, spec((bm, LATENT), False), *part, spec((LATENT, wide)), spec((1, LATENT)), spec((wide, 1)), spec((1, bm))),
        scratch_shapes=[packed_rows(2 * LATENT), pltpu.VMEM((4 * LATENT, 128), F32)] + mlp_sums(2 * LATENT) + mlp_sums(LATENT, wide) + [pltpu.VMEM((wide, 1), F32), pltpu.VMEM((1, bm), F32), pltpu.VMEM((slots, LATENT), F32), DMA((STORES,))],
        compiler_params=params(),
        name="turn",
    )(served, want, *landed, node, x, target, level, land, count, *block, *dec, bias)


def gather_slots(r, bm):
    clear(r._g_slots)
    def body(g_node):
        chosen = pick(r.want[...], pl.program_id(0) * bm, bm)
        g = g_node[...]
        high = g.astype(BF16)
        rest = g - high.astype(F32)
        middle = rest.astype(BF16)
        small = (rest - middle.astype(F32)).astype(BF16)
        r._g_slots[...] += mm(chosen, high) + (mm(chosen, middle) + mm(chosen, small))
    pltpu.emit_pipeline(body, grid=(r.g_node.shape[0] // bm,), in_specs=[rows_block(bm)], out_specs=[])(r.g_node)


def edge_back_kernel(n, chunks, groups, at, node_at, geo_at, tail_at, bm, r):
    me = lax.axis_index("dev")
    greet_start(n, me)
    loads = Loads(r, r.lsem)
    nodes = node_at is not None
    landing = [name for name in vars(r) if name.startswith("landed_in")]
    early = ["p_in", "p_out", "p_vec", *landing, "g_slots_in", "slots_in", "sums_s"] if nodes else []
    late = ["e_in", "e_out", "e_vec"] + (["g_in", "g_out", "g_vec"] if geo_at is not None else [])
    loads.start(*early)
    loads.start(*late)
    flats = Stores(flat_refs(r, groups), chunks, r.fsem)
    stores = [flats]
    if tail_at is not None:
        flats.put(r.tail, tail_at)
    count = r.want.shape[0]
    here, back, out = (several(r, name) for name in ("here", "back", "landed"))
    if nodes:
        loads.wait(*early)
        us = [r._slots_in[...].astype(BF16), r._sums_s[...]]
        pre = first_half(us, r._p_in, r._p_vec)
        sigma, act = activate(pre)
        hat, inv = second_half(act, r._p_out, r._p_vec)
        g = r._g_slots_in[...] + mm(same_rows(r.want, r.served), slot_rows(several(r, "_landed_in")))
        low = norm_back(g, hat, inv, r._p_vec, None)
        g_pre = act_back(low, pre, sigma, r._p_out)
        source = several(r, "away")
        put_slot_rows(source, mm_nt(g_pre, r._p_in[LATENT:, :]).astype(BF16))
    else:
        source = several(r, "outgoing")
    greet_wait(n)
    swap_start(n, me, source, here, r.own.at[0], r.s1, r.r1)
    if nodes:
        r._g_slots[...] = g + mm_nt(g_pre, r._p_in[:LATENT, :])
        stores += store_all(r, r.ssem, "g_slots")
        clear(r.n_in, r.n_out, r.n_vec)
    clear(r.d_in, r.d_out, r.d_vec)
    def node_rows(first, last):
        if not nodes:
            return
        def body(g_node, low_in, sums_in, g_prev):
            i = first + pl.program_id(0)
            us = [low_in[...], sums_in[...]]
            pre = first_half(us, r._p_in, r._p_vec)
            sigma, act = activate(pre)
            hat, inv = second_half(act, r._p_out, r._p_vec)
            g = g_node[...] + mm(place(r.served[...], i * bm, bm), slot_rows(several(r, "_landed_in")))
            low = norm_back(g, hat, inv, r._p_vec, r.n_vec)
            g_pre = act_back(low, pre, sigma, r._p_out)
            weight_sums(us, act, low, g_pre, r.n_in, r.n_out, r.n_vec)
            g_prev[...] = g + mm_nt(g_pre, r._p_in[:LATENT, :])
        block = pl.BlockSpec((bm, LATENT), lambda i: (first + i, 0))
        pltpu.emit_pipeline(body, grid=(last - first,), in_specs=[block] * 3, out_specs=[block])(r.g_node, r.low, r.sums, r.g_prev)
    blocks = r.g_node.shape[0] // bm if nodes else 0
    node_rows(0, blocks // 2)
    if not nodes:
        gather_slots(r, bm)
    loads.wait(*late)
    us = [r.edge_low[...], r.sent[...], r.recv[...]]
    pre = first_half(us, r._e_in, r._e_vec)
    sigma, act = activate(pre)
    hat, inv = second_half(act, r._e_out, r._e_vec)
    pick_r = pick(r.pos[:, 1:2], 0, count)
    put_s, put_r = place(r.pos_s[...], 0, count), place(r.pos_r[...], 0, count)
    swap_wait(n, me, source, here, r.own.at[0], r.s1, r.r1)
    g = mm(pick_r, slot_rows(here))
    if hasattr(r, "g_edge"):
        g = r.g_edge[...] + g
    low = norm_back(g, hat, inv, r._e_vec, r.d_vec)
    g_pre = act_back(low, pre, sigma, r._e_out)
    s = mm_nt(g_pre, r._e_in[LATENT : 2 * LATENT, :]).astype(BF16)
    v = mm_nt(g_pre, r._e_in[2 * LATENT :, :]).astype(BF16)
    put_slot_rows(back, (mm(put_s, s) + mm(put_r, v)).astype(BF16))
    swap_start(n, me, back, out, r.own.at[1], r.s2, r.r2)
    prev = g + mm_nt(g_pre, r._e_in[:LATENT, :])
    r.edge_prev[...] = prev
    weight_sums(us, act, low, g_pre, r.d_in, r.d_out, r.d_vec)
    pack(r.packed, 0, 3 * LATENT, r.d_in, r.d_out, r.d_vec)
    flats.put(r.packed, at)
    if geo_at is not None:
        c_us = [r.geo[...]]
        c_pre = first_half(c_us, r._g_in, r._g_vec)
        c_sigma, c_act = activate(c_pre)
        c_hat, c_inv = second_half(c_act, r._g_out, r._g_vec)
        clear(r.c_in, r.c_out, r.c_vec)
        c_low = norm_back(prev, c_hat, c_inv, r._g_vec, r.c_vec)
        c_g = act_back(c_low, c_pre, c_sigma, r._g_out)
        weight_sums(c_us, c_act, c_low, c_g, r.c_in, r.c_out, r.c_vec)
        pack(r.c_packed, 0, GEO, r.c_in, r.c_out, r.c_vec)
        flats.put(r.c_packed, geo_at)
    node_rows(blocks // 2, blocks)
    if nodes:
        pack(r.n_packed, 0, 2 * LATENT, r.n_in, r.n_out, r.n_vec)
        flats.put(r.n_packed, node_at)
    if not nodes:
        stores += store_all(r, r.ssem, "g_slots")
    swap_wait(n, me, back, out, r.own.at[1], r.s2, r.r2)
    for store in stores:
        store.wait()


def sums_scratch(prefix, rows_in):
    return dict(zip((prefix + "_in", prefix + "_out", prefix + "_vec"), mlp_sums(rows_in)))


def edge_backward(n, parts, cid, ins, routes, edge_block, chunks, flats, at, g_edge=None, outgoing=None, g_node=None, tail=None, tail_at=None, node=None, node_at=None, geo=None, geo_at=None, bm=512):
    want, served, pos, pos_s, pos_r = routes
    count = want.shape[0]
    edges = pos.shape[0]
    shapes = [(n, p, LATENT) for p in parts]
    V = pl.BlockSpec(memory_space=pltpu.VMEM)
    inputs = dict(want=(want, V), served=(served, V), pos=(pos, V), pos_s=(pos_s, V), pos_r=(pos_r, V))
    inputs |= {name: (value, V) for name, value in zip(("edge_low", "sent", "recv"), ins)} | weights("e", edge_block)
    scratch = held("_e", edge_block) | swap_scratch(shapes, n) | sums_scratch("d", 3 * LATENT)
    scratch |= dict(packed=packed_rows(3 * LATENT), lsem=DMA((16,)), ssem=DMA((2,)), fsem=DMA((STORES,)))
    outputs = dict(edge_prev=(shaped(edges, LATENT), V)) | numbered("landed", [(shaped(*s, dtype=BF16), ANY) for s in shapes])
    places = [(at, scratch["packed"].shape[0])]
    if g_edge is not None:
        inputs |= dict(g_edge=(g_edge, V))
    if outgoing is not None:
        inputs |= numbered("outgoing", [(v, ANY) for v in outgoing]) | dict(g_node=(g_node, ANY))
        outputs |= dict(g_slots=(shaped(count, LATENT), ANY))
        scratch |= dict(_g_slots=pltpu.VMEM((count, LATENT), F32))
    if tail is not None:
        inputs |= dict(tail=(tail, V))
        places.append((tail_at, tail.shape[0]))
    if node is not None:
        inputs |= numbered("landed_in", [(v, ANY) for v in node[0]])
        for name, value in zip(("g_slots_in", "slots_in", "sums_s", "g_node", "low", "sums"), node[1:]):
            inputs[name] = (value, ANY)
        inputs |= weights("p", node[7])
        scratch |= held("_p", node[7]) | sums_scratch("n", 2 * LATENT)
        f = pltpu.VMEM((count, LATENT), F32)
        scratch |= numbered("_landed_in", [pltpu.VMEM(s, BF16) for s in shapes]) | dict(n_packed=packed_rows(2 * LATENT), _g_slots_in=f, _slots_in=f, _g_slots=f, _sums_s=pltpu.VMEM((count, LATENT), BF16))
        rows = node[4].shape[0]
        places.append((node_at, scratch["n_packed"].shape[0]))
        outputs |= dict(g_prev=(shaped(rows, LATENT), ANY), g_slots=(shaped(count, LATENT), ANY))
    if geo is not None:
        inputs |= dict(geo=(geo[0], V)) | weights("g", geo[1])
        scratch |= held("_g", geo[1]) | sums_scratch("c", geo[0].shape[1]) | dict(c_packed=packed_rows(GEO))
        places.append((geo_at, scratch["c_packed"].shape[0]))
    groups = chunks.groups(*places)
    aliases = {}
    for group in groups:
        outputs[f"flat{group}"] = (shaped(*chunks.shape(group)), ANY)
        if group in flats:
            inputs[f"flat{group}_in"] = (flats[group], ANY)
            aliases[f"flat{group}_in"] = f"flat{group}"
    body = functools.partial(edge_back_kernel, n, chunks, groups, at, node_at, geo_at, tail_at, bm)
    made = named_call(body, "edge_backward", inputs, outputs, scratch, aliases=aliases, cid=cid)
    flats.update(flat_refs(made, groups))
    return made


def encode_back_rows(first, bm, served, landed, g_node, x, w_in, w_out, vec, d_in, d_out, d_vec):
    pre = contract(x[...], w_in[:VARS, :], 0, 0) + vec[0:1, :]
    sigma, act = activate(pre)
    hat, inv = second_half(act, w_out, vec)
    g = g_node[...] + mm(place(served[...], first, bm), slot_rows(landed))
    g_post = norm_back(g, hat, inv, vec, d_vec)
    g_pre = act_back(g_post, pre, sigma, w_out)
    weight_sums([], act, g_post, g_pre, d_in, d_out, d_vec)
    d_in[:VARS, :] += mm(x[...], g_pre)


def encode_pack(packed, d_in, d_out, d_vec):
    packed[0:4, :] = jnp.zeros((4, 128), F32)
    pack(packed, 4, VARS, d_in, d_out, d_vec)


def encode_back_kernel(parts, bm, chunks, served, *refs):
    landed, refs = refs[:parts], refs[parts:]
    g_node, x, w_in, w_out, vec, flat_in, flat, packed, d_in, d_out, d_vec, sem = refs
    i = pl.program_id(0)
    @pl.when(i == 0)
    def _():
        clear(d_in, d_out, d_vec)
    encode_back_rows(i * bm, bm, served, landed, g_node, x, w_in, w_out, vec, d_in, d_out, d_vec)
    @pl.when(i == pl.num_programs(0) - 1)
    def _():
        encode_pack(packed, d_in, d_out, d_vec)
        stores = Stores({0: flat}, chunks, sem)
        stores.put(packed, 0)
        stores.wait()


def encode_backward(served, landed, g_node, x, block, chunks, flat, bm=512):
    k, rows = block[0].shape[0], x.shape[1]
    slots = served.shape[1]
    return pl.pallas_call(
        functools.partial(encode_back_kernel, len(landed), bm, chunks),
        grid=(rows // bm,),
        out_shape=shaped(*flat.shape),
        in_specs=[spec((1, slots)), *(spec(p.shape) for p in landed), spec((bm, LATENT), False), pl.BlockSpec((VARS, bm), lambda i: (0, i))] + [spec(a.shape) for a in block] + [ANY],
        out_specs=ANY,
        scratch_shapes=[packed_rows(VARS, 4)] + mlp_sums(k) + [DMA((STORES,))],
        input_output_aliases={6 + len(landed): 0},
        compiler_params=params(),
        name="encode_backward",
    )(served, *landed, g_node, x, *block, flat)


def relay_plan(segments, share_rows):
    jobs = []
    for block_id, part_name, part_shape, offset, entries in segments:
        if part_name not in ("w_in", "w_out") or part_shape[1] != LATENT:
            continue
        for first in range(0, part_shape[0], LATENT):
            rows = min(LATENT, part_shape[0] - first)
            follow = 0
            if first + rows == part_shape[0]:
                follow = 1 if part_name == "w_in" else 3
            begin = offset // 128 + 4 * first
            end = begin + 4 * (rows + follow)
            parts = []
            at = begin
            while at < end:
                owner, low = divmod(at, share_rows)
                size = min(end - at, share_rows - low)
                base = low // 16 * 16
                span = (low + size - base + 15) // 16 * 16
                parts.append((owner, base, span, low - base, at - begin))
                at += size
            jobs.append((block_id, part_name, first, rows, follow, parts))
    return jobs


class Relay:
    def __init__(self, r, shares):
        self.r, self.shares, self.loads, self.at, self.count = r, shares, {}, 0, 0

    def load(self, job):
        r, mine = self.r, []
        for owner, base, span, skip, to in job[5]:
            place = pl.ds(self.at, span)
            copy = pltpu.make_async_copy(self.shares.at[owner, pl.ds(base, span)], r.stage.at[place], r.isem.at[self.count])
            copy.start()
            mine.append((copy, place, span, skip, to))
            self.at += span
            self.count += 1
        self.loads[job[:3]] = mine

    def run(self, job, target, vec):
        _, name, _, rows, follow, _ = job
        lines = self.r.lines
        for copy, place, span, skip, to in self.loads[job[:3]]:
            copy.wait()
            lines[pl.ds(16 + to - skip, span), :] = self.r.stage[place, :].astype(F32)
        for j in range(4):
            target[:rows, 128 * j : 128 * (j + 1)] = lines[pl.ds(16 + j, rows, stride=4), :].astype(BF16)
        if rows < target.shape[0]:
            target[rows:, :] = jnp.zeros((target.shape[0] - rows, LATENT), BF16)
        for i in range(follow):
            row = i if name == "w_in" else i + 1
            for j in range(4):
                p = 16 + 4 * (rows + i) + j
                vec[row : row + 1, 128 * j : 128 * (j + 1)] = lines[p : p + 1, :]


class Gather:
    def __init__(self, r, w, o):
        self.r, self.w, self.o = r, w, o
        self.me, z, y, x, c = where_am_i()
        self.z = z
        half = w.shape[0] // 2
        self.A, self.B = pl.ds(0, half), pl.ds(half, half)
        self.dev = lambda zz, fy=0, fx=0: device_at(zz, y + fy * (1 - 2 * y), x + fx * (1 - 2 * x), c)
        self.tx, self.ty, self.tc = self.dev(z, 0, 1), self.dev(z, 1, 0), device_at(z, y, x, 1 - c)
        self.up, self.down = self.dev(jnp.minimum(z + 1, 3)), self.dev(jnp.maximum(z - 1, 0))
        def by_plane(*v):
            return jnp.where(z == 0, v[0], jnp.where(z == 1, v[1], jnp.where(z == 2, v[2], v[3])))
        self.come = [z, by_plane(1, 0, 1, 2), by_plane(2, 2, 3, 1), by_plane(3, 3, 0, 0)]
        self.go = [z, by_plane(1, 0, 1, 2), by_plane(2, 2, 0, 0), by_plane(3, 3, 3, 1)]
        self.sends, self.sibling, self.seen = [], [], 0

    def send(self, *args):
        copy = remote(*args)
        copy.start()
        self.sends.append(copy)

    def share(self, k, part=None):
        ref = self.w if k == 0 else self.o.at[self.dev(self.go[k])]
        return ref if part is None else ref.at[part]

    def to_sibling(self, slot, part=None, source=None):
        r, i = self.r, len(self.sibling)
        ref = self.o.at[slot] if part is None else self.o.at[slot, part]
        self.send(ref if source is None else source, ref, r.bs.at[i], r.br.at[i], self.tc)
        self.sibling.append(part)

    def from_sibling(self, count):
        r = self.r
        for i in range(self.seen, count):
            part = self.sibling[i]
            ref = self.o.at[self.me] if part is None else self.o.at[self.me, part]
            remote(ref, ref, r.bs.at[i], r.br.at[i], self.tc).wait_recv()
        self.seen = count

    def onward(self, i, wait=False):
        r, z, plane = self.r, self.z, self.come[i]
        slot = self.dev(plane)
        source = self.w if i == 0 else self.o.at[slot]
        for d, target, here in ((0, self.up, (plane <= z) & (z < 3)), (1, self.down, (plane >= z) & (z > 0))):
            @pl.when(here)
            def _():
                copy = remote(source, self.o.at[slot], r.zs.at[d, i], r.zr.at[plane], target)
                if wait:
                    copy.wait_send()
                else:
                    copy.start()

    def begin(self):
        r = self.r
        self.mine = pltpu.make_async_copy(self.w, self.o.at[self.me], r.gown.at[0])
        self.mine.start()
        self.spread(0)
        self.onward(0)
        self.to_sibling(self.me, None, self.w)

    def arrive(self, i):
        slot = self.dev(self.come[i])
        remote(self.w, self.o.at[slot], self.r.zs.at[0, i], self.r.zr.at[self.come[i]], self.tc).wait_recv()
        self.onward(i)
        self.to_sibling(slot)

    def spread(self, k):
        r, slot = self.r, self.dev(self.go[k])
        self.send(self.share(k, self.A), self.o.at[slot, self.A], r.hs.at[k, 0], r.hr.at[k, 0], self.tx)
        self.send(self.share(k, self.B), self.o.at[slot, self.B], r.hs.at[k, 1], r.hr.at[k, 1], self.ty)

    def second(self, k):
        r, o, zz = self.r, self.o, self.go[k]
        s, sx, sy = self.dev(zz), self.dev(zz, 0, 1), self.dev(zz, 1, 0)
        self.send(self.share(k, self.A), o.at[s, self.A], r.cs.at[k, 0], r.cr.at[k, 0], self.ty)
        self.send(self.share(k, self.B), o.at[s, self.B], r.ds.at[k, 0], r.dr.at[k, 0], self.tx)
        remote(o.at[sx, self.A], o.at[sx, self.A], r.hs.at[k, 0], r.hr.at[k, 0], self.tx).wait_recv()
        self.send(o.at[sx, self.A], o.at[sx, self.A], r.cs.at[k, 1], r.cr.at[k, 1], self.ty)
        remote(o.at[sy, self.B], o.at[sy, self.B], r.hs.at[k, 1], r.hr.at[k, 1], self.ty).wait_recv()
        self.send(o.at[sy, self.B], o.at[sy, self.B], r.ds.at[k, 1], r.dr.at[k, 1], self.tx)
        self.to_sibling(sx, self.A)
        self.to_sibling(sy, self.B)

    def third(self, k):
        r, o, zz = self.r, self.o, self.go[k]
        for slot, part, ss, rr, i, target in (
            (self.dev(zz, 1, 0), self.A, r.cs, r.cr, 0, self.ty),
            (self.dev(zz, 0, 1), self.B, r.ds, r.dr, 0, self.tx),
            (self.dev(zz, 1, 1), self.A, r.cs, r.cr, 1, self.ty),
            (self.dev(zz, 1, 1), self.B, r.ds, r.dr, 1, self.tx),
        ):
            remote(o.at[slot, part], o.at[slot, part], ss.at[k, i], rr.at[k, i], target).wait_recv()
            self.to_sibling(slot, part)

    def finish(self):
        for i in range(4):
            self.onward(i, True)
        for copy in self.sends:
            copy.wait_send()


def as_column(row):
    return jnp.transpose(jnp.broadcast_to(row, (128, row.shape[1])))[:, 0:1]


def route(n, parts, r):
    owner = jnp.concatenate([r.owners[0:1, :], r.owners[1:2, :]], axis=1)
    local = jnp.concatenate([r.locals[0:1, :], r.locals[1:2, :]], axis=1)
    wants, edges = owner.shape[1], r.owners.shape[1]
    earlier = lax.broadcasted_iota(jnp.int32, (wants, wants), 0) < lax.broadcasted_iota(jnp.int32, (wants, wants), 1)
    same = (as_column(owner) == owner) & earlier
    rank = jnp.sum(jnp.where(same, 1.0, 0.0), axis=0, keepdims=True).astype(jnp.int32)
    position = owner * parts[0] + rank
    if len(parts) > 1:
        position = jnp.where(rank < parts[0], position, n * parts[0] + owner * parts[1] + rank - parts[0])
    r.pos_s[...], r.pos_r[...] = position[:, :edges], position[:, edges:]
    column = as_column(position)
    r.pos[:, 0:1], r.pos[:, 1:2] = column[:edges, :], column[edges:, :]
    slots = n * sum(parts)
    match = lax.broadcasted_iota(jnp.int32, (slots, wants), 0) == position
    asking = jnp.sum(jnp.where(match, local.astype(F32) + 1.0, 0.0), axis=1, keepdims=True).astype(jnp.int32) - 1
    put_slot_rows(several(r, "ask"), jnp.broadcast_to(asking, (slots, 128)))


def count_mask(r):
    sea = (lax.broadcasted_iota(jnp.int32, (VARS, 1), 0) < SEA_VARS).astype(jnp.int32)
    total = jnp.zeros((1, 128), F32)
    for i in range(r.level.shape[1] // 128):
        at = slice(128 * i, 128 * (i + 1))
        total += col((r._level[:, at] * (1 - sea * r.land[:, at])).astype(F32))
    r.number[...] = jnp.zeros_like(r.number)
    r.number[0:1, :] = total


def start_kernel(n, parts, jobs, bm, r):
    me = lax.axis_index("dev")
    gather = Gather(r, r.w, r.shares)
    greet_start(n, me)
    mask = pltpu.make_async_copy(r.level, r._level, r.gown.at[2])
    mask.start()
    rows = r.master.shape[0]
    r.w[rows // 16 * 16 :, :] = jnp.zeros_like(r.w[rows // 16 * 16 :, :])
    r.w[:rows, :] = r.master[...].astype(BF16)
    greet_wait(n)
    gather.begin()
    route(n, parts, r)
    asks, asked = several(r, "ask"), several(r, "asked")
    swap_start(n, me, asks, asked, r.aown, r.a1, r.b1)
    mask.wait()
    count_mask(r)
    number = pltpu.make_async_copy(r.number, r.numbers.at[me], r.gown.at[1])
    number.start()
    def go(j, carry):
        t = lax.rem(me + j, n)
        remote(r.number, r.numbers.at[me], r.ns.at[j], r.nr.at[j], t).start()
        return carry
    lax.fori_loop(1, n, go, 0)
    gather.second(0)
    gather.arrive(1)
    gather.spread(1)
    gather.third(0)
    gather.second(1)
    gather.arrive(2)
    gather.arrive(3)
    gather.spread(2)
    gather.third(1)
    gather.second(2)
    swap_wait(n, me, asks, asked, r.aown, r.a1, r.b1)
    columns = slot_rows(asked)
    r.want[...] = columns[:, 0:1]
    r.served[...] = jnp.transpose(columns)[0:1, :]
    chosen = pick(r.want[...], 0, r.x.shape[1])
    rows = contract(chosen, r.x[...], 1, 1).astype(BF16)
    gather.spread(3)
    gather.third(2)
    plane_0 = len(gather.sibling)
    gather.second(3)
    gather.from_sibling(plane_0)
    gather.mine.wait()
    relay = Relay(r, r.shares)
    block = [[job for job in jobs if job[0] == b] for b in range(jobs[-1][0] + 1)]
    names = ["p", "g", "e"]
    def into(b):
        for job in block[b]:
            target = getattr(r, "_" + names[b] + job[1][1:])
            relay.run(job, target.at[pl.ds(job[2], min(LATENT, target.shape[0] - job[2]))], getattr(r, "_" + names[b] + "_vec"))
    for vec in (r._p_vec, r._g_vec, r._e_vec, r.vecs):
        vec[...] = jnp.zeros_like(vec)
    for job in block[0]:
        relay.load(job)
    into(0)
    for job in block[1]:
        relay.load(job)
    _, act = activate(contract(rows, r._p_in[:VARS, :], 1, 0) + r._p_vec[0:1, :])
    hat, _ = second_half(act, r._p_out, r._p_vec)
    r._slots[...] = scale_shift(hat, r._p_vec)
    away, here, back, out = (several(r, name) for name in ("away", "here", "back", "landed"))
    put_slot_rows(away, r._slots[...].astype(BF16))
    swap_start(n, me, away, here, r.own.at[0], r.s1, r.r1)
    stores = store_all(r, r.ssem, "slots")
    def body(node, low):
        i = pl.program_id(0)
        u = r.x[:, pl.ds(pl.multiple_of(i * bm, bm), bm)]
        _, act = activate(contract(u, r._p_in[:VARS, :], 0, 0) + r._p_vec[0:1, :])
        hat, _ = second_half(act, r._p_out, r._p_vec)
        new = scale_shift(hat, r._p_vec)
        node[...] = new
        low[...] = new.astype(BF16)
    pltpu.emit_pipeline(body, grid=(r.node.shape[0] // bm,), in_specs=[], out_specs=[rows_block(bm)] * 2)(r.node, r.low)
    gather.third(3)
    gather.from_sibling(len(gather.sibling))
    for b in range(2, len(block)):
        for job in block[b]:
            relay.load(job)
    into(1)
    into(2)
    _, act = activate(first_half([r.source[...]], r._g_in, r._g_vec))
    hat, _ = second_half(act, r._g_out, r._g_vec)
    r._edge[...] = scale_shift(hat, r._g_vec)
    e = r._edge[...].astype(BF16)
    r.edge_low[...] = e
    count = r.want.shape[0]
    pre = first_half([e], r._e_in, r._e_vec)
    pick_s, pick_r = pick(r.pos[:, 0:1], 0, count), pick(r.pos[:, 1:2], 0, count)
    put_r = place(r.pos_r[...], 0, count)
    kept = [f"m{b}{part}" for b in range(3) for part in ("_in", "_out", "_vec")]
    for i, name in enumerate(kept):
        b, part = int(name[1]), name[2:]
        copy = pltpu.make_async_copy(getattr(r, "_" + names[b] + part), getattr(r, name), r.osem.at[i])
        copy.start()
        stores.append(copy)
    swap_wait(n, me, away, here, r.own.at[0], r.s1, r.r1)
    rows = slot_rows(here)
    s = mm(pick_s, rows).astype(BF16)
    v = mm(pick_r, rows).astype(BF16)
    pre = pre + mm(s, r._e_in[LATENT : 2 * LATENT, :]) + mm(v, r._e_in[2 * LATENT :, :])
    _, act = activate(pre)
    hat, _ = second_half(act, r._e_out, r._e_vec)
    new = r._edge[...] + scale_shift(hat, r._e_vec)
    put_slot_rows(back, mm(put_r, new.astype(BF16)).astype(BF16))
    swap_start(n, me, back, out, r.own.at[1], r.s2, r.r2)
    r.edge[...] = new
    r.sent[...], r.recv[...] = s, v
    at = len(kept)
    late = [job for b in range(3, len(block)) for job in block[b]]
    for i, job in enumerate(late):
        b, name, first = job[:3]
        relay.run(job, r.made.at[i], r.vecs.at[b])
        copy = pltpu.make_async_copy(r.made.at[i], getattr(r, f"m{b}{name[1:]}").at[pl.ds(first, LATENT)], r.osem.at[at + i])
        copy.start()
        stores.append(copy)
    at += len(late)
    for b in range(3, len(block)):
        copy = pltpu.make_async_copy(r.vecs.at[b], getattr(r, f"m{b}_vec"), r.osem.at[at + b])
        copy.start()
        stores.append(copy)
    gather.finish()
    def end(j, carry):
        t = lax.rem(me + j, n)
        remote(r.number, r.numbers.at[me], r.ns.at[j], r.nr.at[j], t).wait()
        return carry
    lax.fori_loop(1, n, end, 0)
    number.wait()
    for store in stores:
        store.wait()
    swap_wait(n, me, back, out, r.own.at[1], r.s2, r.r2)


def start(n, parts, cid, master, owners, locals_, level, land, source, x, segments, share_rows, bm=512):
    pad_rows = (share_rows + 31) // 32 * 32
    jobs = relay_plan(segments, share_rows)
    blocks = segments[-1][0] + 1
    count, edges, rows = n * sum(parts), source.shape[0], x.shape[1]
    V = pl.BlockSpec(memory_space=pltpu.VMEM)
    tables = [(n, p, 128) for p in parts]
    shapes = [(n, p, LATENT) for p in parts]
    inputs = dict(master=(master, V), owners=(owners, V), locals=(locals_, V), level=(level, ANY), land=(land, V), source=(source, V), x=(x, V))
    index = lambda *s: (shaped(*s, dtype=jnp.int32), V)
    low = lambda r: shaped(r, LATENT, dtype=BF16)
    outputs = dict(shares=(shaped(n, pad_rows, 128, dtype=BF16), ANY), numbers=(shaped(n, 8, 128), ANY))
    outputs |= dict(pos=index(edges, 2), pos_s=index(1, edges), pos_r=index(1, edges))
    outputs |= dict(want=index(count, 1), served=index(1, count))
    outputs |= dict(edge=(shaped(edges, LATENT), V), edge_low=(low(edges), V), sent=(low(edges), V), recv=(low(edges), V))
    outputs |= numbered("landed", [(shaped(*s, dtype=BF16), ANY) for s in shapes])
    outputs |= dict(node=(shaped(rows, LATENT), ANY), low=(low(rows), ANY), slots=(shaped(count, LATENT), ANY))
    made = {}
    for b, name, shape, _, _ in segments:
        if name in ("w_in", "w_out") and shape[1] == LATENT:
            made[f"m{b}{name[1:]}"] = (-(-shape[0] // 128) * 128, LATENT)
    outputs |= {name: (shaped(*shape, dtype=BF16), ANY) for name, shape in made.items()}
    outputs |= {f"m{b}_vec": (shaped(8, LATENT), ANY) for b in range(blocks)}
    scratch = swap_scratch(shapes, n)
    for name in ("ask", "asked"):
        scratch |= numbered(name, [pltpu.VMEM(s, jnp.int32) for s in tables])
    scratch |= dict(w=pltpu.VMEM((pad_rows, 128), BF16), number=pltpu.VMEM((8, 128), F32), _level=pltpu.VMEM(level.shape, jnp.int32))
    scratch |= dict(aown=DMA((len(parts),)), a1=DMA((len(parts), n)), b1=DMA((len(parts), n)), ns=DMA((n,)), nr=DMA((n,)), gown=DMA((3,)))
    for b, name in enumerate(("_p", "_g", "_e")):
        scratch |= {name + "_in": pltpu.VMEM(made[f"m{b}_in"], BF16), name + "_out": pltpu.VMEM(made[f"m{b}_out"], BF16), name + "_vec": pltpu.VMEM((8, LATENT), F32)}
    stage = sum(part[2] for job in jobs for part in job[5])
    late = sum(1 for job in jobs if job[0] > 2)
    scratch |= dict(_slots=pltpu.VMEM((count, LATENT), F32), _edge=pltpu.VMEM((edges, LATENT), F32), ssem=DMA((1,)))
    scratch |= dict(stage=pltpu.VMEM((stage, 128), BF16), lines=pltpu.VMEM((16 + 4 * LATENT + 64, 128), F32), made=pltpu.VMEM((late, LATENT, LATENT), BF16))
    scratch |= dict(vecs=pltpu.VMEM((blocks, 8, LATENT), F32), isem=DMA((sum(len(job[5]) for job in jobs),)), osem=DMA((9 + late + blocks,)))
    scratch |= dict(zs=DMA((2, 4)), zr=DMA((4,)), bs=DMA((28,)), br=DMA((28,)))
    for name in ("h", "c", "d"):
        scratch |= {name + "s": DMA((4, 2)), name + "r": DMA((4, 2))}
    return named_call(functools.partial(start_kernel, n, parts, jobs, bm), "start", inputs, outputs, scratch, cid=cid)


def accumulate(dst, src, rows):
    step = 80
    whole = rows // step
    def body(i, carry):
        at = pl.ds(pl.multiple_of(i * step, 8), step)
        dst[at] = dst[at] + src[at]
        return carry
    lax.fori_loop(0, whole, body, 0)
    if rows % step:
        at = pl.ds(whole * step, rows % step)
        dst[at] = dst[at] + src[at]


def where_am_i():
    me = lax.axis_index("dev")
    return me, me // 8, lax.rem(me // 4, 2), lax.rem(me // 2, 2), lax.rem(me, 2)


def device_at(z, y, x, c):
    return ((z * 2 + y) * 2 + x) * 2 + c


def plane_scratch(units, rows):
    upper = rows // 16 * 8
    lower = rows - upper
    F = lambda *s: pltpu.VMEM((units,) + s + (128,), F32)
    refs = dict(pL=F(4, rows), pR=F(4, rows), pYA=F(2, upper), pXA=F(upper), pXB=F(2, lower), pYB=F(lower))
    sems = {}
    for name, count in (("c", 4), ("a1", 2), ("a2", 1), ("b1", 2), ("b2", 1)):
        sems["p" + name + "s"] = DMA((units, count))
        sems["p" + name + "r"] = DMA((units, count))
    return refs | sems | dict(pl=DMA((units, 4)))


class PlaneSum:
    def __init__(self, r, rows):
        self.r, self.rows = r, rows
        self.upper = rows // 16 * 8
        self.A, self.B = pl.ds(0, self.upper), pl.ds(self.upper, rows - self.upper)
        _, z, y, x, c = where_am_i()
        self.y, self.x, self.c = y, x, c
        self.tx, self.ty, self.tc = device_at(z, y, 1 - x, c), device_at(z, 1 - y, x, c), device_at(z, y, x, 1 - c)
        self.own = y * 2 + x
        self.sends = []

    def send(self, *args):
        copy = remote(*args)
        copy.start()
        self.sends.append(copy)

    def fetch(self, u, source):
        r = self.r
        self.example = source(0, 0)
        for i in range(4):
            self.send(source(i, 1 - self.c), r.pR.at[u, i], r.pcs.at[u, i], r.pcr.at[u, i], self.tc)
            pltpu.make_async_copy(source(i, self.c), r.pL.at[u, i], r.pl.at[u, i]).start()

    def pair(self, u):
        r, L = self.r, self.r.pL
        for i in range(4):
            pltpu.make_async_copy(self.example, L.at[u, i], r.pl.at[u, i]).wait()
            remote(L.at[u, i], r.pR.at[u, i], r.pcs.at[u, i], r.pcr.at[u, i], self.tc).wait_recv()
            accumulate(L.at[u, i], r.pR.at[u, i], self.rows)
        for j in range(2):
            self.send(L.at[u, (1 - self.y) * 2 + j, self.A], r.pYA.at[u, j], r.pa1s.at[u, j], r.pa1r.at[u, j], self.ty)
            self.send(L.at[u, j * 2 + 1 - self.x, self.B], r.pXB.at[u, j], r.pb1s.at[u, j], r.pb1r.at[u, j], self.tx)

    def middle(self, u):
        r, L = self.r, self.r.pL
        up, low = self.upper, self.rows - self.upper
        for j in range(2):
            remote(L.at[u, 0, self.A], r.pYA.at[u, j], r.pa1s.at[u, j], r.pa1r.at[u, j], self.ty).wait_recv()
            accumulate(L.at[u, self.y * 2 + j, self.A], r.pYA.at[u, j], up)
        self.send(L.at[u, self.y * 2 + 1 - self.x, self.A], r.pXA.at[u], r.pa2s.at[u, 0], r.pa2r.at[u, 0], self.tx)
        for j in range(2):
            remote(L.at[u, 0, self.B], r.pXB.at[u, j], r.pb1s.at[u, j], r.pb1r.at[u, j], self.tx).wait_recv()
            accumulate(L.at[u, j * 2 + self.x, self.B], r.pXB.at[u, j], low)
        self.send(L.at[u, (1 - self.y) * 2 + self.x, self.B], r.pYB.at[u], r.pb2s.at[u, 0], r.pb2r.at[u, 0], self.ty)

    def last(self, u):
        r, L = self.r, self.r.pL
        remote(L.at[u, 0, self.A], r.pXA.at[u], r.pa2s.at[u, 0], r.pa2r.at[u, 0], self.tx).wait_recv()
        accumulate(L.at[u, self.own, self.A], r.pXA.at[u], self.upper)
        remote(L.at[u, 0, self.B], r.pYB.at[u], r.pb2s.at[u, 0], r.pb2r.at[u, 0], self.ty).wait_recv()
        accumulate(L.at[u, self.own, self.B], r.pYB.at[u], self.rows - self.upper)

    def result(self, u):
        return self.r.pL.at[u, self.own]

    def finish(self):
        for copy in self.sends:
            copy.wait_send()


def reduce_kernel(n, chunks, share_rows, lead, bm, r):
    me, z, y, x, c = where_am_i()
    greet(n, me)
    rows = chunks.rows
    plane = PlaneSum(r, rows)
    def by_plane(*goals):
        return jnp.where(z == 0, goals[0], jnp.where(z == 1, goals[1], jnp.where(z == 2, goals[2], goals[3])))
    goal = [by_plane(2, 3, 3, 1), by_plane(1, 2, 0, 0), by_plane(3, 0, 1, 2), z]

    def fetch(u):
        if u < 4:
            plane.fetch(u, lambda i, core: r.flat0.at[goal[u] * 8 + i * 2 + core])

    def along(u):
        at = lax.rem(z - goal[u] + 4, 4) - 1
        return remote(plane.result(u), r.zq.at[at], r.zqs.at[u], r.zqr.at[at], device_at(goal[u], y, x, c))

    fetch(0)
    clear(r.d_in, r.d_out, r.d_vec)
    plane.pair(0)
    def body(g_node, x_rows):
        encode_back_rows(pl.program_id(0) * bm, bm, r.served, several(r, "landed"), g_node, x_rows, r.p_in, r.p_out, r.p_vec, r.d_in, r.d_out, r.d_vec)
    pltpu.emit_pipeline(body, grid=(r.g_node.shape[0] // bm,), in_specs=[rows_block(bm), pl.BlockSpec((VARS, bm), lambda i: (0, i))], out_specs=[])(r.g_node, r.x)
    encode_pack(r.packed, r.d_in, r.d_out, r.d_vec)
    stores = Stores({0: r.flat0}, chunks, r.fsem)
    stores.put(r.packed, 0)
    stores.wait()
    fetch(1)
    plane.middle(0)
    for u in (1, 2, 3):
        fetch(u + 1)
        plane.pair(u)
        plane.last(u - 1)
        along(u - 1).start()
        plane.middle(u)
    plane.last(3)
    first = lax.rem(lead + share_rows * me, 8)
    r.both[0:8, :] = jnp.zeros((8, 128), F32)
    width = r.err.shape[1] // 128
    for j in range(8):
        r.both[8 + j : 9 + j, :] = r.err[:, 128 * j : 128 * (j + 1)] if j < width else jnp.zeros((1, 128), F32)
    own = plane.result(3)

    def piece(at, count):
        rows_here = pl.ds(at, count)
        v = own[rows_here] + r.zq[0, rows_here] + (r.zq[1, rows_here] + r.zq[2, rows_here])
        r.out[rows_here] = v
        row = at + lax.broadcasted_iota(jnp.int32, v.shape, 0)
        v = jnp.where((row >= first) & (row < first + share_rows), v, 0.0)
        v = v * v
        r.both[0:8, :] += jnp.sum(v.reshape(count // 8, 8, 128), axis=0)

    for at in range(3):
        remote(own, r.zq.at[at], r.zqs.at[at], r.zqr.at[at], plane.tc).wait_recv()
    step = 80
    def several_tiles(i, carry):
        piece(pl.multiple_of(i * step, 8), step)
        return carry
    lax.fori_loop(0, rows // step, several_tiles, 0)
    if rows % step:
        piece(rows // step * step, rows % step)
    q_own = pltpu.make_async_copy(r.both, r.all.at[me], r.own)
    q_own.start()
    def go(j, carry):
        t = lax.rem(me + j, n)
        remote(r.both, r.all.at[me], r.qs.at[j], r.qr.at[j], t).start()
        return carry
    lax.fori_loop(1, n, go, 0)
    plane.finish()
    for u in range(3):
        along(u).wait_send()
    def end(j, carry):
        t = lax.rem(me + j, n)
        remote(r.both, r.all.at[me], r.qs.at[j], r.qr.at[j], t).wait()
        return carry
    lax.fori_loop(1, n, end, 0)
    q_own.wait()
    r.sums[...] = jnp.sum(r.all[...], axis=0)


def reduce_gradient(n, chunks, flat, errors, share_rows, lead, encoder, cid, bm=512):
    served, landed, g_node, x, block = encoder
    V = pl.BlockSpec(memory_space=pltpu.VMEM)
    F = lambda *s: pltpu.VMEM(s + (128,), F32)
    rows = chunks.rows
    inputs = dict(flat_in=(flat, ANY), err=(errors, V), served=(served, V), g_node=(g_node, ANY), x=(x, ANY))
    inputs |= numbered("landed", [(v, V) for v in landed])
    inputs |= {name: (v, V) for name, v in zip(("p_in", "p_out", "p_vec"), block)}
    outputs = dict(flat0=(shaped(*flat.shape), ANY), out=(shaped(rows, 128), V), sums=(shaped(16, 128), V))
    scratch = plane_scratch(4, rows) | dict(zq=F(3, rows), zqs=DMA((3,)), zqr=DMA((3,)))
    scratch |= dict(both=F(16), all=F(n, 16), own=DMA, qs=DMA((n,)), qr=DMA((n,)), packed=packed_rows(VARS, 4), fsem=DMA((STORES,)))
    scratch |= sums_scratch("d", block[0].shape[0])
    body = functools.partial(reduce_kernel, n, chunks, share_rows, lead, bm)
    made = named_call(body, "reduce_gradient", inputs, outputs, scratch, aliases=dict(flat_in="flat0"), cid=cid)
    return made.out, jnp.sum(made.sums[:8]), jnp.sum(made.sums[8:])


def make_parts(capacity):
    whole = capacity // 16 * 16
    rest = (capacity - whole + 3) // 4 * 4
    return [rows for rows in (whole, rest) if rows]


def make_asks(edge_owners, edge_local, devices, parts):
    owner = edge_owners.reshape(-1)
    local = edge_local.reshape(-1)
    wants = owner.shape[0]
    order = jnp.arange(wants, dtype=jnp.int32)
    before = (owner[:, None] == owner[None, :]) & (order[None, :] < order[:, None])
    ranking = jnp.sum(before.astype(jnp.int32), axis=1)
    capacity = sum(parts)
    slots = jnp.arange(devices * capacity, dtype=jnp.int32)
    place = owner * capacity + ranking
    asking = jnp.sum(jnp.where(slots[:, None] == place[None, :], local[None, :] + 1, 0), axis=1) - 1
    position = owner * parts[0] + ranking
    if len(parts) > 1:
        position = jnp.where(ranking < parts[0], position, devices * parts[0] + owner * parts[1] + ranking - parts[0])
    return (position, asking.reshape(devices, capacity))


def widen(values, width):
    return jnp.pad(values, ((0, 0), (0, width - values.shape[1])))


def make_block(params):
    rows = params["w_in"].shape[0]
    w_in = jnp.pad(params["w_in"], ((0, -rows % 128), (0, 0)))
    w_out = widen(params["w_out"], (params["w_out"].shape[1] + 127) // 128 * 128)
    names = [name for name in ("b_in", "b_out", "gain", "shift") if name in params]
    vectors = [widen(params[name][None], LATENT) for name in names]
    vectors.append(jnp.zeros((8 - len(vectors), LATENT), jnp.bfloat16))
    return (w_in, w_out, jnp.concatenate(vectors).astype(jnp.float32))


def relaid_blocks(made, segments, share_rows):
    shares = made.shares
    def rows_of(first, last):
        parts = []
        while first < last:
            owner, low = divmod(first, share_rows)
            size = min(last - first, share_rows - low)
            parts.append(shares[owner, low : low + size])
            first += size
        return jnp.concatenate(parts) if len(parts) > 1 else parts[0]
    [(shape, begin, size)] = [(s, o, e) for _, name, s, o, e in segments if name == "w_out" and s[1] != LATENT]
    wide = shape[1]
    first, end = begin // 128, (begin + size) // 128
    w_out = widen(rows_of(first, end).reshape(shape), (wide + 127) // 128 * 128)
    bias = rows_of(end, end + (wide + 127) // 128).reshape(-1)[:wide, None].astype(jnp.float32)
    blocks = []
    for b in range(segments[-1][0] + 1):
        get = lambda part: getattr(made, f"m{b}{part}", w_out)
        blocks.append((get("_in"), get("_out"), get("_vec")))
    return blocks, bias


def local(
    inputs,
    targets,
    geometry,
    land_sea,
    level_mask,
    edge_owners,
    edge_local,
    step_count,
    master,
    first_moment,
    second_moment,
    ema,
):
    segments, total = layout(LATENT, VARS, GEO, LAYERS)
    devices = lax.axis_size("dev")
    share = master.shape[0]
    mine = devices == 32 and share % 128 == 0
    parts = make_parts(5 * edge_owners.shape[0] // (2 * devices))
    capacity = sum(parts)
    x = inputs.T
    geo = widen(geometry, 128)
    level, land = level_mask.T, land_sea[None, :]
    if mine:
        share_rows = share // 128
        begun = start(devices, parts, 1, master.reshape(share_rows, 128), edge_owners.T, edge_local.T, level, land, geo, x, segments, share_rows)
        blocks, bias = relaid_blocks(begun, segments, share_rows)
        want, served, pos, pos_s, pos_r = begun.want, begun.served, begun.pos, begun.pos_s, begun.pos_r
        count = jnp.sum(begun.numbers)
    else:
        position, asking = make_asks(edge_owners, edge_local, devices, parts)
        pos = position.reshape(-1, 2)
        pos_s, pos_r = pos[:, 0][None, :], pos[:, 1][None, :]
        ocean = (jnp.arange(VARS) < SEA_VARS).astype(jnp.int32)
        counted = jnp.sum(level_mask * (1 - land_sea[:, None] * ocean[None, :])).astype(jnp.float32)
        full_weights = lax.all_gather(master.astype(jnp.bfloat16), "dev", axis=0, tiled=True)
        whole = unpack(full_weights, segments)
        blocks = [make_block(b) for b in whole]
        bias = whole[-1]["b_out"][:, None].astype(jnp.float32)
        served = lax.all_to_all(asking, "dev", 0, 0, tiled=True)
        count = lax.psum(counted, "dev")
        served = jnp.concatenate([served[:, sum(parts[:i]) : sum(parts[: i + 1])].reshape(-1) for i in range(len(parts))])
        want = served[:, None]
        served = served[None, :]
    routes = (want, served, pos, pos_s, pos_r)
    if mine:
        done = [begun]
    else:
        done = [edge_forward(devices, parts, 3, geo, routes, blocks[2], blocks[0], inputs.shape[0], x=x, geo_block=blocks[1])]
    for k in range(1, LAYERS):
        f = done[-1]
        done.append(
            edge_forward(
                devices, parts, 4, f.edge, routes, blocks[2 + 2 * k], blocks[1 + 2 * k], inputs.shape[0],
                landed=several(f, "landed"), node=f.node, slots=f.slots,
            )
        )
    pieces = [4 * s for s in (VARS + LATENT + 4, GEO + LATENT + 4) + (3 * LATENT + LATENT + 4, 2 * LATENT + LATENT + 4) * LAYERS]
    lead = 4
    places = [0] + [lead + sum(pieces[: i + 1]) for i in range(len(pieces))]
    flat_rows = (lead + PARAMS // 128 + 15) // 16 * 16 + 8
    if mine:
        begins = [(lead + share_rows * d) // 8 * 8 for d in range(devices)]
        chunks = Chunks(begins, (share_rows + 6 + 15) // 16 * 16, [0, 32])
    else:
        chunks = Chunks([0], flat_rows, [0, 1])
    dec_at = places[-1]
    tail_at = dec_at + 4 * LATENT
    k = LAYERS - 1
    flat, g_node, *outgoing, d_out, d_first, d_bias, errors = turn(
        served, want, several(done[k], "landed"), done[k].node, x, targets.T, level, land, count.reshape(1, 1),
        blocks[3 + 2 * k], blocks[-1], bias, chunks, places[3 + 2 * k], dec_at,
    )
    flats = {len(chunks.cuts) - 2: flat}
    tail = jnp.concatenate([d_first[0], d_out[:, :VARS].reshape(-1), d_bias[:VARS, 0]])
    tail_rows = flat_rows - tail_at
    tail = jnp.pad(tail, (0, tail_rows * 128 - tail.shape[0])).reshape(tail_rows, 128)
    g_edge, landed = None, None
    for k in reversed(range(LAYERS)):
        more = {}
        if k == LAYERS - 1:
            more |= dict(outgoing=outgoing, g_node=g_node, tail=tail, tail_at=tail_at)
        else:
            more |= dict(
                node=(landed, g_slots, done[k].slots, done[k + 1].sums_s, g_node, done[k].low, done[k + 1].sums, blocks[3 + 2 * k]),
                node_at=places[3 + 2 * k],
            )
        if k == 0:
            more |= dict(geo=(geo, blocks[1]), geo_at=places[1])
        f = done[k]
        b = edge_backward(
            devices, parts, 5 + (LAYERS - 1 - k), (f.edge_low, f.sent, f.recv), routes, blocks[2 + 2 * k], chunks, flats, places[2 + 2 * k],
            g_edge=g_edge, **more,
        )
        g_edge, landed = b.edge_prev, several(b, "landed")
        g_slots = b.g_slots
        if k < LAYERS - 1:
            g_node = b.g_prev
    if mine:
        encoder = (served, landed, g_node, x, blocks[0])
        summed, squares, error_sum = reduce_gradient(devices, chunks, flats[0], errors, share_rows, lead, encoder, 2)
        skip = lax.rem(lead + share_rows * lax.axis_index("dev"), 8)
        own_grad = lax.dynamic_slice_in_dim(summed, skip, share_rows).reshape(-1)
    else:
        flat = encode_backward(served, landed, g_node, x, blocks[0], chunks, flats[0])
        own_grad = lax.psum_scatter(flat[0, lead : lead + PARAMS // 128].reshape(-1), "dev", scatter_dimension=0, tiled=True)
        error_sum, squares = lax.psum((jnp.sum(errors), jnp.sum(own_grad * own_grad)), "dev")
    grad_norm = jnp.sqrt(squares)
    loss = error_sum / jnp.maximum(count, 1.0)
    clipped = own_grad * jnp.minimum(1.0, clip_limit / grad_norm)
    step = step_count[0].astype(jnp.float32)
    new_first = beta_one * first_moment + (1.0 - beta_one) * clipped
    new_second = beta_two * second_moment + (1.0 - beta_two) * clipped * clipped
    first_hat = new_first / (1.0 - beta_one**step)
    second_hat = new_second / (1.0 - beta_two**step)
    new_master = master - learn_rate * (
        first_hat / (jnp.sqrt(second_hat) + adam_eps) + decay_rate * master
    )
    new_ema = ema_keep * ema + (1.0 - ema_keep) * new_master
    return (new_master, new_first, new_second, new_ema, loss, grad_norm)


def solution(mesh):
    in_specs = (
        P("dev", None),
        P("dev", None),
        P("dev", None),
        P("dev"),
        P("dev", None),
        P("dev", None),
        P("dev", None),
        P(),
        P("dev"),
        P("dev"),
        P("dev"),
        P("dev"),
    )
    out_specs = (P("dev"), P("dev"), P("dev"), P("dev"), P(), P())
    return jax.shard_map(local, mesh=mesh, in_specs=in_specs, out_specs=out_specs, check_vma=False)
```

```python
import functools
import types

import jax
import jax.numpy as jnp
import numpy as np
from jax import lax
from jax.experimental import pallas as pl
from jax.experimental.pallas import tpu as pltpu
from jax.sharding import PartitionSpec as P

LATENT = 512
VARS = 227
GEO = 4
SEA_VARS = 4
LAYERS = 3
PARAMS = 6545408


norm_eps = 1e-05
clip_limit = 0.01
beta_one = 0.9
beta_two = 0.999
adam_eps = 1e-08
learn_rate = 0.03
decay_rate = 0.1
ema_keep = 0.9


def layout(width, variables, geometry, layers):
    shapes = [(variables, width, True), (geometry, width, True)]
    for k in range(layers):
        shapes.append((3 * width, width, True))
        shapes.append((2 * width, width, True))
    shapes.append((width, variables, False))
    segments = []
    offset = 0
    for block_id, (fan_in, fan_out, normed) in enumerate(shapes):
        members = [
            ("w_in", (fan_in, width)),
            ("b_in", (width,)),
            ("w_out", (width, fan_out)),
            ("b_out", (fan_out,)),
        ]
        if normed:
            members = members + [("gain", (fan_out,)), ("shift", (fan_out,))]
        for part_name, part_shape in members:
            entries = int(np.prod(part_shape))
            segments.append((block_id, part_name, part_shape, offset, entries))
            offset += entries
    return (segments, offset)


def unpack(flat, segments):
    blocks = [dict() for k in range(segments[-1][0] + 1)]
    for block_id, part_name, part_shape, offset, entries in segments:
        blocks[block_id][part_name] = flat[offset : offset + entries].reshape(part_shape)
    return blocks


MESH = pl.DeviceIdType.MESH

def remote(src, dst, send, recv, target):
    return pltpu.make_async_remote_copy(src, dst, send, recv, device_id=(target,), device_id_type=MESH)

def greet(n, me):
    barrier = pltpu.get_barrier_semaphore()
    def hello(j, c):
        pl.semaphore_signal(barrier, inc=1, device_id=(lax.rem(me + j, n),), device_id_type=MESH)
        return c
    lax.fori_loop(1, n, hello, 0)
    pl.semaphore_wait(barrier, n - 1)


F32, BF16 = jnp.float32, jnp.bfloat16
VMEM_LIMIT = 60 << 20
ANY = pl.BlockSpec(memory_space=pl.ANY)
DMA = pltpu.SemaphoreType.DMA


def mm(a, b):
    return jnp.dot(a, b, preferred_element_type=F32)


def mm_nt(a, b):
    return lax.dot_general(a, b, (((1,), (1,)), ((), ())), preferred_element_type=F32)


def mm_tn(a, b):
    return lax.dot_general(a, b, (((0,), (0,)), ((), ())), preferred_element_type=F32)


def contract(a, b, left, right):
    return lax.dot_general(a, b, (((left,), (right,)), ((), ())), preferred_element_type=F32)


def col(v):
    return jnp.sum(v, axis=0, keepdims=True)


def pick(slots, first, rows):
    r = first + lax.broadcasted_iota(jnp.int32, (slots.shape[0], rows), 1)
    return jnp.where(slots == r, 1.0, 0.0).astype(BF16)


def place(slots, first, rows):
    r = first + lax.broadcasted_iota(jnp.int32, (rows, slots.shape[1]), 0)
    return jnp.where(slots == r, 1.0, 0.0).astype(BF16)


def first_half(us, w_in, vec):
    pre = vec[0:1, :]
    at = 0
    for u in us:
        pre = pre + mm(u, w_in[at : at + u.shape[1], :])
        at += u.shape[1]
    return pre


def activate(pre):
    sigma = jax.nn.sigmoid(pre)
    return sigma, (pre * sigma).astype(BF16)


def normalize(post):
    centred = post - jnp.mean(post, axis=-1, keepdims=True)
    inv = lax.rsqrt(jnp.mean(centred * centred, axis=-1, keepdims=True) + norm_eps)
    return centred * inv, inv


def second_half(act, w_out, vec):
    return normalize(mm(act, w_out[...]) + vec[1:2, :])


def scale_shift(hat, vec):
    return hat * vec[2:3, :] + vec[3:4, :]


def norm_back(g, hat, inv, vec, d_vec):
    if d_vec is not None:
        d_vec[2:3, :] += col(g * hat)
        d_vec[3:4, :] += col(g)
    s = g * vec[2:3, :]
    post = inv * (
        s - jnp.mean(s, axis=-1, keepdims=True) - hat * jnp.mean(s * hat, axis=-1, keepdims=True)
    )
    return post.astype(BF16)


def act_back(low, pre, sigma, w_out):
    g_act = mm_nt(low, w_out[...])
    return (g_act * sigma * (1.0 + pre * (1.0 - sigma))).astype(BF16)


def weight_sums(us, act, low, g_pre, d_in, d_out, d_vec):
    d_out[...] += mm_tn(act, low)
    d_vec[1:2, : low.shape[1]] += col(low.astype(F32))
    d_vec[0:1, :] += col(g_pre.astype(F32))
    at = 0
    for u in us:
        d_in[at : at + u.shape[1], :] += mm_tn(u, g_pre)
        at += u.shape[1]


def pack_matrix(packed, ref, rows, at):
    for j in range(4):
        packed[pl.ds(at + j, rows, stride=4), :] = ref[:rows, 128 * j : 128 * (j + 1)]
    return at + 4 * rows


def pack(packed, lead, rows_in, d_in, d_out, d_vec):
    def vector(i, at):
        for j in range(4):
            packed[at + j : at + j + 1, :] = d_vec[i : i + 1, 128 * j : 128 * (j + 1)]
        return at + 4
    at = pack_matrix(packed, d_in, rows_in, lead)
    at = vector(0, at)
    at = pack_matrix(packed, d_out, d_out.shape[0], at)
    for i in (1, 2, 3):
        at = vector(i, at)


def clear(*refs):
    for ref in refs:
        ref[...] = jnp.zeros_like(ref)


def spec(shape, fixed=True):
    if fixed:
        return pl.BlockSpec(shape, lambda i: (0,) * len(shape))
    return pl.BlockSpec(shape, lambda i: (i,) + (0,) * (len(shape) - 1))


def params(**more):
    return pltpu.CompilerParams(vmem_limit_bytes=VMEM_LIMIT, **more)


def shaped(*shape, dtype=F32):
    return jax.ShapeDtypeStruct(shape, dtype)


class Chunks:
    def __init__(self, begins, rows, cuts):
        self.begins, self.rows, self.cuts = begins, rows, cuts

    def shape(self, group):
        return (self.cuts[group + 1] - self.cuts[group], self.rows, 128)

    def pieces(self, at, size):
        found = []
        for group in range(len(self.cuts) - 1):
            for owner in range(self.cuts[group], self.cuts[group + 1]):
                begin = self.begins[owner]
                low, high = max(at, begin), min(at + size, begin + self.rows)
                if low < high:
                    found.append((group, owner - self.cuts[group], low - begin, low - at, high - low))
        return found

    def groups(self, *places):
        return sorted({p[0] for at, size in places for p in self.pieces(at, size)})


class Stores:
    def __init__(self, refs, chunks, sem):
        self.refs, self.chunks, self.sem, self.copies = refs, chunks, sem, []

    def put(self, packed, at):
        for group, owner, row, skip, size in self.chunks.pieces(at, packed.shape[0]):
            source = packed.at[pl.ds(skip, size)]
            copy = pltpu.make_async_copy(source, self.refs[group].at[owner, pl.ds(row, size)], self.sem.at[len(self.copies)])
            copy.start()
            self.copies.append(copy)

    def wait(self):
        for copy in self.copies:
            copy.wait()


STORES = 48


def flat_refs(r, groups):
    return {group: getattr(r, f"flat{group}") for group in groups}


def mlp_sums(rows_in, wide=LATENT):
    return [pltpu.VMEM((rows_in, LATENT), F32), pltpu.VMEM((LATENT, wide), F32), pltpu.VMEM((8, LATENT), F32)]


def packed_rows(rows_in, lead=0):
    return pltpu.VMEM((lead + 4 * rows_in + 4 * LATENT + 16, 128), F32)


def named_call(body, name, inputs, outputs, scratch, aliases=None, cid=None):
    names = [*inputs, *outputs, *scratch]
    aliases = {list(inputs).index(i): list(outputs).index(o) for i, o in (aliases or {}).items()}
    def kernel(*refs):
        body(types.SimpleNamespace(**dict(zip(names, refs))))
    more = {} if cid is None else dict(collective_id=cid, has_side_effects=True)
    values = pl.pallas_call(
        kernel,
        out_shape=tuple(shape for shape, _ in outputs.values()),
        in_specs=[s for _, s in inputs.values()],
        out_specs=tuple(s for _, s in outputs.values()),
        scratch_shapes=list(scratch.values()),
        input_output_aliases=aliases,
        compiler_params=params(**more),
        name=name,
    )(*[v for v, _ in inputs.values()])
    return types.SimpleNamespace(**dict(zip(outputs, values)))


def swap_start(n, me, srcs, dsts, own, ssem, rsem):
    for i, (src, dst) in enumerate(zip(srcs, dsts)):
        pltpu.make_async_copy(src.at[me], dst.at[me], own.at[i]).start()
    def go(j, c):
        t = lax.rem(me + j, n)
        for i, (src, dst) in enumerate(zip(srcs, dsts)):
            remote(src.at[t], dst.at[me], ssem.at[i, j], rsem.at[i, j], t).start()
        return c
    lax.fori_loop(1, n, go, 0)


def swap_wait(n, me, srcs, dsts, own, ssem, rsem):
    def end(j, c):
        t = lax.rem(me + j, n)
        for i, (src, dst) in enumerate(zip(srcs, dsts)):
            remote(src.at[t], dst.at[me], ssem.at[i, j], rsem.at[i, j], t).wait()
        return c
    lax.fori_loop(1, n, end, 0)
    for i, (src, dst) in enumerate(zip(srcs, dsts)):
        pltpu.make_async_copy(src.at[me], dst.at[me], own.at[i]).wait()


def several(r, name):
    return [getattr(r, f"{name}{i}") for i in range(4) if hasattr(r, f"{name}{i}")]


def numbered(name, values):
    return {f"{name}{i}": value for i, value in enumerate(values)}


def slot_rows(refs):
    rows = [ref[...].reshape(ref.shape[0] * ref.shape[1], ref.shape[2]) for ref in refs]
    return rows[0] if len(rows) == 1 else jnp.concatenate(rows, axis=0)


def put_slot_rows(refs, rows):
    at = 0
    for ref in refs:
        size = ref.shape[0] * ref.shape[1]
        ref[...] = rows[at : at + size, :].reshape(ref.shape)
        at += size


def greet_start(n, me):
    barrier = pltpu.get_barrier_semaphore()
    def hello(j, c):
        pl.semaphore_signal(barrier, inc=1, device_id=(lax.rem(me + j, n),), device_id_type=MESH)
        return c
    lax.fori_loop(1, n, hello, 0)


def greet_wait(n):
    pl.semaphore_wait(pltpu.get_barrier_semaphore(), n - 1)


class Loads:
    def __init__(self, r, sem):
        self.r, self.sem, self.copies = r, sem, {}

    def start(self, *names):
        for name in names:
            copy = pltpu.make_async_copy(getattr(self.r, name), getattr(self.r, "_" + name), self.sem.at[len(self.copies)])
            copy.start()
            self.copies[name] = copy

    def wait(self, *names):
        for name in names:
            self.copies[name].wait()


def store_all(r, sem, *names):
    copies = [pltpu.make_async_copy(getattr(r, "_" + name), getattr(r, name), sem.at[i]) for i, name in enumerate(names)]
    for copy in copies:
        copy.start()
    return copies


def same_rows(want, served):
    return jnp.where((want[...] == served[...]) & (want[...] >= 0), 1.0, 0.0).astype(BF16)


def swap_scratch(shapes, n):
    parts = len(shapes)
    scratch = dict(own=DMA((2, parts)), s1=DMA((parts, n)), r1=DMA((parts, n)), s2=DMA((parts, n)), r2=DMA((parts, n)))
    for name in ("away", "here", "back"):
        scratch |= numbered(name, [pltpu.VMEM(shape, BF16) for shape in shapes])
    return scratch


def held(prefix, block):
    return {prefix + part: pltpu.VMEM(a.shape, a.dtype) for part, a in zip(("_in", "_out", "_vec"), block)}


def weights(prefix, block):
    return {prefix + part: (a, ANY) for part, a in zip(("_in", "_out", "_vec"), block)}


def rows_block(bm, width=LATENT):
    return pl.BlockSpec((bm, width), lambda i: (i, 0))


def edge_kernel(n, first, bm, r):
    me = lax.axis_index("dev")
    greet_start(n, me)
    loads = Loads(r, r.lsem)
    node_weights = ["p_in", "p_out", "p_vec"]
    landing = [name for name in vars(r) if name.startswith("landed_in")]
    early = node_weights + ([] if first else [*landing, "slots_in"])
    late = ["e_in", "e_out", "e_vec"] + (["g_in", "g_out", "g_vec"] if first else [])
    loads.start(*early)
    loads.start(*late)
    loads.wait(*early)
    count = r.want.shape[0]
    if first:
        asked = contract(pick(r.want[...], 0, r.x.shape[1]), r.x[...], 1, 1).astype(BF16)
        pre = contract(asked, r._p_in[:VARS, :], 1, 0) + r._p_vec[0:1, :]
    else:
        landed = slot_rows(several(r, "_landed_in"))
        got = mm(same_rows(r.want, r.served), landed).astype(BF16)
        r._sums_s[...] = got
        old = r._slots_in[...]
        pre = first_half([old.astype(BF16), got], r._p_in, r._p_vec)
    _, act = activate(pre)
    hat, _ = second_half(act, r._p_out, r._p_vec)
    slots = scale_shift(hat, r._p_vec)
    if not first:
        slots = old + slots
    r._slots[...] = slots
    away, here, back, out = (several(r, name) for name in ("away", "here", "back", "landed"))
    put_slot_rows(away, slots.astype(BF16))
    greet_wait(n)
    swap_start(n, me, away, here, r.own.at[0], r.s1, r.r1)
    stores = store_all(r, r.ssem, *(["slots"] if first else ["slots", "sums_s"]))
    loads.wait(*late)
    if first:
        _, act = activate(first_half([r.source[...]], r._g_in, r._g_vec))
        hat, _ = second_half(act, r._g_out, r._g_vec)
        r._edge[...] = scale_shift(hat, r._g_vec)
    else:
        r._edge[...] = r.source[...]
    e = r._edge[...].astype(BF16)
    r.edge_low[...] = e
    r._pre[...] = first_half([e], r._e_in, r._e_vec)
    if first:
        def body(node, low):
            i = pl.program_id(0)
            u = r.x[:, pl.ds(pl.multiple_of(i * bm, bm), bm)]
            _, act = activate(contract(u, r._p_in[:VARS, :], 0, 0) + r._p_vec[0:1, :])
            hat, _ = second_half(act, r._p_out, r._p_vec)
            new = scale_shift(hat, r._p_vec)
            node[...] = new
            low[...] = new.astype(BF16)
        pltpu.emit_pipeline(body, grid=(r.node.shape[0] // bm,), in_specs=[], out_specs=[rows_block(bm)] * 2)(r.node, r.low)
    else:
        def body(node_in, node, low, sums):
            i = pl.program_id(0)
            got = mm(place(r.served[...], i * bm, bm), slot_rows(several(r, "_landed_in"))).astype(BF16)
            sums[...] = got
            old = node_in[...]
            _, act = activate(first_half([old.astype(BF16), got], r._p_in, r._p_vec))
            hat, _ = second_half(act, r._p_out, r._p_vec)
            new = old + scale_shift(hat, r._p_vec)
            node[...] = new
            low[...] = new.astype(BF16)
        pltpu.emit_pipeline(body, grid=(r.node.shape[0] // bm,), in_specs=[rows_block(bm)], out_specs=[rows_block(bm)] * 3)(r.node_in, r.node, r.low, r.sums)
    pick_s, pick_r = pick(r.pos[:, 0:1], 0, count), pick(r.pos[:, 1:2], 0, count)
    put_r = place(r.pos_r[...], 0, count)
    swap_wait(n, me, away, here, r.own.at[0], r.s1, r.r1)
    rows = slot_rows(here)
    s = mm(pick_s, rows).astype(BF16)
    v = mm(pick_r, rows).astype(BF16)
    pre = r._pre[...] + mm(s, r._e_in[LATENT : 2 * LATENT, :]) + mm(v, r._e_in[2 * LATENT :, :])
    _, act = activate(pre)
    hat, _ = second_half(act, r._e_out, r._e_vec)
    new = r._edge[...] + scale_shift(hat, r._e_vec)
    put_slot_rows(back, mm(put_r, new.astype(BF16)).astype(BF16))
    swap_start(n, me, back, out, r.own.at[1], r.s2, r.r2)
    r.edge[...] = new
    r.sent[...], r.recv[...] = s, v
    for store in stores:
        store.wait()
    swap_wait(n, me, back, out, r.own.at[1], r.s2, r.r2)


def edge_forward(n, parts, cid, source, routes, edge_block, node_block, rows, x=None, geo_block=None, landed=None, node=None, slots=None, bm=512):
    first = x is not None
    want, served, pos, pos_s, pos_r = routes
    count = want.shape[0]
    edges = source.shape[0]
    shapes = [(n, p, LATENT) for p in parts]
    V = pl.BlockSpec(memory_space=pltpu.VMEM)
    inputs = dict(source=(source, V), want=(want, V), served=(served, V), pos=(pos, V), pos_r=(pos_r, V))
    inputs |= weights("p", node_block) | weights("e", edge_block)
    scratch = held("_p", node_block) | held("_e", edge_block) | swap_scratch(shapes, n)
    scratch |= dict(_slots=pltpu.VMEM((count, LATENT), F32), _edge=pltpu.VMEM((edges, LATENT), F32), _pre=pltpu.VMEM((edges, LATENT), F32), lsem=DMA((12,)), ssem=DMA((2,)))
    low = lambda r: shaped(r, LATENT, dtype=BF16)
    outputs = dict(edge=(shaped(edges, LATENT), V), edge_low=(low(edges), V), sent=(low(edges), V), recv=(low(edges), V)) | numbered("landed", [(shaped(*s, dtype=BF16), ANY) for s in shapes])
    outputs |= dict(node=(shaped(rows, LATENT), ANY), low=(low(rows), ANY), slots=(shaped(count, LATENT), ANY))
    if first:
        inputs |= dict(x=(x, V)) | weights("g", geo_block)
        scratch |= held("_g", geo_block)
    else:
        inputs |= numbered("landed_in", [(v, ANY) for v in landed]) | dict(node_in=(node, ANY), slots_in=(slots, ANY))
        scratch |= numbered("_landed_in", [pltpu.VMEM(s, BF16) for s in shapes]) | dict(_slots_in=pltpu.VMEM((count, LATENT), F32), _sums_s=pltpu.VMEM((count, LATENT), BF16))
        outputs |= dict(sums=(low(rows), ANY), sums_s=(low(count), ANY))
    return named_call(functools.partial(edge_kernel, n, first, bm), "edge_forward", inputs, outputs, scratch, cid=cid)


def turn_kernel(parts, bm, chunks, group, at, dec_at, served, want, *refs):
    landed, refs = refs[:parts], refs[parts:]
    flat, g_prev, *outs = refs[13 : 15 + parts]
    node, x, target, level, land, count, w_in, w_out, vec, c_in, c_out, c_vec, c_bias = refs[:13]
    d_out_o, d_first_o, d_bias_o, err_o, packed, packed2, d_in, d_out, d_vec, e_in, e_out, e_vec, e_bias, err, acc, sem = refs[13 + 2 + parts:]
    i = pl.program_id(0)
    @pl.when(i == 0)
    def _():
        clear(d_in, d_out, d_vec, e_in, e_out, e_vec, e_bias, err, acc)
    got = mm(place(served[...], i * bm, bm), slot_rows(landed)).astype(BF16)
    old = node[...]
    low = old.astype(BF16)
    pre = first_half([low, got], w_in, vec)
    sigma, act = activate(pre)
    hat, inv = second_half(act, w_out, vec)
    u = (old + scale_shift(hat, vec)).astype(BF16)
    c_pre = first_half([u], c_in, c_vec)
    c_sigma, c_act = activate(c_pre)
    wide = c_out.shape[1]
    post = contract(c_out[...], c_act, 0, 1)
    sea = (lax.broadcasted_iota(jnp.int32, (VARS, 1), 0) < SEA_VARS).astype(F32)
    mask = level[...].astype(F32) * (1.0 - sea * land[...].astype(F32))
    residual = x[...].astype(F32) + (post[:VARS, :] + c_bias[...]) - target[...]
    divisor = jnp.maximum(count[...], 1.0)
    err[...] += jnp.sum(mask * residual * residual, axis=0, keepdims=True)
    g = 2.0 * mask * residual / divisor
    g_low = jnp.concatenate([g, jnp.zeros((wide - VARS, bm), F32)], axis=0).astype(BF16)
    e_bias[...] += jnp.sum(g_low.astype(F32), axis=1, keepdims=True)
    e_out[...] += contract(c_act, g_low, 0, 1)
    g_act = contract(g_low, c_out[...], 0, 1)
    c_g = (g_act * c_sigma * (1.0 + c_pre * (1.0 - c_sigma))).astype(BF16)
    e_vec[0:1, :] += col(c_g.astype(F32))
    e_in[...] += mm_tn(u, c_g)
    g_node = mm_nt(c_g, c_in[...])
    g_post = norm_back(g_node, hat, inv, vec, d_vec)
    g_pre = act_back(g_post, pre, sigma, w_out)
    weight_sums([low, got], act, g_post, g_pre, d_in, d_out, d_vec)
    g_prev[...] = g_node + mm_nt(g_pre, w_in[:LATENT, :])
    acc[...] += mm(pick(want[...], i * bm, bm), mm_nt(g_pre, w_in[LATENT:, :]).astype(BF16))
    @pl.when(i == pl.num_programs(0) - 1)
    def _():
        put_slot_rows(outs, acc[...].astype(BF16))
        d_out_o[...] = e_out[...]
        d_first_o[...] = e_vec[0:1, :]
        d_bias_o[...] = e_bias[...]
        err_o[...] = err[...]
        stores = Stores({group: flat}, chunks, sem)
        pack_matrix(packed2, e_in, LATENT, 0)
        stores.put(packed2, dec_at)
        pack(packed, 0, 2 * LATENT, d_in, d_out, d_vec)
        stores.put(packed, at)
        stores.wait()


def turn(served, want, landed, node, x, target, level, land, count, block, dec, bias, chunks, at, dec_at, bm=512):
    rows = node.shape[0]
    slots = want.shape[0]
    wide = dec[1].shape[1]
    [group] = chunks.groups((at, dec_at + 4 * LATENT - at))
    v = lambda height: pl.BlockSpec((height, bm), lambda i: (0, i))
    part = [spec(p.shape) for p in landed]
    return pl.pallas_call(
        functools.partial(turn_kernel, len(landed), bm, chunks, group, at, dec_at),
        grid=(rows // bm,),
        out_shape=(shaped(*chunks.shape(group)), shaped(rows, LATENT), *(shaped(*p.shape, dtype=BF16) for p in landed), shaped(LATENT, wide), shaped(1, LATENT), shaped(wide, 1), shaped(1, bm)),
        in_specs=[spec((1, slots)), spec((slots, 1)), *part, spec((bm, LATENT), False), v(VARS), v(VARS), v(VARS), v(1), spec((1, 1))] + [spec(a.shape) for a in (*block, *dec, bias)],
        out_specs=(ANY, spec((bm, LATENT), False), *part, spec((LATENT, wide)), spec((1, LATENT)), spec((wide, 1)), spec((1, bm))),
        scratch_shapes=[packed_rows(2 * LATENT), pltpu.VMEM((4 * LATENT, 128), F32)] + mlp_sums(2 * LATENT) + mlp_sums(LATENT, wide) + [pltpu.VMEM((wide, 1), F32), pltpu.VMEM((1, bm), F32), pltpu.VMEM((slots, LATENT), F32), DMA((STORES,))],
        compiler_params=params(),
        name="turn",
    )(served, want, *landed, node, x, target, level, land, count, *block, *dec, bias)


def gather_slots(r, bm):
    clear(r._g_slots)
    def body(g_node):
        chosen = pick(r.want[...], pl.program_id(0) * bm, bm)
        g = g_node[...]
        high = g.astype(BF16)
        rest = g - high.astype(F32)
        middle = rest.astype(BF16)
        small = (rest - middle.astype(F32)).astype(BF16)
        r._g_slots[...] += mm(chosen, high) + (mm(chosen, middle) + mm(chosen, small))
    pltpu.emit_pipeline(body, grid=(r.g_node.shape[0] // bm,), in_specs=[rows_block(bm)], out_specs=[])(r.g_node)


def edge_back_kernel(n, chunks, groups, at, node_at, geo_at, tail_at, bm, r):
    me = lax.axis_index("dev")
    greet_start(n, me)
    loads = Loads(r, r.lsem)
    nodes = node_at is not None
    landing = [name for name in vars(r) if name.startswith("landed_in")]
    early = ["p_in", "p_out", "p_vec", *landing, "g_slots_in", "slots_in", "sums_s"] if nodes else []
    late = ["e_in", "e_out", "e_vec"] + (["g_in", "g_out", "g_vec"] if geo_at is not None else [])
    loads.start(*early)
    loads.start(*late)
    flats = Stores(flat_refs(r, groups), chunks, r.fsem)
    stores = [flats]
    if tail_at is not None:
        flats.put(r.tail, tail_at)
    count = r.want.shape[0]
    here, back, out = (several(r, name) for name in ("here", "back", "landed"))
    if nodes:
        loads.wait(*early)
        us = [r._slots_in[...].astype(BF16), r._sums_s[...]]
        pre = first_half(us, r._p_in, r._p_vec)
        sigma, act = activate(pre)
        hat, inv = second_half(act, r._p_out, r._p_vec)
        g = r._g_slots_in[...] + mm(same_rows(r.want, r.served), slot_rows(several(r, "_landed_in")))
        low = norm_back(g, hat, inv, r._p_vec, None)
        g_pre = act_back(low, pre, sigma, r._p_out)
        source = several(r, "away")
        put_slot_rows(source, mm_nt(g_pre, r._p_in[LATENT:, :]).astype(BF16))
    else:
        source = several(r, "outgoing")
    greet_wait(n)
    swap_start(n, me, source, here, r.own.at[0], r.s1, r.r1)
    if nodes:
        r._g_slots[...] = g + mm_nt(g_pre, r._p_in[:LATENT, :])
        stores += store_all(r, r.ssem, "g_slots")
        clear(r.n_in, r.n_out, r.n_vec)
    clear(r.d_in, r.d_out, r.d_vec)
    def node_rows(first, last):
        if not nodes:
            return
        def body(g_node, low_in, sums_in, g_prev):
            i = first + pl.program_id(0)
            us = [low_in[...], sums_in[...]]
            pre = first_half(us, r._p_in, r._p_vec)
            sigma, act = activate(pre)
            hat, inv = second_half(act, r._p_out, r._p_vec)
            g = g_node[...] + mm(place(r.served[...], i * bm, bm), slot_rows(several(r, "_landed_in")))
            low = norm_back(g, hat, inv, r._p_vec, r.n_vec)
            g_pre = act_back(low, pre, sigma, r._p_out)
            weight_sums(us, act, low, g_pre, r.n_in, r.n_out, r.n_vec)
            g_prev[...] = g + mm_nt(g_pre, r._p_in[:LATENT, :])
        block = pl.BlockSpec((bm, LATENT), lambda i: (first + i, 0))
        pltpu.emit_pipeline(body, grid=(last - first,), in_specs=[block] * 3, out_specs=[block])(r.g_node, r.low, r.sums, r.g_prev)
    blocks = r.g_node.shape[0] // bm if nodes else 0
    node_rows(0, blocks // 2)
    if not nodes:
        gather_slots(r, bm)
    loads.wait(*late)
    us = [r.edge_low[...], r.sent[...], r.recv[...]]
    pre = first_half(us, r._e_in, r._e_vec)
    sigma, act = activate(pre)
    hat, inv = second_half(act, r._e_out, r._e_vec)
    pick_r = pick(r.pos[:, 1:2], 0, count)
    put_s, put_r = place(r.pos_s[...], 0, count), place(r.pos_r[...], 0, count)
    swap_wait(n, me, source, here, r.own.at[0], r.s1, r.r1)
    g = mm(pick_r, slot_rows(here))
    if hasattr(r, "g_edge"):
        g = r.g_edge[...] + g
    low = norm_back(g, hat, inv, r._e_vec, r.d_vec)
    g_pre = act_back(low, pre, sigma, r._e_out)
    s = mm_nt(g_pre, r._e_in[LATENT : 2 * LATENT, :]).astype(BF16)
    v = mm_nt(g_pre, r._e_in[2 * LATENT :, :]).astype(BF16)
    put_slot_rows(back, (mm(put_s, s) + mm(put_r, v)).astype(BF16))
    swap_start(n, me, back, out, r.own.at[1], r.s2, r.r2)
    prev = g + mm_nt(g_pre, r._e_in[:LATENT, :])
    r.edge_prev[...] = prev
    weight_sums(us, act, low, g_pre, r.d_in, r.d_out, r.d_vec)
    pack(r.packed, 0, 3 * LATENT, r.d_in, r.d_out, r.d_vec)
    flats.put(r.packed, at)
    if geo_at is not None:
        c_us = [r.geo[...]]
        c_pre = first_half(c_us, r._g_in, r._g_vec)
        c_sigma, c_act = activate(c_pre)
        c_hat, c_inv = second_half(c_act, r._g_out, r._g_vec)
        clear(r.c_in, r.c_out, r.c_vec)
        c_low = norm_back(prev, c_hat, c_inv, r._g_vec, r.c_vec)
        c_g = act_back(c_low, c_pre, c_sigma, r._g_out)
        weight_sums(c_us, c_act, c_low, c_g, r.c_in, r.c_out, r.c_vec)
        pack(r.c_packed, 0, GEO, r.c_in, r.c_out, r.c_vec)
        flats.put(r.c_packed, geo_at)
    node_rows(blocks // 2, blocks)
    if nodes:
        pack(r.n_packed, 0, 2 * LATENT, r.n_in, r.n_out, r.n_vec)
        flats.put(r.n_packed, node_at)
    if not nodes:
        stores += store_all(r, r.ssem, "g_slots")
    swap_wait(n, me, back, out, r.own.at[1], r.s2, r.r2)
    for store in stores:
        store.wait()


def sums_scratch(prefix, rows_in):
    return dict(zip((prefix + "_in", prefix + "_out", prefix + "_vec"), mlp_sums(rows_in)))


def edge_backward(n, parts, cid, ins, routes, edge_block, chunks, flats, at, g_edge=None, outgoing=None, g_node=None, tail=None, tail_at=None, node=None, node_at=None, geo=None, geo_at=None, bm=512):
    want, served, pos, pos_s, pos_r = routes
    count = want.shape[0]
    edges = pos.shape[0]
    shapes = [(n, p, LATENT) for p in parts]
    V = pl.BlockSpec(memory_space=pltpu.VMEM)
    inputs = dict(want=(want, V), served=(served, V), pos=(pos, V), pos_s=(pos_s, V), pos_r=(pos_r, V))
    inputs |= {name: (value, V) for name, value in zip(("edge_low", "sent", "recv"), ins)} | weights("e", edge_block)
    scratch = held("_e", edge_block) | swap_scratch(shapes, n) | sums_scratch("d", 3 * LATENT)
    scratch |= dict(packed=packed_rows(3 * LATENT), lsem=DMA((16,)), ssem=DMA((2,)), fsem=DMA((STORES,)))
    outputs = dict(edge_prev=(shaped(edges, LATENT), V)) | numbered("landed", [(shaped(*s, dtype=BF16), ANY) for s in shapes])
    places = [(at, scratch["packed"].shape[0])]
    if g_edge is not None:
        inputs |= dict(g_edge=(g_edge, V))
    if outgoing is not None:
        inputs |= numbered("outgoing", [(v, ANY) for v in outgoing]) | dict(g_node=(g_node, ANY))
        outputs |= dict(g_slots=(shaped(count, LATENT), ANY))
        scratch |= dict(_g_slots=pltpu.VMEM((count, LATENT), F32))
    if tail is not None:
        inputs |= dict(tail=(tail, V))
        places.append((tail_at, tail.shape[0]))
    if node is not None:
        inputs |= numbered("landed_in", [(v, ANY) for v in node[0]])
        for name, value in zip(("g_slots_in", "slots_in", "sums_s", "g_node", "low", "sums"), node[1:]):
            inputs[name] = (value, ANY)
        inputs |= weights("p", node[7])
        scratch |= held("_p", node[7]) | sums_scratch("n", 2 * LATENT)
        f = pltpu.VMEM((count, LATENT), F32)
        scratch |= numbered("_landed_in", [pltpu.VMEM(s, BF16) for s in shapes]) | dict(n_packed=packed_rows(2 * LATENT), _g_slots_in=f, _slots_in=f, _g_slots=f, _sums_s=pltpu.VMEM((count, LATENT), BF16))
        rows = node[4].shape[0]
        places.append((node_at, scratch["n_packed"].shape[0]))
        outputs |= dict(g_prev=(shaped(rows, LATENT), ANY), g_slots=(shaped(count, LATENT), ANY))
    if geo is not None:
        inputs |= dict(geo=(geo[0], V)) | weights("g", geo[1])
        scratch |= held("_g", geo[1]) | sums_scratch("c", geo[0].shape[1]) | dict(c_packed=packed_rows(GEO))
        places.append((geo_at, scratch["c_packed"].shape[0]))
    groups = chunks.groups(*places)
    aliases = {}
    for group in groups:
        outputs[f"flat{group}"] = (shaped(*chunks.shape(group)), ANY)
        if group in flats:
            inputs[f"flat{group}_in"] = (flats[group], ANY)
            aliases[f"flat{group}_in"] = f"flat{group}"
    body = functools.partial(edge_back_kernel, n, chunks, groups, at, node_at, geo_at, tail_at, bm)
    made = named_call(body, "edge_backward", inputs, outputs, scratch, aliases=aliases, cid=cid)
    flats.update(flat_refs(made, groups))
    return made


def encode_back_rows(first, bm, served, landed, g_node, x, w_in, w_out, vec, d_in, d_out, d_vec):
    pre = contract(x[...], w_in[:VARS, :], 0, 0) + vec[0:1, :]
    sigma, act = activate(pre)
    hat, inv = second_half(act, w_out, vec)
    g = g_node[...] + mm(place(served[...], first, bm), slot_rows(landed))
    g_post = norm_back(g, hat, inv, vec, d_vec)
    g_pre = act_back(g_post, pre, sigma, w_out)
    weight_sums([], act, g_post, g_pre, d_in, d_out, d_vec)
    d_in[:VARS, :] += mm(x[...], g_pre)


def encode_pack(packed, d_in, d_out, d_vec):
    packed[0:4, :] = jnp.zeros((4, 128), F32)
    pack(packed, 4, VARS, d_in, d_out, d_vec)


def encode_back_kernel(parts, bm, chunks, served, *refs):
    landed, refs = refs[:parts], refs[parts:]
    g_node, x, w_in, w_out, vec, flat_in, flat, packed, d_in, d_out, d_vec, sem = refs
    i = pl.program_id(0)
    @pl.when(i == 0)
    def _():
        clear(d_in, d_out, d_vec)
    encode_back_rows(i * bm, bm, served, landed, g_node, x, w_in, w_out, vec, d_in, d_out, d_vec)
    @pl.when(i == pl.num_programs(0) - 1)
    def _():
        encode_pack(packed, d_in, d_out, d_vec)
        stores = Stores({0: flat}, chunks, sem)
        stores.put(packed, 0)
        stores.wait()


def encode_backward(served, landed, g_node, x, block, chunks, flat, bm=512):
    k, rows = block[0].shape[0], x.shape[1]
    slots = served.shape[1]
    return pl.pallas_call(
        functools.partial(encode_back_kernel, len(landed), bm, chunks),
        grid=(rows // bm,),
        out_shape=shaped(*flat.shape),
        in_specs=[spec((1, slots)), *(spec(p.shape) for p in landed), spec((bm, LATENT), False), pl.BlockSpec((VARS, bm), lambda i: (0, i))] + [spec(a.shape) for a in block] + [ANY],
        out_specs=ANY,
        scratch_shapes=[packed_rows(VARS, 4)] + mlp_sums(k) + [DMA((STORES,))],
        input_output_aliases={6 + len(landed): 0},
        compiler_params=params(),
        name="encode_backward",
    )(served, *landed, g_node, x, *block, flat)


def relay_plan(segments, share_rows):
    jobs = []
    for block_id, part_name, part_shape, offset, entries in segments:
        if part_name not in ("w_in", "w_out") or part_shape[1] != LATENT:
            continue
        for first in range(0, part_shape[0], LATENT):
            rows = min(LATENT, part_shape[0] - first)
            follow = 0
            if first + rows == part_shape[0]:
                follow = 1 if part_name == "w_in" else 3
            begin = offset // 128 + 4 * first
            end = begin + 4 * (rows + follow)
            parts = []
            at = begin
            while at < end:
                owner, low = divmod(at, share_rows)
                size = min(end - at, share_rows - low)
                base = low // 16 * 16
                span = (low + size - base + 15) // 16 * 16
                parts.append((owner, base, span, low - base, at - begin))
                at += size
            jobs.append((block_id, part_name, first, rows, follow, parts))
    return jobs


class Relay:
    def __init__(self, r, shares):
        self.r, self.shares, self.loads, self.at, self.count = r, shares, {}, 0, 0

    def load(self, job):
        r, mine = self.r, []
        for owner, base, span, skip, to in job[5]:
            place = pl.ds(self.at, span)
            copy = pltpu.make_async_copy(self.shares.at[owner, pl.ds(base, span)], r.stage.at[place], r.isem.at[self.count])
            copy.start()
            mine.append((copy, place, span, skip, to))
            self.at += span
            self.count += 1
        self.loads[job[:3]] = mine

    def run(self, job, target, vec):
        _, name, _, rows, follow, _ = job
        lines = self.r.lines
        for copy, place, span, skip, to in self.loads[job[:3]]:
            copy.wait()
            lines[pl.ds(16 + to - skip, span), :] = self.r.stage[place, :].astype(F32)
        for j in range(4):
            target[:rows, 128 * j : 128 * (j + 1)] = lines[pl.ds(16 + j, rows, stride=4), :].astype(BF16)
        if rows < target.shape[0]:
            target[rows:, :] = jnp.zeros((target.shape[0] - rows, LATENT), BF16)
        for i in range(follow):
            row = i if name == "w_in" else i + 1
            for j in range(4):
                p = 16 + 4 * (rows + i) + j
                vec[row : row + 1, 128 * j : 128 * (j + 1)] = lines[p : p + 1, :]


class Gather:
    def __init__(self, r, w, o):
        self.r, self.w, self.o = r, w, o
        self.me, z, y, x, c = where_am_i()
        self.z = z
        half = w.shape[0] // 2
        self.A, self.B = pl.ds(0, half), pl.ds(half, half)
        self.dev = lambda zz, fy=0, fx=0: device_at(zz, y + fy * (1 - 2 * y), x + fx * (1 - 2 * x), c)
        self.tx, self.ty, self.tc = self.dev(z, 0, 1), self.dev(z, 1, 0), device_at(z, y, x, 1 - c)
        self.up, self.down = self.dev(jnp.minimum(z + 1, 3)), self.dev(jnp.maximum(z - 1, 0))
        def by_plane(*v):
            return jnp.where(z == 0, v[0], jnp.where(z == 1, v[1], jnp.where(z == 2, v[2], v[3])))
        self.come = [z, by_plane(1, 0, 1, 2), by_plane(2, 2, 3, 1), by_plane(3, 3, 0, 0)]
        self.go = [z, by_plane(1, 0, 1, 2), by_plane(2, 2, 0, 0), by_plane(3, 3, 3, 1)]
        self.sends, self.spreads, self.sibling, self.seen = [], {}, [], 0

    def send(self, *args):
        copy = remote(*args)
        copy.start()
        self.sends.append(copy)

    def share(self, k, part=None):
        ref = self.w if k == 0 else self.o.at[self.dev(self.go[k])]
        return ref if part is None else ref.at[part]

    def to_sibling(self, slot, part=None, source=None):
        r, i = self.r, len(self.sibling)
        ref = self.o.at[slot] if part is None else self.o.at[slot, part]
        self.send(ref if source is None else source, ref, r.bs.at[i], r.br.at[i], self.tc)
        self.sibling.append(part)

    def from_sibling(self, count):
        r = self.r
        for i in range(self.seen, count):
            part = self.sibling[i]
            ref = self.o.at[self.me] if part is None else self.o.at[self.me, part]
            remote(ref, ref, r.bs.at[i], r.br.at[i], self.tc).wait_recv()
        self.seen = count

    def onward(self, i, wait=False):
        r, z, plane = self.r, self.z, self.come[i]
        slot = self.dev(plane)
        source = self.w if i == 0 else self.o.at[slot]
        for d, target, here in ((0, self.up, (plane <= z) & (z < 3)), (1, self.down, (plane >= z) & (z > 0))):
            @pl.when(here)
            def _():
                copy = remote(source, self.o.at[slot], r.zs.at[d, i], r.zr.at[plane], target)
                if wait:
                    copy.wait_send()
                else:
                    copy.start()

    def begin(self):
        r = self.r
        self.mine = pltpu.make_async_copy(self.w, self.o.at[self.me], r.gown.at[0])
        self.mine.start()
        self.spread(0)
        self.onward(0)
        self.to_sibling(self.me, None, self.w)

    def arrive(self, i):
        slot = self.dev(self.come[i])
        remote(self.w, self.o.at[slot], self.r.zs.at[0, i], self.r.zr.at[self.come[i]], self.tc).wait_recv()
        self.onward(i)
        self.to_sibling(slot)

    def spread(self, k, when=None):
        r, slot = self.r, self.dev(self.go[k])
        copies = [
            remote(self.share(k, self.A), self.o.at[slot, self.A], r.hs.at[k, 0], r.hr.at[k, 0], self.tx),
            remote(self.share(k, self.B), self.o.at[slot, self.B], r.hs.at[k, 1], r.hr.at[k, 1], self.ty),
        ]
        if when is None:
            for copy in copies:
                copy.start()
        else:
            @pl.when(when)
            def _():
                for copy in copies:
                    copy.start()
        self.spreads[k] = copies

    def second(self, k):
        r, o, zz = self.r, self.o, self.go[k]
        s, sx, sy = self.dev(zz), self.dev(zz, 0, 1), self.dev(zz, 1, 0)
        self.send(self.share(k, self.A), o.at[s, self.A], r.cs.at[k, 0], r.cr.at[k, 0], self.ty)
        self.send(self.share(k, self.B), o.at[s, self.B], r.ds.at[k, 0], r.dr.at[k, 0], self.tx)
        remote(o.at[sx, self.A], o.at[sx, self.A], r.hs.at[k, 0], r.hr.at[k, 0], self.tx).wait_recv()
        self.send(o.at[sx, self.A], o.at[sx, self.A], r.cs.at[k, 1], r.cr.at[k, 1], self.ty)
        remote(o.at[sy, self.B], o.at[sy, self.B], r.hs.at[k, 1], r.hr.at[k, 1], self.ty).wait_recv()
        self.send(o.at[sy, self.B], o.at[sy, self.B], r.ds.at[k, 1], r.dr.at[k, 1], self.tx)
        self.to_sibling(sx, self.A)
        self.to_sibling(sy, self.B)

    def third(self, k):
        r, o, zz = self.r, self.o, self.go[k]
        for slot, part, ss, rr, i, target in (
            (self.dev(zz, 1, 0), self.A, r.cs, r.cr, 0, self.ty),
            (self.dev(zz, 0, 1), self.B, r.ds, r.dr, 0, self.tx),
            (self.dev(zz, 1, 1), self.A, r.cs, r.cr, 1, self.ty),
            (self.dev(zz, 1, 1), self.B, r.ds, r.dr, 1, self.tx),
        ):
            remote(o.at[slot, part], o.at[slot, part], ss.at[k, i], rr.at[k, i], target).wait_recv()
            self.to_sibling(slot, part)

    def finish(self):
        for i in range(4):
            self.onward(i, True)
        for copy in self.sends + [copy for pair in self.spreads.values() for copy in pair]:
            copy.wait_send()


def as_column(row):
    return jnp.transpose(jnp.broadcast_to(row, (128, row.shape[1])))[:, 0:1]


def route(n, parts, r):
    owner = jnp.concatenate([r.owners[0:1, :], r.owners[1:2, :]], axis=1)
    local = jnp.concatenate([r.locals[0:1, :], r.locals[1:2, :]], axis=1)
    wants, edges = owner.shape[1], r.owners.shape[1]
    earlier = lax.broadcasted_iota(jnp.int32, (wants, wants), 0) < lax.broadcasted_iota(jnp.int32, (wants, wants), 1)
    same = (as_column(owner) == owner) & earlier
    rank = jnp.sum(jnp.where(same, 1.0, 0.0), axis=0, keepdims=True).astype(jnp.int32)
    position = owner * parts[0] + rank
    if len(parts) > 1:
        position = jnp.where(rank < parts[0], position, n * parts[0] + owner * parts[1] + rank - parts[0])
    r.pos_s[...], r.pos_r[...] = position[:, :edges], position[:, edges:]
    column = as_column(position)
    r.pos[:, 0:1], r.pos[:, 1:2] = column[:edges, :], column[edges:, :]
    slots = n * sum(parts)
    match = lax.broadcasted_iota(jnp.int32, (slots, wants), 0) == position
    asking = jnp.sum(jnp.where(match, local.astype(F32) + 1.0, 0.0), axis=1, keepdims=True).astype(jnp.int32) - 1
    put_slot_rows(several(r, "ask"), jnp.broadcast_to(asking, (slots, 128)))


def count_mask(r):
    sea = (lax.broadcasted_iota(jnp.int32, (VARS, 1), 0) < SEA_VARS).astype(jnp.int32)
    total = jnp.zeros((1, 128), F32)
    for i in range(r.level.shape[1] // 128):
        at = slice(128 * i, 128 * (i + 1))
        total += col((r._level[:, at] * (1 - sea * r.land[:, at])).astype(F32))
    r.number[...] = jnp.zeros_like(r.number)
    r.number[0:1, :] = total


def start_kernel(n, parts, jobs, bm, r):
    me = lax.axis_index("dev")
    gather = Gather(r, r.w, r.shares)
    greet_start(n, me)
    mask = pltpu.make_async_copy(r.level, r._level, r.gown.at[2])
    mask.start()
    rows = r.master.shape[0]
    r.w[rows // 16 * 16 :, :] = jnp.zeros_like(r.w[rows // 16 * 16 :, :])
    r.w[:rows, :] = r.master[...].astype(BF16)
    greet_wait(n)
    gather.begin()
    route(n, parts, r)
    asks, asked = several(r, "ask"), several(r, "asked")
    swap_start(n, me, asks, asked, r.aown, r.a1, r.b1)
    mask.wait()
    count_mask(r)
    number = pltpu.make_async_copy(r.number, r.numbers.at[me], r.gown.at[1])
    number.start()
    def go(j, carry):
        t = lax.rem(me + j, n)
        remote(r.number, r.numbers.at[me], r.ns.at[j], r.nr.at[j], t).start()
        return carry
    lax.fori_loop(1, n, go, 0)
    gather.second(0)
    gather.arrive(1)
    gather.spread(1)
    gather.arrive(2)
    gather.third(0)
    gather.second(1)
    gather.spread(2, gather.z < 2)
    gather.arrive(3)
    gather.spread(2, gather.z >= 2)
    gather.third(1)
    gather.second(2)
    swap_wait(n, me, asks, asked, r.aown, r.a1, r.b1)
    columns = slot_rows(asked)
    r.want[...] = columns[:, 0:1]
    r.served[...] = jnp.transpose(columns)[0:1, :]
    chosen = pick(r.want[...], 0, r.x.shape[1])
    rows = contract(chosen, r.x[...], 1, 1).astype(BF16)
    gather.spread(3)
    gather.third(2)
    plane_0 = len(gather.sibling)
    gather.second(3)
    gather.from_sibling(plane_0)
    gather.mine.wait()
    relay = Relay(r, r.shares)
    block = [[job for job in jobs if job[0] == b] for b in range(jobs[-1][0] + 1)]
    names = ["p", "g", "e"]
    def into(b):
        for job in block[b]:
            target = getattr(r, "_" + names[b] + job[1][1:])
            relay.run(job, target.at[pl.ds(job[2], min(LATENT, target.shape[0] - job[2]))], getattr(r, "_" + names[b] + "_vec"))
    for vec in (r._p_vec, r._g_vec, r._e_vec, r.vecs):
        vec[...] = jnp.zeros_like(vec)
    for job in block[0]:
        relay.load(job)
    into(0)
    for job in block[1]:
        relay.load(job)
    _, act = activate(contract(rows, r._p_in[:VARS, :], 1, 0) + r._p_vec[0:1, :])
    hat, _ = second_half(act, r._p_out, r._p_vec)
    r._slots[...] = scale_shift(hat, r._p_vec)
    away, here, back, out = (several(r, name) for name in ("away", "here", "back", "landed"))
    put_slot_rows(away, r._slots[...].astype(BF16))
    swap_start(n, me, away, here, r.own.at[0], r.s1, r.r1)
    stores = store_all(r, r.ssem, "slots")
    def body(node, low):
        i = pl.program_id(0)
        u = r.x[:, pl.ds(pl.multiple_of(i * bm, bm), bm)]
        _, act = activate(contract(u, r._p_in[:VARS, :], 0, 0) + r._p_vec[0:1, :])
        hat, _ = second_half(act, r._p_out, r._p_vec)
        new = scale_shift(hat, r._p_vec)
        node[...] = new
        low[...] = new.astype(BF16)
    pltpu.emit_pipeline(body, grid=(r.node.shape[0] // bm,), in_specs=[], out_specs=[rows_block(bm)] * 2)(r.node, r.low)
    gather.third(3)
    gather.from_sibling(len(gather.sibling))
    for b in range(2, len(block)):
        for job in block[b]:
            relay.load(job)
    into(1)
    into(2)
    _, act = activate(first_half([r.source[...]], r._g_in, r._g_vec))
    hat, _ = second_half(act, r._g_out, r._g_vec)
    r._edge[...] = scale_shift(hat, r._g_vec)
    e = r._edge[...].astype(BF16)
    r.edge_low[...] = e
    count = r.want.shape[0]
    pre = first_half([e], r._e_in, r._e_vec)
    pick_s, pick_r = pick(r.pos[:, 0:1], 0, count), pick(r.pos[:, 1:2], 0, count)
    put_r = place(r.pos_r[...], 0, count)
    kept = [f"m{b}{part}" for b in range(3) for part in ("_in", "_out", "_vec")]
    for i, name in enumerate(kept):
        b, part = int(name[1]), name[2:]
        copy = pltpu.make_async_copy(getattr(r, "_" + names[b] + part), getattr(r, name), r.osem.at[i])
        copy.start()
        stores.append(copy)
    swap_wait(n, me, away, here, r.own.at[0], r.s1, r.r1)
    rows = slot_rows(here)
    s = mm(pick_s, rows).astype(BF16)
    v = mm(pick_r, rows).astype(BF16)
    pre = pre + mm(s, r._e_in[LATENT : 2 * LATENT, :]) + mm(v, r._e_in[2 * LATENT :, :])
    _, act = activate(pre)
    hat, _ = second_half(act, r._e_out, r._e_vec)
    new = r._edge[...] + scale_shift(hat, r._e_vec)
    put_slot_rows(back, mm(put_r, new.astype(BF16)).astype(BF16))
    swap_start(n, me, back, out, r.own.at[1], r.s2, r.r2)
    r.edge[...] = new
    r.sent[...], r.recv[...] = s, v
    at = len(kept)
    late = [job for b in range(3, len(block)) for job in block[b]]
    for i, job in enumerate(late):
        b, name, first = job[:3]
        relay.run(job, r.made.at[i], r.vecs.at[b])
        copy = pltpu.make_async_copy(r.made.at[i], getattr(r, f"m{b}{name[1:]}").at[pl.ds(first, LATENT)], r.osem.at[at + i])
        copy.start()
        stores.append(copy)
    at += len(late)
    for b in range(3, len(block)):
        copy = pltpu.make_async_copy(r.vecs.at[b], getattr(r, f"m{b}_vec"), r.osem.at[at + b])
        copy.start()
        stores.append(copy)
    gather.finish()
    def end(j, carry):
        t = lax.rem(me + j, n)
        remote(r.number, r.numbers.at[me], r.ns.at[j], r.nr.at[j], t).wait()
        return carry
    lax.fori_loop(1, n, end, 0)
    number.wait()
    for store in stores:
        store.wait()
    swap_wait(n, me, back, out, r.own.at[1], r.s2, r.r2)


def start(n, parts, cid, master, owners, locals_, level, land, source, x, segments, share_rows, bm=512):
    pad_rows = (share_rows + 31) // 32 * 32
    jobs = relay_plan(segments, share_rows)
    blocks = segments[-1][0] + 1
    count, edges, rows = n * sum(parts), source.shape[0], x.shape[1]
    V = pl.BlockSpec(memory_space=pltpu.VMEM)
    tables = [(n, p, 128) for p in parts]
    shapes = [(n, p, LATENT) for p in parts]
    inputs = dict(master=(master, V), owners=(owners, V), locals=(locals_, V), level=(level, ANY), land=(land, V), source=(source, V), x=(x, V))
    index = lambda *s: (shaped(*s, dtype=jnp.int32), V)
    low = lambda r: shaped(r, LATENT, dtype=BF16)
    outputs = dict(shares=(shaped(n, pad_rows, 128, dtype=BF16), ANY), numbers=(shaped(n, 8, 128), ANY))
    outputs |= dict(pos=index(edges, 2), pos_s=index(1, edges), pos_r=index(1, edges))
    outputs |= dict(want=index(count, 1), served=index(1, count))
    outputs |= dict(edge=(shaped(edges, LATENT), V), edge_low=(low(edges), V), sent=(low(edges), V), recv=(low(edges), V))
    outputs |= numbered("landed", [(shaped(*s, dtype=BF16), ANY) for s in shapes])
    outputs |= dict(node=(shaped(rows, LATENT), ANY), low=(low(rows), ANY), slots=(shaped(count, LATENT), ANY))
    made = {}
    for b, name, shape, _, _ in segments:
        if name in ("w_in", "w_out") and shape[1] == LATENT:
            made[f"m{b}{name[1:]}"] = (-(-shape[0] // 128) * 128, LATENT)
    outputs |= {name: (shaped(*shape, dtype=BF16), ANY) for name, shape in made.items()}
    outputs |= {f"m{b}_vec": (shaped(8, LATENT), ANY) for b in range(blocks)}
    scratch = swap_scratch(shapes, n)
    for name in ("ask", "asked"):
        scratch |= numbered(name, [pltpu.VMEM(s, jnp.int32) for s in tables])
    scratch |= dict(w=pltpu.VMEM((pad_rows, 128), BF16), number=pltpu.VMEM((8, 128), F32), _level=pltpu.VMEM(level.shape, jnp.int32))
    scratch |= dict(aown=DMA((len(parts),)), a1=DMA((len(parts), n)), b1=DMA((len(parts), n)), ns=DMA((n,)), nr=DMA((n,)), gown=DMA((3,)))
    for b, name in enumerate(("_p", "_g", "_e")):
        scratch |= {name + "_in": pltpu.VMEM(made[f"m{b}_in"], BF16), name + "_out": pltpu.VMEM(made[f"m{b}_out"], BF16), name + "_vec": pltpu.VMEM((8, LATENT), F32)}
    stage = sum(part[2] for job in jobs for part in job[5])
    late = sum(1 for job in jobs if job[0] > 2)
    scratch |= dict(_slots=pltpu.VMEM((count, LATENT), F32), _edge=pltpu.VMEM((edges, LATENT), F32), ssem=DMA((1,)))
    scratch |= dict(stage=pltpu.VMEM((stage, 128), BF16), lines=pltpu.VMEM((16 + 4 * LATENT + 64, 128), F32), made=pltpu.VMEM((late, LATENT, LATENT), BF16))
    scratch |= dict(vecs=pltpu.VMEM((blocks, 8, LATENT), F32), isem=DMA((sum(len(job[5]) for job in jobs),)), osem=DMA((9 + late + blocks,)))
    scratch |= dict(zs=DMA((2, 4)), zr=DMA((4,)), bs=DMA((28,)), br=DMA((28,)))
    for name in ("h", "c", "d"):
        scratch |= {name + "s": DMA((4, 2)), name + "r": DMA((4, 2))}
    return named_call(functools.partial(start_kernel, n, parts, jobs, bm), "start", inputs, outputs, scratch, cid=cid)


def accumulate(dst, src, rows):
    step = 80
    whole = rows // step
    def body(i, carry):
        at = pl.ds(pl.multiple_of(i * step, 8), step)
        dst[at] = dst[at] + src[at]
        return carry
    lax.fori_loop(0, whole, body, 0)
    if rows % step:
        at = pl.ds(whole * step, rows % step)
        dst[at] = dst[at] + src[at]


def where_am_i():
    me = lax.axis_index("dev")
    return me, me // 8, lax.rem(me // 4, 2), lax.rem(me // 2, 2), lax.rem(me, 2)


def device_at(z, y, x, c):
    return ((z * 2 + y) * 2 + x) * 2 + c


def plane_scratch(units, rows):
    upper = rows // 16 * 8
    lower = rows - upper
    F = lambda *s: pltpu.VMEM((units,) + s + (128,), F32)
    refs = dict(pL=F(4, rows), pR=F(4, rows), pYA=F(2, upper), pXA=F(upper), pXB=F(2, lower), pYB=F(lower))
    sems = {}
    for name, count in (("c", 4), ("a1", 2), ("a2", 1), ("b1", 2), ("b2", 1)):
        sems["p" + name + "s"] = DMA((units, count))
        sems["p" + name + "r"] = DMA((units, count))
    return refs | sems | dict(pl=DMA((units, 4)))


class PlaneSum:
    def __init__(self, r, rows):
        self.r, self.rows = r, rows
        self.upper = rows // 16 * 8
        self.A, self.B = pl.ds(0, self.upper), pl.ds(self.upper, rows - self.upper)
        _, z, y, x, c = where_am_i()
        self.y, self.x, self.c = y, x, c
        self.tx, self.ty, self.tc = device_at(z, y, 1 - x, c), device_at(z, 1 - y, x, c), device_at(z, y, x, 1 - c)
        self.own = y * 2 + x
        self.sends = []

    def send(self, *args):
        copy = remote(*args)
        copy.start()
        self.sends.append(copy)

    def fetch(self, u, source):
        r = self.r
        self.example = source(0, 0)
        for i in range(4):
            self.send(source(i, 1 - self.c), r.pR.at[u, i], r.pcs.at[u, i], r.pcr.at[u, i], self.tc)
            pltpu.make_async_copy(source(i, self.c), r.pL.at[u, i], r.pl.at[u, i]).start()

    def pair(self, u):
        r, L = self.r, self.r.pL
        for i in range(4):
            pltpu.make_async_copy(self.example, L.at[u, i], r.pl.at[u, i]).wait()
            remote(L.at[u, i], r.pR.at[u, i], r.pcs.at[u, i], r.pcr.at[u, i], self.tc).wait_recv()
            accumulate(L.at[u, i], r.pR.at[u, i], self.rows)
        for j in range(2):
            self.send(L.at[u, (1 - self.y) * 2 + j, self.A], r.pYA.at[u, j], r.pa1s.at[u, j], r.pa1r.at[u, j], self.ty)
            self.send(L.at[u, j * 2 + 1 - self.x, self.B], r.pXB.at[u, j], r.pb1s.at[u, j], r.pb1r.at[u, j], self.tx)

    def middle(self, u):
        r, L = self.r, self.r.pL
        up, low = self.upper, self.rows - self.upper
        for j in range(2):
            remote(L.at[u, 0, self.A], r.pYA.at[u, j], r.pa1s.at[u, j], r.pa1r.at[u, j], self.ty).wait_recv()
            accumulate(L.at[u, self.y * 2 + j, self.A], r.pYA.at[u, j], up)
        self.send(L.at[u, self.y * 2 + 1 - self.x, self.A], r.pXA.at[u], r.pa2s.at[u, 0], r.pa2r.at[u, 0], self.tx)
        for j in range(2):
            remote(L.at[u, 0, self.B], r.pXB.at[u, j], r.pb1s.at[u, j], r.pb1r.at[u, j], self.tx).wait_recv()
            accumulate(L.at[u, j * 2 + self.x, self.B], r.pXB.at[u, j], low)
        self.send(L.at[u, (1 - self.y) * 2 + self.x, self.B], r.pYB.at[u], r.pb2s.at[u, 0], r.pb2r.at[u, 0], self.ty)

    def last(self, u):
        r, L = self.r, self.r.pL
        remote(L.at[u, 0, self.A], r.pXA.at[u], r.pa2s.at[u, 0], r.pa2r.at[u, 0], self.tx).wait_recv()
        accumulate(L.at[u, self.own, self.A], r.pXA.at[u], self.upper)
        remote(L.at[u, 0, self.B], r.pYB.at[u], r.pb2s.at[u, 0], r.pb2r.at[u, 0], self.ty).wait_recv()
        accumulate(L.at[u, self.own, self.B], r.pYB.at[u], self.rows - self.upper)

    def result(self, u):
        return self.r.pL.at[u, self.own]

    def finish(self):
        for copy in self.sends:
            copy.wait_send()


def reduce_kernel(n, chunks, share_rows, lead, bm, r):
    me, z, y, x, c = where_am_i()
    greet(n, me)
    rows = chunks.rows
    plane = PlaneSum(r, rows)
    def by_plane(*goals):
        return jnp.where(z == 0, goals[0], jnp.where(z == 1, goals[1], jnp.where(z == 2, goals[2], goals[3])))
    goal = [by_plane(2, 3, 3, 1), by_plane(1, 2, 0, 0), by_plane(3, 0, 1, 2), z]

    def fetch(u):
        if u < 4:
            plane.fetch(u, lambda i, core: r.flat0.at[goal[u] * 8 + i * 2 + core])

    def along(u):
        at = lax.rem(z - goal[u] + 4, 4) - 1
        return remote(plane.result(u), r.zq.at[at], r.zqs.at[u], r.zqr.at[at], device_at(goal[u], y, x, c))

    fetch(0)
    clear(r.d_in, r.d_out, r.d_vec)
    plane.pair(0)
    def body(g_node, x_rows):
        encode_back_rows(pl.program_id(0) * bm, bm, r.served, several(r, "landed"), g_node, x_rows, r.p_in, r.p_out, r.p_vec, r.d_in, r.d_out, r.d_vec)
    pltpu.emit_pipeline(body, grid=(r.g_node.shape[0] // bm,), in_specs=[rows_block(bm), pl.BlockSpec((VARS, bm), lambda i: (0, i))], out_specs=[])(r.g_node, r.x)
    encode_pack(r.packed, r.d_in, r.d_out, r.d_vec)
    stores = Stores({0: r.flat0}, chunks, r.fsem)
    stores.put(r.packed, 0)
    stores.wait()
    fetch(1)
    plane.middle(0)
    for u in (1, 2, 3):
        fetch(u + 1)
        plane.pair(u)
        plane.last(u - 1)
        along(u - 1).start()
        plane.middle(u)
    plane.last(3)
    first = lax.rem(lead + share_rows * me, 8)
    r.both[0:8, :] = jnp.zeros((8, 128), F32)
    width = r.err.shape[1] // 128
    for j in range(8):
        r.both[8 + j : 9 + j, :] = r.err[:, 128 * j : 128 * (j + 1)] if j < width else jnp.zeros((1, 128), F32)
    own = plane.result(3)

    def piece(at, count):
        rows_here = pl.ds(at, count)
        v = own[rows_here] + r.zq[0, rows_here] + (r.zq[1, rows_here] + r.zq[2, rows_here])
        r.out[rows_here] = v
        row = at + lax.broadcasted_iota(jnp.int32, v.shape, 0)
        v = jnp.where((row >= first) & (row < first + share_rows), v, 0.0)
        v = v * v
        r.both[0:8, :] += jnp.sum(v.reshape(count // 8, 8, 128), axis=0)

    for at in range(3):
        remote(own, r.zq.at[at], r.zqs.at[at], r.zqr.at[at], plane.tc).wait_recv()
    step = 80
    def several_tiles(i, carry):
        piece(pl.multiple_of(i * step, 8), step)
        return carry
    lax.fori_loop(0, rows // step, several_tiles, 0)
    if rows % step:
        piece(rows // step * step, rows % step)
    q_own = pltpu.make_async_copy(r.both, r.all.at[me], r.own)
    q_own.start()
    def go(j, carry):
        t = lax.rem(me + j, n)
        remote(r.both, r.all.at[me], r.qs.at[j], r.qr.at[j], t).start()
        return carry
    lax.fori_loop(1, n, go, 0)
    plane.finish()
    for u in range(3):
        along(u).wait_send()
    def end(j, carry):
        t = lax.rem(me + j, n)
        remote(r.both, r.all.at[me], r.qs.at[j], r.qr.at[j], t).wait()
        return carry
    lax.fori_loop(1, n, end, 0)
    q_own.wait()
    sums = jnp.sum(r.all[...], axis=0)
    whole = lambda v: jnp.sum(jnp.sum(v, axis=1, keepdims=True), axis=0, keepdims=True)
    norm = jnp.sqrt(whole(sums[0:8, :]))
    r.norm[...] = norm
    r.factor[...] = jnp.minimum(1.0, clip_limit / norm)
    r.error[...] = whole(sums[8:16, :])


def reduce_gradient(n, chunks, flat, errors, share_rows, lead, encoder, cid, bm=512):
    served, landed, g_node, x, block = encoder
    V = pl.BlockSpec(memory_space=pltpu.VMEM)
    F = lambda *s: pltpu.VMEM(s + (128,), F32)
    rows = chunks.rows
    inputs = dict(flat_in=(flat, ANY), err=(errors, V), served=(served, V), g_node=(g_node, ANY), x=(x, ANY))
    inputs |= numbered("landed", [(v, V) for v in landed])
    inputs |= {name: (v, V) for name, v in zip(("p_in", "p_out", "p_vec"), block)}
    outputs = dict(flat0=(shaped(*flat.shape), ANY), out=(shaped(rows, 128), V)) | {name: (shaped(1, 1), V) for name in ("norm", "factor", "error")}
    scratch = plane_scratch(4, rows) | dict(zq=F(3, rows), zqs=DMA((3,)), zqr=DMA((3,)))
    scratch |= dict(both=F(16), all=F(n, 16), own=DMA, qs=DMA((n,)), qr=DMA((n,)), packed=packed_rows(VARS, 4), fsem=DMA((STORES,)))
    scratch |= sums_scratch("d", block[0].shape[0])
    body = functools.partial(reduce_kernel, n, chunks, share_rows, lead, bm)
    made = named_call(body, "reduce_gradient", inputs, outputs, scratch, aliases=dict(flat_in="flat0"), cid=cid)
    return made.out, made.norm[0, 0], made.factor[0, 0], made.error[0, 0]


def make_parts(capacity):
    whole = capacity // 16 * 16
    rest = (capacity - whole + 3) // 4 * 4
    return [rows for rows in (whole, rest) if rows]


def make_asks(edge_owners, edge_local, devices, parts):
    owner = edge_owners.reshape(-1)
    local = edge_local.reshape(-1)
    wants = owner.shape[0]
    order = jnp.arange(wants, dtype=jnp.int32)
    before = (owner[:, None] == owner[None, :]) & (order[None, :] < order[:, None])
    ranking = jnp.sum(before.astype(jnp.int32), axis=1)
    capacity = sum(parts)
    slots = jnp.arange(devices * capacity, dtype=jnp.int32)
    place = owner * capacity + ranking
    asking = jnp.sum(jnp.where(slots[:, None] == place[None, :], local[None, :] + 1, 0), axis=1) - 1
    position = owner * parts[0] + ranking
    if len(parts) > 1:
        position = jnp.where(ranking < parts[0], position, devices * parts[0] + owner * parts[1] + ranking - parts[0])
    return (position, asking.reshape(devices, capacity))


def widen(values, width):
    return jnp.pad(values, ((0, 0), (0, width - values.shape[1])))


def make_block(params):
    rows = params["w_in"].shape[0]
    w_in = jnp.pad(params["w_in"], ((0, -rows % 128), (0, 0)))
    w_out = widen(params["w_out"], (params["w_out"].shape[1] + 127) // 128 * 128)
    names = [name for name in ("b_in", "b_out", "gain", "shift") if name in params]
    vectors = [widen(params[name][None], LATENT) for name in names]
    vectors.append(jnp.zeros((8 - len(vectors), LATENT), jnp.bfloat16))
    return (w_in, w_out, jnp.concatenate(vectors).astype(jnp.float32))


def relaid_blocks(made, segments, share_rows):
    shares = made.shares
    def rows_of(first, last):
        parts = []
        while first < last:
            owner, low = divmod(first, share_rows)
            size = min(last - first, share_rows - low)
            parts.append(shares[owner, low : low + size])
            first += size
        return jnp.concatenate(parts) if len(parts) > 1 else parts[0]
    [(shape, begin, size)] = [(s, o, e) for _, name, s, o, e in segments if name == "w_out" and s[1] != LATENT]
    wide = shape[1]
    first, end = begin // 128, (begin + size) // 128
    w_out = widen(rows_of(first, end).reshape(shape), (wide + 127) // 128 * 128)
    bias = rows_of(end, end + (wide + 127) // 128).reshape(-1)[:wide, None].astype(jnp.float32)
    blocks = []
    for b in range(segments[-1][0] + 1):
        get = lambda part: getattr(made, f"m{b}{part}", w_out)
        blocks.append((get("_in"), get("_out"), get("_vec")))
    return blocks, bias


def local(
    inputs,
    targets,
    geometry,
    land_sea,
    level_mask,
    edge_owners,
    edge_local,
    step_count,
    master,
    first_moment,
    second_moment,
    ema,
):
    segments, total = layout(LATENT, VARS, GEO, LAYERS)
    devices = lax.axis_size("dev")
    share = master.shape[0]
    mine = devices == 32 and share % 128 == 0
    parts = make_parts(5 * edge_owners.shape[0] // (2 * devices))
    capacity = sum(parts)
    x = inputs.T
    geo = widen(geometry, 128)
    level, land = level_mask.T, land_sea[None, :]
    if mine:
        share_rows = share // 128
        begun = start(devices, parts, 1, master.reshape(share_rows, 128), edge_owners.T, edge_local.T, level, land, geo, x, segments, share_rows)
        blocks, bias = relaid_blocks(begun, segments, share_rows)
        want, served, pos, pos_s, pos_r = begun.want, begun.served, begun.pos, begun.pos_s, begun.pos_r
        count = jnp.sum(begun.numbers)
    else:
        position, asking = make_asks(edge_owners, edge_local, devices, parts)
        pos = position.reshape(-1, 2)
        pos_s, pos_r = pos[:, 0][None, :], pos[:, 1][None, :]
        ocean = (jnp.arange(VARS) < SEA_VARS).astype(jnp.int32)
        counted = jnp.sum(level_mask * (1 - land_sea[:, None] * ocean[None, :])).astype(jnp.float32)
        full_weights = lax.all_gather(master.astype(jnp.bfloat16), "dev", axis=0, tiled=True)
        whole = unpack(full_weights, segments)
        blocks = [make_block(b) for b in whole]
        bias = whole[-1]["b_out"][:, None].astype(jnp.float32)
        served = lax.all_to_all(asking, "dev", 0, 0, tiled=True)
        count = lax.psum(counted, "dev")
        served = jnp.concatenate([served[:, sum(parts[:i]) : sum(parts[: i + 1])].reshape(-1) for i in range(len(parts))])
        want = served[:, None]
        served = served[None, :]
    routes = (want, served, pos, pos_s, pos_r)
    if mine:
        done = [begun]
    else:
        done = [edge_forward(devices, parts, 3, geo, routes, blocks[2], blocks[0], inputs.shape[0], x=x, geo_block=blocks[1])]
    for k in range(1, LAYERS):
        f = done[-1]
        done.append(
            edge_forward(
                devices, parts, 4, f.edge, routes, blocks[2 + 2 * k], blocks[1 + 2 * k], inputs.shape[0],
                landed=several(f, "landed"), node=f.node, slots=f.slots,
            )
        )
    pieces = [4 * s for s in (VARS + LATENT + 4, GEO + LATENT + 4) + (3 * LATENT + LATENT + 4, 2 * LATENT + LATENT + 4) * LAYERS]
    lead = 4
    places = [0] + [lead + sum(pieces[: i + 1]) for i in range(len(pieces))]
    flat_rows = (lead + PARAMS // 128 + 15) // 16 * 16 + 8
    if mine:
        begins = [(lead + share_rows * d) // 8 * 8 for d in range(devices)]
        chunks = Chunks(begins, (share_rows + 6 + 15) // 16 * 16, [0, 32])
    else:
        chunks = Chunks([0], flat_rows, [0, 1])
    dec_at = places[-1]
    tail_at = dec_at + 4 * LATENT
    k = LAYERS - 1
    flat, g_node, *outgoing, d_out, d_first, d_bias, errors = turn(
        served, want, several(done[k], "landed"), done[k].node, x, targets.T, level, land, count.reshape(1, 1),
        blocks[3 + 2 * k], blocks[-1], bias, chunks, places[3 + 2 * k], dec_at,
    )
    flats = {len(chunks.cuts) - 2: flat}
    tail = jnp.concatenate([d_first[0], d_out[:, :VARS].reshape(-1), d_bias[:VARS, 0]])
    tail_rows = flat_rows - tail_at
    tail = jnp.pad(tail, (0, tail_rows * 128 - tail.shape[0])).reshape(tail_rows, 128)
    g_edge, landed = None, None
    for k in reversed(range(LAYERS)):
        more = {}
        if k == LAYERS - 1:
            more |= dict(outgoing=outgoing, g_node=g_node, tail=tail, tail_at=tail_at)
        else:
            more |= dict(
                node=(landed, g_slots, done[k].slots, done[k + 1].sums_s, g_node, done[k].low, done[k + 1].sums, blocks[3 + 2 * k]),
                node_at=places[3 + 2 * k],
            )
        if k == 0:
            more |= dict(geo=(geo, blocks[1]), geo_at=places[1])
        f = done[k]
        b = edge_backward(
            devices, parts, 5 + (LAYERS - 1 - k), (f.edge_low, f.sent, f.recv), routes, blocks[2 + 2 * k], chunks, flats, places[2 + 2 * k],
            g_edge=g_edge, **more,
        )
        g_edge, landed = b.edge_prev, several(b, "landed")
        g_slots = b.g_slots
        if k < LAYERS - 1:
            g_node = b.g_prev
    if mine:
        encoder = (served, landed, g_node, x, blocks[0])
        summed, grad_norm, factor, error_sum = reduce_gradient(devices, chunks, flats[0], errors, share_rows, lead, encoder, 2)
        skip = lax.rem(lead + share_rows * lax.axis_index("dev"), 8)
        own_grad = lax.dynamic_slice_in_dim(summed, skip, share_rows).reshape(-1)
    else:
        flat = encode_backward(served, landed, g_node, x, blocks[0], chunks, flats[0])
        own_grad = lax.psum_scatter(flat[0, lead : lead + PARAMS // 128].reshape(-1), "dev", scatter_dimension=0, tiled=True)
        error_sum, squares = lax.psum((jnp.sum(errors), jnp.sum(own_grad * own_grad)), "dev")
        grad_norm = jnp.sqrt(squares)
        factor = jnp.minimum(1.0, clip_limit / grad_norm)
    loss = error_sum / jnp.maximum(count, 1.0)
    clipped = own_grad * factor
    step = step_count[0].astype(jnp.float32)
    new_first = beta_one * first_moment + (1.0 - beta_one) * clipped
    new_second = beta_two * second_moment + (1.0 - beta_two) * clipped * clipped
    first_hat = new_first / (1.0 - beta_one**step)
    second_hat = new_second / (1.0 - beta_two**step)
    new_master = master - learn_rate * (
        first_hat / (jnp.sqrt(second_hat) + adam_eps) + decay_rate * master
    )
    new_ema = ema_keep * ema + (1.0 - ema_keep) * new_master
    return (new_master, new_first, new_second, new_ema, loss, grad_norm)


def solution(mesh):
    in_specs = (
        P("dev", None),
        P("dev", None),
        P("dev", None),
        P("dev"),
        P("dev", None),
        P("dev", None),
        P("dev", None),
        P(),
        P("dev"),
        P("dev"),
        P("dev"),
        P("dev"),
    )
    out_specs = (P("dev"), P("dev"), P("dev"), P("dev"), P(), P())
    return jax.shard_map(local, mesh=mesh, in_specs=in_specs, out_specs=out_specs, check_vma=False)
```

```python
import functools
import types

import jax
import jax.numpy as jnp
import numpy as np
from jax import lax
from jax.experimental import pallas as pl
from jax.experimental.pallas import tpu as pltpu
from jax.sharding import PartitionSpec as P

LATENT = 512
VARS = 227
GEO = 4
SEA_VARS = 4
LAYERS = 3
PARAMS = 6545408


norm_eps = 1e-05
clip_limit = 0.01
beta_one = 0.9
beta_two = 0.999
adam_eps = 1e-08
learn_rate = 0.03
decay_rate = 0.1
ema_keep = 0.9


def layout(width, variables, geometry, layers):
    shapes = [(variables, width, True), (geometry, width, True)]
    for k in range(layers):
        shapes.append((3 * width, width, True))
        shapes.append((2 * width, width, True))
    shapes.append((width, variables, False))
    segments = []
    offset = 0
    for block_id, (fan_in, fan_out, normed) in enumerate(shapes):
        members = [
            ("w_in", (fan_in, width)),
            ("b_in", (width,)),
            ("w_out", (width, fan_out)),
            ("b_out", (fan_out,)),
        ]
        if normed:
            members = members + [("gain", (fan_out,)), ("shift", (fan_out,))]
        for part_name, part_shape in members:
            entries = int(np.prod(part_shape))
            segments.append((block_id, part_name, part_shape, offset, entries))
            offset += entries
    return (segments, offset)


def unpack(flat, segments):
    blocks = [dict() for k in range(segments[-1][0] + 1)]
    for block_id, part_name, part_shape, offset, entries in segments:
        blocks[block_id][part_name] = flat[offset : offset + entries].reshape(part_shape)
    return blocks


MESH = pl.DeviceIdType.MESH

def remote(src, dst, send, recv, target):
    return pltpu.make_async_remote_copy(src, dst, send, recv, device_id=(target,), device_id_type=MESH)

def greet(n, me):
    barrier = pltpu.get_barrier_semaphore()
    def hello(j, c):
        pl.semaphore_signal(barrier, inc=1, device_id=(lax.rem(me + j, n),), device_id_type=MESH)
        return c
    lax.fori_loop(1, n, hello, 0)
    pl.semaphore_wait(barrier, n - 1)


F32, BF16 = jnp.float32, jnp.bfloat16
VMEM_LIMIT = 60 << 20
ANY = pl.BlockSpec(memory_space=pl.ANY)
DMA = pltpu.SemaphoreType.DMA


def mm(a, b):
    return jnp.dot(a, b, preferred_element_type=F32)


def mm_nt(a, b):
    return lax.dot_general(a, b, (((1,), (1,)), ((), ())), preferred_element_type=F32)


def mm_tn(a, b):
    return lax.dot_general(a, b, (((0,), (0,)), ((), ())), preferred_element_type=F32)


def contract(a, b, left, right):
    return lax.dot_general(a, b, (((left,), (right,)), ((), ())), preferred_element_type=F32)


def col(v):
    return jnp.sum(v, axis=0, keepdims=True)


def pick(slots, first, rows):
    r = first + lax.broadcasted_iota(jnp.int32, (slots.shape[0], rows), 1)
    return jnp.where(slots == r, 1.0, 0.0).astype(BF16)


def place(slots, first, rows):
    r = first + lax.broadcasted_iota(jnp.int32, (rows, slots.shape[1]), 0)
    return jnp.where(slots == r, 1.0, 0.0).astype(BF16)


def first_half(us, w_in, vec):
    pre = vec[0:1, :]
    at = 0
    for u in us:
        pre = pre + mm(u, w_in[at : at + u.shape[1], :])
        at += u.shape[1]
    return pre


def activate(pre):
    sigma = jax.nn.sigmoid(pre)
    return sigma, (pre * sigma).astype(BF16)


def normalize(post):
    centred = post - jnp.mean(post, axis=-1, keepdims=True)
    inv = lax.rsqrt(jnp.mean(centred * centred, axis=-1, keepdims=True) + norm_eps)
    return centred * inv, inv


def second_half(act, w_out, vec):
    return normalize(mm(act, w_out[...]) + vec[1:2, :])


def scale_shift(hat, vec):
    return hat * vec[2:3, :] + vec[3:4, :]


def norm_back(g, hat, inv, vec, d_vec):
    if d_vec is not None:
        d_vec[2:3, :] += col(g * hat)
        d_vec[3:4, :] += col(g)
    s = g * vec[2:3, :]
    post = inv * (
        s - jnp.mean(s, axis=-1, keepdims=True) - hat * jnp.mean(s * hat, axis=-1, keepdims=True)
    )
    return post.astype(BF16)


def act_back(low, pre, sigma, w_out):
    g_act = mm_nt(low, w_out[...])
    return (g_act * sigma * (1.0 + pre * (1.0 - sigma))).astype(BF16)


def weight_sums(us, act, low, g_pre, d_in, d_out, d_vec):
    d_out[...] += mm_tn(act, low)
    d_vec[1:2, : low.shape[1]] += col(low.astype(F32))
    d_vec[0:1, :] += col(g_pre.astype(F32))
    at = 0
    for u in us:
        d_in[at : at + u.shape[1], :] += mm_tn(u, g_pre)
        at += u.shape[1]


def pack_matrix(packed, ref, rows, at):
    for j in range(4):
        packed[pl.ds(at + j, rows, stride=4), :] = ref[:rows, 128 * j : 128 * (j + 1)]
    return at + 4 * rows


def pack(packed, lead, rows_in, d_in, d_out, d_vec):
    def vector(i, at):
        for j in range(4):
            packed[at + j : at + j + 1, :] = d_vec[i : i + 1, 128 * j : 128 * (j + 1)]
        return at + 4
    at = pack_matrix(packed, d_in, rows_in, lead)
    at = vector(0, at)
    at = pack_matrix(packed, d_out, d_out.shape[0], at)
    for i in (1, 2, 3):
        at = vector(i, at)


def clear(*refs):
    for ref in refs:
        ref[...] = jnp.zeros_like(ref)


def spec(shape, fixed=True):
    if fixed:
        return pl.BlockSpec(shape, lambda i: (0,) * len(shape))
    return pl.BlockSpec(shape, lambda i: (i,) + (0,) * (len(shape) - 1))


def params(**more):
    return pltpu.CompilerParams(vmem_limit_bytes=VMEM_LIMIT, **more)


def shaped(*shape, dtype=F32):
    return jax.ShapeDtypeStruct(shape, dtype)


class Chunks:
    def __init__(self, begins, rows, cuts):
        self.begins, self.rows, self.cuts = begins, rows, cuts

    def shape(self, group):
        return (self.cuts[group + 1] - self.cuts[group], self.rows, 128)

    def pieces(self, at, size):
        found = []
        for group in range(len(self.cuts) - 1):
            for owner in range(self.cuts[group], self.cuts[group + 1]):
                begin = self.begins[owner]
                low, high = max(at, begin), min(at + size, begin + self.rows)
                if low < high:
                    found.append((group, owner - self.cuts[group], low - begin, low - at, high - low))
        return found

    def groups(self, *places):
        return sorted({p[0] for at, size in places for p in self.pieces(at, size)})


class Stores:
    def __init__(self, refs, chunks, sem):
        self.refs, self.chunks, self.sem, self.copies = refs, chunks, sem, []

    def put(self, packed, at):
        for group, owner, row, skip, size in self.chunks.pieces(at, packed.shape[0]):
            source = packed.at[pl.ds(skip, size)]
            copy = pltpu.make_async_copy(source, self.refs[group].at[owner, pl.ds(row, size)], self.sem.at[len(self.copies)])
            copy.start()
            self.copies.append(copy)

    def wait(self):
        for copy in self.copies:
            copy.wait()


STORES = 48


def flat_refs(r, groups):
    return {group: getattr(r, f"flat{group}") for group in groups}


def mlp_sums(rows_in, wide=LATENT):
    return [pltpu.VMEM((rows_in, LATENT), F32), pltpu.VMEM((LATENT, wide), F32), pltpu.VMEM((8, LATENT), F32)]


def packed_rows(rows_in, lead=0):
    return pltpu.VMEM((lead + 4 * rows_in + 4 * LATENT + 16, 128), F32)


def named_call(body, name, inputs, outputs, scratch, aliases=None, cid=None):
    names = [*inputs, *outputs, *scratch]
    aliases = {list(inputs).index(i): list(outputs).index(o) for i, o in (aliases or {}).items()}
    def kernel(*refs):
        body(types.SimpleNamespace(**dict(zip(names, refs))))
    more = {} if cid is None else dict(collective_id=cid, has_side_effects=True)
    values = pl.pallas_call(
        kernel,
        out_shape=tuple(shape for shape, _ in outputs.values()),
        in_specs=[s for _, s in inputs.values()],
        out_specs=tuple(s for _, s in outputs.values()),
        scratch_shapes=list(scratch.values()),
        input_output_aliases=aliases,
        compiler_params=params(**more),
        name=name,
    )(*[v for v, _ in inputs.values()])
    return types.SimpleNamespace(**dict(zip(outputs, values)))


def swap_start(n, me, srcs, dsts, own, ssem, rsem):
    for i, (src, dst) in enumerate(zip(srcs, dsts)):
        pltpu.make_async_copy(src.at[me], dst.at[me], own.at[i]).start()
    def go(j, c):
        t = lax.rem(me + j, n)
        for i, (src, dst) in enumerate(zip(srcs, dsts)):
            remote(src.at[t], dst.at[me], ssem.at[i, j], rsem.at[i, j], t).start()
        return c
    lax.fori_loop(1, n, go, 0)


def swap_wait(n, me, srcs, dsts, own, ssem, rsem):
    def end(j, c):
        t = lax.rem(me + j, n)
        for i, (src, dst) in enumerate(zip(srcs, dsts)):
            remote(src.at[t], dst.at[me], ssem.at[i, j], rsem.at[i, j], t).wait()
        return c
    lax.fori_loop(1, n, end, 0)
    for i, (src, dst) in enumerate(zip(srcs, dsts)):
        pltpu.make_async_copy(src.at[me], dst.at[me], own.at[i]).wait()


def several(r, name):
    return [getattr(r, f"{name}{i}") for i in range(4) if hasattr(r, f"{name}{i}")]


def numbered(name, values):
    return {f"{name}{i}": value for i, value in enumerate(values)}


def slot_rows(refs):
    rows = [ref[...].reshape(ref.shape[0] * ref.shape[1], ref.shape[2]) for ref in refs]
    return rows[0] if len(rows) == 1 else jnp.concatenate(rows, axis=0)


def put_slot_rows(refs, rows):
    at = 0
    for ref in refs:
        size = ref.shape[0] * ref.shape[1]
        ref[...] = rows[at : at + size, :].reshape(ref.shape)
        at += size


def greet_start(n, me):
    barrier = pltpu.get_barrier_semaphore()
    def hello(j, c):
        pl.semaphore_signal(barrier, inc=1, device_id=(lax.rem(me + j, n),), device_id_type=MESH)
        return c
    lax.fori_loop(1, n, hello, 0)


def greet_wait(n):
    pl.semaphore_wait(pltpu.get_barrier_semaphore(), n - 1)


class Loads:
    def __init__(self, r, sem):
        self.r, self.sem, self.copies = r, sem, {}

    def start(self, *names):
        for name in names:
            copy = pltpu.make_async_copy(getattr(self.r, name), getattr(self.r, "_" + name), self.sem.at[len(self.copies)])
            copy.start()
            self.copies[name] = copy

    def wait(self, *names):
        for name in names:
            self.copies[name].wait()


def store_all(r, sem, *names):
    copies = [pltpu.make_async_copy(getattr(r, "_" + name), getattr(r, name), sem.at[i]) for i, name in enumerate(names)]
    for copy in copies:
        copy.start()
    return copies


def same_rows(want, served):
    return jnp.where((want[...] == served[...]) & (want[...] >= 0), 1.0, 0.0).astype(BF16)


def swap_scratch(shapes, n):
    parts = len(shapes)
    scratch = dict(own=DMA((2, parts)), s1=DMA((parts, n)), r1=DMA((parts, n)), s2=DMA((parts, n)), r2=DMA((parts, n)))
    for name in ("away", "here", "back"):
        scratch |= numbered(name, [pltpu.VMEM(shape, BF16) for shape in shapes])
    return scratch


def held(prefix, block):
    return {prefix + part: pltpu.VMEM(a.shape, a.dtype) for part, a in zip(("_in", "_out", "_vec"), block)}


def weights(prefix, block):
    return {prefix + part: (a, ANY) for part, a in zip(("_in", "_out", "_vec"), block)}


def rows_block(bm, width=LATENT):
    return pl.BlockSpec((bm, width), lambda i: (i, 0))


def edge_kernel(n, first, bm, r):
    me = lax.axis_index("dev")
    greet_start(n, me)
    loads = Loads(r, r.lsem)
    node_weights = ["p_in", "p_out", "p_vec"]
    landing = [name for name in vars(r) if name.startswith("landed_in")]
    early = node_weights + ([] if first else [*landing, "slots_in"])
    late = ["e_in", "e_out", "e_vec"] + (["g_in", "g_out", "g_vec"] if first else [])
    loads.start(*early)
    loads.start(*late)
    loads.wait(*early)
    count = r.want.shape[0]
    if first:
        asked = contract(pick(r.want[...], 0, r.x.shape[1]), r.x[...], 1, 1).astype(BF16)
        pre = contract(asked, r._p_in[:VARS, :], 1, 0) + r._p_vec[0:1, :]
    else:
        landed = slot_rows(several(r, "_landed_in"))
        got = mm(same_rows(r.want, r.served), landed).astype(BF16)
        r._sums_s[...] = got
        old = r._slots_in[...]
        pre = first_half([old.astype(BF16), got], r._p_in, r._p_vec)
    _, act = activate(pre)
    hat, _ = second_half(act, r._p_out, r._p_vec)
    slots = scale_shift(hat, r._p_vec)
    if not first:
        slots = old + slots
    r._slots[...] = slots
    away, here, back, out = (several(r, name) for name in ("away", "here", "back", "landed"))
    put_slot_rows(away, slots.astype(BF16))
    greet_wait(n)
    swap_start(n, me, away, here, r.own.at[0], r.s1, r.r1)
    stores = store_all(r, r.ssem, *(["slots"] if first else ["slots", "sums_s"]))
    loads.wait(*late)
    if first:
        _, act = activate(first_half([r.source[...]], r._g_in, r._g_vec))
        hat, _ = second_half(act, r._g_out, r._g_vec)
        r._edge[...] = scale_shift(hat, r._g_vec)
    else:
        r._edge[...] = r.source[...]
    e = r._edge[...].astype(BF16)
    r.edge_low[...] = e
    r._pre[...] = first_half([e], r._e_in, r._e_vec)
    if first:
        def body(node, low):
            i = pl.program_id(0)
            u = r.x[:, pl.ds(pl.multiple_of(i * bm, bm), bm)]
            _, act = activate(contract(u, r._p_in[:VARS, :], 0, 0) + r._p_vec[0:1, :])
            hat, _ = second_half(act, r._p_out, r._p_vec)
            new = scale_shift(hat, r._p_vec)
            node[...] = new
            low[...] = new.astype(BF16)
        pltpu.emit_pipeline(body, grid=(r.node.shape[0] // bm,), in_specs=[], out_specs=[rows_block(bm)] * 2)(r.node, r.low)
    else:
        def body(node_in, node, low, sums):
            i = pl.program_id(0)
            got = mm(place(r.served[...], i * bm, bm), slot_rows(several(r, "_landed_in"))).astype(BF16)
            sums[...] = got
            old = node_in[...]
            _, act = activate(first_half([old.astype(BF16), got], r._p_in, r._p_vec))
            hat, _ = second_half(act, r._p_out, r._p_vec)
            new = old + scale_shift(hat, r._p_vec)
            node[...] = new
            low[...] = new.astype(BF16)
        pltpu.emit_pipeline(body, grid=(r.node.shape[0] // bm,), in_specs=[rows_block(bm)], out_specs=[rows_block(bm)] * 3)(r.node_in, r.node, r.low, r.sums)
    pick_s, pick_r = pick(r.pos[:, 0:1], 0, count), pick(r.pos[:, 1:2], 0, count)
    put_r = place(r.pos_r[...], 0, count)
    swap_wait(n, me, away, here, r.own.at[0], r.s1, r.r1)
    rows = slot_rows(here)
    s = mm(pick_s, rows).astype(BF16)
    v = mm(pick_r, rows).astype(BF16)
    pre = r._pre[...] + mm(s, r._e_in[LATENT : 2 * LATENT, :]) + mm(v, r._e_in[2 * LATENT :, :])
    _, act = activate(pre)
    hat, _ = second_half(act, r._e_out, r._e_vec)
    new = r._edge[...] + scale_shift(hat, r._e_vec)
    put_slot_rows(back, mm(put_r, new.astype(BF16)).astype(BF16))
    swap_start(n, me, back, out, r.own.at[1], r.s2, r.r2)
    r.edge[...] = new
    r.sent[...], r.recv[...] = s, v
    for store in stores:
        store.wait()
    swap_wait(n, me, back, out, r.own.at[1], r.s2, r.r2)


def edge_forward(n, parts, cid, source, routes, edge_block, node_block, rows, x=None, geo_block=None, landed=None, node=None, slots=None, bm=512):
    first = x is not None
    want, served, pos, pos_s, pos_r = routes
    count = want.shape[0]
    edges = source.shape[0]
    shapes = [(n, p, LATENT) for p in parts]
    V = pl.BlockSpec(memory_space=pltpu.VMEM)
    inputs = dict(source=(source, V), want=(want, V), served=(served, V), pos=(pos, V), pos_r=(pos_r, V))
    inputs |= weights("p", node_block) | weights("e", edge_block)
    scratch = held("_p", node_block) | held("_e", edge_block) | swap_scratch(shapes, n)
    scratch |= dict(_slots=pltpu.VMEM((count, LATENT), F32), _edge=pltpu.VMEM((edges, LATENT), F32), _pre=pltpu.VMEM((edges, LATENT), F32), lsem=DMA((12,)), ssem=DMA((2,)))
    low = lambda r: shaped(r, LATENT, dtype=BF16)
    outputs = dict(edge=(shaped(edges, LATENT), V), edge_low=(low(edges), V), sent=(low(edges), V), recv=(low(edges), V)) | numbered("landed", [(shaped(*s, dtype=BF16), ANY) for s in shapes])
    outputs |= dict(node=(shaped(rows, LATENT), ANY), low=(low(rows), ANY), slots=(shaped(count, LATENT), ANY))
    if first:
        inputs |= dict(x=(x, V)) | weights("g", geo_block)
        scratch |= held("_g", geo_block)
    else:
        inputs |= numbered("landed_in", [(v, ANY) for v in landed]) | dict(node_in=(node, ANY), slots_in=(slots, ANY))
        scratch |= numbered("_landed_in", [pltpu.VMEM(s, BF16) for s in shapes]) | dict(_slots_in=pltpu.VMEM((count, LATENT), F32), _sums_s=pltpu.VMEM((count, LATENT), BF16))
        outputs |= dict(sums=(low(rows), ANY), sums_s=(low(count), ANY))
    return named_call(functools.partial(edge_kernel, n, first, bm), "edge_forward", inputs, outputs, scratch, cid=cid)


def turn_kernel(parts, bm, chunks, group, at, dec_at, served, want, *refs):
    landed, refs = refs[:parts], refs[parts:]
    flat, g_prev, *outs = refs[13 : 15 + parts]
    node, x, target, level, land, count, w_in, w_out, vec, c_in, c_out, c_vec, c_bias = refs[:13]
    d_out_o, d_first_o, d_bias_o, err_o, packed, packed2, d_in, d_out, d_vec, e_in, e_out, e_vec, e_bias, err, acc, sem = refs[13 + 2 + parts:]
    i = pl.program_id(0)
    @pl.when(i == 0)
    def _():
        clear(d_in, d_out, d_vec, e_in, e_out, e_vec, e_bias, err, acc)
    got = mm(place(served[...], i * bm, bm), slot_rows(landed)).astype(BF16)
    old = node[...]
    low = old.astype(BF16)
    pre = first_half([low, got], w_in, vec)
    sigma, act = activate(pre)
    hat, inv = second_half(act, w_out, vec)
    u = (old + scale_shift(hat, vec)).astype(BF16)
    c_pre = first_half([u], c_in, c_vec)
    c_sigma, c_act = activate(c_pre)
    wide = c_out.shape[1]
    post = contract(c_out[...], c_act, 0, 1)
    sea = (lax.broadcasted_iota(jnp.int32, (VARS, 1), 0) < SEA_VARS).astype(F32)
    mask = level[...].astype(F32) * (1.0 - sea * land[...].astype(F32))
    residual = x[...].astype(F32) + (post[:VARS, :] + c_bias[...]) - target[...]
    divisor = jnp.maximum(count[...], 1.0)
    err[...] += jnp.sum(mask * residual * residual, axis=0, keepdims=True)
    g = 2.0 * mask * residual / divisor
    g_low = jnp.concatenate([g, jnp.zeros((wide - VARS, bm), F32)], axis=0).astype(BF16)
    e_bias[...] += jnp.sum(g_low.astype(F32), axis=1, keepdims=True)
    e_out[...] += contract(c_act, g_low, 0, 1)
    g_act = contract(g_low, c_out[...], 0, 1)
    c_g = (g_act * c_sigma * (1.0 + c_pre * (1.0 - c_sigma))).astype(BF16)
    e_vec[0:1, :] += col(c_g.astype(F32))
    e_in[...] += mm_tn(u, c_g)
    g_node = mm_nt(c_g, c_in[...])
    g_post = norm_back(g_node, hat, inv, vec, d_vec)
    g_pre = act_back(g_post, pre, sigma, w_out)
    weight_sums([low, got], act, g_post, g_pre, d_in, d_out, d_vec)
    g_prev[...] = g_node + mm_nt(g_pre, w_in[:LATENT, :])
    acc[...] += mm(pick(want[...], i * bm, bm), mm_nt(g_pre, w_in[LATENT:, :]).astype(BF16))
    @pl.when(i == pl.num_programs(0) - 1)
    def _():
        put_slot_rows(outs, acc[...].astype(BF16))
        d_out_o[...] = e_out[...]
        d_first_o[...] = e_vec[0:1, :]
        d_bias_o[...] = e_bias[...]
        err_o[...] = err[...]
        stores = Stores({group: flat}, chunks, sem)
        pack_matrix(packed2, e_in, LATENT, 0)
        stores.put(packed2, dec_at)
        pack(packed, 0, 2 * LATENT, d_in, d_out, d_vec)
        stores.put(packed, at)
        stores.wait()


def turn(served, want, landed, node, x, target, level, land, count, block, dec, bias, chunks, at, dec_at, bm=1024):
    rows = node.shape[0]
    slots = want.shape[0]
    wide = dec[1].shape[1]
    [group] = chunks.groups((at, dec_at + 4 * LATENT - at))
    v = lambda height: pl.BlockSpec((height, bm), lambda i: (0, i))
    part = [spec(p.shape) for p in landed]
    return pl.pallas_call(
        functools.partial(turn_kernel, len(landed), bm, chunks, group, at, dec_at),
        grid=(rows // bm,),
        out_shape=(shaped(*chunks.shape(group)), shaped(rows, LATENT), *(shaped(*p.shape, dtype=BF16) for p in landed), shaped(LATENT, wide), shaped(1, LATENT), shaped(wide, 1), shaped(1, bm)),
        in_specs=[spec((1, slots)), spec((slots, 1)), *part, spec((bm, LATENT), False), v(VARS), v(VARS), v(VARS), v(1), spec((1, 1))] + [spec(a.shape) for a in (*block, *dec, bias)],
        out_specs=(ANY, spec((bm, LATENT), False), *part, spec((LATENT, wide)), spec((1, LATENT)), spec((wide, 1)), spec((1, bm))),
        scratch_shapes=[packed_rows(2 * LATENT), pltpu.VMEM((4 * LATENT, 128), F32)] + mlp_sums(2 * LATENT) + mlp_sums(LATENT, wide) + [pltpu.VMEM((wide, 1), F32), pltpu.VMEM((1, bm), F32), pltpu.VMEM((slots, LATENT), F32), DMA((STORES,))],
        compiler_params=params(),
        name="turn",
    )(served, want, *landed, node, x, target, level, land, count, *block, *dec, bias)


def gather_slots(r, bm):
    clear(r._g_slots)
    def body(g_node):
        chosen = pick(r.want[...], pl.program_id(0) * bm, bm)
        g = g_node[...]
        high = g.astype(BF16)
        rest = g - high.astype(F32)
        middle = rest.astype(BF16)
        small = (rest - middle.astype(F32)).astype(BF16)
        r._g_slots[...] += mm(chosen, high) + (mm(chosen, middle) + mm(chosen, small))
    pltpu.emit_pipeline(body, grid=(r.g_node.shape[0] // bm,), in_specs=[rows_block(bm)], out_specs=[])(r.g_node)


def edge_back_kernel(n, chunks, groups, at, node_at, geo_at, tail_at, bm, r):
    me = lax.axis_index("dev")
    greet_start(n, me)
    loads = Loads(r, r.lsem)
    nodes = node_at is not None
    landing = [name for name in vars(r) if name.startswith("landed_in")]
    early = ["p_in", "p_out", "p_vec", *landing, "g_slots_in", "slots_in", "sums_s"] if nodes else []
    late = ["e_in", "e_out", "e_vec"] + (["g_in", "g_out", "g_vec"] if geo_at is not None else [])
    loads.start(*early)
    loads.start(*late)
    flats = Stores(flat_refs(r, groups), chunks, r.fsem)
    stores = [flats]
    if tail_at is not None:
        flats.put(r.tail, tail_at)
    count = r.want.shape[0]
    here, back, out = (several(r, name) for name in ("here", "back", "landed"))
    if nodes:
        loads.wait(*early)
        us = [r._slots_in[...].astype(BF16), r._sums_s[...]]
        pre = first_half(us, r._p_in, r._p_vec)
        sigma, act = activate(pre)
        hat, inv = second_half(act, r._p_out, r._p_vec)
        g = r._g_slots_in[...] + mm(same_rows(r.want, r.served), slot_rows(several(r, "_landed_in")))
        low = norm_back(g, hat, inv, r._p_vec, None)
        g_pre = act_back(low, pre, sigma, r._p_out)
        source = several(r, "away")
        put_slot_rows(source, mm_nt(g_pre, r._p_in[LATENT:, :]).astype(BF16))
    else:
        source = several(r, "outgoing")
    greet_wait(n)
    swap_start(n, me, source, here, r.own.at[0], r.s1, r.r1)
    if nodes:
        r._g_slots[...] = g + mm_nt(g_pre, r._p_in[:LATENT, :])
        stores += store_all(r, r.ssem, "g_slots")
        clear(r.n_in, r.n_out, r.n_vec)
    clear(r.d_in, r.d_out, r.d_vec)
    def node_rows(first, last):
        if not nodes:
            return
        def body(g_node, low_in, sums_in, g_prev):
            i = first + pl.program_id(0)
            us = [low_in[...], sums_in[...]]
            pre = first_half(us, r._p_in, r._p_vec)
            sigma, act = activate(pre)
            hat, inv = second_half(act, r._p_out, r._p_vec)
            g = g_node[...] + mm(place(r.served[...], i * bm, bm), slot_rows(several(r, "_landed_in")))
            low = norm_back(g, hat, inv, r._p_vec, r.n_vec)
            g_pre = act_back(low, pre, sigma, r._p_out)
            weight_sums(us, act, low, g_pre, r.n_in, r.n_out, r.n_vec)
            g_prev[...] = g + mm_nt(g_pre, r._p_in[:LATENT, :])
        block = pl.BlockSpec((bm, LATENT), lambda i: (first + i, 0))
        pltpu.emit_pipeline(body, grid=(last - first,), in_specs=[block] * 3, out_specs=[block])(r.g_node, r.low, r.sums, r.g_prev)
    blocks = r.g_node.shape[0] // bm if nodes else 0
    node_rows(0, blocks // 2)
    if not nodes:
        gather_slots(r, bm)
    loads.wait(*late)
    us = [r.edge_low[...], r.sent[...], r.recv[...]]
    pre = first_half(us, r._e_in, r._e_vec)
    sigma, act = activate(pre)
    hat, inv = second_half(act, r._e_out, r._e_vec)
    pick_r = pick(r.pos[:, 1:2], 0, count)
    put_s, put_r = place(r.pos_s[...], 0, count), place(r.pos_r[...], 0, count)
    swap_wait(n, me, source, here, r.own.at[0], r.s1, r.r1)
    g = mm(pick_r, slot_rows(here))
    if hasattr(r, "g_edge"):
        g = r.g_edge[...] + g
    low = norm_back(g, hat, inv, r._e_vec, r.d_vec)
    g_pre = act_back(low, pre, sigma, r._e_out)
    s = mm_nt(g_pre, r._e_in[LATENT : 2 * LATENT, :]).astype(BF16)
    v = mm_nt(g_pre, r._e_in[2 * LATENT :, :]).astype(BF16)
    put_slot_rows(back, (mm(put_s, s) + mm(put_r, v)).astype(BF16))
    swap_start(n, me, back, out, r.own.at[1], r.s2, r.r2)
    prev = g + mm_nt(g_pre, r._e_in[:LATENT, :])
    r.edge_prev[...] = prev
    weight_sums(us, act, low, g_pre, r.d_in, r.d_out, r.d_vec)
    pack(r.packed, 0, 3 * LATENT, r.d_in, r.d_out, r.d_vec)
    flats.put(r.packed, at)
    if geo_at is not None:
        c_us = [r.geo[...]]
        c_pre = first_half(c_us, r._g_in, r._g_vec)
        c_sigma, c_act = activate(c_pre)
        c_hat, c_inv = second_half(c_act, r._g_out, r._g_vec)
        clear(r.c_in, r.c_out, r.c_vec)
        c_low = norm_back(prev, c_hat, c_inv, r._g_vec, r.c_vec)
        c_g = act_back(c_low, c_pre, c_sigma, r._g_out)
        weight_sums(c_us, c_act, c_low, c_g, r.c_in, r.c_out, r.c_vec)
        pack(r.c_packed, 0, GEO, r.c_in, r.c_out, r.c_vec)
        flats.put(r.c_packed, geo_at)
    node_rows(blocks // 2, blocks)
    if nodes:
        pack(r.n_packed, 0, 2 * LATENT, r.n_in, r.n_out, r.n_vec)
        flats.put(r.n_packed, node_at)
    if not nodes:
        stores += store_all(r, r.ssem, "g_slots")
    swap_wait(n, me, back, out, r.own.at[1], r.s2, r.r2)
    for store in stores:
        store.wait()


def sums_scratch(prefix, rows_in):
    return dict(zip((prefix + "_in", prefix + "_out", prefix + "_vec"), mlp_sums(rows_in)))


def edge_backward(n, parts, cid, ins, routes, edge_block, chunks, flats, at, g_edge=None, outgoing=None, g_node=None, tail=None, tail_at=None, node=None, node_at=None, geo=None, geo_at=None, bm=512):
    want, served, pos, pos_s, pos_r = routes
    count = want.shape[0]
    edges = pos.shape[0]
    shapes = [(n, p, LATENT) for p in parts]
    V = pl.BlockSpec(memory_space=pltpu.VMEM)
    inputs = dict(want=(want, V), served=(served, V), pos=(pos, V), pos_s=(pos_s, V), pos_r=(pos_r, V))
    inputs |= {name: (value, V) for name, value in zip(("edge_low", "sent", "recv"), ins)} | weights("e", edge_block)
    scratch = held("_e", edge_block) | swap_scratch(shapes, n) | sums_scratch("d", 3 * LATENT)
    scratch |= dict(packed=packed_rows(3 * LATENT), lsem=DMA((16,)), ssem=DMA((2,)), fsem=DMA((STORES,)))
    outputs = dict(edge_prev=(shaped(edges, LATENT), V)) | numbered("landed", [(shaped(*s, dtype=BF16), ANY) for s in shapes])
    places = [(at, scratch["packed"].shape[0])]
    if g_edge is not None:
        inputs |= dict(g_edge=(g_edge, V))
    if outgoing is not None:
        inputs |= numbered("outgoing", [(v, ANY) for v in outgoing]) | dict(g_node=(g_node, ANY))
        outputs |= dict(g_slots=(shaped(count, LATENT), ANY))
        scratch |= dict(_g_slots=pltpu.VMEM((count, LATENT), F32))
    if tail is not None:
        inputs |= dict(tail=(tail, V))
        places.append((tail_at, tail.shape[0]))
    if node is not None:
        inputs |= numbered("landed_in", [(v, ANY) for v in node[0]])
        for name, value in zip(("g_slots_in", "slots_in", "sums_s", "g_node", "low", "sums"), node[1:]):
            inputs[name] = (value, ANY)
        inputs |= weights("p", node[7])
        scratch |= held("_p", node[7]) | sums_scratch("n", 2 * LATENT)
        f = pltpu.VMEM((count, LATENT), F32)
        scratch |= numbered("_landed_in", [pltpu.VMEM(s, BF16) for s in shapes]) | dict(n_packed=packed_rows(2 * LATENT), _g_slots_in=f, _slots_in=f, _g_slots=f, _sums_s=pltpu.VMEM((count, LATENT), BF16))
        rows = node[4].shape[0]
        places.append((node_at, scratch["n_packed"].shape[0]))
        outputs |= dict(g_prev=(shaped(rows, LATENT), ANY), g_slots=(shaped(count, LATENT), ANY))
    if geo is not None:
        inputs |= dict(geo=(geo[0], V)) | weights("g", geo[1])
        scratch |= held("_g", geo[1]) | sums_scratch("c", geo[0].shape[1]) | dict(c_packed=packed_rows(GEO))
        places.append((geo_at, scratch["c_packed"].shape[0]))
    groups = chunks.groups(*places)
    aliases = {}
    for group in groups:
        outputs[f"flat{group}"] = (shaped(*chunks.shape(group)), ANY)
        if group in flats:
            inputs[f"flat{group}_in"] = (flats[group], ANY)
            aliases[f"flat{group}_in"] = f"flat{group}"
    body = functools.partial(edge_back_kernel, n, chunks, groups, at, node_at, geo_at, tail_at, bm)
    made = named_call(body, "edge_backward", inputs, outputs, scratch, aliases=aliases, cid=cid)
    flats.update(flat_refs(made, groups))
    return made


def encode_back_rows(first, bm, served, landed, g_node, x, w_in, w_out, vec, d_in, d_out, d_vec):
    pre = contract(x[...], w_in[:VARS, :], 0, 0) + vec[0:1, :]
    sigma, act = activate(pre)
    hat, inv = second_half(act, w_out, vec)
    g = g_node[...] + mm(place(served[...], first, bm), slot_rows(landed))
    g_post = norm_back(g, hat, inv, vec, d_vec)
    g_pre = act_back(g_post, pre, sigma, w_out)
    weight_sums([], act, g_post, g_pre, d_in, d_out, d_vec)
    d_in[:VARS, :] += mm(x[...], g_pre)


def encode_pack(packed, d_in, d_out, d_vec):
    packed[0:4, :] = jnp.zeros((4, 128), F32)
    pack(packed, 4, VARS, d_in, d_out, d_vec)


def encode_back_kernel(parts, bm, chunks, served, *refs):
    landed, refs = refs[:parts], refs[parts:]
    g_node, x, w_in, w_out, vec, flat_in, flat, packed, d_in, d_out, d_vec, sem = refs
    i = pl.program_id(0)
    @pl.when(i == 0)
    def _():
        clear(d_in, d_out, d_vec)
    encode_back_rows(i * bm, bm, served, landed, g_node, x, w_in, w_out, vec, d_in, d_out, d_vec)
    @pl.when(i == pl.num_programs(0) - 1)
    def _():
        encode_pack(packed, d_in, d_out, d_vec)
        stores = Stores({0: flat}, chunks, sem)
        stores.put(packed, 0)
        stores.wait()


def encode_backward(served, landed, g_node, x, block, chunks, flat, bm=512):
    k, rows = block[0].shape[0], x.shape[1]
    slots = served.shape[1]
    return pl.pallas_call(
        functools.partial(encode_back_kernel, len(landed), bm, chunks),
        grid=(rows // bm,),
        out_shape=shaped(*flat.shape),
        in_specs=[spec((1, slots)), *(spec(p.shape) for p in landed), spec((bm, LATENT), False), pl.BlockSpec((VARS, bm), lambda i: (0, i))] + [spec(a.shape) for a in block] + [ANY],
        out_specs=ANY,
        scratch_shapes=[packed_rows(VARS, 4)] + mlp_sums(k) + [DMA((STORES,))],
        input_output_aliases={6 + len(landed): 0},
        compiler_params=params(),
        name="encode_backward",
    )(served, *landed, g_node, x, *block, flat)


def relay_plan(segments, share_rows):
    jobs = []
    for block_id, part_name, part_shape, offset, entries in segments:
        if part_name not in ("w_in", "w_out") or part_shape[1] != LATENT:
            continue
        for first in range(0, part_shape[0], LATENT):
            rows = min(LATENT, part_shape[0] - first)
            follow = 0
            if first + rows == part_shape[0]:
                follow = 1 if part_name == "w_in" else 3
            begin = offset // 128 + 4 * first
            end = begin + 4 * (rows + follow)
            parts = []
            at = begin
            while at < end:
                owner, low = divmod(at, share_rows)
                size = min(end - at, share_rows - low)
                base = low // 16 * 16
                span = (low + size - base + 15) // 16 * 16
                parts.append((owner, base, span, low - base, at - begin))
                at += size
            jobs.append((block_id, part_name, first, rows, follow, parts))
    return jobs


class Relay:
    def __init__(self, r, shares):
        self.r, self.shares, self.loads, self.at, self.count = r, shares, {}, 0, 0

    def load(self, job):
        r, mine = self.r, []
        for owner, base, span, skip, to in job[5]:
            place = pl.ds(self.at, span)
            copy = pltpu.make_async_copy(self.shares.at[owner, pl.ds(base, span)], r.stage.at[place], r.isem.at[self.count])
            copy.start()
            mine.append((copy, place, span, skip, to))
            self.at += span
            self.count += 1
        self.loads[job[:3]] = mine

    def run(self, job, target, vec):
        _, name, _, rows, follow, _ = job
        lines = self.r.lines
        for copy, place, span, skip, to in self.loads[job[:3]]:
            copy.wait()
            lines[pl.ds(16 + to - skip, span), :] = self.r.stage[place, :].astype(F32)
        for j in range(4):
            target[:rows, 128 * j : 128 * (j + 1)] = lines[pl.ds(16 + j, rows, stride=4), :].astype(BF16)
        if rows < target.shape[0]:
            target[rows:, :] = jnp.zeros((target.shape[0] - rows, LATENT), BF16)
        for i in range(follow):
            row = i if name == "w_in" else i + 1
            for j in range(4):
                p = 16 + 4 * (rows + i) + j
                vec[row : row + 1, 128 * j : 128 * (j + 1)] = lines[p : p + 1, :]


class Gather:
    def __init__(self, r, w, o):
        self.r, self.w, self.o = r, w, o
        self.me, z, y, x, c = where_am_i()
        self.z = z
        half = w.shape[0] // 2
        self.A, self.B = pl.ds(0, half), pl.ds(half, half)
        self.dev = lambda zz, fy=0, fx=0: device_at(zz, y + fy * (1 - 2 * y), x + fx * (1 - 2 * x), c)
        self.tx, self.ty, self.tc = self.dev(z, 0, 1), self.dev(z, 1, 0), device_at(z, y, x, 1 - c)
        self.up, self.down = self.dev(jnp.minimum(z + 1, 3)), self.dev(jnp.maximum(z - 1, 0))
        def by_plane(*v):
            return jnp.where(z == 0, v[0], jnp.where(z == 1, v[1], jnp.where(z == 2, v[2], v[3])))
        self.come = [z, by_plane(1, 0, 1, 2), by_plane(2, 2, 3, 1), by_plane(3, 3, 0, 0)]
        self.go = [z, by_plane(1, 0, 1, 2), by_plane(2, 2, 0, 0), by_plane(3, 3, 3, 1)]
        self.sends, self.spreads, self.sibling, self.seen = [], {}, [], 0

    def send(self, *args):
        copy = remote(*args)
        copy.start()
        self.sends.append(copy)

    def share(self, k, part=None):
        ref = self.w if k == 0 else self.o.at[self.dev(self.go[k])]
        return ref if part is None else ref.at[part]

    def to_sibling(self, slot, part=None, source=None):
        r, i = self.r, len(self.sibling)
        ref = self.o.at[slot] if part is None else self.o.at[slot, part]
        self.send(ref if source is None else source, ref, r.bs.at[i], r.br.at[i], self.tc)
        self.sibling.append(part)

    def from_sibling(self, count):
        r = self.r
        for i in range(self.seen, count):
            part = self.sibling[i]
            ref = self.o.at[self.me] if part is None else self.o.at[self.me, part]
            remote(ref, ref, r.bs.at[i], r.br.at[i], self.tc).wait_recv()
        self.seen = count

    def onward(self, i, wait=False):
        r, z, plane = self.r, self.z, self.come[i]
        slot = self.dev(plane)
        source = self.w if i == 0 else self.o.at[slot]
        for d, target, here in ((0, self.up, (plane <= z) & (z < 3)), (1, self.down, (plane >= z) & (z > 0))):
            @pl.when(here)
            def _():
                copy = remote(source, self.o.at[slot], r.zs.at[d, i], r.zr.at[plane], target)
                if wait:
                    copy.wait_send()
                else:
                    copy.start()

    def begin(self):
        r = self.r
        self.mine = pltpu.make_async_copy(self.w, self.o.at[self.me], r.gown.at[0])
        self.mine.start()
        self.spread(0)
        self.onward(0)
        self.to_sibling(self.me, None, self.w)

    def arrive(self, i):
        slot = self.dev(self.come[i])
        remote(self.w, self.o.at[slot], self.r.zs.at[0, i], self.r.zr.at[self.come[i]], self.tc).wait_recv()
        self.onward(i)
        self.to_sibling(slot)

    def spread(self, k, when=None):
        r, slot = self.r, self.dev(self.go[k])
        copies = [
            remote(self.share(k, self.A), self.o.at[slot, self.A], r.hs.at[k, 0], r.hr.at[k, 0], self.tx),
            remote(self.share(k, self.B), self.o.at[slot, self.B], r.hs.at[k, 1], r.hr.at[k, 1], self.ty),
        ]
        if when is None:
            for copy in copies:
                copy.start()
        else:
            @pl.when(when)
            def _():
                for copy in copies:
                    copy.start()
        self.spreads[k] = copies

    def second(self, k):
        r, o, zz = self.r, self.o, self.go[k]
        s, sx, sy = self.dev(zz), self.dev(zz, 0, 1), self.dev(zz, 1, 0)
        self.send(self.share(k, self.A), o.at[s, self.A], r.cs.at[k, 0], r.cr.at[k, 0], self.ty)
        self.send(self.share(k, self.B), o.at[s, self.B], r.ds.at[k, 0], r.dr.at[k, 0], self.tx)
        remote(o.at[sx, self.A], o.at[sx, self.A], r.hs.at[k, 0], r.hr.at[k, 0], self.tx).wait_recv()
        self.send(o.at[sx, self.A], o.at[sx, self.A], r.cs.at[k, 1], r.cr.at[k, 1], self.ty)
        remote(o.at[sy, self.B], o.at[sy, self.B], r.hs.at[k, 1], r.hr.at[k, 1], self.ty).wait_recv()
        self.send(o.at[sy, self.B], o.at[sy, self.B], r.ds.at[k, 1], r.dr.at[k, 1], self.tx)
        self.to_sibling(sx, self.A)
        self.to_sibling(sy, self.B)

    def third(self, k):
        r, o, zz = self.r, self.o, self.go[k]
        for slot, part, ss, rr, i, target in (
            (self.dev(zz, 1, 0), self.A, r.cs, r.cr, 0, self.ty),
            (self.dev(zz, 0, 1), self.B, r.ds, r.dr, 0, self.tx),
            (self.dev(zz, 1, 1), self.A, r.cs, r.cr, 1, self.ty),
            (self.dev(zz, 1, 1), self.B, r.ds, r.dr, 1, self.tx),
        ):
            remote(o.at[slot, part], o.at[slot, part], ss.at[k, i], rr.at[k, i], target).wait_recv()
            self.to_sibling(slot, part)

    def finish(self):
        for i in range(4):
            self.onward(i, True)
        for copy in self.sends + [copy for pair in self.spreads.values() for copy in pair]:
            copy.wait_send()


def as_column(row):
    return jnp.transpose(jnp.broadcast_to(row, (128, row.shape[1])))[:, 0:1]


def route(n, parts, r):
    owner = jnp.concatenate([r.owners[0:1, :], r.owners[1:2, :]], axis=1)
    local = jnp.concatenate([r.locals[0:1, :], r.locals[1:2, :]], axis=1)
    wants, edges = owner.shape[1], r.owners.shape[1]
    earlier = lax.broadcasted_iota(jnp.int32, (wants, wants), 0) < lax.broadcasted_iota(jnp.int32, (wants, wants), 1)
    same = (as_column(owner) == owner) & earlier
    rank = jnp.sum(jnp.where(same, 1.0, 0.0), axis=0, keepdims=True).astype(jnp.int32)
    position = owner * parts[0] + rank
    if len(parts) > 1:
        position = jnp.where(rank < parts[0], position, n * parts[0] + owner * parts[1] + rank - parts[0])
    r.pos_s[...], r.pos_r[...] = position[:, :edges], position[:, edges:]
    column = as_column(position)
    r.pos[:, 0:1], r.pos[:, 1:2] = column[:edges, :], column[edges:, :]
    slots = n * sum(parts)
    match = lax.broadcasted_iota(jnp.int32, (slots, wants), 0) == position
    asking = jnp.sum(jnp.where(match, local.astype(F32) + 1.0, 0.0), axis=1, keepdims=True).astype(jnp.int32) - 1
    put_slot_rows(several(r, "ask"), jnp.broadcast_to(asking, (slots, 128)))


def count_mask(r):
    sea = (lax.broadcasted_iota(jnp.int32, (VARS, 1), 0) < SEA_VARS).astype(jnp.int32)
    total = jnp.zeros((1, 128), F32)
    for i in range(r.level.shape[1] // 128):
        at = slice(128 * i, 128 * (i + 1))
        total += col((r._level[:, at] * (1 - sea * r.land[:, at])).astype(F32))
    r.number[...] = jnp.zeros_like(r.number)
    r.number[0:1, :] = total


def start_kernel(n, parts, jobs, bm, r):
    me = lax.axis_index("dev")
    gather = Gather(r, r.w, r.shares)
    greet_start(n, me)
    mask = pltpu.make_async_copy(r.level, r._level, r.gown.at[2])
    mask.start()
    rows = r.master.shape[0]
    r.w[rows // 16 * 16 :, :] = jnp.zeros_like(r.w[rows // 16 * 16 :, :])
    r.w[:rows, :] = r.master[...].astype(BF16)
    greet_wait(n)
    gather.begin()
    route(n, parts, r)
    asks, asked = several(r, "ask"), several(r, "asked")
    swap_start(n, me, asks, asked, r.aown, r.a1, r.b1)
    mask.wait()
    count_mask(r)
    number = pltpu.make_async_copy(r.number, r.numbers.at[me], r.gown.at[1])
    number.start()
    def go(j, carry):
        t = lax.rem(me + j, n)
        remote(r.number, r.numbers.at[me], r.ns.at[j], r.nr.at[j], t).start()
        return carry
    lax.fori_loop(1, n, go, 0)
    gather.second(0)
    gather.arrive(1)
    gather.spread(1)
    gather.arrive(2)
    gather.third(0)
    gather.second(1)
    gather.spread(2, gather.z < 2)
    gather.arrive(3)
    gather.spread(2, gather.z >= 2)
    gather.third(1)
    gather.second(2)
    swap_wait(n, me, asks, asked, r.aown, r.a1, r.b1)
    columns = slot_rows(asked)
    r.want[...] = columns[:, 0:1]
    r.served[...] = jnp.transpose(columns)[0:1, :]
    chosen = pick(r.want[...], 0, r.x.shape[1])
    rows = contract(chosen, r.x[...], 1, 1).astype(BF16)
    gather.spread(3)
    gather.third(2)
    plane_0 = len(gather.sibling)
    gather.second(3)
    gather.from_sibling(plane_0)
    gather.mine.wait()
    relay = Relay(r, r.shares)
    block = [[job for job in jobs if job[0] == b] for b in range(jobs[-1][0] + 1)]
    names = ["p", "g", "e"]
    def into(b):
        for job in block[b]:
            target = getattr(r, "_" + names[b] + job[1][1:])
            relay.run(job, target.at[pl.ds(job[2], min(LATENT, target.shape[0] - job[2]))], getattr(r, "_" + names[b] + "_vec"))
    for vec in (r._p_vec, r._g_vec, r._e_vec, r.vecs):
        vec[...] = jnp.zeros_like(vec)
    for job in block[0]:
        relay.load(job)
    into(0)
    for job in block[1]:
        relay.load(job)
    _, act = activate(contract(rows, r._p_in[:VARS, :], 1, 0) + r._p_vec[0:1, :])
    hat, _ = second_half(act, r._p_out, r._p_vec)
    r._slots[...] = scale_shift(hat, r._p_vec)
    away, here, back, out = (several(r, name) for name in ("away", "here", "back", "landed"))
    put_slot_rows(away, r._slots[...].astype(BF16))
    swap_start(n, me, away, here, r.own.at[0], r.s1, r.r1)
    stores = store_all(r, r.ssem, "slots")
    def body(node, low):
        i = pl.program_id(0)
        u = r.x[:, pl.ds(pl.multiple_of(i * bm, bm), bm)]
        _, act = activate(contract(u, r._p_in[:VARS, :], 0, 0) + r._p_vec[0:1, :])
        hat, _ = second_half(act, r._p_out, r._p_vec)
        new = scale_shift(hat, r._p_vec)
        node[...] = new
        low[...] = new.astype(BF16)
    pltpu.emit_pipeline(body, grid=(r.node.shape[0] // bm,), in_specs=[], out_specs=[rows_block(bm)] * 2)(r.node, r.low)
    gather.third(3)
    gather.from_sibling(len(gather.sibling))
    for b in range(2, len(block)):
        for job in block[b]:
            relay.load(job)
    into(1)
    into(2)
    _, act = activate(first_half([r.source[...]], r._g_in, r._g_vec))
    hat, _ = second_half(act, r._g_out, r._g_vec)
    r._edge[...] = scale_shift(hat, r._g_vec)
    e = r._edge[...].astype(BF16)
    r.edge_low[...] = e
    count = r.want.shape[0]
    pre = first_half([e], r._e_in, r._e_vec)
    pick_s, pick_r = pick(r.pos[:, 0:1], 0, count), pick(r.pos[:, 1:2], 0, count)
    put_r = place(r.pos_r[...], 0, count)
    kept = [f"m{b}{part}" for b in range(3) for part in ("_in", "_out", "_vec")]
    for i, name in enumerate(kept):
        b, part = int(name[1]), name[2:]
        copy = pltpu.make_async_copy(getattr(r, "_" + names[b] + part), getattr(r, name), r.osem.at[i])
        copy.start()
        stores.append(copy)
    swap_wait(n, me, away, here, r.own.at[0], r.s1, r.r1)
    rows = slot_rows(here)
    s = mm(pick_s, rows).astype(BF16)
    v = mm(pick_r, rows).astype(BF16)
    pre = pre + mm(s, r._e_in[LATENT : 2 * LATENT, :]) + mm(v, r._e_in[2 * LATENT :, :])
    _, act = activate(pre)
    hat, _ = second_half(act, r._e_out, r._e_vec)
    new = r._edge[...] + scale_shift(hat, r._e_vec)
    put_slot_rows(back, mm(put_r, new.astype(BF16)).astype(BF16))
    swap_start(n, me, back, out, r.own.at[1], r.s2, r.r2)
    r.edge[...] = new
    r.sent[...], r.recv[...] = s, v
    at = len(kept)
    late = [job for b in range(3, len(block)) for job in block[b]]
    for i, job in enumerate(late):
        b, name, first = job[:3]
        relay.run(job, r.made.at[i], r.vecs.at[b])
        copy = pltpu.make_async_copy(r.made.at[i], getattr(r, f"m{b}{name[1:]}").at[pl.ds(first, LATENT)], r.osem.at[at + i])
        copy.start()
        stores.append(copy)
    at += len(late)
    for b in range(3, len(block)):
        copy = pltpu.make_async_copy(r.vecs.at[b], getattr(r, f"m{b}_vec"), r.osem.at[at + b])
        copy.start()
        stores.append(copy)
    gather.finish()
    def end(j, carry):
        t = lax.rem(me + j, n)
        remote(r.number, r.numbers.at[me], r.ns.at[j], r.nr.at[j], t).wait()
        return carry
    lax.fori_loop(1, n, end, 0)
    number.wait()
    for store in stores:
        store.wait()
    swap_wait(n, me, back, out, r.own.at[1], r.s2, r.r2)


def start(n, parts, cid, master, owners, locals_, level, land, source, x, segments, share_rows, bm=512):
    pad_rows = (share_rows + 31) // 32 * 32
    jobs = relay_plan(segments, share_rows)
    blocks = segments[-1][0] + 1
    count, edges, rows = n * sum(parts), source.shape[0], x.shape[1]
    V = pl.BlockSpec(memory_space=pltpu.VMEM)
    tables = [(n, p, 128) for p in parts]
    shapes = [(n, p, LATENT) for p in parts]
    inputs = dict(master=(master, V), owners=(owners, V), locals=(locals_, V), level=(level, ANY), land=(land, V), source=(source, V), x=(x, V))
    index = lambda *s: (shaped(*s, dtype=jnp.int32), V)
    low = lambda r: shaped(r, LATENT, dtype=BF16)
    outputs = dict(shares=(shaped(n, pad_rows, 128, dtype=BF16), ANY), numbers=(shaped(n, 8, 128), ANY))
    outputs |= dict(pos=index(edges, 2), pos_s=index(1, edges), pos_r=index(1, edges))
    outputs |= dict(want=index(count, 1), served=index(1, count))
    outputs |= dict(edge=(shaped(edges, LATENT), V), edge_low=(low(edges), V), sent=(low(edges), V), recv=(low(edges), V))
    outputs |= numbered("landed", [(shaped(*s, dtype=BF16), ANY) for s in shapes])
    outputs |= dict(node=(shaped(rows, LATENT), ANY), low=(low(rows), ANY), slots=(shaped(count, LATENT), ANY))
    made = {}
    for b, name, shape, _, _ in segments:
        if name in ("w_in", "w_out") and shape[1] == LATENT:
            made[f"m{b}{name[1:]}"] = (-(-shape[0] // 128) * 128, LATENT)
    outputs |= {name: (shaped(*shape, dtype=BF16), ANY) for name, shape in made.items()}
    outputs |= {f"m{b}_vec": (shaped(8, LATENT), ANY) for b in range(blocks)}
    scratch = swap_scratch(shapes, n)
    for name in ("ask", "asked"):
        scratch |= numbered(name, [pltpu.VMEM(s, jnp.int32) for s in tables])
    scratch |= dict(w=pltpu.VMEM((pad_rows, 128), BF16), number=pltpu.VMEM((8, 128), F32), _level=pltpu.VMEM(level.shape, jnp.int32))
    scratch |= dict(aown=DMA((len(parts),)), a1=DMA((len(parts), n)), b1=DMA((len(parts), n)), ns=DMA((n,)), nr=DMA((n,)), gown=DMA((3,)))
    for b, name in enumerate(("_p", "_g", "_e")):
        scratch |= {name + "_in": pltpu.VMEM(made[f"m{b}_in"], BF16), name + "_out": pltpu.VMEM(made[f"m{b}_out"], BF16), name + "_vec": pltpu.VMEM((8, LATENT), F32)}
    stage = sum(part[2] for job in jobs for part in job[5])
    late = sum(1 for job in jobs if job[0] > 2)
    scratch |= dict(_slots=pltpu.VMEM((count, LATENT), F32), _edge=pltpu.VMEM((edges, LATENT), F32), ssem=DMA((1,)))
    scratch |= dict(stage=pltpu.VMEM((stage, 128), BF16), lines=pltpu.VMEM((16 + 4 * LATENT + 64, 128), F32), made=pltpu.VMEM((late, LATENT, LATENT), BF16))
    scratch |= dict(vecs=pltpu.VMEM((blocks, 8, LATENT), F32), isem=DMA((sum(len(job[5]) for job in jobs),)), osem=DMA((9 + late + blocks,)))
    scratch |= dict(zs=DMA((2, 4)), zr=DMA((4,)), bs=DMA((28,)), br=DMA((28,)))
    for name in ("h", "c", "d"):
        scratch |= {name + "s": DMA((4, 2)), name + "r": DMA((4, 2))}
    return named_call(functools.partial(start_kernel, n, parts, jobs, bm), "start", inputs, outputs, scratch, cid=cid)


def accumulate(dst, src, rows):
    step = 80
    whole = rows // step
    def body(i, carry):
        at = pl.ds(pl.multiple_of(i * step, 8), step)
        dst[at] = dst[at] + src[at]
        return carry
    lax.fori_loop(0, whole, body, 0)
    if rows % step:
        at = pl.ds(whole * step, rows % step)
        dst[at] = dst[at] + src[at]


def where_am_i():
    me = lax.axis_index("dev")
    return me, me // 8, lax.rem(me // 4, 2), lax.rem(me // 2, 2), lax.rem(me, 2)


def device_at(z, y, x, c):
    return ((z * 2 + y) * 2 + x) * 2 + c


def plane_scratch(units, rows):
    upper = rows // 16 * 8
    lower = rows - upper
    F = lambda *s: pltpu.VMEM((units,) + s + (128,), F32)
    refs = dict(pL=F(4, rows), pR=F(4, rows), pYA=F(2, upper), pXA=F(upper), pXB=F(2, lower), pYB=F(lower))
    sems = {}
    for name, count in (("c", 4), ("a1", 2), ("a2", 1), ("b1", 2), ("b2", 1)):
        sems["p" + name + "s"] = DMA((units, count))
        sems["p" + name + "r"] = DMA((units, count))
    return refs | sems | dict(pl=DMA((units, 4)))


class PlaneSum:
    def __init__(self, r, rows):
        self.r, self.rows = r, rows
        self.upper = rows // 16 * 8
        self.A, self.B = pl.ds(0, self.upper), pl.ds(self.upper, rows - self.upper)
        _, z, y, x, c = where_am_i()
        self.y, self.x, self.c = y, x, c
        self.tx, self.ty, self.tc = device_at(z, y, 1 - x, c), device_at(z, 1 - y, x, c), device_at(z, y, x, 1 - c)
        self.own = y * 2 + x
        self.sends = []

    def send(self, *args):
        copy = remote(*args)
        copy.start()
        self.sends.append(copy)

    def fetch(self, u, source):
        r = self.r
        self.example = source(0, 0)
        for i in range(4):
            self.send(source(i, 1 - self.c), r.pR.at[u, i], r.pcs.at[u, i], r.pcr.at[u, i], self.tc)
            pltpu.make_async_copy(source(i, self.c), r.pL.at[u, i], r.pl.at[u, i]).start()

    def pair(self, u):
        r, L = self.r, self.r.pL
        for i in range(4):
            pltpu.make_async_copy(self.example, L.at[u, i], r.pl.at[u, i]).wait()
            remote(L.at[u, i], r.pR.at[u, i], r.pcs.at[u, i], r.pcr.at[u, i], self.tc).wait_recv()
            accumulate(L.at[u, i], r.pR.at[u, i], self.rows)
        for j in range(2):
            self.send(L.at[u, (1 - self.y) * 2 + j, self.A], r.pYA.at[u, j], r.pa1s.at[u, j], r.pa1r.at[u, j], self.ty)
            self.send(L.at[u, j * 2 + 1 - self.x, self.B], r.pXB.at[u, j], r.pb1s.at[u, j], r.pb1r.at[u, j], self.tx)

    def middle(self, u):
        r, L = self.r, self.r.pL
        up, low = self.upper, self.rows - self.upper
        for j in range(2):
            remote(L.at[u, 0, self.A], r.pYA.at[u, j], r.pa1s.at[u, j], r.pa1r.at[u, j], self.ty).wait_recv()
            accumulate(L.at[u, self.y * 2 + j, self.A], r.pYA.at[u, j], up)
        self.send(L.at[u, self.y * 2 + 1 - self.x, self.A], r.pXA.at[u], r.pa2s.at[u, 0], r.pa2r.at[u, 0], self.tx)
        for j in range(2):
            remote(L.at[u, 0, self.B], r.pXB.at[u, j], r.pb1s.at[u, j], r.pb1r.at[u, j], self.tx).wait_recv()
            accumulate(L.at[u, j * 2 + self.x, self.B], r.pXB.at[u, j], low)
        self.send(L.at[u, (1 - self.y) * 2 + self.x, self.B], r.pYB.at[u], r.pb2s.at[u, 0], r.pb2r.at[u, 0], self.ty)

    def last(self, u):
        r, L = self.r, self.r.pL
        remote(L.at[u, 0, self.A], r.pXA.at[u], r.pa2s.at[u, 0], r.pa2r.at[u, 0], self.tx).wait_recv()
        accumulate(L.at[u, self.own, self.A], r.pXA.at[u], self.upper)
        remote(L.at[u, 0, self.B], r.pYB.at[u], r.pb2s.at[u, 0], r.pb2r.at[u, 0], self.ty).wait_recv()
        accumulate(L.at[u, self.own, self.B], r.pYB.at[u], self.rows - self.upper)

    def result(self, u):
        return self.r.pL.at[u, self.own]

    def finish(self):
        for copy in self.sends:
            copy.wait_send()


def reduce_kernel(n, chunks, share_rows, lead, bm, r):
    me, z, y, x, c = where_am_i()
    greet(n, me)
    rows = chunks.rows
    plane = PlaneSum(r, rows)
    def by_plane(*goals):
        return jnp.where(z == 0, goals[0], jnp.where(z == 1, goals[1], jnp.where(z == 2, goals[2], goals[3])))
    goal = [by_plane(2, 3, 3, 1), by_plane(1, 2, 0, 0), by_plane(3, 0, 1, 2), z]

    def fetch(u):
        if u < 4:
            plane.fetch(u, lambda i, core: r.flat0.at[goal[u] * 8 + i * 2 + core])

    def along(u):
        at = lax.rem(z - goal[u] + 4, 4) - 1
        return remote(plane.result(u), r.zq.at[at], r.zqs.at[u], r.zqr.at[at], device_at(goal[u], y, x, c))

    fetch(0)
    clear(r.d_in, r.d_out, r.d_vec)
    plane.pair(0)
    def body(g_node, x_rows):
        encode_back_rows(pl.program_id(0) * bm, bm, r.served, several(r, "landed"), g_node, x_rows, r.p_in, r.p_out, r.p_vec, r.d_in, r.d_out, r.d_vec)
    pltpu.emit_pipeline(body, grid=(r.g_node.shape[0] // bm,), in_specs=[rows_block(bm), pl.BlockSpec((VARS, bm), lambda i: (0, i))], out_specs=[])(r.g_node, r.x)
    encode_pack(r.packed, r.d_in, r.d_out, r.d_vec)
    stores = Stores({0: r.flat0}, chunks, r.fsem)
    stores.put(r.packed, 0)
    stores.wait()
    fetch(1)
    plane.middle(0)
    for u in (1, 2, 3):
        fetch(u + 1)
        plane.pair(u)
        plane.last(u - 1)
        along(u - 1).start()
        plane.middle(u)
    plane.last(3)
    first = lax.rem(lead + share_rows * me, 8)
    r.both[0:8, :] = jnp.zeros((8, 128), F32)
    width = r.err.shape[1] // 128
    for j in range(8):
        r.both[8 + j : 9 + j, :] = r.err[:, 128 * j : 128 * (j + 1)] if j < width else jnp.zeros((1, 128), F32)
    own = plane.result(3)

    def piece(at, count):
        rows_here = pl.ds(at, count)
        v = own[rows_here] + r.zq[0, rows_here] + (r.zq[1, rows_here] + r.zq[2, rows_here])
        r.out[rows_here] = v
        row = at + lax.broadcasted_iota(jnp.int32, v.shape, 0)
        v = jnp.where((row >= first) & (row < first + share_rows), v, 0.0)
        v = v * v
        r.both[0:8, :] += jnp.sum(v.reshape(count // 8, 8, 128), axis=0)

    for at in range(3):
        remote(own, r.zq.at[at], r.zqs.at[at], r.zqr.at[at], plane.tc).wait_recv()
    step = 80
    def several_tiles(i, carry):
        piece(pl.multiple_of(i * step, 8), step)
        return carry
    lax.fori_loop(0, rows // step, several_tiles, 0)
    if rows % step:
        piece(rows // step * step, rows % step)
    q_own = pltpu.make_async_copy(r.both, r.all.at[me], r.own)
    q_own.start()
    def go(j, carry):
        t = lax.rem(me + j, n)
        remote(r.both, r.all.at[me], r.qs.at[j], r.qr.at[j], t).start()
        return carry
    lax.fori_loop(1, n, go, 0)
    plane.finish()
    for u in range(3):
        along(u).wait_send()
    def end(j, carry):
        t = lax.rem(me + j, n)
        remote(r.both, r.all.at[me], r.qs.at[j], r.qr.at[j], t).wait()
        return carry
    lax.fori_loop(1, n, end, 0)
    q_own.wait()
    sums = jnp.sum(r.all[...], axis=0)
    whole = lambda v: jnp.sum(jnp.sum(v, axis=1, keepdims=True), axis=0, keepdims=True)
    norm = jnp.sqrt(whole(sums[0:8, :]))
    r.norm[...] = norm
    r.factor[...] = jnp.minimum(1.0, clip_limit / norm)
    r.error[...] = whole(sums[8:16, :])


def reduce_gradient(n, chunks, flat, errors, share_rows, lead, encoder, cid, bm=512):
    served, landed, g_node, x, block = encoder
    V = pl.BlockSpec(memory_space=pltpu.VMEM)
    F = lambda *s: pltpu.VMEM(s + (128,), F32)
    rows = chunks.rows
    inputs = dict(flat_in=(flat, ANY), err=(errors, V), served=(served, V), g_node=(g_node, ANY), x=(x, ANY))
    inputs |= numbered("landed", [(v, V) for v in landed])
    inputs |= {name: (v, V) for name, v in zip(("p_in", "p_out", "p_vec"), block)}
    outputs = dict(flat0=(shaped(*flat.shape), ANY), out=(shaped(rows, 128), V)) | {name: (shaped(1, 1), V) for name in ("norm", "factor", "error")}
    scratch = plane_scratch(4, rows) | dict(zq=F(3, rows), zqs=DMA((3,)), zqr=DMA((3,)))
    scratch |= dict(both=F(16), all=F(n, 16), own=DMA, qs=DMA((n,)), qr=DMA((n,)), packed=packed_rows(VARS, 4), fsem=DMA((STORES,)))
    scratch |= sums_scratch("d", block[0].shape[0])
    body = functools.partial(reduce_kernel, n, chunks, share_rows, lead, bm)
    made = named_call(body, "reduce_gradient", inputs, outputs, scratch, aliases=dict(flat_in="flat0"), cid=cid)
    return made.out, made.norm[0, 0], made.factor[0, 0], made.error[0, 0]


def make_parts(capacity):
    whole = capacity // 16 * 16
    rest = (capacity - whole + 3) // 4 * 4
    return [rows for rows in (whole, rest) if rows]


def make_asks(edge_owners, edge_local, devices, parts):
    owner = edge_owners.reshape(-1)
    local = edge_local.reshape(-1)
    wants = owner.shape[0]
    order = jnp.arange(wants, dtype=jnp.int32)
    before = (owner[:, None] == owner[None, :]) & (order[None, :] < order[:, None])
    ranking = jnp.sum(before.astype(jnp.int32), axis=1)
    capacity = sum(parts)
    slots = jnp.arange(devices * capacity, dtype=jnp.int32)
    place = owner * capacity + ranking
    asking = jnp.sum(jnp.where(slots[:, None] == place[None, :], local[None, :] + 1, 0), axis=1) - 1
    position = owner * parts[0] + ranking
    if len(parts) > 1:
        position = jnp.where(ranking < parts[0], position, devices * parts[0] + owner * parts[1] + ranking - parts[0])
    return (position, asking.reshape(devices, capacity))


def widen(values, width):
    return jnp.pad(values, ((0, 0), (0, width - values.shape[1])))


def make_block(params):
    rows = params["w_in"].shape[0]
    w_in = jnp.pad(params["w_in"], ((0, -rows % 128), (0, 0)))
    w_out = widen(params["w_out"], (params["w_out"].shape[1] + 127) // 128 * 128)
    names = [name for name in ("b_in", "b_out", "gain", "shift") if name in params]
    vectors = [widen(params[name][None], LATENT) for name in names]
    vectors.append(jnp.zeros((8 - len(vectors), LATENT), jnp.bfloat16))
    return (w_in, w_out, jnp.concatenate(vectors).astype(jnp.float32))


def relaid_blocks(made, segments, share_rows):
    shares = made.shares
    def rows_of(first, last):
        parts = []
        while first < last:
            owner, low = divmod(first, share_rows)
            size = min(last - first, share_rows - low)
            parts.append(shares[owner, low : low + size])
            first += size
        return jnp.concatenate(parts) if len(parts) > 1 else parts[0]
    [(shape, begin, size)] = [(s, o, e) for _, name, s, o, e in segments if name == "w_out" and s[1] != LATENT]
    wide = shape[1]
    first, end = begin // 128, (begin + size) // 128
    w_out = widen(rows_of(first, end).reshape(shape), (wide + 127) // 128 * 128)
    bias = rows_of(end, end + (wide + 127) // 128).reshape(-1)[:wide, None].astype(jnp.float32)
    blocks = []
    for b in range(segments[-1][0] + 1):
        get = lambda part: getattr(made, f"m{b}{part}", w_out)
        blocks.append((get("_in"), get("_out"), get("_vec")))
    return blocks, bias


def local(
    inputs,
    targets,
    geometry,
    land_sea,
    level_mask,
    edge_owners,
    edge_local,
    step_count,
    master,
    first_moment,
    second_moment,
    ema,
):
    segments, total = layout(LATENT, VARS, GEO, LAYERS)
    devices = lax.axis_size("dev")
    share = master.shape[0]
    mine = devices == 32 and share % 128 == 0
    parts = make_parts(5 * edge_owners.shape[0] // (2 * devices))
    capacity = sum(parts)
    x = inputs.T
    geo = widen(geometry, 128)
    level, land = level_mask.T, land_sea[None, :]
    if mine:
        share_rows = share // 128
        begun = start(devices, parts, 1, master.reshape(share_rows, 128), edge_owners.T, edge_local.T, level, land, geo, x, segments, share_rows)
        blocks, bias = relaid_blocks(begun, segments, share_rows)
        want, served, pos, pos_s, pos_r = begun.want, begun.served, begun.pos, begun.pos_s, begun.pos_r
        count = jnp.sum(begun.numbers)
    else:
        position, asking = make_asks(edge_owners, edge_local, devices, parts)
        pos = position.reshape(-1, 2)
        pos_s, pos_r = pos[:, 0][None, :], pos[:, 1][None, :]
        ocean = (jnp.arange(VARS) < SEA_VARS).astype(jnp.int32)
        counted = jnp.sum(level_mask * (1 - land_sea[:, None] * ocean[None, :])).astype(jnp.float32)
        full_weights = lax.all_gather(master.astype(jnp.bfloat16), "dev", axis=0, tiled=True)
        whole = unpack(full_weights, segments)
        blocks = [make_block(b) for b in whole]
        bias = whole[-1]["b_out"][:, None].astype(jnp.float32)
        served = lax.all_to_all(asking, "dev", 0, 0, tiled=True)
        count = lax.psum(counted, "dev")
        served = jnp.concatenate([served[:, sum(parts[:i]) : sum(parts[: i + 1])].reshape(-1) for i in range(len(parts))])
        want = served[:, None]
        served = served[None, :]
    routes = (want, served, pos, pos_s, pos_r)
    if mine:
        done = [begun]
    else:
        done = [edge_forward(devices, parts, 3, geo, routes, blocks[2], blocks[0], inputs.shape[0], x=x, geo_block=blocks[1])]
    for k in range(1, LAYERS):
        f = done[-1]
        done.append(
            edge_forward(
                devices, parts, 4, f.edge, routes, blocks[2 + 2 * k], blocks[1 + 2 * k], inputs.shape[0],
                landed=several(f, "landed"), node=f.node, slots=f.slots,
            )
        )
    pieces = [4 * s for s in (VARS + LATENT + 4, GEO + LATENT + 4) + (3 * LATENT + LATENT + 4, 2 * LATENT + LATENT + 4) * LAYERS]
    lead = 4
    places = [0] + [lead + sum(pieces[: i + 1]) for i in range(len(pieces))]
    flat_rows = (lead + PARAMS // 128 + 15) // 16 * 16 + 8
    if mine:
        begins = [(lead + share_rows * d) // 8 * 8 for d in range(devices)]
        chunks = Chunks(begins, (share_rows + 6 + 15) // 16 * 16, [0, 32])
    else:
        chunks = Chunks([0], flat_rows, [0, 1])
    dec_at = places[-1]
    tail_at = dec_at + 4 * LATENT
    k = LAYERS - 1
    flat, g_node, *outgoing, d_out, d_first, d_bias, errors = turn(
        served, want, several(done[k], "landed"), done[k].node, x, targets.T, level, land, count.reshape(1, 1),
        blocks[3 + 2 * k], blocks[-1], bias, chunks, places[3 + 2 * k], dec_at,
    )
    flats = {len(chunks.cuts) - 2: flat}
    tail = jnp.concatenate([d_first[0], d_out[:, :VARS].reshape(-1), d_bias[:VARS, 0]])
    tail_rows = flat_rows - tail_at
    tail = jnp.pad(tail, (0, tail_rows * 128 - tail.shape[0])).reshape(tail_rows, 128)
    g_edge, landed = None, None
    for k in reversed(range(LAYERS)):
        more = {}
        if k == LAYERS - 1:
            more |= dict(outgoing=outgoing, g_node=g_node, tail=tail, tail_at=tail_at)
        else:
            more |= dict(
                node=(landed, g_slots, done[k].slots, done[k + 1].sums_s, g_node, done[k].low, done[k + 1].sums, blocks[3 + 2 * k]),
                node_at=places[3 + 2 * k],
            )
        if k == 0:
            more |= dict(geo=(geo, blocks[1]), geo_at=places[1])
        f = done[k]
        b = edge_backward(
            devices, parts, 5 + (LAYERS - 1 - k), (f.edge_low, f.sent, f.recv), routes, blocks[2 + 2 * k], chunks, flats, places[2 + 2 * k],
            g_edge=g_edge, **more,
        )
        g_edge, landed = b.edge_prev, several(b, "landed")
        g_slots = b.g_slots
        if k < LAYERS - 1:
            g_node = b.g_prev
    if mine:
        encoder = (served, landed, g_node, x, blocks[0])
        summed, grad_norm, factor, error_sum = reduce_gradient(devices, chunks, flats[0], errors, share_rows, lead, encoder, 2)
        skip = lax.rem(lead + share_rows * lax.axis_index("dev"), 8)
        own_grad = lax.dynamic_slice_in_dim(summed, skip, share_rows).reshape(-1)
    else:
        flat = encode_backward(served, landed, g_node, x, blocks[0], chunks, flats[0])
        own_grad = lax.psum_scatter(flat[0, lead : lead + PARAMS // 128].reshape(-1), "dev", scatter_dimension=0, tiled=True)
        error_sum, squares = lax.psum((jnp.sum(errors), jnp.sum(own_grad * own_grad)), "dev")
        grad_norm = jnp.sqrt(squares)
        factor = jnp.minimum(1.0, clip_limit / grad_norm)
    loss = error_sum / jnp.maximum(count, 1.0)
    clipped = own_grad * factor
    step = step_count[0].astype(jnp.float32)
    new_first = beta_one * first_moment + (1.0 - beta_one) * clipped
    new_second = beta_two * second_moment + (1.0 - beta_two) * clipped * clipped
    first_hat = new_first / (1.0 - beta_one**step)
    second_hat = new_second / (1.0 - beta_two**step)
    new_master = master - learn_rate * (
        first_hat / (jnp.sqrt(second_hat) + adam_eps) + decay_rate * master
    )
    new_ema = ema_keep * ema + (1.0 - ema_keep) * new_master
    return (new_master, new_first, new_second, new_ema, loss, grad_norm)


def solution(mesh):
    in_specs = (
        P("dev", None),
        P("dev", None),
        P("dev", None),
        P("dev"),
        P("dev", None),
        P("dev", None),
        P("dev", None),
        P(),
        P("dev"),
        P("dev"),
        P("dev"),
        P("dev"),
    )
    out_specs = (P("dev"), P("dev"), P("dev"), P("dev"), P(), P())
    return jax.shard_map(local, mesh=mesh, in_specs=in_specs, out_specs=out_specs, check_vma=False)
```
